32 devices in a mesh: dp: 4 (over z), row: 4 (over y, core), col: 2 (over x).
Axes of the slice: x: 2, y: 2, z: 4, core: 2. Of those that a mesh axis runs over, the one named last changes fastest.
Arguments:
- tokens: bfloat16 [4096, 2048], P(('dp', 'col'), 'row'), may hold values from -6 to 6
- ln1_gain: float32 [2048], P('row'), may hold values from 0.5 to 2
- ln1_shift: float32 [2048], P('row'), may hold values from -3 to 3
- qkv_weight: bfloat16 [2048, 16, 3, 128], P('row', 'col'), may hold values from -1 to 1
- qv_bias: float32 [16, 2, 128], P('col'), may hold values from -3 to 3
- out_weight: bfloat16 [16, 128, 2048], P('col', None, 'row'), may hold values from -1.5 to 1.5
- out_bias: float32 [2048], P('row'), may hold values from -3 to 3
- ln2_gain: float32 [2048], P('row'), may hold values from 0.5 to 2
- ln2_shift: float32 [2048], P('row'), may hold values from -3 to 3
- up_weight: bfloat16 [2048, 8192], P('row', 'col'), may hold values from -1 to 1
- up_bias: float32 [8192], P('col'), may hold values from -3 to 3
- down_weight: bfloat16 [8192, 2048], P('col', 'row'), may hold values from -0.125 to 0.125
- down_bias: float32 [2048], P('row'), may hold values from -3 to 3
- span_starts: int32 [4, 2], P('dp'), may hold values from 0 to 768, as said below
- cotangent: bfloat16 [4096, 2048], P(('dp', 'col'), 'row'), may hold values from -6 to 6
Outputs:
- output: bfloat16 [4096, 2048], P(('dp', 'col'), 'row')
- tokens_grad: bfloat16 [4096, 2048], P(('dp', 'col'), 'row')
- ln1_gain_grad: float32 [2048], P('row')
- ln1_shift_grad: float32 [2048], P('row')
- qkv_weight_grad: float32 [2048, 16, 3, 128], P('row', 'col')
- qv_bias_grad: float32 [16, 2, 128], P('col')
- out_weight_grad: float32 [16, 128, 2048], P('col', None, 'row')
- out_bias_grad: float32 [2048], P('row')
- ln2_gain_grad: float32 [2048], P('row')
- ln2_shift_grad: float32 [2048], P('row')
- up_weight_grad: float32 [2048, 8192], P('row', 'col')
- up_bias_grad: float32 [8192], P('col')
- down_weight_grad: float32 [8192, 2048], P('col', 'row')
- down_bias_grad: float32 [2048], P('row')
The draws below stay inside these ranges and needn't reach their ends.
Inputs may be any that keep to these rules, and one draw needn't show every extreme that they name: `span_starts`: each entry is a multiple of 256; the 2 entries of one sequence are distinct; row s belongs to sequence s.
All inputs are finite; a program needn't handle non-finite values.
Results may differ from the reference program's by a relative error of at most 0.015.
Values may be sent and summed in bfloat16 or wider, within the bound.
A program may use at most 192 MiB of HBM per device.

```python
import math
from functools import partial
import jax
import jax.numpy as jnp
from jax import lax

D = 2048
HEADS = 16
HEAD = 128
FF = 8192
NSPAN = 2
SPAN = 256
QBLOCK = 256
LENGTH = 1024
SEQ_ALL = 4
TOKENS = 4096


def draw_span_starts(key, part):
    row_keys = jax.random.split(key, SEQ_ALL)

    def draw_row(row_key):
        ordering = jax.random.permutation(row_key, LENGTH // SPAN)
        return ordering[:NSPAN] * SPAN
    return jax.vmap(draw_row)(row_keys).astype(jnp.int32)


def draw_up_weight(key, part):
    entries = jnp.clip(jax.random.normal(jax.random.fold_in(key, 11), (D, FF), jnp.float32), -6.0, 6.0)
    common = jnp.clip(jax.random.normal(jax.random.fold_in(key, 12), (FF,), jnp.float32), -4.0, 4.0)
    values = (entries + 0.5 * common[None, :]) * float(D) ** (-0.5)
    return values.astype(jnp.bfloat16)


def draw_qkv_weight(key, part):
    entries = jnp.clip(jax.random.normal(jax.random.fold_in(key, 21), (D, HEADS, 3, HEAD), jnp.float32), -6.0, 6.0)
    common = jnp.clip(jax.random.normal(jax.random.fold_in(key, 22), (HEADS, HEAD), jnp.float32), -4.0, 4.0)
    picked = (jnp.arange(3, dtype=jnp.int32) == 2).astype(jnp.float32)
    values = (entries + 0.5 * common[None, :, None, :] * picked[None, None, :, None]) * float(D) ** (-0.5)
    return values.astype(jnp.bfloat16)


def shard_levels(rng, shape, cuts, least, high):
    level, own = 1.0, jax.random.fold_in(rng, 6)
    for axis_at, blocks in cuts:
        steps = jnp.exp(jax.random.uniform(jax.random.fold_in(own, axis_at), (blocks,), jnp.float32, least / len(cuts), high / len(cuts)))
        level = level * jnp.repeat(steps, shape[axis_at] // blocks).reshape([-1 if axis == axis_at else 1 for axis in range(len(shape))])
    return level


def noise(rng, shape, width, most, shards=(), kind=jnp.bfloat16):
    loudness = shard_levels(rng, shape, shards, -0.22, 0.18) if shards else 1.0
    values = jax.random.normal(rng, shape, jnp.float32) * width * loudness
    return jnp.minimum(jnp.maximum(values, -most), most).astype(kind)


def setup_inputs(seed: int = 0) -> dict:
    arg_keys = jax.random.split(jax.random.key(seed), 16)
    tokens = noise(arg_keys[0], (TOKENS, D), 1.0, 6.0, ((0, 8), (1, 4)))
    ln1_gain = jnp.clip(jnp.exp(math.log(2.0) - 1.3862944 * jax.random.uniform(arg_keys[1], (D,), jnp.float32) ** shard_levels(arg_keys[1], (D,), ((0, 4),), -0.2, 0.2)), 0.5, 2.0)
    ln1_shift = noise(arg_keys[2], (D,), 0.5, 3.0, ((0, 4),), jnp.float32)
    qkv_weight = draw_qkv_weight(jax.random.fold_in(arg_keys[15], 71), 0)
    qv_bias = noise(arg_keys[4], (HEADS, 2, HEAD), 0.5, 3.0, ((0, 2),), jnp.float32)
    out_weight = noise(arg_keys[5], (HEADS, HEAD, D), (D // 128) ** -0.5, 1.5, ((0, 2), (2, 4)))
    out_bias = noise(arg_keys[6], (D,), 0.5, 3.0, ((0, 4),), jnp.float32)
    ln2_gain = jnp.clip(jnp.exp(math.log(2.0) - 1.3862944 * jax.random.uniform(arg_keys[7], (D,), jnp.float32) ** shard_levels(arg_keys[7], (D,), ((0, 4),), -0.2, 0.2)), 0.5, 2.0)
    ln2_shift = noise(arg_keys[8], (D,), 0.5, 3.0, ((0, 4),), jnp.float32)
    up_weight = draw_up_weight(jax.random.fold_in(arg_keys[15], 71), 0)
    up_bias = noise(arg_keys[10], (FF,), 0.5, 3.0, ((0, 2),), jnp.float32)
    down_weight = noise(arg_keys[11], (FF, D), (FF // 4) ** -0.5, 0.125, ((0, 2), (1, 4)))
    down_bias = noise(arg_keys[12], (D,), 0.5, 3.0, ((0, 4),), jnp.float32)
    span_starts = draw_span_starts(jax.random.fold_in(arg_keys[15], 71), 0)
    cotangent = noise(arg_keys[14], (TOKENS, D), 1.0, 6.0, ((0, 8), (1, 4)))
    return dict(tokens=tokens, ln1_gain=ln1_gain, ln1_shift=ln1_shift, qkv_weight=qkv_weight, qv_bias=qv_bias, out_weight=out_weight, out_bias=out_bias, ln2_gain=ln2_gain, ln2_shift=ln2_shift, up_weight=up_weight, up_bias=up_bias, down_weight=down_weight, down_bias=down_bias, span_starts=span_starts, cotangent=cotangent)


@jax.custom_vjp
def low(v):
    return lax.optimization_barrier(v.astype(jnp.bfloat16)).astype(jnp.float32)

@jax.custom_vjp
def low_back(v):
    return v

def low_keep(v):
    return (low(v), None)

def low_pass(kept, grad):
    return (grad,)

def back_keep(v):
    return (v, None)

def back_low(kept, grad):
    return (low(grad),)
low.defvjp(low_keep, low_pass)
low_back.defvjp(back_keep, back_low)
precise = lax.Precision.HIGHEST
epsilon = 1e-05
masked_score = -1e+30

def gelu_tanh(values):
    return 0.5 * values * (1.0 + jnp.tanh(0.7978845608028654 * (values + 0.044715 * values * values * values)))

def high_dot(left_side, right_side):
    return jnp.dot(left_side, right_side, precision=precise, preferred_element_type=jnp.float32)

def layer_norm(values, gain_row, bias_row):
    center = lax.optimization_barrier(jnp.mean(values, axis=-1, keepdims=True))
    spread = lax.optimization_barrier(jnp.mean(values * values, axis=-1, keepdims=True)) - center * center
    return (values - center) * lax.rsqrt(spread + epsilon) * gain_row + bias_row

def attend_sequence(queries, key_rows, value_rows, image_marks):
    positions = jnp.arange(LENGTH, dtype=jnp.int32)
    token_image = jnp.repeat(image_marks, SPAN)
    factor = 1.0 / math.sqrt(HEAD)

    def block_scores(block_index):
        begin = block_index * QBLOCK
        query_block = lax.dynamic_slice_in_dim(queries, begin, QBLOCK, 0)
        query_pos = begin + jnp.arange(QBLOCK, dtype=jnp.int32)
        query_image = lax.dynamic_slice_in_dim(token_image, begin, QBLOCK, 0)
        scores = low_back(factor * jnp.einsum('qhd,khd->hqk', query_block, key_rows, precision=precise))
        earlier = positions[None, :] <= query_pos[:, None]
        same_span = (positions[None, :] // SPAN == query_pos[:, None] // SPAN) & (query_image[:, None] > 0)
        allowed = earlier | same_span
        scores = jnp.where(allowed[None], scores, masked_score)
        highest = lax.optimization_barrier(jnp.max(scores, axis=2, keepdims=True))
        weights = jnp.exp(scores - highest)
        probabilities = weights / lax.optimization_barrier(jnp.sum(weights, axis=2, keepdims=True))
        return jnp.einsum('hqk,khd->qhd', low(probabilities), value_rows, precision=precise)
    blocks = lax.map(jax.checkpoint(block_scores), jnp.arange(LENGTH // QBLOCK, dtype=jnp.int32))
    return blocks.reshape(LENGTH, HEADS, HEAD)

def forward(flags, tokens, ln1_gain, ln1_shift, qkv_weight, qv_bias, out_weight, out_bias, ln2_gain, ln2_shift, up_weight, up_bias, down_weight, down_bias):
    normed1 = low(layer_norm(tokens, ln1_gain, ln1_shift))
    mixed = high_dot(normed1, qkv_weight.reshape(D, HEADS * 3 * HEAD)).reshape(TOKENS, HEADS, 3, HEAD)
    queries = low(low_back(mixed[:, :, 0] + qv_bias[:, 0]))
    key_rows = low(low_back(mixed[:, :, 1]))
    value_rows = low(low_back(mixed[:, :, 2] + qv_bias[:, 1]))

    def one_sequence(carry_in, pieces):
        return (carry_in, attend_sequence(pieces[0], pieces[1], pieces[2], pieces[3]))
    shaped = (queries.reshape(SEQ_ALL, LENGTH, HEADS, HEAD), key_rows.reshape(SEQ_ALL, LENGTH, HEADS, HEAD), value_rows.reshape(SEQ_ALL, LENGTH, HEADS, HEAD), flags)
    unused, attended = lax.scan(one_sequence, jnp.zeros((), jnp.float32), shaped)
    attended = low(low_back(attended.reshape(TOKENS, HEADS * HEAD)))
    branch = low_back(high_dot(attended, out_weight.reshape(HEADS * HEAD, D)) + out_bias)
    residual = tokens + branch
    normed2 = low(layer_norm(residual, ln2_gain, ln2_shift))
    up_sums = low_back(high_dot(normed2, up_weight) + up_bias)
    hidden = low(gelu_tanh(up_sums))
    return residual + low_back(high_dot(hidden, down_weight) + down_bias)

def reference(tokens, ln1_gain, ln1_shift, qkv_weight, qv_bias, out_weight, out_bias, ln2_gain, ln2_shift, up_weight, up_bias, down_weight, down_bias, span_starts, cotangent):
    slot_ids = jnp.arange(LENGTH // SPAN, dtype=jnp.int32)
    flags = lax.optimization_barrier(jnp.sum((span_starts[:, :, None] // SPAN == slot_ids[None, None, :]).astype(jnp.int32), axis=1))
    params = (tokens.astype(jnp.float32), ln1_gain, ln1_shift, qkv_weight.astype(jnp.float32), qv_bias, out_weight.astype(jnp.float32), out_bias, ln2_gain, ln2_shift, up_weight.astype(jnp.float32), up_bias, down_weight.astype(jnp.float32), down_bias)
    output, pullback = jax.vjp(partial(forward, flags), *params)
    grads = pullback(cotangent.astype(jnp.float32))
    return (output.astype(jnp.bfloat16), grads[0].astype(jnp.bfloat16), grads[1], grads[2], grads[3], grads[4], grads[5], grads[6], grads[7], grads[8], grads[9], grads[10], grads[11], grads[12])
```

```python
import functools
import math

import jax
import jax.numpy as jnp
from jax import lax
from jax.experimental import pallas as pl
from jax.experimental.pallas import tpu as pltpu
from jax.sharding import PartitionSpec as P

MESH = pl.DeviceIdType.MESH

D = 2048
HEAD = 128
SEQS = 1
SPAN = 256
BLOCK = 512


epsilon = 1e-05
masked_score = -1e30


def gelu_tanh(values):
    return (
        0.5
        * values
        * (1.0 + jnp.tanh(0.7978845608028654 * (values + 0.044715 * values * values * values)))
    )


def gather_columns(block_data):
    return lax.all_gather(block_data, "col", axis=0, tiled=True)


def gather_rows(block_data):
    return lax.all_gather(block_data, "row", axis=0, tiled=True)


def product(left_side, right_side, flipped):
    if flipped:
        return lax.dot_general(
            left_side, right_side, (((1,), (1,)), ((), ())), preferred_element_type=jnp.float32
        )
    return jnp.dot(left_side, right_side, preferred_element_type=jnp.float32)


def outer_sum(left_side, right_side):
    return lax.dot_general(
        left_side, right_side, (((0,), (0,)), ((), ())), preferred_element_type=jnp.float32
    )


def sum_rows(left_side, right_side, flipped):
    wide_left = lax.all_to_all(left_side, "row", split_axis=0, concat_axis=1, tiled=True)
    if flipped:
        wide_right = lax.all_gather(right_side, "row", axis=1, tiled=True)
    else:
        wide_right = lax.all_gather(right_side, "row", axis=0, tiled=True)
    return product(wide_left, wide_right, flipped)


def sum_columns(left_side, right_side, flipped):
    return lax.psum_scatter(
        product(left_side, right_side, flipped), "col", scatter_dimension=0, tiled=True
    )


def row_totals(first_sum, second_sum):
    return lax.psum((first_sum, second_sum), "row")


def norm_forward(values, gain_row, bias_row):
    totals, squares = row_totals(jnp.sum(values, axis=1), jnp.sum(values * values, axis=1))
    center = totals / D
    spread = squares / D - center * center
    inverse = lax.rsqrt(spread + epsilon)
    standard = (values - center[:, None]) * inverse[:, None]
    return (standard, inverse, (standard * gain_row + bias_row).astype(jnp.bfloat16))


def norm_backward(upstream, standard, inverse, gain_row):
    scaled = upstream * gain_row
    first_sum, second_sum = row_totals(jnp.sum(scaled, axis=1), jnp.sum(scaled * standard, axis=1))
    gradient = inverse[:, None] * (
        scaled - first_sum[:, None] / D - standard * (second_sum[:, None] / D)
    )
    return (gradient, jnp.sum(upstream * standard, axis=0), jnp.sum(upstream, axis=0))


def visible(query_pos, query_image, key_pos):
    earlier = key_pos[None, :] <= query_pos[:, None]
    same_span = (key_pos[None, :] // SPAN == query_pos[:, None] // SPAN) & (
        query_image[:, None] > 0
    )
    return earlier | same_span


def attention_forward(queries, key_value, token_image, row_offset, seq_length, block_rows):
    own_rows, head_count, width = queries.shape
    factor = 1.0 / math.sqrt(width)

    def block_forward(block_index):
        local = block_index * block_rows
        start_pos = row_offset + local
        query_block = lax.dynamic_slice_in_dim(queries, local, block_rows, 0)
        query_pos = start_pos + jnp.arange(block_rows, dtype=jnp.int32)
        query_image = lax.dynamic_slice_in_dim(token_image, start_pos, block_rows, 0)
        begin = start_pos // seq_length * seq_length // block_rows
        finish = start_pos // block_rows + 1

        def key_step(key_index, state_in):
            running, weight_sum, gathered = state_in
            key_begin = key_index * block_rows
            key_block = lax.dynamic_slice_in_dim(key_value, key_begin, block_rows, 0)
            key_pos = key_begin + jnp.arange(block_rows, dtype=jnp.int32)
            allowed = visible(query_pos, query_image, key_pos)
            scores = (
                jnp.einsum(
                    "qhd,khd->hqk",
                    query_block,
                    key_block[:, :, 0],
                    preferred_element_type=jnp.float32,
                )
                * factor
            )
            scores = jnp.where(allowed[None], scores, masked_score)
            highest = jnp.maximum(running, jnp.max(scores, axis=2))
            weights = jnp.exp(scores - highest[:, :, None])
            shrink = jnp.exp(running - highest)
            weight_sum = weight_sum * shrink + jnp.sum(weights, axis=2)
            gathered = gathered * shrink.T[:, :, None] + jnp.einsum(
                "hqk,khd->qhd",
                weights.astype(jnp.bfloat16),
                key_block[:, :, 1],
                preferred_element_type=jnp.float32,
            )
            return (highest, weight_sum, gathered)

        initial = (
            jnp.full((head_count, block_rows), masked_score, jnp.float32),
            jnp.zeros((head_count, block_rows), jnp.float32),
            jnp.zeros((block_rows, head_count, width), jnp.float32),
        )
        running, weight_sum, gathered = lax.fori_loop(begin, finish, key_step, initial)
        return (gathered / weight_sum.T[:, :, None], running + jnp.log(weight_sum))

    result, logsum = lax.map(block_forward, jnp.arange(own_rows // block_rows, dtype=jnp.int32))
    return (result.reshape(own_rows, head_count, width), logsum)


def attention_backward(
    queries,
    key_value,
    attended_full,
    logsum,
    d_attended,
    token_image,
    row_offset,
    seq_length,
    block_rows,
):
    own_rows, head_count, width = queries.shape
    factor = 1.0 / math.sqrt(width)
    row_dots = jnp.sum(d_attended.astype(jnp.float32) * attended_full, axis=2)

    def block_backward(block_index, state_out):
        d_queries, d_pairs = state_out
        local = block_index * block_rows
        start_pos = row_offset + local
        query_block = lax.dynamic_slice_in_dim(queries, local, block_rows, 0)
        dout_block = lax.dynamic_slice_in_dim(d_attended, local, block_rows, 0)
        dots_block = lax.dynamic_slice_in_dim(row_dots, local, block_rows, 0).T
        logsum_block = logsum[block_index]
        query_pos = start_pos + jnp.arange(block_rows, dtype=jnp.int32)
        query_image = lax.dynamic_slice_in_dim(token_image, start_pos, block_rows, 0)
        begin = start_pos // seq_length * seq_length // block_rows
        finish = start_pos // block_rows + 1

        def key_step(key_index, state_in):
            d_query, d_keys = state_in
            key_begin = key_index * block_rows
            key_block = lax.dynamic_slice_in_dim(key_value, key_begin, block_rows, 0)
            key_pos = key_begin + jnp.arange(block_rows, dtype=jnp.int32)
            allowed = visible(query_pos, query_image, key_pos)
            scores = (
                jnp.einsum(
                    "qhd,khd->hqk",
                    query_block,
                    key_block[:, :, 0],
                    preferred_element_type=jnp.float32,
                )
                * factor
            )
            scores = jnp.where(allowed[None], scores, masked_score)
            probabilities = jnp.exp(scores - logsum_block[:, :, None])
            d_probs = jnp.einsum(
                "qhd,khd->hqk", dout_block, key_block[:, :, 1], preferred_element_type=jnp.float32
            )
            d_scores = (probabilities * (d_probs - dots_block[:, :, None])).astype(jnp.bfloat16)
            d_query = d_query + jnp.einsum(
                "hqk,khd->qhd", d_scores, key_block[:, :, 0], preferred_element_type=jnp.float32
            )
            d_key = (
                jnp.einsum(
                    "hqk,qhd->khd", d_scores, query_block, preferred_element_type=jnp.float32
                )
                * factor
            )
            d_value = jnp.einsum(
                "hqk,qhd->khd",
                probabilities.astype(jnp.bfloat16),
                dout_block,
                preferred_element_type=jnp.float32,
            )
            previous = lax.dynamic_slice_in_dim(d_keys, key_begin, block_rows, 0)
            d_keys = lax.dynamic_update_slice_in_dim(
                d_keys, previous + jnp.stack([d_key, d_value], axis=2), key_begin, 0
            )
            return (d_query, d_keys)

        d_query, d_pairs = lax.fori_loop(
            begin,
            finish,
            key_step,
            (jnp.zeros((block_rows, head_count, width), jnp.float32), d_pairs),
        )
        d_queries = lax.dynamic_update_slice_in_dim(d_queries, d_query * factor, local, 0)
        return (d_queries, d_pairs)

    initial = (
        jnp.zeros((own_rows, head_count, width), jnp.float32),
        jnp.zeros((key_value.shape[0], head_count, 2, width), jnp.float32),
    )
    return lax.fori_loop(0, own_rows // block_rows, block_backward, initial)


def general_plan(
    tokens,
    ln1_gain,
    ln1_shift,
    qkv_weight,
    qv_bias,
    out_weight,
    out_bias,
    ln2_gain,
    ln2_shift,
    up_weight,
    up_bias,
    down_weight,
    down_bias,
    span_starts,
    cotangent,
):
    col_rows, row_width = tokens.shape
    group_rows = col_rows * lax.axis_size("col")
    own_rows = group_rows // lax.axis_size("row")
    head_count = qkv_weight.shape[1]
    seq_length = group_rows // SEQS
    block_rows = BLOCK - own_rows % BLOCK
    row_offset = lax.axis_index("row") * own_rows
    slot_count = seq_length // SPAN
    image_marks = jnp.sum(
        (
            span_starts[:, :, None] // SPAN
            == jnp.arange(slot_count, dtype=jnp.int32)[None, None, :]
        ).astype(jnp.int32),
        axis=1,
    )
    token_image = jnp.broadcast_to(
        image_marks.reshape(-1)[:, None], (group_rows // SPAN, SPAN)
    ).reshape(group_rows)
    qkv_flat = qkv_weight.reshape(row_width, head_count * 3 * HEAD)
    out_flat = out_weight.reshape(head_count * HEAD, row_width)
    inputs = tokens.astype(jnp.float32)
    standard1, inverse1, normed1 = norm_forward(inputs, ln1_gain, ln1_shift)
    normed1_all = gather_columns(normed1)
    mixed_sums = sum_rows(normed1_all, qkv_flat, False).reshape(own_rows, head_count, 3, HEAD)
    queries = (mixed_sums[:, :, 0] + qv_bias[:, 0]).astype(jnp.bfloat16)
    key_value_own = jnp.stack(
        [mixed_sums[:, :, 1], mixed_sums[:, :, 2] + qv_bias[:, 1]], axis=2
    ).astype(jnp.bfloat16)
    key_value = gather_rows(key_value_own)
    attended_full, logsum = attention_forward(
        queries, key_value, token_image, row_offset, seq_length, block_rows
    )
    attended = attended_full.astype(jnp.bfloat16).reshape(own_rows, head_count * HEAD)
    attended_all = gather_rows(attended)
    residual = inputs + (sum_columns(attended_all, out_flat, False) + out_bias)
    standard2, inverse2, normed2 = norm_forward(residual, ln2_gain, ln2_shift)
    normed2_all = gather_columns(normed2)
    up_sums = sum_rows(normed2_all, up_weight, False) + up_bias
    hidden = gelu_tanh(up_sums).astype(jnp.bfloat16)
    hidden_all = gather_rows(hidden)
    output = (residual + (sum_columns(hidden_all, down_weight, False) + down_bias)).astype(
        jnp.bfloat16
    )
    d_output = cotangent.astype(jnp.float32)
    d_output_all = gather_columns(cotangent)
    down_grad = outer_sum(hidden_all, d_output_all)
    down_bias_grad = jnp.sum(d_output_all, axis=0, dtype=jnp.float32)
    d_hidden = sum_rows(d_output_all, down_weight, True)
    d_upper = jax.vjp(gelu_tanh, up_sums)[1](d_hidden)[0].astype(jnp.bfloat16)
    d_upper_all = gather_rows(d_upper)
    normed2_use = gather_columns(normed2)
    up_grad = outer_sum(normed2_use, d_upper_all)
    up_bias_grad = jnp.sum(d_upper_all, axis=0, dtype=jnp.float32)
    d_normed2 = sum_columns(d_upper_all, up_weight, True)
    d_norm2, gain2_grad, shift2_grad = norm_backward(d_normed2, standard2, inverse2, ln2_gain)
    d_residual = d_output + d_norm2
    d_branch = d_residual.astype(jnp.bfloat16)
    d_branch_all = gather_columns(d_branch)
    out_grad = outer_sum(attended_all, d_branch_all)
    out_bias_grad = jnp.sum(d_branch_all, axis=0, dtype=jnp.float32)
    d_attended = (
        sum_rows(d_branch_all, out_flat, True)
        .astype(jnp.bfloat16)
        .reshape(own_rows, head_count, HEAD)
    )
    d_queries, d_pairs = attention_backward(
        queries,
        key_value,
        attended_full,
        logsum,
        d_attended,
        token_image,
        row_offset,
        seq_length,
        block_rows,
    )
    d_pairs_own = lax.psum_scatter(d_pairs, "row", scatter_dimension=0, tiled=True)
    d_mixed = jnp.concatenate([d_queries[:, :, None], d_pairs_own], axis=2).astype(jnp.bfloat16)
    d_mixed_all = gather_rows(d_mixed)
    normed1_use = gather_columns(normed1)
    d_mixed_flat = d_mixed_all.reshape(group_rows, head_count * 3 * HEAD)
    qkv_grad = outer_sum(normed1_use, d_mixed_flat)
    mixed_totals = jnp.sum(d_mixed_all, axis=0, dtype=jnp.float32)
    qv_bias_grad = jnp.stack([mixed_totals[:, 0], mixed_totals[:, 2]], axis=1)
    d_normed1 = sum_columns(d_mixed_flat, qkv_flat, True)
    d_norm1, gain1_grad, shift1_grad = norm_backward(d_normed1, standard1, inverse1, ln1_gain)
    tokens_grad = (d_residual + d_norm1).astype(jnp.bfloat16)
    norm_sums = lax.psum((gain1_grad, shift1_grad, gain2_grad, shift2_grad), ("dp", "col"))
    weight_sums = lax.psum(
        (
            qkv_grad,
            qv_bias_grad,
            out_grad,
            out_bias_grad,
            up_grad,
            up_bias_grad,
            down_grad,
            down_bias_grad,
        ),
        "dp",
    )
    return (
        output,
        tokens_grad,
        norm_sums[0],
        norm_sums[1],
        weight_sums[0].reshape(row_width, head_count, 3, HEAD),
        weight_sums[1],
        weight_sums[2].reshape(head_count, HEAD, row_width),
        weight_sums[3],
        norm_sums[2],
        norm_sums[3],
        weight_sums[4],
        weight_sums[5],
        weight_sums[6],
        weight_sums[7],
    )


def places():
    row, col = lax.axis_index("row"), lax.axis_index("col")
    side, core = row // 2, row % 2
    return col, side, core

def partners():
    col, side, core = places()
    return ({"col": 1 - col}, {"row": (1 - side) * 2 + core}, {"row": side * 2 + 1 - core})

def greet():
    barrier = pltpu.get_barrier_semaphore()
    for partner in partners():
        pl.semaphore_signal(barrier, inc=1, device_id=partner, device_id_type=MESH)
    pl.semaphore_wait(barrier, 3)

def block(ref, col, side, core, rows, width, part=None):
    begin, count = col * rows, rows
    if part is not None:
        begin, count = begin + part * (rows // 2), rows // 2
    left = (side * 2 + core) * width
    return ref.at[pl.ds(pl.multiple_of(begin, count), count), pl.ds(pl.multiple_of(left, width), width)]

def send(ref_from, ref_to, sends, recvs, at, partner):
    copy = pltpu.make_async_remote_copy(src_ref=ref_from, dst_ref=ref_to, send_sem=sends.at[at], recv_sem=recvs.at[at], device_id=partner, device_id_type=MESH)
    copy.start()
    return copy

def spread(out, rows, width, sends, recvs, base):
    col, side, core = places()
    to_x, to_y, to_core = partners()
    def go(at, which, partner, part=None):
        ref = block(out, *which, rows, width, part)
        return send(ref, ref, sends, recvs, base + at, partner)
    own, ox, oy, od = (col, side, core), (1 - col, side, core), (col, 1 - side, core), (1 - col, 1 - side, core)
    c0 = go(0, own, to_x)
    c1 = go(1, own, to_y)
    c2 = go(2, own, to_core)
    c0.wait_recv()
    c3 = go(3, ox, to_y, 0)
    c1.wait_recv()
    c4 = go(4, oy, to_x, 1)
    c5 = go(5, ox, to_core)
    c6 = go(6, oy, to_core)
    c3.wait_recv()
    c4.wait_recv()
    c7 = go(7, od, to_core)
    for c in (c2, c5, c6, c7):
        c.wait_recv()
    for c in (c0, c1, c2, c3, c4, c5, c6, c7):
        c.wait_send()

def gather_kernel(x_ref, out, sends, recvs):
    rows, width = x_ref.shape
    greet()
    col, side, core = places()
    block(out, col, side, core, rows, width)[...] = x_ref[...]
    spread(out, rows, width, sends, recvs, 0)

def gather_plane(x, cid):
    rows, width = x.shape
    return pl.pallas_call(gather_kernel, out_shape=jax.ShapeDtypeStruct((2*rows,4*width), x.dtype),
        in_specs=[pl.BlockSpec(memory_space=pltpu.VMEM)], out_specs=pl.BlockSpec(memory_space=pltpu.VMEM),
        scratch_shapes=[pltpu.SemaphoreType.DMA((8,)), pltpu.SemaphoreType.DMA((8,))],
        compiler_params=pltpu.CompilerParams(collective_id=cid, has_side_effects=True, vmem_limit_bytes=50<<20))(x)

def sum_to_owner(part_ref, got, keep, diag, half_x, half_y, to_send, from_xy, sends, recvs, rows, width):
    col, side, core = places()
    to_x, to_y, to_core = partners()
    half = rows // 2
    spots = ((1-col,1-side),(col,1-side),(1-col,side),(col,side))
    copies = []
    for i,(a,b) in enumerate(spots):
        copies.append(send(block(part_ref, a, b, 1-core, rows, width), got.at[i], sends, recvs, i, to_core))
    f32 = jnp.float32
    copies[0].wait_recv()
    diag[...] = (block(part_ref, 1-col, 1-side, core, rows, width)[...].astype(f32) + got[0].astype(f32)).astype(diag.dtype)
    dx = send(diag.at[pl.ds(0,half)], half_x, sends, recvs, 4, to_x)
    dy = send(diag.at[pl.ds(half,half)], half_y, sends, recvs, 5, to_y)
    copies[1].wait_recv()
    copies[2].wait_recv()
    dx.wait_recv()
    py = block(part_ref, col, 1-side, core, rows, width)
    px = block(part_ref, 1-col, side, core, rows, width)
    ty = to_send.at[0]
    tx = to_send.at[1]
    ty[pl.ds(0,half)] = (py[pl.ds(0,half)].astype(f32) + got[1,pl.ds(0,half)].astype(f32) + half_x[...].astype(f32)).astype(diag.dtype)
    ty[pl.ds(half,half)] = (py[pl.ds(half,half)].astype(f32) + got[1,pl.ds(half,half)].astype(f32)).astype(diag.dtype)
    cy = send(ty, from_xy.at[0], sends, recvs, 6, to_y)
    dy.wait_recv()
    tx[pl.ds(0,half)] = (px[pl.ds(0,half)].astype(f32) + got[2,pl.ds(0,half)].astype(f32)).astype(diag.dtype)
    tx[pl.ds(half,half)] = (px[pl.ds(half,half)].astype(f32) + got[2,pl.ds(half,half)].astype(f32) + half_y[...].astype(f32)).astype(diag.dtype)
    cx = send(tx, from_xy.at[1], sends, recvs, 7, to_x)
    copies[3].wait_recv()
    keep[...] = block(part_ref, col, side, core, rows, width)[...].astype(f32) + got[3].astype(f32)
    cy.wait_recv()
    cx.wait_recv()
    for c in copies + [dx, dy, cy, cx]:
        c.wait_send()
    return keep[...] + from_xy[0].astype(f32) + from_xy[1].astype(f32)

def sum_scratch(rows, width, dt):
    return [pltpu.VMEM((4,rows,width),dt), pltpu.VMEM((rows,width),jnp.float32), pltpu.VMEM((rows,width),dt),
            pltpu.VMEM((rows//2,width),dt), pltpu.VMEM((rows//2,width),dt), pltpu.VMEM((2,rows,width),dt), pltpu.VMEM((2,rows,width),dt)]

def reduce_kernel(part_ref, out, *scratch):
    *bufs, sends, recvs = scratch
    rows, width = out.shape
    greet()
    out[...] = sum_to_owner(part_ref, *bufs, sends, recvs, rows, width)

def reduce_plane(part, cid):
    rows, width = part.shape[0]//2, part.shape[1]//4
    return pl.pallas_call(reduce_kernel, out_shape=jax.ShapeDtypeStruct((rows,width), jnp.float32),
        in_specs=[pl.BlockSpec(memory_space=pltpu.VMEM)], out_specs=pl.BlockSpec(memory_space=pltpu.VMEM),
        scratch_shapes=sum_scratch(rows,width,part.dtype)+[pltpu.SemaphoreType.DMA((8,)), pltpu.SemaphoreType.DMA((8,))],
        compiler_params=pltpu.CompilerParams(collective_id=cid, has_side_effects=True, vmem_limit_bytes=50<<20))(part)

def total_kernel(part_ref, out, *scratch):
    *bufs, sends, recvs = scratch
    rows, width = out.shape[0]//2, out.shape[1]//4
    greet()
    own = sum_to_owner(part_ref, *bufs, sends, recvs, rows, width)
    col, side, core = places()
    block(out, col, side, core, rows, width)[...] = own.astype(out.dtype)
    spread(out, rows, width, sends, recvs, 8)

def total_plane(part, cid):
    rows, width = part.shape[0]//2, part.shape[1]//4
    return pl.pallas_call(total_kernel, out_shape=jax.ShapeDtypeStruct(part.shape, part.dtype),
        in_specs=[pl.BlockSpec(memory_space=pltpu.VMEM)], out_specs=pl.BlockSpec(memory_space=pltpu.VMEM),
        scratch_shapes=sum_scratch(rows,width,part.dtype)+[pltpu.SemaphoreType.DMA((16,)), pltpu.SemaphoreType.DMA((16,))],
        compiler_params=pltpu.CompilerParams(collective_id=cid, has_side_effects=True, vmem_limit_bytes=50<<20))(part)


def shift_rows(pieces):
    row, count = lax.axis_index("row"), pieces.shape[0]
    result = pieces
    for step in range(1, count):
        pairs = [(k, (k + step) % count) for k in range(count)]
        sent = lax.dynamic_index_in_dim(pieces, (row + step) % count, 0, keepdims=True)
        got = lax.ppermute(sent, "row", pairs)
        result = lax.dynamic_update_slice_in_dim(result, got, (row + count - step) % count, 0)
    return result


def dp_total(share):
    place = lax.axis_index("dp")
    f32 = jnp.float32
    inner = (place == 1) | (place == 2)
    came = lax.ppermute(share, "dp", [(0, 1), (3, 2)])
    half = (share.astype(f32) + came.astype(f32)).astype(share.dtype)
    across = lax.ppermute(half, "dp", [(1, 2), (2, 1)])
    total = (half.astype(f32) + across.astype(f32)).astype(share.dtype)
    back = lax.ppermute(total, "dp", [(1, 0), (2, 3)])
    return jnp.where(inner, total, back)


def norm_stats(values):
    center = jnp.mean(values, axis=1, keepdims=True)
    spread_of = jnp.mean(values * values, axis=1, keepdims=True) - center * center
    return center, lax.rsqrt(spread_of + epsilon)


def mask_of(span_starts, length):
    marks = jnp.sum(
        (span_starts[0][:, None] // SPAN == jnp.arange(length // SPAN, dtype=jnp.int32)[None, :]).astype(jnp.int32),
        axis=0,
    )
    places_of = jnp.arange(length, dtype=jnp.int32)
    image = jnp.repeat(marks, SPAN)
    return visible(places_of, image, places_of)


def plane_plan(
    tokens,
    ln1_gain,
    ln1_shift,
    qkv_weight,
    qv_bias,
    out_weight,
    out_bias,
    ln2_gain,
    ln2_shift,
    up_weight,
    up_bias,
    down_weight,
    down_bias,
    span_starts,
    cotangent,
):
    f32, bf16 = jnp.float32, jnp.bfloat16
    rows, width = tokens.shape
    row_count = lax.axis_size("row")
    col, row = lax.axis_index("col"), lax.axis_index("row")
    length, full = rows * lax.axis_size("col"), width * row_count
    heads = qkv_weight.shape[1] // row_count
    hidden_count = up_weight.shape[1] // row_count
    factor = 1.0 / math.sqrt(HEAD)

    def own(values):
        return lax.dynamic_slice(values, (col * rows, row * width), (rows, width))

    def own_width(values):
        return lax.dynamic_slice_in_dim(values, row * width, width, values.ndim - 1)

    def wide(vector):
        return lax.all_gather(vector, "row", axis=0, tiled=True)

    qkv_flat = shift_rows(
        jnp.moveaxis(qkv_weight.reshape(width, row_count, heads * 3 * HEAD), 1, 0)
    ).reshape(full, heads * 3 * HEAD)
    out_flat = jnp.moveaxis(
        shift_rows(out_weight.reshape(row_count, heads * HEAD, width)), 0, 1
    ).reshape(heads * HEAD, full)
    up_flat = shift_rows(jnp.moveaxis(up_weight.reshape(width, row_count, hidden_count), 1, 0)).reshape(
        full, hidden_count
    )
    down_flat = jnp.moveaxis(
        shift_rows(down_weight.reshape(row_count, hidden_count, width)), 0, 1
    ).reshape(hidden_count, full)
    vectors = wide(jnp.stack([ln1_gain, ln1_shift, out_bias, ln2_gain, ln2_shift], axis=0).T)
    gain1, shift1, branch_bias, gain2, shift2 = [vectors[:, k] for k in range(5)]
    own_qv = lax.dynamic_slice_in_dim(qv_bias, row * heads, heads, 0)
    own_up_bias = lax.dynamic_slice_in_dim(up_bias, row * hidden_count, hidden_count, 0)
    allowed = mask_of(span_starts, length)

    tokens_all = gather_plane(tokens, 1)
    cot_all = gather_plane(cotangent, 2)
    inputs = tokens_all.astype(f32)
    center1, inverse1 = norm_stats(inputs)
    normed1 = ((inputs - center1) * inverse1 * gain1 + shift1).astype(bf16)
    mixed = product(normed1, qkv_flat, False).reshape(length, heads, 3, HEAD)
    queries = (mixed[:, :, 0] + own_qv[:, 0]).astype(bf16)
    key_rows = mixed[:, :, 1].astype(bf16)
    value_rows = (mixed[:, :, 2] + own_qv[:, 1]).astype(bf16)
    scores = jnp.einsum("qhd,khd->hqk", queries, key_rows, preferred_element_type=f32) * factor
    scores = jnp.where(allowed[None], scores, masked_score)
    weights = jnp.exp(scores - jnp.max(scores, axis=2, keepdims=True))
    probs = weights / jnp.sum(weights, axis=2, keepdims=True)
    low_probs = probs.astype(bf16)
    attended = jnp.einsum("hqk,khd->qhd", low_probs, value_rows, preferred_element_type=f32)
    attended = attended.astype(bf16).reshape(length, heads * HEAD)
    branch = total_plane(product(attended, out_flat, False).astype(bf16), 3)
    residual = inputs + (branch.astype(f32) + branch_bias)
    center2, inverse2 = norm_stats(residual)
    standard2 = (residual - center2) * inverse2
    normed2 = (standard2 * gain2 + shift2).astype(bf16)
    up_sums = product(normed2, up_flat, False) + own_up_bias
    hidden = gelu_tanh(up_sums).astype(bf16)
    d_hidden = product(cot_all, down_flat, True)
    d_upper = jax.vjp(gelu_tanh, up_sums)[1](d_hidden)[0].astype(bf16)

    parts = 4
    piece = hidden_count // parts
    down_grads, up_grads = [], []
    for part in range(parts):
        grad = outer_sum(hidden[:, part * piece : (part + 1) * piece], cot_all).astype(bf16)
        grad = shift_rows(jnp.moveaxis(grad.reshape(piece, row_count, width), 1, 0))
        down_grads.append(dp_total(grad))
    for part in range(parts):
        grad = outer_sum(normed2, d_upper[:, part * piece : (part + 1) * piece]).astype(bf16)
        up_grads.append(dp_total(shift_rows(grad.reshape(row_count, width, piece))))

    d_normed2 = total_plane(product(d_upper, up_flat, True).astype(bf16), 4).astype(f32)
    scaled = d_normed2 * gain2
    d_residual = cot_all.astype(f32) + inverse2 * (
        scaled
        - jnp.mean(scaled, axis=1, keepdims=True)
        - standard2 * jnp.mean(scaled * standard2, axis=1, keepdims=True)
    )
    d_branch = d_residual.astype(bf16)
    out_grad = outer_sum(attended, d_branch).astype(bf16)
    out_grad = dp_total(shift_rows(jnp.moveaxis(out_grad.reshape(heads * HEAD, row_count, width), 1, 0)))
    d_attended = product(d_branch, out_flat, True).astype(bf16).reshape(length, heads, HEAD)
    d_probs = jnp.einsum("qhd,khd->hqk", d_attended, value_rows, preferred_element_type=f32)
    dots = jnp.sum(probs * d_probs, axis=2, keepdims=True)
    d_scores = (probs * (d_probs - dots)).astype(bf16)
    d_query = jnp.einsum("hqk,khd->qhd", d_scores, key_rows, preferred_element_type=f32) * factor
    d_key = jnp.einsum("hqk,qhd->khd", d_scores, queries, preferred_element_type=f32) * factor
    d_value = jnp.einsum("hqk,qhd->khd", low_probs, d_attended, preferred_element_type=f32)
    d_mixed = jnp.stack([d_query, d_key, d_value], axis=2).astype(bf16)
    d_flat = d_mixed.reshape(length, heads * 3 * HEAD)
    qkv_grads = []
    for head in range(heads):
        grad = outer_sum(normed1, d_flat[:, head * 3 * HEAD : (head + 1) * 3 * HEAD]).astype(bf16)
        qkv_grads.append(dp_total(shift_rows(grad.reshape(row_count, width, 3 * HEAD))))
    d_normed1 = reduce_plane(product(d_flat, qkv_flat, True).astype(bf16), 5)

    standard1 = own((inputs - center1) * inverse1)
    own_inverse1 = lax.dynamic_slice_in_dim(inverse1, col * rows, rows, 0)
    d_norm1, gain1_grad, shift1_grad = norm_backward(
        d_normed1, standard1, own_inverse1[:, 0], ln1_gain
    )
    tokens_grad = (own(d_residual) + d_norm1).astype(bf16)
    sums_out = reduce_plane(product(hidden, down_flat, False).astype(bf16), 6)
    output = (own(residual) + (sums_out + down_bias)).astype(bf16)

    own_n2 = own_width(d_normed2)
    near = [
        jnp.sum(own_n2 * own_width(standard2), axis=0),
        jnp.sum(own_n2, axis=0),
        jnp.sum(own_width(d_branch), axis=0, dtype=f32),
        jnp.sum(own_width(cot_all), axis=0, dtype=f32),
    ]
    totals = jnp.sum(d_mixed, axis=0, dtype=f32)
    spread_sums = [
        jnp.sum(d_upper, axis=0, dtype=f32),
        jnp.stack([totals[:, 0], totals[:, 2]], axis=1).reshape(heads * 2 * HEAD),
    ]
    slots = [lax.dynamic_update_index_in_dim(jnp.zeros((row_count,) + v.shape, f32), v, row, 0) for v in spread_sums]
    own_slots = [lax.dynamic_update_index_in_dim(jnp.zeros((row_count,) + v.shape, f32), v, row, 0) for v in near]
    summed = lax.psum(jnp.concatenate(slots + own_slots, axis=1), ("dp", "row"))
    up_bias_grad = summed[:, :hidden_count].reshape(-1)
    begin = hidden_count + heads * 2 * HEAD
    qv_bias_grad = summed[:, hidden_count:begin].reshape(row_count * heads, 2, HEAD)
    mine = lax.dynamic_index_in_dim(summed[:, begin:], row, 0, keepdims=False).reshape(4, width)
    norm1_sums = lax.psum((gain1_grad, shift1_grad), ("dp", "col"))

    down_weight_grad = jnp.stack(down_grads, axis=1).reshape(row_count * hidden_count, width).astype(f32)
    up_weight_grad = jnp.stack(up_grads, axis=1).transpose(2, 0, 1, 3).reshape(width, row_count * hidden_count)
    qkv_weight_grad = jnp.stack(qkv_grads, axis=1).transpose(2, 0, 1, 3)
    return (
        output,
        tokens_grad,
        norm1_sums[0],
        norm1_sums[1],
        qkv_weight_grad.reshape(width, row_count * heads, 3, HEAD).astype(f32),
        qv_bias_grad,
        out_grad.reshape(row_count * heads, HEAD, width).astype(f32),
        mine[2],
        mine[0],
        mine[1],
        up_weight_grad.astype(f32),
        up_bias_grad,
        down_weight_grad,
        mine[3],
    )


def solution(mesh):
    sizes = dict(mesh.shape)
    flat = sizes == {"dp": 4, "row": 4, "col": 2}
    per_device = plane_plan if flat else general_plan
    placed = (
        P(("dp", "col"), "row"),
        P("row"),
        P("row"),
        P("row", "col", None, None),
        P("col", None, None),
        P("col", None, "row"),
        P("row"),
        P("row"),
        P("row"),
        P("row", "col"),
        P("col"),
        P("col", "row"),
        P("row"),
        P("dp", None),
        P(("dp", "col"), "row"),
    )
    return jax.shard_map(
        per_device,
        mesh=mesh,
        in_specs=placed,
        out_specs=(
            P(("dp", "col"), "row"),
            P(("dp", "col"), "row"),
            P("row"),
            P("row"),
            P("row", "col", None, None),
            P("col", None, None),
            P("col", None, "row"),
            P("row"),
            P("row"),
            P("row"),
            P("row", "col"),
            P("col"),
            P("col", "row"),
            P("row"),
        ),
        check_vma=False,
    )
```

```python
import functools
import math

import jax
import jax.numpy as jnp
from jax import lax
from jax.experimental import pallas as pl
from jax.experimental.pallas import tpu as pltpu
from jax.sharding import PartitionSpec as P

MESH = pl.DeviceIdType.MESH

D = 2048
HEAD = 128
SEQS = 1
SPAN = 256
BLOCK = 512


epsilon = 1e-05
masked_score = -1e30


def gelu_tanh(values):
    return (
        0.5
        * values
        * (1.0 + jnp.tanh(0.7978845608028654 * (values + 0.044715 * values * values * values)))
    )


def gather_columns(block_data):
    return lax.all_gather(block_data, "col", axis=0, tiled=True)


def gather_rows(block_data):
    return lax.all_gather(block_data, "row", axis=0, tiled=True)


def product(left_side, right_side, flipped):
    if flipped:
        return lax.dot_general(
            left_side, right_side, (((1,), (1,)), ((), ())), preferred_element_type=jnp.float32
        )
    return jnp.dot(left_side, right_side, preferred_element_type=jnp.float32)


def outer_sum(left_side, right_side):
    return lax.dot_general(
        left_side, right_side, (((0,), (0,)), ((), ())), preferred_element_type=jnp.float32
    )


def sum_rows(left_side, right_side, flipped):
    wide_left = lax.all_to_all(left_side, "row", split_axis=0, concat_axis=1, tiled=True)
    if flipped:
        wide_right = lax.all_gather(right_side, "row", axis=1, tiled=True)
    else:
        wide_right = lax.all_gather(right_side, "row", axis=0, tiled=True)
    return product(wide_left, wide_right, flipped)


def sum_columns(left_side, right_side, flipped):
    return lax.psum_scatter(
        product(left_side, right_side, flipped), "col", scatter_dimension=0, tiled=True
    )


def row_totals(first_sum, second_sum):
    return lax.psum((first_sum, second_sum), "row")


def norm_forward(values, gain_row, bias_row):
    totals, squares = row_totals(jnp.sum(values, axis=1), jnp.sum(values * values, axis=1))
    center = totals / D
    spread = squares / D - center * center
    inverse = lax.rsqrt(spread + epsilon)
    standard = (values - center[:, None]) * inverse[:, None]
    return (standard, inverse, (standard * gain_row + bias_row).astype(jnp.bfloat16))


def norm_backward(upstream, standard, inverse, gain_row):
    scaled = upstream * gain_row
    first_sum, second_sum = row_totals(jnp.sum(scaled, axis=1), jnp.sum(scaled * standard, axis=1))
    gradient = inverse[:, None] * (
        scaled - first_sum[:, None] / D - standard * (second_sum[:, None] / D)
    )
    return (gradient, jnp.sum(upstream * standard, axis=0), jnp.sum(upstream, axis=0))


def visible(query_pos, query_image, key_pos):
    earlier = key_pos[None, :] <= query_pos[:, None]
    same_span = (key_pos[None, :] // SPAN == query_pos[:, None] // SPAN) & (
        query_image[:, None] > 0
    )
    return earlier | same_span


def attention_forward(queries, key_value, token_image, row_offset, seq_length, block_rows):
    own_rows, head_count, width = queries.shape
    factor = 1.0 / math.sqrt(width)

    def block_forward(block_index):
        local = block_index * block_rows
        start_pos = row_offset + local
        query_block = lax.dynamic_slice_in_dim(queries, local, block_rows, 0)
        query_pos = start_pos + jnp.arange(block_rows, dtype=jnp.int32)
        query_image = lax.dynamic_slice_in_dim(token_image, start_pos, block_rows, 0)
        begin = start_pos // seq_length * seq_length // block_rows
        finish = start_pos // block_rows + 1

        def key_step(key_index, state_in):
            running, weight_sum, gathered = state_in
            key_begin = key_index * block_rows
            key_block = lax.dynamic_slice_in_dim(key_value, key_begin, block_rows, 0)
            key_pos = key_begin + jnp.arange(block_rows, dtype=jnp.int32)
            allowed = visible(query_pos, query_image, key_pos)
            scores = (
                jnp.einsum(
                    "qhd,khd->hqk",
                    query_block,
                    key_block[:, :, 0],
                    preferred_element_type=jnp.float32,
                )
                * factor
            )
            scores = jnp.where(allowed[None], scores, masked_score)
            highest = jnp.maximum(running, jnp.max(scores, axis=2))
            weights = jnp.exp(scores - highest[:, :, None])
            shrink = jnp.exp(running - highest)
            weight_sum = weight_sum * shrink + jnp.sum(weights, axis=2)
            gathered = gathered * shrink.T[:, :, None] + jnp.einsum(
                "hqk,khd->qhd",
                weights.astype(jnp.bfloat16),
                key_block[:, :, 1],
                preferred_element_type=jnp.float32,
            )
            return (highest, weight_sum, gathered)

        initial = (
            jnp.full((head_count, block_rows), masked_score, jnp.float32),
            jnp.zeros((head_count, block_rows), jnp.float32),
            jnp.zeros((block_rows, head_count, width), jnp.float32),
        )
        running, weight_sum, gathered = lax.fori_loop(begin, finish, key_step, initial)
        return (gathered / weight_sum.T[:, :, None], running + jnp.log(weight_sum))

    result, logsum = lax.map(block_forward, jnp.arange(own_rows // block_rows, dtype=jnp.int32))
    return (result.reshape(own_rows, head_count, width), logsum)


def attention_backward(
    queries,
    key_value,
    attended_full,
    logsum,
    d_attended,
    token_image,
    row_offset,
    seq_length,
    block_rows,
):
    own_rows, head_count, width = queries.shape
    factor = 1.0 / math.sqrt(width)
    row_dots = jnp.sum(d_attended.astype(jnp.float32) * attended_full, axis=2)

    def block_backward(block_index, state_out):
        d_queries, d_pairs = state_out
        local = block_index * block_rows
        start_pos = row_offset + local
        query_block = lax.dynamic_slice_in_dim(queries, local, block_rows, 0)
        dout_block = lax.dynamic_slice_in_dim(d_attended, local, block_rows, 0)
        dots_block = lax.dynamic_slice_in_dim(row_dots, local, block_rows, 0).T
        logsum_block = logsum[block_index]
        query_pos = start_pos + jnp.arange(block_rows, dtype=jnp.int32)
        query_image = lax.dynamic_slice_in_dim(token_image, start_pos, block_rows, 0)
        begin = start_pos // seq_length * seq_length // block_rows
        finish = start_pos // block_rows + 1

        def key_step(key_index, state_in):
            d_query, d_keys = state_in
            key_begin = key_index * block_rows
            key_block = lax.dynamic_slice_in_dim(key_value, key_begin, block_rows, 0)
            key_pos = key_begin + jnp.arange(block_rows, dtype=jnp.int32)
            allowed = visible(query_pos, query_image, key_pos)
            scores = (
                jnp.einsum(
                    "qhd,khd->hqk",
                    query_block,
                    key_block[:, :, 0],
                    preferred_element_type=jnp.float32,
                )
                * factor
            )
            scores = jnp.where(allowed[None], scores, masked_score)
            probabilities = jnp.exp(scores - logsum_block[:, :, None])
            d_probs = jnp.einsum(
                "qhd,khd->hqk", dout_block, key_block[:, :, 1], preferred_element_type=jnp.float32
            )
            d_scores = (probabilities * (d_probs - dots_block[:, :, None])).astype(jnp.bfloat16)
            d_query = d_query + jnp.einsum(
                "hqk,khd->qhd", d_scores, key_block[:, :, 0], preferred_element_type=jnp.float32
            )
            d_key = (
                jnp.einsum(
                    "hqk,qhd->khd", d_scores, query_block, preferred_element_type=jnp.float32
                )
                * factor
            )
            d_value = jnp.einsum(
                "hqk,qhd->khd",
                probabilities.astype(jnp.bfloat16),
                dout_block,
                preferred_element_type=jnp.float32,
            )
            previous = lax.dynamic_slice_in_dim(d_keys, key_begin, block_rows, 0)
            d_keys = lax.dynamic_update_slice_in_dim(
                d_keys, previous + jnp.stack([d_key, d_value], axis=2), key_begin, 0
            )
            return (d_query, d_keys)

        d_query, d_pairs = lax.fori_loop(
            begin,
            finish,
            key_step,
            (jnp.zeros((block_rows, head_count, width), jnp.float32), d_pairs),
        )
        d_queries = lax.dynamic_update_slice_in_dim(d_queries, d_query * factor, local, 0)
        return (d_queries, d_pairs)

    initial = (
        jnp.zeros((own_rows, head_count, width), jnp.float32),
        jnp.zeros((key_value.shape[0], head_count, 2, width), jnp.float32),
    )
    return lax.fori_loop(0, own_rows // block_rows, block_backward, initial)


def general_plan(
    tokens,
    ln1_gain,
    ln1_shift,
    qkv_weight,
    qv_bias,
    out_weight,
    out_bias,
    ln2_gain,
    ln2_shift,
    up_weight,
    up_bias,
    down_weight,
    down_bias,
    span_starts,
    cotangent,
):
    col_rows, row_width = tokens.shape
    group_rows = col_rows * lax.axis_size("col")
    own_rows = group_rows // lax.axis_size("row")
    head_count = qkv_weight.shape[1]
    seq_length = group_rows // SEQS
    block_rows = BLOCK - own_rows % BLOCK
    row_offset = lax.axis_index("row") * own_rows
    slot_count = seq_length // SPAN
    image_marks = jnp.sum(
        (
            span_starts[:, :, None] // SPAN
            == jnp.arange(slot_count, dtype=jnp.int32)[None, None, :]
        ).astype(jnp.int32),
        axis=1,
    )
    token_image = jnp.broadcast_to(
        image_marks.reshape(-1)[:, None], (group_rows // SPAN, SPAN)
    ).reshape(group_rows)
    qkv_flat = qkv_weight.reshape(row_width, head_count * 3 * HEAD)
    out_flat = out_weight.reshape(head_count * HEAD, row_width)
    inputs = tokens.astype(jnp.float32)
    standard1, inverse1, normed1 = norm_forward(inputs, ln1_gain, ln1_shift)
    normed1_all = gather_columns(normed1)
    mixed_sums = sum_rows(normed1_all, qkv_flat, False).reshape(own_rows, head_count, 3, HEAD)
    queries = (mixed_sums[:, :, 0] + qv_bias[:, 0]).astype(jnp.bfloat16)
    key_value_own = jnp.stack(
        [mixed_sums[:, :, 1], mixed_sums[:, :, 2] + qv_bias[:, 1]], axis=2
    ).astype(jnp.bfloat16)
    key_value = gather_rows(key_value_own)
    attended_full, logsum = attention_forward(
        queries, key_value, token_image, row_offset, seq_length, block_rows
    )
    attended = attended_full.astype(jnp.bfloat16).reshape(own_rows, head_count * HEAD)
    attended_all = gather_rows(attended)
    residual = inputs + (sum_columns(attended_all, out_flat, False) + out_bias)
    standard2, inverse2, normed2 = norm_forward(residual, ln2_gain, ln2_shift)
    normed2_all = gather_columns(normed2)
    up_sums = sum_rows(normed2_all, up_weight, False) + up_bias
    hidden = gelu_tanh(up_sums).astype(jnp.bfloat16)
    hidden_all = gather_rows(hidden)
    output = (residual + (sum_columns(hidden_all, down_weight, False) + down_bias)).astype(
        jnp.bfloat16
    )
    d_output = cotangent.astype(jnp.float32)
    d_output_all = gather_columns(cotangent)
    down_grad = outer_sum(hidden_all, d_output_all)
    down_bias_grad = jnp.sum(d_output_all, axis=0, dtype=jnp.float32)
    d_hidden = sum_rows(d_output_all, down_weight, True)
    d_upper = jax.vjp(gelu_tanh, up_sums)[1](d_hidden)[0].astype(jnp.bfloat16)
    d_upper_all = gather_rows(d_upper)
    normed2_use = gather_columns(normed2)
    up_grad = outer_sum(normed2_use, d_upper_all)
    up_bias_grad = jnp.sum(d_upper_all, axis=0, dtype=jnp.float32)
    d_normed2 = sum_columns(d_upper_all, up_weight, True)
    d_norm2, gain2_grad, shift2_grad = norm_backward(d_normed2, standard2, inverse2, ln2_gain)
    d_residual = d_output + d_norm2
    d_branch = d_residual.astype(jnp.bfloat16)
    d_branch_all = gather_columns(d_branch)
    out_grad = outer_sum(attended_all, d_branch_all)
    out_bias_grad = jnp.sum(d_branch_all, axis=0, dtype=jnp.float32)
    d_attended = (
        sum_rows(d_branch_all, out_flat, True)
        .astype(jnp.bfloat16)
        .reshape(own_rows, head_count, HEAD)
    )
    d_queries, d_pairs = attention_backward(
        queries,
        key_value,
        attended_full,
        logsum,
        d_attended,
        token_image,
        row_offset,
        seq_length,
        block_rows,
    )
    d_pairs_own = lax.psum_scatter(d_pairs, "row", scatter_dimension=0, tiled=True)
    d_mixed = jnp.concatenate([d_queries[:, :, None], d_pairs_own], axis=2).astype(jnp.bfloat16)
    d_mixed_all = gather_rows(d_mixed)
    normed1_use = gather_columns(normed1)
    d_mixed_flat = d_mixed_all.reshape(group_rows, head_count * 3 * HEAD)
    qkv_grad = outer_sum(normed1_use, d_mixed_flat)
    mixed_totals = jnp.sum(d_mixed_all, axis=0, dtype=jnp.float32)
    qv_bias_grad = jnp.stack([mixed_totals[:, 0], mixed_totals[:, 2]], axis=1)
    d_normed1 = sum_columns(d_mixed_flat, qkv_flat, True)
    d_norm1, gain1_grad, shift1_grad = norm_backward(d_normed1, standard1, inverse1, ln1_gain)
    tokens_grad = (d_residual + d_norm1).astype(jnp.bfloat16)
    norm_sums = lax.psum((gain1_grad, shift1_grad, gain2_grad, shift2_grad), ("dp", "col"))
    weight_sums = lax.psum(
        (
            qkv_grad,
            qv_bias_grad,
            out_grad,
            out_bias_grad,
            up_grad,
            up_bias_grad,
            down_grad,
            down_bias_grad,
        ),
        "dp",
    )
    return (
        output,
        tokens_grad,
        norm_sums[0],
        norm_sums[1],
        weight_sums[0].reshape(row_width, head_count, 3, HEAD),
        weight_sums[1],
        weight_sums[2].reshape(head_count, HEAD, row_width),
        weight_sums[3],
        norm_sums[2],
        norm_sums[3],
        weight_sums[4],
        weight_sums[5],
        weight_sums[6],
        weight_sums[7],
    )


def places():
    row, col = lax.axis_index("row"), lax.axis_index("col")
    side, core = row // 2, row % 2
    return col, side, core

def partners():
    col, side, core = places()
    return ({"col": 1 - col}, {"row": (1 - side) * 2 + core}, {"row": side * 2 + 1 - core})

def greet():
    barrier = pltpu.get_barrier_semaphore()
    for partner in partners():
        pl.semaphore_signal(barrier, inc=1, device_id=partner, device_id_type=MESH)
    pl.semaphore_wait(barrier, 3)

def block(ref, col, side, core, rows, width, part=None):
    begin, count = col * rows, rows
    if part is not None:
        begin, count = begin + part * (rows // 2), rows // 2
    left = (side * 2 + core) * width
    return ref.at[pl.ds(pl.multiple_of(begin, count), count), pl.ds(pl.multiple_of(left, width), width)]

def send(ref_from, ref_to, sends, recvs, at, partner):
    copy = pltpu.make_async_remote_copy(src_ref=ref_from, dst_ref=ref_to, send_sem=sends.at[at], recv_sem=recvs.at[at], device_id=partner, device_id_type=MESH)
    copy.start()
    return copy

def spread(out, rows, width, sends, recvs, base):
    col, side, core = places()
    to_x, to_y, to_core = partners()
    def go(at, which, partner, part=None):
        ref = block(out, *which, rows, width, part)
        return send(ref, ref, sends, recvs, base + at, partner)
    own, ox, oy, od = (col, side, core), (1 - col, side, core), (col, 1 - side, core), (1 - col, 1 - side, core)
    c0 = go(0, own, to_x)
    c1 = go(1, own, to_y)
    c2 = go(2, own, to_core)
    c0.wait_recv()
    c3 = go(3, ox, to_y, 0)
    c1.wait_recv()
    c4 = go(4, oy, to_x, 1)
    c5 = go(5, ox, to_core)
    c6 = go(6, oy, to_core)
    c3.wait_recv()
    c4.wait_recv()
    c7 = go(7, od, to_core)
    for c in (c2, c5, c6, c7):
        c.wait_recv()
    for c in (c0, c1, c2, c3, c4, c5, c6, c7):
        c.wait_send()

def gather_kernel(x_ref, out, sends, recvs):
    rows, width = x_ref.shape
    greet()
    col, side, core = places()
    block(out, col, side, core, rows, width)[...] = x_ref[...]
    spread(out, rows, width, sends, recvs, 0)

def gather_plane(x, cid):
    rows, width = x.shape
    return pl.pallas_call(gather_kernel, out_shape=jax.ShapeDtypeStruct((2*rows,4*width), x.dtype),
        in_specs=[pl.BlockSpec(memory_space=pltpu.VMEM)], out_specs=pl.BlockSpec(memory_space=pltpu.VMEM),
        scratch_shapes=[pltpu.SemaphoreType.DMA((8,)), pltpu.SemaphoreType.DMA((8,))],
        compiler_params=pltpu.CompilerParams(collective_id=cid, has_side_effects=True, vmem_limit_bytes=50<<20))(x)

def sum_to_owner(part_ref, got, keep, diag, half_x, half_y, to_send, from_xy, sends, recvs, rows, width):
    col, side, core = places()
    to_x, to_y, to_core = partners()
    half = rows // 2
    spots = ((1-col,1-side),(col,1-side),(1-col,side),(col,side))
    copies = []
    for i,(a,b) in enumerate(spots):
        copies.append(send(block(part_ref, a, b, 1-core, rows, width), got.at[i], sends, recvs, i, to_core))
    f32 = jnp.float32
    copies[0].wait_recv()
    diag[...] = (block(part_ref, 1-col, 1-side, core, rows, width)[...].astype(f32) + got[0].astype(f32)).astype(diag.dtype)
    dx = send(diag.at[pl.ds(0,half)], half_x, sends, recvs, 4, to_x)
    dy = send(diag.at[pl.ds(half,half)], half_y, sends, recvs, 5, to_y)
    copies[1].wait_recv()
    copies[2].wait_recv()
    dx.wait_recv()
    py = block(part_ref, col, 1-side, core, rows, width)
    px = block(part_ref, 1-col, side, core, rows, width)
    ty = to_send.at[0]
    tx = to_send.at[1]
    ty[pl.ds(0,half)] = (py[pl.ds(0,half)].astype(f32) + got[1,pl.ds(0,half)].astype(f32) + half_x[...].astype(f32)).astype(diag.dtype)
    ty[pl.ds(half,half)] = (py[pl.ds(half,half)].astype(f32) + got[1,pl.ds(half,half)].astype(f32)).astype(diag.dtype)
    cy = send(ty, from_xy.at[0], sends, recvs, 6, to_y)
    dy.wait_recv()
    tx[pl.ds(0,half)] = (px[pl.ds(0,half)].astype(f32) + got[2,pl.ds(0,half)].astype(f32)).astype(diag.dtype)
    tx[pl.ds(half,half)] = (px[pl.ds(half,half)].astype(f32) + got[2,pl.ds(half,half)].astype(f32) + half_y[...].astype(f32)).astype(diag.dtype)
    cx = send(tx, from_xy.at[1], sends, recvs, 7, to_x)
    copies[3].wait_recv()
    keep[...] = block(part_ref, col, side, core, rows, width)[...].astype(f32) + got[3].astype(f32)
    cy.wait_recv()
    cx.wait_recv()
    for c in copies + [dx, dy, cy, cx]:
        c.wait_send()
    return keep[...] + from_xy[0].astype(f32) + from_xy[1].astype(f32)

def sum_scratch(rows, width, dt):
    return [pltpu.VMEM((4,rows,width),dt), pltpu.VMEM((rows,width),jnp.float32), pltpu.VMEM((rows,width),dt),
            pltpu.VMEM((rows//2,width),dt), pltpu.VMEM((rows//2,width),dt), pltpu.VMEM((2,rows,width),dt), pltpu.VMEM((2,rows,width),dt)]

def reduce_kernel(part_ref, out, *scratch):
    *bufs, sends, recvs = scratch
    rows, width = out.shape
    greet()
    out[...] = sum_to_owner(part_ref, *bufs, sends, recvs, rows, width)

def reduce_plane(part, cid):
    rows, width = part.shape[0]//2, part.shape[1]//4
    return pl.pallas_call(reduce_kernel, out_shape=jax.ShapeDtypeStruct((rows,width), jnp.float32),
        in_specs=[pl.BlockSpec(memory_space=pltpu.VMEM)], out_specs=pl.BlockSpec(memory_space=pltpu.VMEM),
        scratch_shapes=sum_scratch(rows,width,part.dtype)+[pltpu.SemaphoreType.DMA((8,)), pltpu.SemaphoreType.DMA((8,))],
        compiler_params=pltpu.CompilerParams(collective_id=cid, has_side_effects=True, vmem_limit_bytes=50<<20))(part)

def total_kernel(part_ref, out, *scratch):
    *bufs, sends, recvs = scratch
    rows, width = out.shape[0]//2, out.shape[1]//4
    greet()
    own = sum_to_owner(part_ref, *bufs, sends, recvs, rows, width)
    col, side, core = places()
    block(out, col, side, core, rows, width)[...] = own.astype(out.dtype)
    spread(out, rows, width, sends, recvs, 8)

def total_plane(part, cid):
    rows, width = part.shape[0]//2, part.shape[1]//4
    return pl.pallas_call(total_kernel, out_shape=jax.ShapeDtypeStruct(part.shape, part.dtype),
        in_specs=[pl.BlockSpec(memory_space=pltpu.VMEM)], out_specs=pl.BlockSpec(memory_space=pltpu.VMEM),
        scratch_shapes=sum_scratch(rows,width,part.dtype)+[pltpu.SemaphoreType.DMA((16,)), pltpu.SemaphoreType.DMA((16,))],
        compiler_params=pltpu.CompilerParams(collective_id=cid, has_side_effects=True, vmem_limit_bytes=50<<20))(part)


def put(ref_from, ref_to, sends, recvs, at, partner):
    return pltpu.make_async_remote_copy(
        src_ref=ref_from,
        dst_ref=ref_to,
        send_sem=sends.at[at],
        recv_sem=recvs.at[at],
        device_id=partner,
        device_id_type=MESH,
    )


def strip(begin, count):
    return pl.ds(pl.multiple_of(begin, count), count)


def dot_nt(left, right):
    return lax.dot_general(left, right, (((1,), (1,)), ((), ())), preferred_element_type=jnp.float32)


def dot_tn(left, right):
    return lax.dot_general(left, right, (((0,), (0,)), ((), ())), preferred_element_type=jnp.float32)


def tiled_nt(left, right, target, inner, tile_rows, tile_cols):
    rows, cols = target.shape
    across = cols // tile_cols

    def step(at, none):
        down, side = at // across, at % across
        value = dot_nt(left[strip(down * tile_rows, tile_rows), :inner], right[strip(side * tile_cols, tile_cols), :inner])
        target[strip(down * tile_rows, tile_rows), strip(side * tile_cols, tile_cols)] = value.astype(target.dtype)
        return none

    lax.fori_loop(0, (rows // tile_rows) * across, step, 0)


def tiled_nn(left, right, target, tile_rows, tile_cols):
    rows, cols = target.shape
    across = cols // tile_cols

    def step(at, none):
        down, side = at // across, at % across
        value = jnp.dot(
            left[strip(down * tile_rows, tile_rows), :],
            right[:, strip(side * tile_cols, tile_cols)],
            preferred_element_type=jnp.float32,
        )
        target[strip(down * tile_rows, tile_rows), strip(side * tile_cols, tile_cols)] = value.astype(target.dtype)
        return none

    lax.fori_loop(0, (rows // tile_rows) * across, step, 0)


def reduce_steps(part, result, got, keep, diag, half_x, half_y, to_send, from_xy, sends, recvs, base):
    f32 = jnp.float32
    rows, width = result.shape
    half = rows // 2
    low, high = pl.ds(0, half), pl.ds(half, half)
    col, side, core = places()
    to_x, to_y, to_core = partners()
    spots = ((1 - col, 1 - side), (col, 1 - side), (1 - col, side), (col, side))
    copies = [
        put(block(part, a, b, 1 - core, rows, width), got.at[k], sends, recvs, base + k, to_core)
        for k, (a, b) in enumerate(spots)
    ]
    for copy in copies:
        copy.start()
    mine = [block(part, a, b, core, rows, width) for a, b in spots]
    dx = put(diag.at[low], half_x, sends, recvs, base + 4, to_x)
    dy = put(diag.at[high], half_y, sends, recvs, base + 5, to_y)
    cy = put(to_send.at[0], from_xy.at[0], sends, recvs, base + 6, to_y)
    cx = put(to_send.at[1], from_xy.at[1], sends, recvs, base + 7, to_x)
    yield
    copies[0].wait_recv()
    diag[...] = (mine[0][...].astype(f32) + got[0].astype(f32)).astype(diag.dtype)
    dx.start()
    dy.start()
    copies[1].wait_recv()
    copies[2].wait_recv()
    to_send[0, high] = (mine[1][high].astype(f32) + got[1, high].astype(f32)).astype(diag.dtype)
    to_send[1, low] = (mine[2][low].astype(f32) + got[2, low].astype(f32)).astype(diag.dtype)
    copies[3].wait_recv()
    keep[...] = mine[3][...].astype(f32) + got[3].astype(f32)
    yield
    dx.wait_recv()
    to_send[0, low] = (mine[1][low].astype(f32) + got[1, low].astype(f32) + half_x[...].astype(f32)).astype(diag.dtype)
    cy.start()
    dy.wait_recv()
    to_send[1, high] = (mine[2][high].astype(f32) + got[2, high].astype(f32) + half_y[...].astype(f32)).astype(
        diag.dtype
    )
    cx.start()
    yield
    cy.wait_recv()
    cx.wait_recv()
    result[...] = keep[...] + from_xy[0].astype(f32) + from_xy[1].astype(f32)
    for copy in copies + [dx, dy, cy, cx]:
        copy.wait_send()


def spread_steps(out, rows, width, sends, recvs, base):
    col, side, core = places()
    to_x, to_y, to_core = partners()

    def copy_of(at, which, partner, part=None):
        ref = block(out, *which, rows, width, part)
        return put(ref, ref, sends, recvs, base + at, partner)

    own, ox, oy, od = (col, side, core), (1 - col, side, core), (col, 1 - side, core), (1 - col, 1 - side, core)
    plan = [
        copy_of(0, own, to_x),
        copy_of(1, own, to_y),
        copy_of(2, own, to_core),
        copy_of(3, ox, to_y, 0),
        copy_of(4, oy, to_x, 1),
        copy_of(5, ox, to_core),
        copy_of(6, oy, to_core),
        copy_of(7, od, to_core),
    ]
    for at in (0, 1, 2):
        plan[at].start()
    yield
    plan[0].wait_recv()
    plan[3].start()
    plan[1].wait_recv()
    plan[4].start()
    plan[5].start()
    plan[6].start()
    yield
    plan[3].wait_recv()
    plan[4].wait_recv()
    plan[7].start()
    yield
    for at in (2, 5, 6, 7):
        plan[at].wait_recv()
    for copy in plan:
        copy.wait_send()


CHUNK = 256


def backward_kernel(
    counts,
    hid_h,
    cot_h,
    dup_h,
    n2_h,
    upw_h,
    std_h,
    n1_h,
    qkvw_h,
    downw_h,
    attended,
    outw,
    mixed,
    lse,
    bias,
    inv2,
    gain2,
    down_out,
    up_out,
    out_out,
    qkv_out,
    r_land,
    m_land,
    b_land,
    dres_own,
    dn1_own,
    outp_own,
    sums,
    mixed_sums,
    cot,
    n2,
    std,
    part,
    tot,
    upw,
    hid,
    dup,
    d_att,
    d_mix,
    dk_acc,
    dv_acc,
    g,
    s,
    ld,
    t,
    got_a,
    diag_a,
    hx_a,
    hy_a,
    ts_a,
    fx_a,
    got_b,
    diag_b,
    hx_b,
    hy_b,
    ts_b,
    fx_b,
    keep,
    load_sem,
    ld_sem,
    own_sem,
    z_send,
    z_recv,
    a_send,
    a_recv,
    p_send,
    p_recv,
):
    f32, bf16 = jnp.float32, jnp.bfloat16
    n_down, n_up, n_out, n_qkv = counts
    total = sum(counts)
    plane, row, col = lax.axis_index("dp"), lax.axis_index("row"), lax.axis_index("col")
    length, full = cot.shape
    rows, width = dres_own.shape
    row_count = full // width
    inner = (plane == 1) | (plane == 2)
    outer = jnp.logical_not(inner)
    to_inner = {"dp": plane // 3 + 1}
    to_middle = {"dp": 3 - plane}
    to_outer = {"dp": (plane - 1) * 3}
    side, core = row // 2, row % 2

    loads = [
        (hid_h, hid),
        (cot_h, cot),
        (dup_h, dup),
        (upw_h, upw),
        (n2_h, n2),
        (std_h, std),
        (qkvw_h, upw.at[:, : qkvw_h.shape[1]]),
        (n1_h, std),
        (downw_h, n2),
    ]
    loads = [pltpu.make_async_copy(a, b, load_sem.at[k]) for k, (a, b) in enumerate(loads)]
    for k in range(6):
        loads[k].start()

    barrier = pltpu.get_barrier_semaphore()
    for partner in partners() + ({"row": (1 - side) * 2 + 1 - core},):
        pl.semaphore_signal(barrier, inc=1, device_id=partner, device_id_type=MESH)

    @pl.when(outer)
    def _():
        pl.semaphore_signal(barrier, inc=1, device_id=to_inner, device_id_type=MESH)
        pl.semaphore_wait(barrier, 5)

    @pl.when(inner)
    def _():
        pl.semaphore_signal(barrier, inc=1, device_id=to_middle, device_id_type=MESH)
        pl.semaphore_signal(barrier, inc=1, device_id=to_outer, device_id_type=MESH)
        pl.semaphore_wait(barrier, 6)

    def place(i, source):
        if i < n_down:
            return down_out.at[:, strip(source * n_down * CHUNK + i * CHUNK, CHUNK), :]
        i -= n_down
        if i < n_up:
            return up_out.at[:, :, strip(source * n_up * CHUNK + i * CHUNK, CHUNK)]
        i -= n_up
        if i < n_out:
            return out_out.at[:, strip(source * n_out * CHUNK + i * CHUNK, CHUNK), :]
        i -= n_out
        return qkv_out.at[:, :, strip(source * n_qkv * CHUNK + i * CHUNK, CHUNK)]

    g_slots, s_slots = g.shape[0], s.shape[0]

    def inward(i):
        return put(g.at[i % g_slots], r_land.at[i], z_send, z_recv, i, to_inner)

    def across(i):
        return put(s.at[i % s_slots], m_land.at[i], z_send, z_recv, total + i, to_middle)

    def outward(i):
        return put(t.at[i % s_slots], b_land.at[i], z_send, z_recv, 2 * total + i, to_outer)

    def home(i, step, source):
        target = (row + step) % row_count
        return put(source.at[target], place(i, row), a_send, a_recv, 3 * i + step - 1, {"row": target})

    def home_own(i, source):
        return pltpu.make_async_copy(source.at[row], place(i, row), own_sem.at[i])

    def send_home(i, source):
        for step in range(1, row_count):
            home(i, step, source).start()
        home_own(i, source).start()

    def sent_home(i, source):
        for step in range(1, row_count):
            home(i, step, source).wait_send()
        home_own(i, source).wait()

    def produce(i):
        if i >= g_slots:

            @pl.when(outer)
            def _():
                inward(i - g_slots).wait_send()

        slot = g.at[i % g_slots]
        if i < n_down or n_down + n_up <= i < n_down + n_up + n_out:
            if i < n_down:
                left, begin, right = hid, i * CHUNK, cot
            else:
                left, begin, right = attended, (i - n_down - n_up) * CHUNK, part

            def step(k, none):
                value = dot_tn(left[:, begin : begin + CHUNK], right[:, strip(k * width, width)]).astype(bf16)
                slot[k, 0] = value[:, :CHUNK]
                slot[k, 1] = value[:, CHUNK:]
                return none
        else:
            if i < n_down + n_up:
                left, right, begin = n2, dup, (i - n_down) * CHUNK
            else:
                left, right, begin = std, d_mix, (i - n_down - n_up - n_out) * CHUNK

            def step(k, none):
                value = dot_tn(left[:, strip(k * width, width)], right[:, begin : begin + CHUNK]).astype(bf16)
                slot[k, 0] = value[:CHUNK]
                slot[k, 1] = value[CHUNK:]
                return none

        lax.fori_loop(0, row_count, step, 0)

        @pl.when(outer)
        def _():
            inward(i).start()

    def add(first, target):
        def step(k, none):
            for half in range(2):
                target[k, half] = (first[k, half].astype(f32) + ld[k, half].astype(f32)).astype(bf16)
            return none

        lax.fori_loop(0, row_count, step, 0)

    def fetch(source):
        copy = pltpu.make_async_copy(source, ld, ld_sem)
        copy.start()
        copy.wait()

    def middle(i):
        @pl.when(inner)
        def _():
            inward(i).wait_recv()
            fetch(r_land.at[i])
            add(g.at[i % g_slots], s.at[i % s_slots])
            across(i).start()

    def finish_inner(i):
        @pl.when(inner)
        def _():
            if i >= s_slots:
                outward(i - s_slots).wait_send()
                sent_home(i - s_slots, t.at[i % s_slots])
            across(i).wait_recv()
            fetch(m_land.at[i])
            add(s.at[i % s_slots], t.at[i % s_slots])
            outward(i).start()
            send_home(i, t.at[i % s_slots])
            across(i).wait_send()

    def finish_outer(i):
        @pl.when(outer)
        def _():
            outward(i).wait_recv()
            send_home(i, b_land.at[i])

    def finish(i):
        finish_inner(i)
        if i >= 1:
            finish_outer(i - 1)

    set_a = (got_a, keep, diag_a, hx_a, hy_a, ts_a, fx_a)
    set_b = (got_b, keep, diag_b, hx_b, hy_b, ts_b, fx_b)

    loads[0].wait()
    loads[1].wait()
    produce(0)
    produce(1)
    loads[2].wait()
    loads[3].wait()
    tiled_nt(dup, upw, part, dup.shape[1], 1024, 256)
    loads[6].start()
    first = reduce_steps(part, outp_own, *set_a, p_send, p_recv, 0)
    next(first)
    next(first)
    next(first)
    loads[4].wait()
    loads[5].wait()
    middle(0)
    produce(2)
    next(first, None)
    block(tot, col, side, core, rows, width)[...] = outp_own[...].astype(bf16)
    second = spread_steps(tot, rows, width, p_send, p_recv, 8)
    next(second)
    next(second)
    next(second)
    middle(1)
    produce(3)
    finish(0)
    next(second, None)

    tile = 64
    sums[...] = jnp.zeros_like(sums)

    def norm_step(k, none):
        at = strip(k * tile, tile)
        grad, standard, inverse = tot[at, :].astype(f32), std[at, :].astype(f32), inv2[at, :]
        scaled = grad * gain2[...]
        mean_one = jnp.sum(scaled, axis=1, keepdims=True) / full
        mean_two = jnp.sum(scaled * standard, axis=1, keepdims=True) / full
        d_res = cot[at, :].astype(f32) + inverse * (scaled - mean_one - standard * mean_two)
        low = d_res.astype(bf16)
        part[at, :] = low
        sums[0:1, :] += jnp.sum(grad * standard, axis=0, keepdims=True)
        sums[1:2, :] += jnp.sum(grad, axis=0, keepdims=True)
        sums[2:3, :] += jnp.sum(low.astype(f32), axis=0, keepdims=True)

        @pl.when(k // (rows // tile) == col)
        def _():
            here = strip(row * width, width)
            own = tot[at, here].astype(f32) * gain2[:, here]
            dres_own[strip(k % (rows // tile) * tile, tile), :] = cot[at, here].astype(f32) + inverse * (
                own - mean_one - std[at, here].astype(f32) * mean_two
            )

        return none

    lax.fori_loop(0, length // tile, norm_step, 0)
    loads[7].start()
    tiled_nt(part, outw, d_att, full, 512, 256)
    produce(4)
    middle(2)
    finish(1)

    heads = mixed.shape[1] // (3 * HEAD)
    factor = 1.0 / math.sqrt(HEAD)
    blocks = length // SPAN

    def head_step(head, none):
        base = head * 3 * HEAD
        at_q, at_k, at_v = strip(base, HEAD), strip(base + HEAD, HEAD), strip(base + 2 * HEAD, HEAD)
        at_o = strip(head * HEAD, HEAD)
        dk_acc[...] = jnp.zeros_like(dk_acc)
        dv_acc[...] = jnp.zeros_like(dv_acc)
        for k in range(blocks):
            here = pl.ds(k * SPAN, SPAN)
            seen = (k + 1) * SPAN
            query, dout = mixed[here, at_q], d_att[here, at_o]
            keys, values = mixed[:seen, at_k], mixed[:seen, at_v]
            scores = dot_nt(query, keys) * factor
            last = scores[:, seen - SPAN :] + bias[k]
            scores = last if k == 0 else jnp.concatenate([scores[:, : seen - SPAN], last], axis=1)
            probs = jnp.exp(scores - lse[head, here])
            d_probs = dot_nt(dout, values)
            dots = jnp.sum(probs * d_probs, axis=1, keepdims=True)
            d_scores = (probs * (d_probs - dots)).astype(bf16)
            d_mix[here, at_q] = (jnp.dot(d_scores, keys, preferred_element_type=f32) * factor).astype(bf16)
            dk_acc[:seen] += dot_tn(d_scores, query)
            dv_acc[:seen] += dot_tn(probs.astype(bf16), dout)
        d_mix[:, at_k] = (dk_acc[...] * factor).astype(bf16)
        d_mix[:, at_v] = dv_acc[...].astype(bf16)
        return none

    lax.fori_loop(0, heads, head_step, 0)
    mixed_sums[...] = jnp.sum(d_mix[...].astype(f32), axis=0, keepdims=True)
    produce(5)
    middle(3)
    finish(2)
    loads[6].wait()
    tiled_nt(d_mix, upw, cot, d_mix.shape[1], 1024, 256)
    third = reduce_steps(cot, dn1_own, *set_b, p_send, p_recv, 16)
    next(third)
    next(third)
    produce(6)
    middle(4)
    finish(3)
    next(third)
    next(third, None)
    produce(7)
    loads[8].start()
    middle(5)
    finish(4)
    loads[8].wait()
    tiled_nn(hid, n2, tot, 1024, 256)
    fourth = reduce_steps(tot, outp_own, *set_a, p_send, p_recv, 24)
    next(fourth)
    next(fourth)
    produce(8)
    middle(6)
    finish(5)
    next(fourth)
    next(fourth, None)
    loads[7].wait()
    for k in range(9, total):
        produce(k)
        middle(k - 2)
        finish(k - 3)
    middle(total - 2)
    finish(total - 3)
    middle(total - 1)
    finish(total - 2)
    finish(total - 1)
    finish_outer(total - 1)

    @pl.when(outer)
    def _():
        for k in range(total - g_slots, total):
            inward(k).wait_send()
        for k in range(total):
            sent_home(k, b_land.at[k])

    @pl.when(inner)
    def _():
        for k in range(total - s_slots, total):
            outward(k).wait_send()
            sent_home(k, t.at[k % s_slots])

    for k in range(total):
        for step in range(1, row_count):
            source = (row + row_count - step) % row_count
            put(t.at[0, source], place(k, source), a_send, a_recv, 3 * k + step - 1, {"row": source}).wait_recv()


def backward_plane(cid, hid, cot, dup, n2, upw, std, n1, qkvw, downw, attended, outw, mixed, lse, bias, inv2, gain2):
    f32, bf16 = jnp.float32, jnp.bfloat16
    length, full = cot.shape
    rows, width = length // lax.axis_size("col"), full // lax.axis_size("row")
    row_count = full // width
    counts = (dup.shape[1] // CHUNK, dup.shape[1] // CHUNK, attended.shape[1] // CHUNK, mixed.shape[1] // CHUNK)
    total = sum(counts)
    one = (row_count, width // CHUNK, CHUNK, CHUNK)
    shape = jax.ShapeDtypeStruct
    away, near = pl.BlockSpec(memory_space=pl.ANY), pl.BlockSpec(memory_space=pltpu.VMEM)
    vmem, dma = pltpu.VMEM, pltpu.SemaphoreType.DMA
    sets = [
        vmem((4, rows, width), bf16),
        vmem((rows, width), bf16),
        vmem((rows // 2, width), bf16),
        vmem((rows // 2, width), bf16),
        vmem((2, rows, width), bf16),
        vmem((2, rows, width), bf16),
    ]
    return pl.pallas_call(
        functools.partial(backward_kernel, counts),
        out_shape=[
            shape((2, row_count * counts[0] * CHUNK, CHUNK), bf16),
            shape((2, CHUNK, row_count * counts[1] * CHUNK), bf16),
            shape((2, row_count * counts[2] * CHUNK, CHUNK), bf16),
            shape((2, CHUNK, row_count * counts[3] * CHUNK), bf16),
            shape((total,) + one, bf16),
            shape((total,) + one, bf16),
            shape((total,) + one, bf16),
            shape((rows, width), f32),
            shape((rows, width), f32),
            shape((rows, width), f32),
            shape((8, full), f32),
            shape((1, mixed.shape[1]), f32),
        ],
        in_specs=[away] * 9 + [near] * 7,
        out_specs=[away] * 7 + [near] * 5,
        scratch_shapes=[
            vmem((length, full), bf16),
            vmem((length, full), bf16),
            vmem((length, full), bf16),
            vmem((length, full), bf16),
            vmem((length, full), bf16),
            vmem(upw.shape, bf16),
            vmem(hid.shape, bf16),
            vmem(dup.shape, bf16),
            vmem(attended.shape, bf16),
            vmem(mixed.shape, bf16),
            vmem((length, HEAD), f32),
            vmem((length, HEAD), f32),
            vmem((3,) + one, bf16),
            vmem((2,) + one, bf16),
            vmem(one, bf16),
            vmem((2,) + one, bf16),
        ]
        + sets
        + sets
        + [
            vmem((rows, width), f32),
            dma((9,)),
            dma,
            dma((total,)),
            dma((3 * total,)),
            dma((3 * total,)),
            dma((3 * total,)),
            dma((3 * total,)),
            dma((32,)),
            dma((32,)),
        ],
        compiler_params=pltpu.CompilerParams(
            collective_id=cid, has_side_effects=True, vmem_limit_bytes=64 * 1024 * 1024 - 65536
        ),
        cost_estimate=pl.CostEstimate(flops=40_000_000_000, bytes_accessed=100_000_000, transcendentals=4_000_000),
    )(hid, cot, dup, n2, upw, std, n1, qkvw, downw, attended, outw, mixed, lse, bias, inv2, gain2)


def shift_rows(pieces):
    row, count = lax.axis_index("row"), pieces.shape[0]
    result = pieces
    for step in range(1, count):
        pairs = [(k, (k + step) % count) for k in range(count)]
        sent = lax.dynamic_index_in_dim(pieces, (row + step) % count, 0, keepdims=True)
        got = lax.ppermute(sent, "row", pairs)
        result = lax.dynamic_update_slice_in_dim(result, got, (row + count - step) % count, 0)
    return result


def norm_stats(values):
    center = jnp.mean(values, axis=1, keepdims=True)
    spread_of = jnp.mean(values * values, axis=1, keepdims=True) - center * center
    return center, lax.rsqrt(spread_of + epsilon)


def mask_of(span_starts, length):
    marks = jnp.sum(
        (span_starts[0][:, None] // SPAN == jnp.arange(length // SPAN, dtype=jnp.int32)[None, :]).astype(jnp.int32),
        axis=0,
    )
    places_of = jnp.arange(length, dtype=jnp.int32)
    image = jnp.repeat(marks, SPAN)
    return visible(places_of, image, places_of)


def plane_plan(
    tokens,
    ln1_gain,
    ln1_shift,
    qkv_weight,
    qv_bias,
    out_weight,
    out_bias,
    ln2_gain,
    ln2_shift,
    up_weight,
    up_bias,
    down_weight,
    down_bias,
    span_starts,
    cotangent,
):
    f32, bf16 = jnp.float32, jnp.bfloat16
    rows, width = tokens.shape
    row_count = lax.axis_size("row")
    col, row = lax.axis_index("col"), lax.axis_index("row")
    length, full = rows * lax.axis_size("col"), width * row_count
    heads = qkv_weight.shape[1] // row_count
    hidden_count = up_weight.shape[1] // row_count
    factor = 1.0 / math.sqrt(HEAD)

    def own(values):
        return lax.dynamic_slice(values, (col * rows, row * width), (rows, width))

    def own_width(values):
        return lax.dynamic_slice_in_dim(values, row * width, width, values.ndim - 1)

    def wide(vector):
        return lax.all_gather(vector, "row", axis=0, tiled=True)

    qkv_flat = shift_rows(
        jnp.moveaxis(qkv_weight.reshape(width, row_count, heads * 3 * HEAD), 1, 0)
    ).reshape(full, heads * 3 * HEAD)
    out_flat = jnp.moveaxis(
        shift_rows(out_weight.reshape(row_count, heads * HEAD, width)), 0, 1
    ).reshape(heads * HEAD, full)
    up_flat = shift_rows(jnp.moveaxis(up_weight.reshape(width, row_count, hidden_count), 1, 0)).reshape(
        full, hidden_count
    )
    down_flat = jnp.moveaxis(
        shift_rows(down_weight.reshape(row_count, hidden_count, width)), 0, 1
    ).reshape(hidden_count, full)
    vectors = wide(jnp.stack([ln1_gain, ln1_shift, out_bias, ln2_gain, ln2_shift], axis=0).T)
    gain1, shift1, branch_bias, gain2, shift2 = [vectors[:, k] for k in range(5)]
    own_qv = lax.dynamic_slice_in_dim(qv_bias, row * heads, heads, 0)
    own_up_bias = lax.dynamic_slice_in_dim(up_bias, row * hidden_count, hidden_count, 0)
    allowed = mask_of(span_starts, length)

    tokens_all = gather_plane(tokens, 1)
    cot_all = gather_plane(cotangent, 2)
    inputs = tokens_all.astype(f32)
    center1, inverse1 = norm_stats(inputs)
    normed1 = ((inputs - center1) * inverse1 * gain1 + shift1).astype(bf16)
    mixed = product(normed1, qkv_flat, False).reshape(length, heads, 3, HEAD)
    queries = (mixed[:, :, 0] + own_qv[:, 0]).astype(bf16)
    key_rows = mixed[:, :, 1].astype(bf16)
    value_rows = (mixed[:, :, 2] + own_qv[:, 1]).astype(bf16)
    scores = jnp.einsum("qhd,khd->hqk", queries, key_rows, preferred_element_type=f32) * factor
    scores = jnp.where(allowed[None], scores, masked_score)
    highest = jnp.max(scores, axis=2, keepdims=True)
    weights = jnp.exp(scores - highest)
    weight_sum = jnp.sum(weights, axis=2, keepdims=True)
    logsum = highest + jnp.log(weight_sum)
    attended = jnp.einsum("hqk,khd->qhd", (weights / weight_sum).astype(bf16), value_rows, preferred_element_type=f32)
    attended = attended.astype(bf16).reshape(length, heads * HEAD)
    branch = total_plane(product(attended, out_flat, False).astype(bf16), 3)
    residual = inputs + (branch.astype(f32) + branch_bias)
    center2, inverse2 = norm_stats(residual)
    standard2 = (residual - center2) * inverse2
    normed2 = (standard2 * gain2 + shift2).astype(bf16)
    up_sums = product(normed2, up_flat, False) + own_up_bias
    hidden = gelu_tanh(up_sums).astype(bf16)
    d_hidden = product(cot_all, down_flat, True)
    d_upper = jax.vjp(gelu_tanh, up_sums)[1](d_hidden)[0].astype(bf16)

    blocks = length // SPAN
    places_of = jnp.arange(SPAN, dtype=jnp.int32)
    marked = jnp.any(span_starts[0][:, None] // SPAN == jnp.arange(blocks, dtype=jnp.int32)[None, :], axis=0)
    open_pairs = (places_of[None, :] <= places_of[:, None])[None] | marked[:, None, None]
    bias = jnp.where(open_pairs, 0.0, masked_score).astype(f32)
    mixed_rows = jnp.stack([queries, key_rows, value_rows], axis=2).reshape(length, heads * 3 * HEAD)
    down_grad, up_grad, out_grad, qkv_grad, _, _, _, d_residual, d_normed1, sums_out, sums2, mixed_sums = backward_plane(
        4,
        hidden,
        cot_all,
        d_upper,
        normed2,
        up_flat,
        standard2.astype(bf16),
        normed1,
        qkv_flat,
        down_flat,
        attended,
        out_flat,
        mixed_rows,
        logsum,
        bias,
        inverse2,
        gain2[None],
    )
    standard1 = own((inputs - center1) * inverse1)
    own_inverse1 = lax.dynamic_slice_in_dim(inverse1, col * rows, rows, 0)
    d_norm1, gain1_grad, shift1_grad = norm_backward(
        d_normed1, standard1, own_inverse1[:, 0], ln1_gain
    )
    tokens_grad = (d_residual + d_norm1).astype(bf16)
    output = (own(residual) + (sums_out + down_bias)).astype(bf16)

    near = [
        own_width(sums2[0]),
        own_width(sums2[1]),
        own_width(sums2[2]),
        jnp.sum(own_width(cot_all), axis=0, dtype=f32),
    ]
    totals = mixed_sums.reshape(heads, 3, HEAD)
    spread_sums = [
        jnp.sum(d_upper, axis=0, dtype=f32),
        jnp.stack([totals[:, 0], totals[:, 2]], axis=1).reshape(heads * 2 * HEAD),
    ]
    slots = [lax.dynamic_update_index_in_dim(jnp.zeros((row_count,) + v.shape, f32), v, row, 0) for v in spread_sums]
    own_slots = [lax.dynamic_update_index_in_dim(jnp.zeros((row_count,) + v.shape, f32), v, row, 0) for v in near]
    summed = lax.psum(jnp.concatenate(slots + own_slots, axis=1), ("dp", "row"))
    up_bias_grad = summed[:, :hidden_count].reshape(-1)
    begin = hidden_count + heads * 2 * HEAD
    qv_bias_grad = summed[:, hidden_count:begin].reshape(row_count * heads, 2, HEAD)
    mine = lax.dynamic_index_in_dim(summed[:, begin:], row, 0, keepdims=False).reshape(4, width)
    norm1_sums = lax.psum((gain1_grad, shift1_grad), ("dp", "col"))

    return (
        output,
        tokens_grad,
        norm1_sums[0],
        norm1_sums[1],
        qkv_grad.astype(f32).reshape(width, row_count * heads, 3, HEAD),
        qv_bias_grad,
        jnp.moveaxis(out_grad, 0, 1).astype(f32).reshape(row_count * heads, HEAD, width),
        mine[2],
        mine[0],
        mine[1],
        up_grad.astype(f32).reshape(width, row_count * hidden_count),
        up_bias_grad,
        jnp.moveaxis(down_grad, 0, 1).astype(f32).reshape(row_count * hidden_count, width),
        mine[3],
    )


def solution(mesh):
    sizes = dict(mesh.shape)
    flat = sizes == {"dp": 4, "row": 4, "col": 2}
    per_device = plane_plan if flat else general_plan
    placed = (
        P(("dp", "col"), "row"),
        P("row"),
        P("row"),
        P("row", "col", None, None),
        P("col", None, None),
        P("col", None, "row"),
        P("row"),
        P("row"),
        P("row"),
        P("row", "col"),
        P("col"),
        P("col", "row"),
        P("row"),
        P("dp", None),
        P(("dp", "col"), "row"),
    )
    return jax.shard_map(
        per_device,
        mesh=mesh,
        in_specs=placed,
        out_specs=(
            P(("dp", "col"), "row"),
            P(("dp", "col"), "row"),
            P("row"),
            P("row"),
            P("row", "col", None, None),
            P("col", None, None),
            P("col", None, "row"),
            P("row"),
            P("row"),
            P("row"),
            P("row", "col"),
            P("col"),
            P("col", "row"),
            P("row"),
        ),
        check_vma=False,
    )
```

```python
import functools
import math

import jax
import jax.numpy as jnp
from jax import lax
from jax.experimental import pallas as pl
from jax.experimental.pallas import tpu as pltpu
from jax.sharding import PartitionSpec as P

MESH = pl.DeviceIdType.MESH

D = 2048
HEAD = 128
SEQS = 1
SPAN = 256
BLOCK = 512


epsilon = 1e-05
masked_score = -1e30


def gelu_tanh(values):
    return (
        0.5
        * values
        * (1.0 + jnp.tanh(0.7978845608028654 * (values + 0.044715 * values * values * values)))
    )


def gather_columns(block_data):
    return lax.all_gather(block_data, "col", axis=0, tiled=True)


def gather_rows(block_data):
    return lax.all_gather(block_data, "row", axis=0, tiled=True)


def product(left_side, right_side, flipped):
    if flipped:
        return lax.dot_general(
            left_side, right_side, (((1,), (1,)), ((), ())), preferred_element_type=jnp.float32
        )
    return jnp.dot(left_side, right_side, preferred_element_type=jnp.float32)


def outer_sum(left_side, right_side):
    return lax.dot_general(
        left_side, right_side, (((0,), (0,)), ((), ())), preferred_element_type=jnp.float32
    )


def sum_rows(left_side, right_side, flipped):
    wide_left = lax.all_to_all(left_side, "row", split_axis=0, concat_axis=1, tiled=True)
    if flipped:
        wide_right = lax.all_gather(right_side, "row", axis=1, tiled=True)
    else:
        wide_right = lax.all_gather(right_side, "row", axis=0, tiled=True)
    return product(wide_left, wide_right, flipped)


def sum_columns(left_side, right_side, flipped):
    return lax.psum_scatter(
        product(left_side, right_side, flipped), "col", scatter_dimension=0, tiled=True
    )


def row_totals(first_sum, second_sum):
    return lax.psum((first_sum, second_sum), "row")


def norm_forward(values, gain_row, bias_row):
    totals, squares = row_totals(jnp.sum(values, axis=1), jnp.sum(values * values, axis=1))
    center = totals / D
    spread = squares / D - center * center
    inverse = lax.rsqrt(spread + epsilon)
    standard = (values - center[:, None]) * inverse[:, None]
    return (standard, inverse, (standard * gain_row + bias_row).astype(jnp.bfloat16))


def norm_backward(upstream, standard, inverse, gain_row):
    scaled = upstream * gain_row
    first_sum, second_sum = row_totals(jnp.sum(scaled, axis=1), jnp.sum(scaled * standard, axis=1))
    gradient = inverse[:, None] * (
        scaled - first_sum[:, None] / D - standard * (second_sum[:, None] / D)
    )
    return (gradient, jnp.sum(upstream * standard, axis=0), jnp.sum(upstream, axis=0))


def visible(query_pos, query_image, key_pos):
    earlier = key_pos[None, :] <= query_pos[:, None]
    same_span = (key_pos[None, :] // SPAN == query_pos[:, None] // SPAN) & (
        query_image[:, None] > 0
    )
    return earlier | same_span


def attention_forward(queries, key_value, token_image, row_offset, seq_length, block_rows):
    own_rows, head_count, width = queries.shape
    factor = 1.0 / math.sqrt(width)

    def block_forward(block_index):
        local = block_index * block_rows
        start_pos = row_offset + local
        query_block = lax.dynamic_slice_in_dim(queries, local, block_rows, 0)
        query_pos = start_pos + jnp.arange(block_rows, dtype=jnp.int32)
        query_image = lax.dynamic_slice_in_dim(token_image, start_pos, block_rows, 0)
        begin = start_pos // seq_length * seq_length // block_rows
        finish = start_pos // block_rows + 1

        def key_step(key_index, state_in):
            running, weight_sum, gathered = state_in
            key_begin = key_index * block_rows
            key_block = lax.dynamic_slice_in_dim(key_value, key_begin, block_rows, 0)
            key_pos = key_begin + jnp.arange(block_rows, dtype=jnp.int32)
            allowed = visible(query_pos, query_image, key_pos)
            scores = (
                jnp.einsum(
                    "qhd,khd->hqk",
                    query_block,
                    key_block[:, :, 0],
                    preferred_element_type=jnp.float32,
                )
                * factor
            )
            scores = jnp.where(allowed[None], scores, masked_score)
            highest = jnp.maximum(running, jnp.max(scores, axis=2))
            weights = jnp.exp(scores - highest[:, :, None])
            shrink = jnp.exp(running - highest)
            weight_sum = weight_sum * shrink + jnp.sum(weights, axis=2)
            gathered = gathered * shrink.T[:, :, None] + jnp.einsum(
                "hqk,khd->qhd",
                weights.astype(jnp.bfloat16),
                key_block[:, :, 1],
                preferred_element_type=jnp.float32,
            )
            return (highest, weight_sum, gathered)

        initial = (
            jnp.full((head_count, block_rows), masked_score, jnp.float32),
            jnp.zeros((head_count, block_rows), jnp.float32),
            jnp.zeros((block_rows, head_count, width), jnp.float32),
        )
        running, weight_sum, gathered = lax.fori_loop(begin, finish, key_step, initial)
        return (gathered / weight_sum.T[:, :, None], running + jnp.log(weight_sum))

    result, logsum = lax.map(block_forward, jnp.arange(own_rows // block_rows, dtype=jnp.int32))
    return (result.reshape(own_rows, head_count, width), logsum)


def attention_backward(
    queries,
    key_value,
    attended_full,
    logsum,
    d_attended,
    token_image,
    row_offset,
    seq_length,
    block_rows,
):
    own_rows, head_count, width = queries.shape
    factor = 1.0 / math.sqrt(width)
    row_dots = jnp.sum(d_attended.astype(jnp.float32) * attended_full, axis=2)

    def block_backward(block_index, state_out):
        d_queries, d_pairs = state_out
        local = block_index * block_rows
        start_pos = row_offset + local
        query_block = lax.dynamic_slice_in_dim(queries, local, block_rows, 0)
        dout_block = lax.dynamic_slice_in_dim(d_attended, local, block_rows, 0)
        dots_block = lax.dynamic_slice_in_dim(row_dots, local, block_rows, 0).T
        logsum_block = logsum[block_index]
        query_pos = start_pos + jnp.arange(block_rows, dtype=jnp.int32)
        query_image = lax.dynamic_slice_in_dim(token_image, start_pos, block_rows, 0)
        begin = start_pos // seq_length * seq_length // block_rows
        finish = start_pos // block_rows + 1

        def key_step(key_index, state_in):
            d_query, d_keys = state_in
            key_begin = key_index * block_rows
            key_block = lax.dynamic_slice_in_dim(key_value, key_begin, block_rows, 0)
            key_pos = key_begin + jnp.arange(block_rows, dtype=jnp.int32)
            allowed = visible(query_pos, query_image, key_pos)
            scores = (
                jnp.einsum(
                    "qhd,khd->hqk",
                    query_block,
                    key_block[:, :, 0],
                    preferred_element_type=jnp.float32,
                )
                * factor
            )
            scores = jnp.where(allowed[None], scores, masked_score)
            probabilities = jnp.exp(scores - logsum_block[:, :, None])
            d_probs = jnp.einsum(
                "qhd,khd->hqk", dout_block, key_block[:, :, 1], preferred_element_type=jnp.float32
            )
            d_scores = (probabilities * (d_probs - dots_block[:, :, None])).astype(jnp.bfloat16)
            d_query = d_query + jnp.einsum(
                "hqk,khd->qhd", d_scores, key_block[:, :, 0], preferred_element_type=jnp.float32
            )
            d_key = (
                jnp.einsum(
                    "hqk,qhd->khd", d_scores, query_block, preferred_element_type=jnp.float32
                )
                * factor
            )
            d_value = jnp.einsum(
                "hqk,qhd->khd",
                probabilities.astype(jnp.bfloat16),
                dout_block,
                preferred_element_type=jnp.float32,
            )
            previous = lax.dynamic_slice_in_dim(d_keys, key_begin, block_rows, 0)
            d_keys = lax.dynamic_update_slice_in_dim(
                d_keys, previous + jnp.stack([d_key, d_value], axis=2), key_begin, 0
            )
            return (d_query, d_keys)

        d_query, d_pairs = lax.fori_loop(
            begin,
            finish,
            key_step,
            (jnp.zeros((block_rows, head_count, width), jnp.float32), d_pairs),
        )
        d_queries = lax.dynamic_update_slice_in_dim(d_queries, d_query * factor, local, 0)
        return (d_queries, d_pairs)

    initial = (
        jnp.zeros((own_rows, head_count, width), jnp.float32),
        jnp.zeros((key_value.shape[0], head_count, 2, width), jnp.float32),
    )
    return lax.fori_loop(0, own_rows // block_rows, block_backward, initial)


def general_plan(
    tokens,
    ln1_gain,
    ln1_shift,
    qkv_weight,
    qv_bias,
    out_weight,
    out_bias,
    ln2_gain,
    ln2_shift,
    up_weight,
    up_bias,
    down_weight,
    down_bias,
    span_starts,
    cotangent,
):
    col_rows, row_width = tokens.shape
    group_rows = col_rows * lax.axis_size("col")
    own_rows = group_rows // lax.axis_size("row")
    head_count = qkv_weight.shape[1]
    seq_length = group_rows // SEQS
    block_rows = BLOCK - own_rows % BLOCK
    row_offset = lax.axis_index("row") * own_rows
    slot_count = seq_length // SPAN
    image_marks = jnp.sum(
        (
            span_starts[:, :, None] // SPAN
            == jnp.arange(slot_count, dtype=jnp.int32)[None, None, :]
        ).astype(jnp.int32),
        axis=1,
    )
    token_image = jnp.broadcast_to(
        image_marks.reshape(-1)[:, None], (group_rows // SPAN, SPAN)
    ).reshape(group_rows)
    qkv_flat = qkv_weight.reshape(row_width, head_count * 3 * HEAD)
    out_flat = out_weight.reshape(head_count * HEAD, row_width)
    inputs = tokens.astype(jnp.float32)
    standard1, inverse1, normed1 = norm_forward(inputs, ln1_gain, ln1_shift)
    normed1_all = gather_columns(normed1)
    mixed_sums = sum_rows(normed1_all, qkv_flat, False).reshape(own_rows, head_count, 3, HEAD)
    queries = (mixed_sums[:, :, 0] + qv_bias[:, 0]).astype(jnp.bfloat16)
    key_value_own = jnp.stack(
        [mixed_sums[:, :, 1], mixed_sums[:, :, 2] + qv_bias[:, 1]], axis=2
    ).astype(jnp.bfloat16)
    key_value = gather_rows(key_value_own)
    attended_full, logsum = attention_forward(
        queries, key_value, token_image, row_offset, seq_length, block_rows
    )
    attended = attended_full.astype(jnp.bfloat16).reshape(own_rows, head_count * HEAD)
    attended_all = gather_rows(attended)
    residual = inputs + (sum_columns(attended_all, out_flat, False) + out_bias)
    standard2, inverse2, normed2 = norm_forward(residual, ln2_gain, ln2_shift)
    normed2_all = gather_columns(normed2)
    up_sums = sum_rows(normed2_all, up_weight, False) + up_bias
    hidden = gelu_tanh(up_sums).astype(jnp.bfloat16)
    hidden_all = gather_rows(hidden)
    output = (residual + (sum_columns(hidden_all, down_weight, False) + down_bias)).astype(
        jnp.bfloat16
    )
    d_output = cotangent.astype(jnp.float32)
    d_output_all = gather_columns(cotangent)
    down_grad = outer_sum(hidden_all, d_output_all)
    down_bias_grad = jnp.sum(d_output_all, axis=0, dtype=jnp.float32)
    d_hidden = sum_rows(d_output_all, down_weight, True)
    d_upper = jax.vjp(gelu_tanh, up_sums)[1](d_hidden)[0].astype(jnp.bfloat16)
    d_upper_all = gather_rows(d_upper)
    normed2_use = gather_columns(normed2)
    up_grad = outer_sum(normed2_use, d_upper_all)
    up_bias_grad = jnp.sum(d_upper_all, axis=0, dtype=jnp.float32)
    d_normed2 = sum_columns(d_upper_all, up_weight, True)
    d_norm2, gain2_grad, shift2_grad = norm_backward(d_normed2, standard2, inverse2, ln2_gain)
    d_residual = d_output + d_norm2
    d_branch = d_residual.astype(jnp.bfloat16)
    d_branch_all = gather_columns(d_branch)
    out_grad = outer_sum(attended_all, d_branch_all)
    out_bias_grad = jnp.sum(d_branch_all, axis=0, dtype=jnp.float32)
    d_attended = (
        sum_rows(d_branch_all, out_flat, True)
        .astype(jnp.bfloat16)
        .reshape(own_rows, head_count, HEAD)
    )
    d_queries, d_pairs = attention_backward(
        queries,
        key_value,
        attended_full,
        logsum,
        d_attended,
        token_image,
        row_offset,
        seq_length,
        block_rows,
    )
    d_pairs_own = lax.psum_scatter(d_pairs, "row", scatter_dimension=0, tiled=True)
    d_mixed = jnp.concatenate([d_queries[:, :, None], d_pairs_own], axis=2).astype(jnp.bfloat16)
    d_mixed_all = gather_rows(d_mixed)
    normed1_use = gather_columns(normed1)
    d_mixed_flat = d_mixed_all.reshape(group_rows, head_count * 3 * HEAD)
    qkv_grad = outer_sum(normed1_use, d_mixed_flat)
    mixed_totals = jnp.sum(d_mixed_all, axis=0, dtype=jnp.float32)
    qv_bias_grad = jnp.stack([mixed_totals[:, 0], mixed_totals[:, 2]], axis=1)
    d_normed1 = sum_columns(d_mixed_flat, qkv_flat, True)
    d_norm1, gain1_grad, shift1_grad = norm_backward(d_normed1, standard1, inverse1, ln1_gain)
    tokens_grad = (d_residual + d_norm1).astype(jnp.bfloat16)
    norm_sums = lax.psum((gain1_grad, shift1_grad, gain2_grad, shift2_grad), ("dp", "col"))
    weight_sums = lax.psum(
        (
            qkv_grad,
            qv_bias_grad,
            out_grad,
            out_bias_grad,
            up_grad,
            up_bias_grad,
            down_grad,
            down_bias_grad,
        ),
        "dp",
    )
    return (
        output,
        tokens_grad,
        norm_sums[0],
        norm_sums[1],
        weight_sums[0].reshape(row_width, head_count, 3, HEAD),
        weight_sums[1],
        weight_sums[2].reshape(head_count, HEAD, row_width),
        weight_sums[3],
        norm_sums[2],
        norm_sums[3],
        weight_sums[4],
        weight_sums[5],
        weight_sums[6],
        weight_sums[7],
    )


def places():
    row, col = lax.axis_index("row"), lax.axis_index("col")
    return col, row // 2, row % 2


def partners():
    col, side, core = places()
    return ({"col": 1 - col}, {"row": (1 - side) * 2 + core}, {"row": side * 2 + 1 - core})


def block(ref, col, side, core, rows, width, part=None):
    begin, count = col * rows, rows
    if part is not None:
        begin, count = begin + part * (rows // 2), rows // 2
    return ref.at[strip(begin, count), strip((side * 2 + core) * width, width)]


def put(ref_from, ref_to, sends, recvs, at, partner):
    return pltpu.make_async_remote_copy(
        src_ref=ref_from,
        dst_ref=ref_to,
        send_sem=sends.at[at],
        recv_sem=recvs.at[at],
        device_id=partner,
        device_id_type=MESH,
    )


def strip(begin, count):
    return pl.ds(pl.multiple_of(begin, count), count)


def dot_nt(left, right):
    return lax.dot_general(left, right, (((1,), (1,)), ((), ())), preferred_element_type=jnp.float32)


def dot_tn(left, right):
    return lax.dot_general(left, right, (((0,), (0,)), ((), ())), preferred_element_type=jnp.float32)


def tiled_nt(left, right, target, inner, tile_rows, tile_cols):
    rows, cols = target.shape
    across = cols // tile_cols

    def step(at, none):
        down, side = at // across, at % across
        value = dot_nt(left[strip(down * tile_rows, tile_rows), :inner], right[strip(side * tile_cols, tile_cols), :inner])
        target[strip(down * tile_rows, tile_rows), strip(side * tile_cols, tile_cols)] = value.astype(target.dtype)
        return none

    lax.fori_loop(0, (rows // tile_rows) * across, step, 0)


def tiled_nn(left, right, target, tile_rows, tile_cols):
    rows, cols = target.shape
    across = cols // tile_cols

    def step(at, none):
        down, side = at // across, at % across
        value = jnp.dot(
            left[strip(down * tile_rows, tile_rows), :],
            right[:, strip(side * tile_cols, tile_cols)],
            preferred_element_type=jnp.float32,
        )
        target[strip(down * tile_rows, tile_rows), strip(side * tile_cols, tile_cols)] = value.astype(target.dtype)
        return none

    lax.fori_loop(0, (rows // tile_rows) * across, step, 0)


def reduce_steps(part, result, got, diag, half_x, half_y, to_send, from_xy, sends, recvs, base):
    f32 = jnp.float32
    rows, width = result.shape
    half = rows // 2
    low, high = pl.ds(0, half), pl.ds(half, half)
    col, side, core = places()
    to_x, to_y, to_core = partners()
    spots = ((1 - col, 1 - side), (col, 1 - side), (1 - col, side), (col, side))
    copies = [
        put(block(part, a, b, 1 - core, rows, width), got.at[k], sends, recvs, base + k, to_core)
        for k, (a, b) in enumerate(spots)
    ]
    for copy in copies:
        copy.start()
    mine = [block(part, a, b, core, rows, width) for a, b in spots]
    dx = put(diag.at[low], half_x, sends, recvs, base + 4, to_x)
    dy = put(diag.at[high], half_y, sends, recvs, base + 5, to_y)
    cy = put(to_send.at[0], from_xy.at[0], sends, recvs, base + 6, to_y)
    cx = put(to_send.at[1], from_xy.at[1], sends, recvs, base + 7, to_x)
    yield
    copies[0].wait_recv()
    diag[...] = (mine[0][...].astype(f32) + got[0].astype(f32)).astype(diag.dtype)
    dx.start()
    dy.start()
    copies[1].wait_recv()
    copies[2].wait_recv()
    to_send[0, high] = (mine[1][high].astype(f32) + got[1, high].astype(f32)).astype(diag.dtype)
    to_send[1, low] = (mine[2][low].astype(f32) + got[2, low].astype(f32)).astype(diag.dtype)
    copies[3].wait_recv()
    result[...] = mine[3][...].astype(f32) + got[3].astype(f32)
    yield
    dx.wait_recv()
    to_send[0, low] = (mine[1][low].astype(f32) + got[1, low].astype(f32) + half_x[...].astype(f32)).astype(diag.dtype)
    cy.start()
    dy.wait_recv()
    to_send[1, high] = (mine[2][high].astype(f32) + got[2, high].astype(f32) + half_y[...].astype(f32)).astype(
        diag.dtype
    )
    cx.start()
    yield
    cy.wait_recv()
    cx.wait_recv()
    result[...] = result[...] + from_xy[0].astype(f32) + from_xy[1].astype(f32)
    for copy in copies + [dx, dy, cy, cx]:
        copy.wait_send()


def spread_steps(out, rows, width, sends, recvs, base):
    col, side, core = places()
    to_x, to_y, to_core = partners()

    def copy_of(at, which, partner, part=None):
        ref = block(out, *which, rows, width, part)
        return put(ref, ref, sends, recvs, base + at, partner)

    own, ox, oy, od = (col, side, core), (1 - col, side, core), (col, 1 - side, core), (1 - col, 1 - side, core)
    plan = [
        copy_of(0, own, to_x),
        copy_of(1, own, to_y),
        copy_of(2, own, to_core),
        copy_of(3, ox, to_y, 0),
        copy_of(4, oy, to_x, 1),
        copy_of(5, ox, to_core),
        copy_of(6, oy, to_core),
        copy_of(7, od, to_core),
    ]
    for at in (0, 1, 2):
        plan[at].start()
    yield
    plan[0].wait_recv()
    plan[3].start()
    plan[1].wait_recv()
    plan[4].start()
    plan[5].start()
    plan[6].start()
    yield
    plan[3].wait_recv()
    plan[4].wait_recv()
    plan[7].start()
    yield
    for at in (2, 5, 6, 7):
        plan[at].wait_recv()
    for copy in plan:
        copy.wait_send()


CHUNK = 256


def backward_kernel(
    counts,
    hid_h,
    cot_h,
    slope_h,
    n2_h,
    upw_h,
    std_h,
    n1_h,
    qkvw_h,
    down_nat,
    resid_h,
    attended,
    outw,
    mixed,
    lse,
    bias,
    inv2,
    vec_all,
    std1_own,
    inv1_own,
    down_bias,
    down_out,
    up_out,
    out_out,
    qkv_out,
    r_land,
    m_land,
    b_land,
    downw_land,
    out_block,
    tokens_block,
    small_out,
    cot,
    n2,
    std,
    part,
    tot,
    upw,
    hid,
    dup,
    d_att,
    d_mix,
    dk_acc,
    dv_acc,
    g,
    s,
    ld,
    t,
    got_a,
    diag_a,
    hx_a,
    hy_a,
    ts_a,
    fx_a,
    got_b,
    diag_b,
    hx_b,
    hy_b,
    ts_b,
    fx_b,
    dres_own,
    own_sum,
    sums,
    small,
    x_land,
    dp_land,
    stat_land,
    load_sem,
    ld_sem,
    own_sem,
    z_send,
    z_recv,
    a_send,
    a_recv,
    p_send,
    p_recv,
):
    f32, bf16 = jnp.float32, jnp.bfloat16
    n_down, n_up, n_out, n_qkv = counts
    total = sum(counts)
    plane, row, col = lax.axis_index("dp"), lax.axis_index("row"), lax.axis_index("col")
    length, full = cot.shape
    rows, width = dres_own.shape
    row_count = full // width
    inner = (plane == 1) | (plane == 2)
    outer = jnp.logical_not(inner)
    to_inner = {"dp": plane // 3 + 1}
    to_middle = {"dp": 3 - plane}
    to_outer = {"dp": (plane - 1) * 3}
    side, core = row // 2, row % 2

    loads = [
        (hid_h, hid),
        (cot_h, cot),
        (slope_h, dup),
        (upw_h, upw),
        (n2_h, n2),
        (std_h, std),
        (qkvw_h, upw.at[:, : qkvw_h.shape[1]]),
        (n1_h, std),
        (downw_land, n2),
        (downw_land, tot),
        (resid_h, dres_own),
    ]
    loads = [pltpu.make_async_copy(a, b, load_sem.at[k]) for k, (a, b) in enumerate(loads)]
    for k in range(6):
        loads[k].start()

    dp_count = dp_land.shape[0]
    barrier = pltpu.get_barrier_semaphore()
    others = [{"row": (1 - side) * 2 + 1 - core}] + [{"dp": (plane + k) % dp_count} for k in range(1, dp_count)]
    for partner in partners() + tuple(others):
        pl.semaphore_signal(barrier, inc=1, device_id=partner, device_id_type=MESH)
    pl.semaphore_wait(barrier, 3 + len(others))

    units = hid.shape[1]
    down_sends, down_recvs = [], []
    for step in range(1, row_count):
        target, source = (row + step) % row_count, (row + row_count - step) % row_count
        here, there = downw_land.at[:, strip(row * width, width)], downw_land.at[:, strip(source * width, width)]
        piece = down_nat.at[strip(target * units, units), :]
        down_sends.append(put(piece, here, p_send, p_recv, 32 + step - 1, {"row": target}))
        down_recvs.append(put(piece, there, p_send, p_recv, 32 + step - 1, {"row": source}))
        down_sends[-1].start()
    down_own = pltpu.make_async_copy(
        down_nat.at[strip(row * units, units), :], downw_land.at[:, strip(row * width, width)], own_sem.at[total]
    )
    down_own.start()

    def place(i, source):
        if i < n_down:
            return down_out.at[strip(source * n_down + i // 2 * 2, 2), :, pl.ds(i % 2 * CHUNK, CHUNK)]
        i -= n_down
        if i < n_up:
            return up_out.at[:, :, strip(source * n_up * CHUNK + i * CHUNK, CHUNK)]
        i -= n_up
        if i < n_out:
            return out_out.at[:, strip(source * n_out * CHUNK + i * CHUNK, CHUNK), :]
        i -= n_out
        return qkv_out.at[:, :, strip(source * n_qkv * CHUNK + i * CHUNK, CHUNK)]

    g_slots, s_slots = g.shape[0], s.shape[0]

    def inward(i):
        return put(g.at[i % g_slots], r_land.at[i], z_send, z_recv, i, to_inner)

    def across(i):
        return put(s.at[i % s_slots], m_land.at[i], z_send, z_recv, total + i, to_middle)

    def outward(i):
        return put(t.at[i % s_slots], b_land.at[i], z_send, z_recv, 2 * total + i, to_outer)

    def home(i, step, source):
        target = (row + step) % row_count
        return put(source.at[target], place(i, row), a_send, a_recv, 3 * i + step - 1, {"row": target})

    def home_own(i, source):
        return pltpu.make_async_copy(source.at[row], place(i, row), own_sem.at[i])

    def send_home(i, source):
        for step in range(1, row_count):
            home(i, step, source).start()
        home_own(i, source).start()

    def sent_home(i, source):
        for step in range(1, row_count):
            home(i, step, source).wait_send()
        home_own(i, source).wait()

    def produce(i):
        if i >= g_slots:

            @pl.when(outer)
            def _():
                inward(i - g_slots).wait_send()

        slot = g.at[i % g_slots]
        if i < n_down:
            begin, lane = i // 2 * 2 * CHUNK, i % 2 * CHUNK

            def step(k, none):
                value = dot_tn(hid[:, begin : begin + 2 * CHUNK], cot[:, strip(k * width + lane, CHUNK)]).astype(bf16)
                slot[k, 0] = value[:CHUNK]
                slot[k, 1] = value[CHUNK:]
                return none
        elif n_down + n_up <= i < n_down + n_up + n_out:
            left, begin, right = attended, (i - n_down - n_up) * CHUNK, part

            def step(k, none):
                value = dot_tn(left[:, begin : begin + CHUNK], right[:, strip(k * width, width)]).astype(bf16)
                slot[k, 0] = value[:, :CHUNK]
                slot[k, 1] = value[:, CHUNK:]
                return none
        else:
            if i < n_down + n_up:
                left, right, begin = n2, dup, (i - n_down) * CHUNK
            else:
                left, right, begin = std, d_mix, (i - n_down - n_up - n_out) * CHUNK

            def step(k, none):
                value = dot_tn(left[:, strip(k * width, width)], right[:, begin : begin + CHUNK]).astype(bf16)
                slot[k, 0] = value[:CHUNK]
                slot[k, 1] = value[CHUNK:]
                return none

        lax.fori_loop(0, row_count, step, 0)

        @pl.when(outer)
        def _():
            inward(i).start()

    def add(first, target):
        def step(k, none):
            for half in range(2):
                target[k, half] = (first[k, half].astype(f32) + ld[k, half].astype(f32)).astype(bf16)
            return none

        lax.fori_loop(0, row_count, step, 0)

    def fetch(source):
        copy = pltpu.make_async_copy(source, ld, ld_sem)
        copy.start()
        copy.wait()

    def middle(i):
        @pl.when(inner)
        def _():
            inward(i).wait_recv()
            fetch(r_land.at[i])
            add(g.at[i % g_slots], s.at[i % s_slots])
            across(i).start()

    def finish_inner(i):
        @pl.when(inner)
        def _():
            if i >= s_slots:
                outward(i - s_slots).wait_send()
                sent_home(i - s_slots, t.at[i % s_slots])
            across(i).wait_recv()
            fetch(m_land.at[i])
            add(s.at[i % s_slots], t.at[i % s_slots])
            outward(i).start()
            send_home(i, t.at[i % s_slots])
            across(i).wait_send()

    def finish_outer(i):
        @pl.when(outer)
        def _():
            outward(i).wait_recv()
            send_home(i, b_land.at[i])

    def finish(i):
        finish_inner(i)
        if i >= 1:
            finish_outer(i - 1)

    set_a = (got_a, diag_a, hx_a, hy_a, ts_a, fx_a)
    set_b = (got_b, diag_b, hx_b, hy_b, ts_b, fx_b)
    gain2 = vec_all[3:4, :]

    loads[0].wait()
    loads[1].wait()
    produce(0)
    produce(1)
    sums[...] = jnp.zeros_like(sums)
    middle(0)
    produce(2)
    down_own.wait()
    for copy in down_recvs:
        copy.wait_recv()
    loads[9].start()
    loads[2].wait()
    middle(1)
    produce(3)
    finish(0)
    loads[9].wait()

    def upper_step(k, none):
        down, across_ = k // (units // CHUNK), k % (units // CHUNK)
        at, lanes = strip(down * rows, rows), strip(across_ * CHUNK, CHUNK)
        dup[at, lanes] = (dot_nt(cot[at, :], tot[lanes, :]) * dup[at, lanes].astype(f32)).astype(bf16)
        return none

    lax.fori_loop(0, (length // rows) * (units // CHUNK), upper_step, 0)
    loads[3].wait()
    tiled_nt(dup, upw, part, dup.shape[1], 1024, 256)
    loads[6].start()
    first = reduce_steps(part, own_sum, *set_a, p_send, p_recv, 0)
    next(first)
    next(first)
    loads[4].wait()
    loads[5].wait()
    next(first)
    middle(2)
    produce(4)
    next(first, None)
    block(tot, col, side, core, rows, width)[...] = own_sum[...].astype(bf16)
    second = spread_steps(tot, rows, width, p_send, p_recv, 8)
    next(second)
    finish(1)
    next(second)
    next(second)
    middle(3)
    produce(5)
    next(second, None)

    tile = 64

    def norm_step(k, none):
        at = strip(k * tile, tile)
        grad, standard, inverse = tot[at, :].astype(f32), std[at, :].astype(f32), inv2[at, :]
        scaled = grad * gain2
        mean_one = jnp.sum(scaled, axis=1, keepdims=True) / full
        mean_two = jnp.sum(scaled * standard, axis=1, keepdims=True) / full
        top = cot[at, :].astype(f32)
        low = (top + inverse * (scaled - mean_one - standard * mean_two)).astype(bf16)
        part[at, :] = low
        sums[0:1, :] += jnp.sum(grad * standard, axis=0, keepdims=True)
        sums[1:2, :] += jnp.sum(grad, axis=0, keepdims=True)
        sums[2:3, :] += jnp.sum(low.astype(f32), axis=0, keepdims=True)
        sums[3:4, :] += jnp.sum(top, axis=0, keepdims=True)

        @pl.when(k // (rows // tile) == col)
        def _():
            here = strip(row * width, width)
            own = tot[at, here].astype(f32) * vec_all[3:4, here]
            dres_own[strip(k % (rows // tile) * tile, tile), :] = cot[at, here].astype(f32) + inverse * (
                own - mean_one - std[at, here].astype(f32) * mean_two
            )

        return none

    lax.fori_loop(0, length // tile, norm_step, 0)
    loads[7].start()
    finish(2)
    tiled_nt(part, outw, d_att, full, 512, 256)

    heads = mixed.shape[1] // (3 * HEAD)
    factor = 1.0 / math.sqrt(HEAD)
    blocks = length // SPAN

    def head_step(head, none):
        base = head * 3 * HEAD
        at_q, at_k, at_v = strip(base, HEAD), strip(base + HEAD, HEAD), strip(base + 2 * HEAD, HEAD)
        at_o = strip(head * HEAD, HEAD)
        dk_acc[...] = jnp.zeros_like(dk_acc)
        dv_acc[...] = jnp.zeros_like(dv_acc)
        for k in range(blocks):
            here = pl.ds(k * SPAN, SPAN)
            seen = (k + 1) * SPAN
            query, dout = mixed[here, at_q], d_att[here, at_o]
            keys, values = mixed[:seen, at_k], mixed[:seen, at_v]
            scores = dot_nt(query, keys) * factor
            last = scores[:, seen - SPAN :] + bias[k].astype(f32)
            scores = last if k == 0 else jnp.concatenate([scores[:, : seen - SPAN], last], axis=1)
            probs = jnp.exp(scores - lse[head, here])
            d_probs = dot_nt(dout, values)
            dots = jnp.sum(probs * d_probs, axis=1, keepdims=True)
            d_scores = (probs * (d_probs - dots)).astype(bf16)
            d_mix[here, at_q] = (jnp.dot(d_scores, keys, preferred_element_type=f32) * factor).astype(bf16)
            dk_acc[:seen] += dot_tn(d_scores, query)
            dv_acc[:seen] += dot_tn(probs.astype(bf16), dout)
        d_mix[:, at_k] = (dk_acc[...] * factor).astype(bf16)
        d_mix[:, at_v] = dv_acc[...].astype(bf16)
        return none

    lax.fori_loop(0, heads, head_step, 0)
    middle(4)
    produce(6)
    finish(3)
    loads[6].wait()
    tiled_nt(d_mix, upw, cot, d_mix.shape[1], 1024, 256)
    third = reduce_steps(cot, own_sum, *set_b, p_send, p_recv, 16)
    next(third)
    next(third)
    middle(5)
    produce(7)
    loads[8].start()
    finish(4)
    next(third)
    next(third, None)

    grad1, gain1 = own_sum, vec_all[0:1, strip(row * width, width)]
    scaled1 = grad1[...] * gain1
    first_sum = jnp.sum(scaled1, axis=1, keepdims=True)
    second_sum = jnp.sum(scaled1 * std1_own[...].astype(f32), axis=1, keepdims=True)
    lane = lax.broadcasted_iota(jnp.int32, (rows, 128), 1)
    pair = jnp.where(lane == 0, first_sum, jnp.where(lane == 1, second_sum, 0.0))
    stat_land[row] = pair.T[:8]
    stat_sends, stat_recvs = [], []
    for step in range(1, row_count):
        target, source = (row + step) % row_count, (row + row_count - step) % row_count
        stat_sends.append(put(stat_land.at[row], stat_land.at[row], p_send, p_recv, 35 + step - 1, {"row": target}))
        stat_recvs.append(
            put(stat_land.at[source], stat_land.at[source], p_send, p_recv, 35 + step - 1, {"row": source})
        )
        stat_sends[-1].start()
    small[...] = jnp.zeros_like(small)
    here = strip(row * width, width)
    small[0:1, :] = jnp.sum(grad1[...] * std1_own[...].astype(f32), axis=0, keepdims=True)
    small[1:2, :] = jnp.sum(grad1[...], axis=0, keepdims=True)
    small[2:6, :] = sums[0:4, here]
    uppers = jnp.sum(dup[...].astype(f32), axis=0, keepdims=True)
    for k in range(units // width):
        small[8 + k : 9 + k, :] = uppers[:, k * width : (k + 1) * width]
    mixes = jnp.sum(d_mix[...].astype(f32), axis=0, keepdims=True)
    spot = 8 + units // width
    picked = [mixes[:, (head * 3 + kind) * HEAD : (head * 3 + kind + 1) * HEAD] for head in range(heads) for kind in (0, 2)]
    small[spot : spot + 1, : 2 * heads * HEAD] = jnp.concatenate(picked, axis=1)
    to_x = partners()[0]
    x_copy = put(small.at[pl.ds(0, 8)], x_land, p_send, p_recv, 38, to_x)
    x_copy.start()
    middle(6)
    produce(8)
    finish(5)
    x_copy.wait_recv()
    x_copy.wait_send()
    small[0:2, :] += x_land[0:2, :]
    dp_sends, dp_recvs = [], []
    dp_land[plane] = small[...]
    for step in range(1, dp_count):
        target, source = (plane + step) % dp_count, (plane + dp_count - step) % dp_count
        dp_sends.append(put(dp_land.at[plane], dp_land.at[plane], p_send, p_recv, 39 + step - 1, {"dp": target}))
        dp_recvs.append(put(dp_land.at[source], dp_land.at[source], p_send, p_recv, 39 + step - 1, {"dp": source}))
        dp_sends[-1].start()
    for copy in stat_recvs:
        copy.wait_recv()
    both = stat_land[0]
    for k in range(1, row_count):
        both = both + stat_land[k]
    both = jnp.concatenate([both, jnp.zeros((120, rows), f32)], axis=0).T
    d_norm1 = inv1_own[...] * (
        scaled1 - both[:, 0:1] / full - std1_own[...].astype(f32) * (both[:, 1:2] / full)
    )
    tokens_block[...] = (dres_own[...] + d_norm1).astype(bf16)
    loads[10].start()
    loads[8].wait()
    tiled_nn(hid, n2, tot, 1024, 256)
    fourth = reduce_steps(tot, own_sum, *set_a, p_send, p_recv, 24)
    next(fourth)
    next(fourth)
    middle(7)
    loads[7].wait()
    produce(9)
    finish(6)
    next(fourth)
    next(fourth, None)
    loads[10].wait()
    out_block[...] = (dres_own[...] + (own_sum[...] + down_bias[...])).astype(bf16)
    for copy in dp_recvs:
        copy.wait_recv()
    together = dp_land[0]
    for k in range(1, dp_count):
        together = together + dp_land[k]
    small_out[row] = together
    row_sends, row_recvs = [], []
    for step in range(1, row_count):
        target, source = (row + step) % row_count, (row + row_count - step) % row_count
        row_sends.append(put(small_out.at[row], small_out.at[row], p_send, p_recv, 42 + step - 1, {"row": target}))
        row_recvs.append(
            put(small_out.at[source], small_out.at[source], p_send, p_recv, 42 + step - 1, {"row": source})
        )
        row_sends[-1].start()
    for k in range(10, total):
        middle(k - 2)
        produce(k)
        finish(k - 3)
    middle(total - 2)
    finish(total - 3)
    middle(total - 1)
    finish(total - 2)
    finish(total - 1)
    finish_outer(total - 1)
    for copy in row_recvs:
        copy.wait_recv()
    for copy in down_sends + stat_sends + dp_sends + row_sends:
        copy.wait_send()

    @pl.when(outer)
    def _():
        for k in range(total - g_slots, total):
            inward(k).wait_send()
        for k in range(total):
            sent_home(k, b_land.at[k])

    @pl.when(inner)
    def _():
        for k in range(total - s_slots, total):
            outward(k).wait_send()
            sent_home(k, t.at[k % s_slots])

    for k in range(total):
        for step in range(1, row_count):
            source = (row + row_count - step) % row_count
            put(t.at[0, source], place(k, source), a_send, a_recv, 3 * k + step - 1, {"row": source}).wait_recv()


def backward_plane(
    cid, hid, cot, slope, n2, upw, std, n1, qkvw, down_nat, resid_own, attended, outw, mixed, lse, bias, inv2, vec_all, std1_own, inv1_own, down_bias
):
    f32, bf16 = jnp.float32, jnp.bfloat16
    length, full = cot.shape
    rows, width = length // lax.axis_size("col"), full // lax.axis_size("row")
    row_count, dp_count = full // width, lax.axis_size("dp")
    counts = (slope.shape[1] // CHUNK, slope.shape[1] // CHUNK, attended.shape[1] // CHUNK, mixed.shape[1] // CHUNK)
    total = sum(counts)
    one = (row_count, width // CHUNK, CHUNK, CHUNK)
    shape = jax.ShapeDtypeStruct
    away, near = pl.BlockSpec(memory_space=pl.ANY), pl.BlockSpec(memory_space=pltpu.VMEM)
    vmem, dma = pltpu.VMEM, pltpu.SemaphoreType.DMA
    sets = [
        vmem((4, rows, width), bf16),
        vmem((rows, width), bf16),
        vmem((rows // 2, width), bf16),
        vmem((rows // 2, width), bf16),
        vmem((2, rows, width), bf16),
        vmem((2, rows, width), bf16),
    ]
    return pl.pallas_call(
        functools.partial(backward_kernel, counts),
        out_shape=[
            shape((row_count * counts[0], CHUNK, width), bf16),
            shape((2, CHUNK, row_count * counts[1] * CHUNK), bf16),
            shape((2, row_count * counts[2] * CHUNK, CHUNK), bf16),
            shape((2, CHUNK, row_count * counts[3] * CHUNK), bf16),
            shape((total,) + one, bf16),
            shape((total,) + one, bf16),
            shape((total,) + one, bf16),
            shape((hid.shape[1], full), bf16),
            shape((rows, width), bf16),
            shape((rows, width), bf16),
            shape((row_count, 16, width), f32),
        ],
        in_specs=[away] * 10 + [near] * 10,
        out_specs=[away] * 8 + [near] * 3,
        scratch_shapes=[
            vmem((length, full), bf16),
            vmem((length, full), bf16),
            vmem((length, full), bf16),
            vmem((length, full), bf16),
            vmem((length, full), bf16),
            vmem(upw.shape, bf16),
            vmem(hid.shape, bf16),
            vmem(slope.shape, bf16),
            vmem(attended.shape, bf16),
            vmem(mixed.shape, bf16),
            vmem((length, HEAD), f32),
            vmem((length, HEAD), f32),
            vmem((2,) + one, bf16),
            vmem((2,) + one, bf16),
            vmem(one, bf16),
            vmem((2,) + one, bf16),
        ]
        + sets
        + sets
        + [
            vmem((rows, width), f32),
            vmem((rows, width), f32),
            vmem((8, full), f32),
            vmem((16, width), f32),
            vmem((8, width), f32),
            vmem((dp_count, 16, width), f32),
            vmem((row_count, 8, rows), f32),
            dma((11,)),
            dma,
            dma((total + 1,)),
            dma((3 * total,)),
            dma((3 * total,)),
            dma((3 * total,)),
            dma((3 * total,)),
            dma((45,)),
            dma((45,)),
        ],
        compiler_params=pltpu.CompilerParams(
            collective_id=cid, has_side_effects=True, vmem_limit_bytes=64 * 1024 * 1024 - 65536
        ),
        cost_estimate=pl.CostEstimate(flops=40_000_000_000, bytes_accessed=100_000_000, transcendentals=4_000_000),
    )(hid, cot, slope, n2, upw, std, n1, qkvw, down_nat, resid_own, attended, outw, mixed, lse, bias, inv2, vec_all, std1_own, inv1_own, down_bias)


class Moves:
    def __init__(self, source, target, cut, parts, sends, recvs, base):
        row, plane = lax.axis_index("row"), lax.axis_index("dp")
        side, core = row // 2, row % 2
        parity = plane % 2
        other = {"dp": plane + 1 - 2 * parity}
        twin = side * 2 + 1 - core
        far = ((1 - side) * 2 + core, (1 - side) * 2 + 1 - core)
        self.sibling = put(source(twin), target(row), sends, recvs, base, {"row": twin})
        self.sibling_in = put(source(twin), target(twin), sends, recvs, base, {"row": twin})
        self.outs, self.ins, self.passes, self.gets = [], [], [], []
        at = base + 1
        for step in range(parts // 2):
            for k, device in enumerate(far):
                mine, theirs = 2 * step + parity, 2 * step + 1 - parity
                there, here = cut(target(row), mine), cut(target(device), mine)
                self.outs.append(put(cut(source(device), mine), there, sends, recvs, at, {"row": device}))
                self.ins.append(put(cut(source(device), mine), here, sends, recvs, at, {"row": device}))
                self.passes.append(put(here, here, sends, recvs, at + 1, other))
                lands = cut(target(device), theirs)
                self.gets.append(put(lands, lands, sends, recvs, at + 1, other))
                at += 2

    @staticmethod
    def count(parts):
        return 1 + 2 * parts

    def start(self):
        self.sibling.start()
        self.start_far()

    def start_far(self):
        for copy in self.outs:
            copy.start()

    def forward(self, begin=0, end=None):
        for came, passed in list(zip(self.ins, self.passes))[begin:end]:
            came.wait_recv()
            passed.start()

    def finish(self):
        self.sibling_in.wait_recv()
        for copy in self.gets:
            copy.wait_recv()

    def drain(self):
        self.sibling.wait_send()
        for copy in self.outs + self.passes:
            copy.wait_send()


FAR_PARTS = 4


def forward_kernel(
    tokens,
    cot_in,
    vecs,
    mixed_bias,
    up_bias,
    bias,
    qkv_nat,
    out_nat,
    up_nat,
    cot_all,
    n1_out,
    n2_out,
    std_out,
    upw_out,
    qkvw_out,
    outw_out,
    mixed_out,
    attended_out,
    hid_out,
    slope_out,
    lse,
    inv2,
    vec_all,
    resid_own,
    std1_own,
    inv1_own,
    tok,
    n1,
    part,
    tot,
    qkvw,
    upw,
    outw,
    mixed,
    attended,
    hid,
    slope,
    own_sum,
    got,
    diag,
    hx,
    hy,
    ts,
    fx,
    local_sem,
    w_send,
    w_recv,
    p_send,
    p_recv,
):
    f32, bf16 = jnp.float32, jnp.bfloat16
    plane, row, col = lax.axis_index("dp"), lax.axis_index("row"), lax.axis_index("col")
    side, core = row // 2, row % 2
    rows, width = tokens.shape
    length, full = tok.shape
    row_count = full // width
    heads_width = attended.shape[1]
    units = hid.shape[1]

    barrier = pltpu.get_barrier_semaphore()
    twins = ({"row": (1 - side) * 2 + 1 - core}, {"dp": plane + 1 - 2 * (plane % 2)})
    for partner in partners() + twins:
        pl.semaphore_signal(barrier, inc=1, device_id=partner, device_id_type=MESH)
    pl.semaphore_wait(barrier, 5)

    def cut_rows(ref, part):
        count = ref.shape[0] // FAR_PARTS
        return ref.at[strip(part * count, count)]

    per = qkvw.shape[1]
    count = Moves.count(FAR_PARTS)
    qkv_moves = Moves(
        lambda r: qkv_nat.at[:, strip(r * per, per)],
        lambda r: qkvw.at[strip(r * width, width), :],
        cut_rows,
        FAR_PARTS,
        w_send,
        w_recv,
        0,
    )
    out_moves = Moves(
        lambda r: out_nat.at[strip(r * heads_width, heads_width), :],
        lambda r: outw.at[:, strip(r * width, width)],
        cut_rows,
        FAR_PARTS,
        w_send,
        w_recv,
        count,
    )
    up_moves = Moves(
        lambda r: up_nat.at[:, strip(r * units, units)],
        lambda r: upw.at[strip(r * width, width), :],
        cut_rows,
        FAR_PARTS,
        w_send,
        w_recv,
        2 * count,
    )
    locals_ = [
        (qkv_nat.at[:, strip(row * per, per)], qkvw.at[strip(row * width, width), :]),
        (out_nat.at[strip(row * heads_width, heads_width), :], outw.at[:, strip(row * width, width)]),
        (up_nat.at[:, strip(row * units, units)], upw.at[strip(row * width, width), :]),
        (cot_in, block(cot_all, col, side, core, rows, width)),
        (n1, n1_out),
        (part, n2_out),
        (n1, std_out),
        (upw, upw_out),
        (qkvw, qkvw_out),
        (outw, outw_out),
        (mixed, mixed_out),
        (attended, attended_out),
        (hid, hid_out),
        (slope, slope_out),
    ]
    local = [pltpu.make_async_copy(a, b, local_sem.at[k]) for k, (a, b) in enumerate(locals_)]
    for k in range(4):
        local[k].start()

    block(tok, col, side, core, rows, width)[...] = tokens[...]
    gather = spread_steps(tok, rows, width, p_send, p_recv, 0)
    next(gather)
    vec_all[:, strip(row * width, width)] = vecs[...]
    vec_sends, vec_recvs = [], []
    for step in range(1, row_count):
        target, source = (row + step) % row_count, (row + row_count - step) % row_count
        here, there = vec_all.at[:, strip(row * width, width)], vec_all.at[:, strip(source * width, width)]
        vec_sends.append(put(here, here, p_send, p_recv, 8 + step - 1, {"row": target}))
        vec_recvs.append(put(there, there, p_send, p_recv, 8 + step - 1, {"row": source}))
        vec_sends[-1].start()
    qkv_moves.sibling.start()
    out_moves.sibling.start()
    up_moves.sibling.start()
    next(gather)
    qkv_moves.start_far()
    next(gather)
    next(gather, None)
    for copy in vec_recvs:
        copy.wait_recv()

    tile = 64
    gain1, shift1 = vec_all[0:1, :], vec_all[1:2, :]

    def norm1_step(k, none):
        at = strip(k * tile, tile)
        values = tok[at, :].astype(f32)
        center = jnp.sum(values, axis=1, keepdims=True) / full
        inverse = lax.rsqrt(jnp.sum(values * values, axis=1, keepdims=True) / full - center * center + epsilon)
        n1[at, :] = ((values - center) * inverse * gain1 + shift1).astype(bf16)

        @pl.when(k // (rows // tile) == col)
        def _():
            here = strip(k % (rows // tile) * tile, tile)
            std1_own[here, :] = ((tok[at, strip(row * width, width)].astype(f32) - center) * inverse).astype(bf16)
            inv1_own[here, :] = inverse

        return none

    half_steps = length // tile // 2
    lax.fori_loop(0, half_steps, norm1_step, 0)
    qkv_moves.forward(0, 2)
    lax.fori_loop(half_steps, 2 * half_steps, norm1_step, 0)
    local[4].start()
    qkv_moves.forward(2, 4)
    out_moves.start_far()
    up_moves.start_far()
    qkv_moves.finish()
    local[0].wait()

    def mixed_step(k, none):
        down, across = k // (per // CHUNK), k % (per // CHUNK)
        at, lanes = strip(down * rows, rows), strip(across * CHUNK, CHUNK)
        value = jnp.dot(n1[at, :], qkvw[:, lanes], preferred_element_type=f32)
        mixed[at, lanes] = (value + mixed_bias[:, lanes]).astype(bf16)
        return none

    lax.fori_loop(0, (length // rows) * (per // CHUNK), mixed_step, 0)
    local[8].start()
    local[10].start()
    local[4].wait()

    heads = heads_width // HEAD
    factor = 1.0 / math.sqrt(HEAD)
    blocks = length // SPAN

    def head_step(head, none):
        base = head * 3 * HEAD
        at_q, at_k, at_v = strip(base, HEAD), strip(base + HEAD, HEAD), strip(base + 2 * HEAD, HEAD)
        for k in range(blocks):
            here = pl.ds(k * SPAN, SPAN)
            seen = (k + 1) * SPAN
            scores = dot_nt(mixed[here, at_q], mixed[:seen, at_k]) * factor
            last = scores[:, seen - SPAN :] + bias[k].astype(f32)
            scores = last if k == 0 else jnp.concatenate([scores[:, : seen - SPAN], last], axis=1)
            highest = jnp.max(scores, axis=1, keepdims=True)
            weights = jnp.exp(scores - highest)
            weight_sum = jnp.sum(weights, axis=1, keepdims=True)
            lse[head, here] = highest + jnp.log(weight_sum)
            value = jnp.dot((weights / weight_sum).astype(bf16), mixed[:seen, at_v], preferred_element_type=f32)
            attended[here, strip(head * HEAD, HEAD)] = value.astype(bf16)
        return none

    lax.fori_loop(0, heads, head_step, 0)
    local[11].start()
    out_moves.forward()
    up_moves.forward(0, 4)
    out_moves.finish()
    local[1].wait()
    tiled_nn(attended, outw, part, rows, 512)
    local[9].start()
    add_up = reduce_steps(part, own_sum, got, diag, hx, hy, ts, fx, p_send, p_recv, 11)
    next(add_up)
    next(add_up)
    up_moves.forward(4, 8)
    next(add_up)
    next(add_up, None)
    block(tot, col, side, core, rows, width)[...] = own_sum[...].astype(bf16)
    again = spread_steps(tot, rows, width, p_send, p_recv, 19)
    for k in range(3):
        next(again)
    next(again, None)
    local[3].wait()
    cot_gather = spread_steps(cot_all, rows, width, p_send, p_recv, 27)
    next(cot_gather)

    gain2, shift2, out_bias = vec_all[3:4, :], vec_all[4:5, :], vec_all[2:3, :]

    def norm2_step(k, none):
        at = strip(k * tile, tile)
        values = tok[at, :].astype(f32) + (tot[at, :].astype(f32) + out_bias)
        center = jnp.sum(values, axis=1, keepdims=True) / full
        inverse = lax.rsqrt(jnp.sum(values * values, axis=1, keepdims=True) / full - center * center + epsilon)
        standard = (values - center) * inverse
        inv2[at, :] = inverse
        n1[at, :] = standard.astype(bf16)
        part[at, :] = (standard * gain2 + shift2).astype(bf16)

        @pl.when(k // (rows // tile) == col)
        def _():
            own = strip(row * width, width)
            here = strip(k % (rows // tile) * tile, tile)
            resid_own[here, :] = tok[at, own].astype(f32) + (tot[at, own].astype(f32) + vec_all[2:3, own])

        return none

    lax.fori_loop(0, 2 * half_steps, norm2_step, 0)
    local[5].start()
    local[6].start()
    next(cot_gather)
    up_moves.finish()
    local[2].wait()
    local[7].start()

    def up_step(k, none):
        down, across = k // (units // CHUNK), k % (units // CHUNK)
        at, lanes = strip(down * rows, rows), strip(across * CHUNK, CHUNK)
        u = jnp.dot(part[at, :], upw[:, lanes], preferred_element_type=f32) + up_bias[:, lanes]
        bent = jnp.tanh(0.7978845608028654 * (u + 0.044715 * u * u * u))
        hid[at, lanes] = (0.5 * u * (1.0 + bent)).astype(bf16)
        inside = 0.7978845608028654 * (1.0 + 3 * 0.044715 * u * u)
        slope[at, lanes] = (0.5 * (1.0 + bent) + 0.5 * u * (1.0 - bent * bent) * inside).astype(bf16)
        return none

    lax.fori_loop(0, (length // rows) * (units // CHUNK), up_step, 0)
    local[12].start()
    local[13].start()
    next(cot_gather)
    next(cot_gather, None)
    for k in range(5, 14):
        local[k].wait()
    for moves in (qkv_moves, out_moves, up_moves):
        moves.drain()
    for copy in vec_sends:
        copy.wait_send()


def forward_plane(cid, tokens, cot, vecs, mixed_bias, up_bias, bias, qkv_nat, out_nat, up_nat):
    f32, bf16 = jnp.float32, jnp.bfloat16
    rows, width = tokens.shape
    row_count = lax.axis_size("row")
    length, full = rows * lax.axis_size("col"), width * row_count
    per, heads_width, units = qkv_nat.shape[1] // row_count, out_nat.shape[0] // row_count, up_nat.shape[1] // row_count
    shape = jax.ShapeDtypeStruct
    away, near = pl.BlockSpec(memory_space=pl.ANY), pl.BlockSpec(memory_space=pltpu.VMEM)
    vmem, dma = pltpu.VMEM, pltpu.SemaphoreType.DMA
    wide = shape((length, full), bf16)
    moved = 3 * Moves.count(FAR_PARTS)
    return pl.pallas_call(
        forward_kernel,
        out_shape=[
            wide,
            wide,
            wide,
            wide,
            shape((full, units), bf16),
            shape((full, per), bf16),
            shape((heads_width, full), bf16),
            shape((length, per), bf16),
            shape((length, heads_width), bf16),
            shape((length, units), bf16),
            shape((length, units), bf16),
            shape((heads_width // HEAD, length, 1), f32),
            shape((length, 1), f32),
            shape((8, full), f32),
            shape((rows, width), f32),
            shape((rows, width), bf16),
            shape((rows, 1), f32),
        ],
        in_specs=[near] * 6 + [away] * 3,
        out_specs=[away] * 11 + [near] * 6,
        scratch_shapes=[
            vmem((length, full), bf16),
            vmem((length, full), bf16),
            vmem((length, full), bf16),
            vmem((length, full), bf16),
            vmem((full, per), bf16),
            vmem((full, units), bf16),
            vmem((heads_width, full), bf16),
            vmem((length, per), bf16),
            vmem((length, heads_width), bf16),
            vmem((length, units), bf16),
            vmem((length, units), bf16),
            vmem((rows, width), f32),
            vmem((4, rows, width), bf16),
            vmem((rows, width), bf16),
            vmem((rows // 2, width), bf16),
            vmem((rows // 2, width), bf16),
            vmem((2, rows, width), bf16),
            vmem((2, rows, width), bf16),
            dma((14,)),
            dma((moved,)),
            dma((moved,)),
            dma((35,)),
            dma((35,)),
        ],
        compiler_params=pltpu.CompilerParams(
            collective_id=cid, has_side_effects=True, vmem_limit_bytes=60 * 1024 * 1024
        ),
        cost_estimate=pl.CostEstimate(flops=10_000_000_000, bytes_accessed=60_000_000, transcendentals=4_000_000),
    )(tokens, cot, vecs, mixed_bias, up_bias, bias, qkv_nat, out_nat, up_nat)


def plane_plan(
    tokens,
    ln1_gain,
    ln1_shift,
    qkv_weight,
    qv_bias,
    out_weight,
    out_bias,
    ln2_gain,
    ln2_shift,
    up_weight,
    up_bias,
    down_weight,
    down_bias,
    span_starts,
    cotangent,
):
    f32 = jnp.float32
    rows, width = tokens.shape
    row_count = lax.axis_size("row")
    row = lax.axis_index("row")
    length = rows * lax.axis_size("col")
    heads = qkv_weight.shape[1] // row_count
    units = up_weight.shape[1] // row_count

    blank = jnp.zeros_like(ln1_gain)
    vecs = jnp.stack([ln1_gain, ln1_shift, out_bias, ln2_gain, ln2_shift, blank, blank, blank], axis=0)
    own_qv = lax.dynamic_slice_in_dim(qv_bias, row * heads, heads, 0)
    mixed_bias = jnp.stack([own_qv[:, 0], jnp.zeros_like(own_qv[:, 0]), own_qv[:, 1]], axis=1).reshape(1, -1)
    own_up_bias = lax.dynamic_slice_in_dim(up_bias, row * units, units, 0)[None]
    blocks = length // SPAN
    spots = jnp.arange(SPAN, dtype=jnp.int32)
    marked = jnp.any(span_starts[0][:, None] // SPAN == jnp.arange(blocks, dtype=jnp.int32)[None, :], axis=0)
    open_pairs = (spots[None, :] <= spots[:, None])[None] | marked[:, None, None]
    bias = jnp.where(open_pairs, 0.0, masked_score).astype(jnp.bfloat16)

    (
        cot_all, n1, n2, standard2, upw, qkvw, outw, mixed, attended, hidden, slope,
        lse, inverse2, vec_all, residual_own, standard1_own, inverse1_own,
    ) = forward_plane(
        1,
        tokens,
        cotangent,
        vecs,
        mixed_bias,
        own_up_bias,
        bias,
        qkv_weight.reshape(width, -1),
        out_weight.reshape(-1, width),
        up_weight,
    )
    down_grad, up_grad, out_grad, qkv_grad, _, _, _, _, output, tokens_grad, small = backward_plane(
        2, hidden, cot_all, slope, n2, upw, standard2, n1, qkvw, down_weight, residual_own, attended, outw, mixed, lse, bias,
        inverse2, vec_all, standard1_own, inverse1_own, down_bias[None],
    )
    mine = lax.dynamic_index_in_dim(small, row, 0, keepdims=False)
    spot = 8 + units // width
    return (
        output,
        tokens_grad,
        mine[0],
        mine[1],
        qkv_grad.astype(f32).reshape(width, row_count * heads, 3, HEAD),
        small[:, spot, : 2 * heads * HEAD].reshape(row_count * heads, 2, HEAD),
        jnp.moveaxis(out_grad, 0, 1).astype(f32).reshape(row_count * heads, HEAD, width),
        mine[4],
        mine[2],
        mine[3],
        up_grad.astype(f32).reshape(width, row_count * units),
        small[:, 8:spot].reshape(-1),
        down_grad.astype(f32).reshape(row_count * units, width),
        mine[5],
    )


def solution(mesh):
    sizes = dict(mesh.shape)
    flat = sizes == {"dp": 4, "row": 4, "col": 2}
    per_device = plane_plan if flat else general_plan
    placed = (
        P(("dp", "col"), "row"),
        P("row"),
        P("row"),
        P("row", "col", None, None),
        P("col", None, None),
        P("col", None, "row"),
        P("row"),
        P("row"),
        P("row"),
        P("row", "col"),
        P("col"),
        P("col", "row"),
        P("row"),
        P("dp", None),
        P(("dp", "col"), "row"),
    )
    return jax.shard_map(
        per_device,
        mesh=mesh,
        in_specs=placed,
        out_specs=(
            P(("dp", "col"), "row"),
            P(("dp", "col"), "row"),
            P("row"),
            P("row"),
            P("row", "col", None, None),
            P("col", None, None),
            P("col", None, "row"),
            P("row"),
            P("row"),
            P("row"),
            P("row", "col"),
            P("col"),
            P("col", "row"),
            P("row"),
        ),
        check_vma=False,
    )
```

```python
import functools
import math

import jax
import jax.numpy as jnp
from jax import lax
from jax.experimental import pallas as pl
from jax.experimental.pallas import tpu as pltpu
from jax.sharding import PartitionSpec as P

MESH = pl.DeviceIdType.MESH

D = 2048
HEAD = 128
SEQS = 1
SPAN = 256
BLOCK = 512


epsilon = 1e-05
masked_score = -1e30


def gelu_tanh(values):
    return (
        0.5
        * values
        * (1.0 + jnp.tanh(0.7978845608028654 * (values + 0.044715 * values * values * values)))
    )


def gather_columns(block_data):
    return lax.all_gather(block_data, "col", axis=0, tiled=True)


def gather_rows(block_data):
    return lax.all_gather(block_data, "row", axis=0, tiled=True)


def product(left_side, right_side, flipped):
    if flipped:
        return lax.dot_general(
            left_side, right_side, (((1,), (1,)), ((), ())), preferred_element_type=jnp.float32
        )
    return jnp.dot(left_side, right_side, preferred_element_type=jnp.float32)


def outer_sum(left_side, right_side):
    return lax.dot_general(
        left_side, right_side, (((0,), (0,)), ((), ())), preferred_element_type=jnp.float32
    )


def sum_rows(left_side, right_side, flipped):
    wide_left = lax.all_to_all(left_side, "row", split_axis=0, concat_axis=1, tiled=True)
    if flipped:
        wide_right = lax.all_gather(right_side, "row", axis=1, tiled=True)
    else:
        wide_right = lax.all_gather(right_side, "row", axis=0, tiled=True)
    return product(wide_left, wide_right, flipped)


def sum_columns(left_side, right_side, flipped):
    return lax.psum_scatter(
        product(left_side, right_side, flipped), "col", scatter_dimension=0, tiled=True
    )


def row_totals(first_sum, second_sum):
    return lax.psum((first_sum, second_sum), "row")


def norm_forward(values, gain_row, bias_row):
    totals, squares = row_totals(jnp.sum(values, axis=1), jnp.sum(values * values, axis=1))
    center = totals / D
    spread = squares / D - center * center
    inverse = lax.rsqrt(spread + epsilon)
    standard = (values - center[:, None]) * inverse[:, None]
    return (standard, inverse, (standard * gain_row + bias_row).astype(jnp.bfloat16))


def norm_backward(upstream, standard, inverse, gain_row):
    scaled = upstream * gain_row
    first_sum, second_sum = row_totals(jnp.sum(scaled, axis=1), jnp.sum(scaled * standard, axis=1))
    gradient = inverse[:, None] * (
        scaled - first_sum[:, None] / D - standard * (second_sum[:, None] / D)
    )
    return (gradient, jnp.sum(upstream * standard, axis=0), jnp.sum(upstream, axis=0))


def visible(query_pos, query_image, key_pos):
    earlier = key_pos[None, :] <= query_pos[:, None]
    same_span = (key_pos[None, :] // SPAN == query_pos[:, None] // SPAN) & (
        query_image[:, None] > 0
    )
    return earlier | same_span


def attention_forward(queries, key_value, token_image, row_offset, seq_length, block_rows):
    own_rows, head_count, width = queries.shape
    factor = 1.0 / math.sqrt(width)

    def block_forward(block_index):
        local = block_index * block_rows
        start_pos = row_offset + local
        query_block = lax.dynamic_slice_in_dim(queries, local, block_rows, 0)
        query_pos = start_pos + jnp.arange(block_rows, dtype=jnp.int32)
        query_image = lax.dynamic_slice_in_dim(token_image, start_pos, block_rows, 0)
        begin = start_pos // seq_length * seq_length // block_rows
        finish = start_pos // block_rows + 1

        def key_step(key_index, state_in):
            running, weight_sum, gathered = state_in
            key_begin = key_index * block_rows
            key_block = lax.dynamic_slice_in_dim(key_value, key_begin, block_rows, 0)
            key_pos = key_begin + jnp.arange(block_rows, dtype=jnp.int32)
            allowed = visible(query_pos, query_image, key_pos)
            scores = (
                jnp.einsum(
                    "qhd,khd->hqk",
                    query_block,
                    key_block[:, :, 0],
                    preferred_element_type=jnp.float32,
                )
                * factor
            )
            scores = jnp.where(allowed[None], scores, masked_score)
            highest = jnp.maximum(running, jnp.max(scores, axis=2))
            weights = jnp.exp(scores - highest[:, :, None])
            shrink = jnp.exp(running - highest)
            weight_sum = weight_sum * shrink + jnp.sum(weights, axis=2)
            gathered = gathered * shrink.T[:, :, None] + jnp.einsum(
                "hqk,khd->qhd",
                weights.astype(jnp.bfloat16),
                key_block[:, :, 1],
                preferred_element_type=jnp.float32,
            )
            return (highest, weight_sum, gathered)

        initial = (
            jnp.full((head_count, block_rows), masked_score, jnp.float32),
            jnp.zeros((head_count, block_rows), jnp.float32),
            jnp.zeros((block_rows, head_count, width), jnp.float32),
        )
        running, weight_sum, gathered = lax.fori_loop(begin, finish, key_step, initial)
        return (gathered / weight_sum.T[:, :, None], running + jnp.log(weight_sum))

    result, logsum = lax.map(block_forward, jnp.arange(own_rows // block_rows, dtype=jnp.int32))
    return (result.reshape(own_rows, head_count, width), logsum)


def attention_backward(
    queries,
    key_value,
    attended_full,
    logsum,
    d_attended,
    token_image,
    row_offset,
    seq_length,
    block_rows,
):
    own_rows, head_count, width = queries.shape
    factor = 1.0 / math.sqrt(width)
    row_dots = jnp.sum(d_attended.astype(jnp.float32) * attended_full, axis=2)

    def block_backward(block_index, state_out):
        d_queries, d_pairs = state_out
        local = block_index * block_rows
        start_pos = row_offset + local
        query_block = lax.dynamic_slice_in_dim(queries, local, block_rows, 0)
        dout_block = lax.dynamic_slice_in_dim(d_attended, local, block_rows, 0)
        dots_block = lax.dynamic_slice_in_dim(row_dots, local, block_rows, 0).T
        logsum_block = logsum[block_index]
        query_pos = start_pos + jnp.arange(block_rows, dtype=jnp.int32)
        query_image = lax.dynamic_slice_in_dim(token_image, start_pos, block_rows, 0)
        begin = start_pos // seq_length * seq_length // block_rows
        finish = start_pos // block_rows + 1

        def key_step(key_index, state_in):
            d_query, d_keys = state_in
            key_begin = key_index * block_rows
            key_block = lax.dynamic_slice_in_dim(key_value, key_begin, block_rows, 0)
            key_pos = key_begin + jnp.arange(block_rows, dtype=jnp.int32)
            allowed = visible(query_pos, query_image, key_pos)
            scores = (
                jnp.einsum(
                    "qhd,khd->hqk",
                    query_block,
                    key_block[:, :, 0],
                    preferred_element_type=jnp.float32,
                )
                * factor
            )
            scores = jnp.where(allowed[None], scores, masked_score)
            probabilities = jnp.exp(scores - logsum_block[:, :, None])
            d_probs = jnp.einsum(
                "qhd,khd->hqk", dout_block, key_block[:, :, 1], preferred_element_type=jnp.float32
            )
            d_scores = (probabilities * (d_probs - dots_block[:, :, None])).astype(jnp.bfloat16)
            d_query = d_query + jnp.einsum(
                "hqk,khd->qhd", d_scores, key_block[:, :, 0], preferred_element_type=jnp.float32
            )
            d_key = (
                jnp.einsum(
                    "hqk,qhd->khd", d_scores, query_block, preferred_element_type=jnp.float32
                )
                * factor
            )
            d_value = jnp.einsum(
                "hqk,qhd->khd",
                probabilities.astype(jnp.bfloat16),
                dout_block,
                preferred_element_type=jnp.float32,
            )
            previous = lax.dynamic_slice_in_dim(d_keys, key_begin, block_rows, 0)
            d_keys = lax.dynamic_update_slice_in_dim(
                d_keys, previous + jnp.stack([d_key, d_value], axis=2), key_begin, 0
            )
            return (d_query, d_keys)

        d_query, d_pairs = lax.fori_loop(
            begin,
            finish,
            key_step,
            (jnp.zeros((block_rows, head_count, width), jnp.float32), d_pairs),
        )
        d_queries = lax.dynamic_update_slice_in_dim(d_queries, d_query * factor, local, 0)
        return (d_queries, d_pairs)

    initial = (
        jnp.zeros((own_rows, head_count, width), jnp.float32),
        jnp.zeros((key_value.shape[0], head_count, 2, width), jnp.float32),
    )
    return lax.fori_loop(0, own_rows // block_rows, block_backward, initial)


def general_plan(
    tokens,
    ln1_gain,
    ln1_shift,
    qkv_weight,
    qv_bias,
    out_weight,
    out_bias,
    ln2_gain,
    ln2_shift,
    up_weight,
    up_bias,
    down_weight,
    down_bias,
    span_starts,
    cotangent,
):
    col_rows, row_width = tokens.shape
    group_rows = col_rows * lax.axis_size("col")
    own_rows = group_rows // lax.axis_size("row")
    head_count = qkv_weight.shape[1]
    seq_length = group_rows // SEQS
    block_rows = BLOCK - own_rows % BLOCK
    row_offset = lax.axis_index("row") * own_rows
    slot_count = seq_length // SPAN
    image_marks = jnp.sum(
        (
            span_starts[:, :, None] // SPAN
            == jnp.arange(slot_count, dtype=jnp.int32)[None, None, :]
        ).astype(jnp.int32),
        axis=1,
    )
    token_image = jnp.broadcast_to(
        image_marks.reshape(-1)[:, None], (group_rows // SPAN, SPAN)
    ).reshape(group_rows)
    qkv_flat = qkv_weight.reshape(row_width, head_count * 3 * HEAD)
    out_flat = out_weight.reshape(head_count * HEAD, row_width)
    inputs = tokens.astype(jnp.float32)
    standard1, inverse1, normed1 = norm_forward(inputs, ln1_gain, ln1_shift)
    normed1_all = gather_columns(normed1)
    mixed_sums = sum_rows(normed1_all, qkv_flat, False).reshape(own_rows, head_count, 3, HEAD)
    queries = (mixed_sums[:, :, 0] + qv_bias[:, 0]).astype(jnp.bfloat16)
    key_value_own = jnp.stack(
        [mixed_sums[:, :, 1], mixed_sums[:, :, 2] + qv_bias[:, 1]], axis=2
    ).astype(jnp.bfloat16)
    key_value = gather_rows(key_value_own)
    attended_full, logsum = attention_forward(
        queries, key_value, token_image, row_offset, seq_length, block_rows
    )
    attended = attended_full.astype(jnp.bfloat16).reshape(own_rows, head_count * HEAD)
    attended_all = gather_rows(attended)
    residual = inputs + (sum_columns(attended_all, out_flat, False) + out_bias)
    standard2, inverse2, normed2 = norm_forward(residual, ln2_gain, ln2_shift)
    normed2_all = gather_columns(normed2)
    up_sums = sum_rows(normed2_all, up_weight, False) + up_bias
    hidden = gelu_tanh(up_sums).astype(jnp.bfloat16)
    hidden_all = gather_rows(hidden)
    output = (residual + (sum_columns(hidden_all, down_weight, False) + down_bias)).astype(
        jnp.bfloat16
    )
    d_output = cotangent.astype(jnp.float32)
    d_output_all = gather_columns(cotangent)
    down_grad = outer_sum(hidden_all, d_output_all)
    down_bias_grad = jnp.sum(d_output_all, axis=0, dtype=jnp.float32)
    d_hidden = sum_rows(d_output_all, down_weight, True)
    d_upper = jax.vjp(gelu_tanh, up_sums)[1](d_hidden)[0].astype(jnp.bfloat16)
    d_upper_all = gather_rows(d_upper)
    normed2_use = gather_columns(normed2)
    up_grad = outer_sum(normed2_use, d_upper_all)
    up_bias_grad = jnp.sum(d_upper_all, axis=0, dtype=jnp.float32)
    d_normed2 = sum_columns(d_upper_all, up_weight, True)
    d_norm2, gain2_grad, shift2_grad = norm_backward(d_normed2, standard2, inverse2, ln2_gain)
    d_residual = d_output + d_norm2
    d_branch = d_residual.astype(jnp.bfloat16)
    d_branch_all = gather_columns(d_branch)
    out_grad = outer_sum(attended_all, d_branch_all)
    out_bias_grad = jnp.sum(d_branch_all, axis=0, dtype=jnp.float32)
    d_attended = (
        sum_rows(d_branch_all, out_flat, True)
        .astype(jnp.bfloat16)
        .reshape(own_rows, head_count, HEAD)
    )
    d_queries, d_pairs = attention_backward(
        queries,
        key_value,
        attended_full,
        logsum,
        d_attended,
        token_image,
        row_offset,
        seq_length,
        block_rows,
    )
    d_pairs_own = lax.psum_scatter(d_pairs, "row", scatter_dimension=0, tiled=True)
    d_mixed = jnp.concatenate([d_queries[:, :, None], d_pairs_own], axis=2).astype(jnp.bfloat16)
    d_mixed_all = gather_rows(d_mixed)
    normed1_use = gather_columns(normed1)
    d_mixed_flat = d_mixed_all.reshape(group_rows, head_count * 3 * HEAD)
    qkv_grad = outer_sum(normed1_use, d_mixed_flat)
    mixed_totals = jnp.sum(d_mixed_all, axis=0, dtype=jnp.float32)
    qv_bias_grad = jnp.stack([mixed_totals[:, 0], mixed_totals[:, 2]], axis=1)
    d_normed1 = sum_columns(d_mixed_flat, qkv_flat, True)
    d_norm1, gain1_grad, shift1_grad = norm_backward(d_normed1, standard1, inverse1, ln1_gain)
    tokens_grad = (d_residual + d_norm1).astype(jnp.bfloat16)
    norm_sums = lax.psum((gain1_grad, shift1_grad, gain2_grad, shift2_grad), ("dp", "col"))
    weight_sums = lax.psum(
        (
            qkv_grad,
            qv_bias_grad,
            out_grad,
            out_bias_grad,
            up_grad,
            up_bias_grad,
            down_grad,
            down_bias_grad,
        ),
        "dp",
    )
    return (
        output,
        tokens_grad,
        norm_sums[0],
        norm_sums[1],
        weight_sums[0].reshape(row_width, head_count, 3, HEAD),
        weight_sums[1],
        weight_sums[2].reshape(head_count, HEAD, row_width),
        weight_sums[3],
        norm_sums[2],
        norm_sums[3],
        weight_sums[4],
        weight_sums[5],
        weight_sums[6],
        weight_sums[7],
    )


def places():
    row, col = lax.axis_index("row"), lax.axis_index("col")
    return col, row // 2, row % 2


def partners():
    col, side, core = places()
    return ({"col": 1 - col}, {"row": (1 - side) * 2 + core}, {"row": side * 2 + 1 - core})


def block(ref, col, side, core, rows, width, part=None):
    begin, count = col * rows, rows
    if part is not None:
        begin, count = begin + part * (rows // 2), rows // 2
    return ref.at[strip(begin, count), strip((side * 2 + core) * width, width)]


def put(ref_from, ref_to, sends, recvs, at, partner):
    return pltpu.make_async_remote_copy(
        src_ref=ref_from,
        dst_ref=ref_to,
        send_sem=sends.at[at],
        recv_sem=recvs.at[at],
        device_id=partner,
        device_id_type=MESH,
    )


def strip(begin, count):
    return pl.ds(pl.multiple_of(begin, count), count)


def dot_nt(left, right):
    return lax.dot_general(left, right, (((1,), (1,)), ((), ())), preferred_element_type=jnp.float32)


def dot_tn(left, right):
    return lax.dot_general(left, right, (((0,), (0,)), ((), ())), preferred_element_type=jnp.float32)


def tiled_nt(left, right, target, inner, tile_rows, tile_cols):
    rows, cols = target.shape
    across = cols // tile_cols

    def step(at, none):
        down, side = at // across, at % across
        value = dot_nt(left[strip(down * tile_rows, tile_rows), :inner], right[strip(side * tile_cols, tile_cols), :inner])
        target[strip(down * tile_rows, tile_rows), strip(side * tile_cols, tile_cols)] = value.astype(target.dtype)
        return none

    lax.fori_loop(0, (rows // tile_rows) * across, step, 0)


def tiled_nn(left, right, target, tile_rows, tile_cols):
    rows, cols = target.shape
    across = cols // tile_cols

    def step(at, none):
        down, side = at // across, at % across
        value = jnp.dot(
            left[strip(down * tile_rows, tile_rows), :],
            right[:, strip(side * tile_cols, tile_cols)],
            preferred_element_type=jnp.float32,
        )
        target[strip(down * tile_rows, tile_rows), strip(side * tile_cols, tile_cols)] = value.astype(target.dtype)
        return none

    lax.fori_loop(0, (rows // tile_rows) * across, step, 0)


def reduce_steps(part, result, got, diag, half_x, half_y, to_send, from_xy, sends, recvs, base):
    f32 = jnp.float32
    rows, width = result.shape
    half = rows // 2
    low, high = pl.ds(0, half), pl.ds(half, half)
    col, side, core = places()
    to_x, to_y, to_core = partners()
    spots = ((1 - col, 1 - side), (col, 1 - side), (1 - col, side), (col, side))
    copies = [
        put(block(part, a, b, 1 - core, rows, width), got.at[k], sends, recvs, base + k, to_core)
        for k, (a, b) in enumerate(spots)
    ]
    for copy in copies:
        copy.start()
    mine = [block(part, a, b, core, rows, width) for a, b in spots]
    dx = put(diag.at[low], half_x, sends, recvs, base + 4, to_x)
    dy = put(diag.at[high], half_y, sends, recvs, base + 5, to_y)
    cy = put(to_send.at[0], from_xy.at[0], sends, recvs, base + 6, to_y)
    cx = put(to_send.at[1], from_xy.at[1], sends, recvs, base + 7, to_x)
    yield
    copies[0].wait_recv()
    diag[...] = (mine[0][...].astype(f32) + got[0].astype(f32)).astype(diag.dtype)
    dx.start()
    dy.start()
    copies[1].wait_recv()
    copies[2].wait_recv()
    to_send[0, high] = (mine[1][high].astype(f32) + got[1, high].astype(f32)).astype(diag.dtype)
    to_send[1, low] = (mine[2][low].astype(f32) + got[2, low].astype(f32)).astype(diag.dtype)
    copies[3].wait_recv()
    result[...] = mine[3][...].astype(f32) + got[3].astype(f32)
    yield
    dx.wait_recv()
    to_send[0, low] = (mine[1][low].astype(f32) + got[1, low].astype(f32) + half_x[...].astype(f32)).astype(diag.dtype)
    cy.start()
    dy.wait_recv()
    to_send[1, high] = (mine[2][high].astype(f32) + got[2, high].astype(f32) + half_y[...].astype(f32)).astype(
        diag.dtype
    )
    cx.start()
    yield
    cy.wait_recv()
    cx.wait_recv()
    result[...] = result[...] + from_xy[0].astype(f32) + from_xy[1].astype(f32)
    for copy in copies + [dx, dy, cy, cx]:
        copy.wait_send()


def spread_steps(out, rows, width, sends, recvs, base):
    col, side, core = places()
    to_x, to_y, to_core = partners()

    def copy_of(at, which, partner, part=None):
        ref = block(out, *which, rows, width, part)
        return put(ref, ref, sends, recvs, base + at, partner)

    own, ox, oy, od = (col, side, core), (1 - col, side, core), (col, 1 - side, core), (1 - col, 1 - side, core)
    plan = [
        copy_of(0, own, to_x),
        copy_of(1, own, to_y),
        copy_of(2, own, to_core),
        copy_of(3, ox, to_y, 0),
        copy_of(4, oy, to_x, 1),
        copy_of(5, ox, to_core),
        copy_of(6, oy, to_core),
        copy_of(7, od, to_core),
    ]
    for at in (0, 1, 2):
        plan[at].start()
    yield
    plan[0].wait_recv()
    plan[3].start()
    plan[1].wait_recv()
    plan[4].start()
    plan[5].start()
    plan[6].start()
    yield
    plan[3].wait_recv()
    plan[4].wait_recv()
    plan[7].start()
    yield
    for at in (2, 5, 6, 7):
        plan[at].wait_recv()
    for copy in plan:
        copy.wait_send()


CHUNK = 256


def backward_kernel(
    counts,
    hid_h,
    cot_h,
    slope_h,
    n2_h,
    upw_h,
    std_h,
    n1_h,
    qkvw_h,
    down_nat,
    resid_h,
    attended,
    outw,
    mixed,
    stats,
    marks,
    vec_all,
    std1_own,
    inv1_own,
    down_bias,
    down_out,
    up_out,
    out_out,
    qkv_out,
    b_land,
    downw_land,
    out_block,
    tokens_block,
    small_out,
    cot,
    n2,
    std,
    part,
    tot,
    upw,
    hid,
    dup,
    d_att,
    d_mix,
    dk_acc,
    dv_acc,
    g,
    s,
    t,
    r_land,
    m_land,
    got_a,
    diag_a,
    hx_a,
    hy_a,
    ts_a,
    fx_a,
    got_b,
    diag_b,
    hx_b,
    hy_b,
    ts_b,
    fx_b,
    dres_own,
    own_sum,
    sums,
    small,
    x_land,
    dp_land,
    stat_land,
    load_sem,
    credit,
    own_sem,
    z_send,
    z_recv,
    a_send,
    a_recv,
    p_send,
    p_recv,
):
    f32, bf16 = jnp.float32, jnp.bfloat16
    n_down, n_up, n_out, n_qkv = counts
    total = sum(counts)
    plane, row, col = lax.axis_index("dp"), lax.axis_index("row"), lax.axis_index("col")
    length, full = cot.shape
    rows, width = dres_own.shape
    row_count = full // width
    inner = (plane == 1) | (plane == 2)
    outer = jnp.logical_not(inner)
    to_inner = {"dp": plane // 3 + 1}
    to_middle = {"dp": 3 - plane}
    to_outer = {"dp": (plane - 1) * 3}
    side, core = row // 2, row % 2

    loads = [
        (hid_h, hid),
        (cot_h, cot),
        (slope_h, dup),
        (upw_h, upw),
        (n2_h, n2),
        (std_h, std),
        (qkvw_h, upw.at[:, : qkvw_h.shape[1]]),
        (n1_h, std),
        (downw_land, n2),
        (downw_land, tot),
        (resid_h, dres_own),
    ]
    loads = [pltpu.make_async_copy(a, b, load_sem.at[k]) for k, (a, b) in enumerate(loads)]
    for k in range(6):
        loads[k].start()

    dp_count = dp_land.shape[0]
    barrier = pltpu.get_barrier_semaphore()
    others = [{"row": (1 - side) * 2 + 1 - core}] + [{"dp": (plane + k) % dp_count} for k in range(1, dp_count)]
    for partner in partners() + tuple(others):
        pl.semaphore_signal(barrier, inc=1, device_id=partner, device_id_type=MESH)
    pl.semaphore_wait(barrier, 3 + len(others))

    units = hid.shape[1]
    down_sends, down_recvs = [], []
    for step in range(1, row_count):
        target, source = (row + step) % row_count, (row + row_count - step) % row_count
        here, there = downw_land.at[:, strip(row * width, width)], downw_land.at[:, strip(source * width, width)]
        piece = down_nat.at[strip(target * units, units), :]
        down_sends.append(put(piece, here, p_send, p_recv, 32 + step - 1, {"row": target}))
        down_recvs.append(put(piece, there, p_send, p_recv, 32 + step - 1, {"row": source}))
        down_sends[-1].start()
    down_own = pltpu.make_async_copy(
        down_nat.at[strip(row * units, units), :], downw_land.at[:, strip(row * width, width)], own_sem.at[2 * total]
    )
    down_own.start()

    def place(u, source):
        i, half = u // 2, u % 2
        if i < n_down:
            return down_out.at[source * n_down + i // 2 * 2 + half, :, pl.ds(i % 2 * CHUNK, CHUNK)]
        i -= n_down
        if i < n_up:
            return up_out.at[half, :, strip(source * n_up * CHUNK + i * CHUNK, CHUNK)]
        i -= n_up
        if i < n_out:
            return out_out.at[source * n_out + i, :, pl.ds(half * CHUNK, CHUNK)]
        i -= n_out
        return qkv_out.at[half, :, strip(source * n_qkv * CHUNK + i * CHUNK, CHUNK)]

    g_slots, s_slots, t_slots, r_slots, m_slots = g.shape[0], s.shape[0], t.shape[0], r_land.shape[0], m_land.shape[0]
    pieces = 2 * total

    def made(u):
        return g.at[u // 2 % g_slots, :, u % 2]

    def inward(u):
        return put(made(u), r_land.at[u % r_slots], z_send, z_recv, u, to_inner)

    def across(u):
        return put(s.at[u % s_slots], m_land.at[u % m_slots], z_send, z_recv, pieces + u, to_middle)

    def outward(u):
        return put(t.at[u % t_slots], b_land.at[u], z_send, z_recv, 2 * pieces + u, to_outer)

    def home(u, step, source):
        target = (row + step) % row_count
        return put(source.at[target], place(u, row), a_send, a_recv, 3 * u + step - 1, {"row": target})

    def home_own(u, source):
        return pltpu.make_async_copy(source.at[row], place(u, row), own_sem.at[u])

    def send_home(u, source):
        for step in range(1, row_count):
            home(u, step, source).start()
        home_own(u, source).start()

    def sent_home(u, source):
        for step in range(1, row_count):
            home(u, step, source).wait_send()
        home_own(u, source).wait()

    def produce(i):
        if i >= g_slots:

            @pl.when(outer)
            def _():
                inward(2 * (i - g_slots)).wait_send()
                inward(2 * (i - g_slots) + 1).wait_send()

        slot = g.at[i % g_slots]
        if i < n_down:
            begin, lane = i // 2 * 2 * CHUNK, i % 2 * CHUNK

            def step(k, none):
                value = dot_tn(hid[:, begin : begin + 2 * CHUNK], cot[:, strip(k * width + lane, CHUNK)]).astype(bf16)
                slot[k, 0] = value[:CHUNK]
                slot[k, 1] = value[CHUNK:]
                return none
        elif n_down + n_up <= i < n_down + n_up + n_out:
            left, begin, right = attended, (i - n_down - n_up) * CHUNK, part

            def step(k, none):
                value = dot_tn(left[:, begin : begin + CHUNK], right[:, strip(k * width, width)]).astype(bf16)
                slot[k, 0] = value[:, :CHUNK]
                slot[k, 1] = value[:, CHUNK:]
                return none
        else:
            if i < n_down + n_up:
                left, right, begin = n2, dup, (i - n_down) * CHUNK
            else:
                left, right, begin = std, d_mix, (i - n_down - n_up - n_out) * CHUNK

            def step(k, none):
                value = dot_tn(left[:, strip(k * width, width)], right[:, begin : begin + CHUNK]).astype(bf16)
                slot[k, 0] = value[:CHUNK]
                slot[k, 1] = value[CHUNK:]
                return none

        lax.fori_loop(0, row_count, step, 0)

    def launch(u):
        @pl.when(outer)
        def _():
            if u >= r_slots:
                pl.semaphore_wait(credit, 1)
            inward(u).start()

    def add(first, second, target):
        for k in range(row_count):
            target[k] = (first[k].astype(f32) + second[k].astype(f32)).astype(bf16)

    def middle(u):
        @pl.when(inner)
        def _():
            inward(u).wait_recv()
            add(made(u), r_land.at[u % r_slots], s.at[u % s_slots])
            across(u).start()
            if u + r_slots < pieces:
                pl.semaphore_signal(credit, inc=1, device_id=to_outer, device_id_type=MESH)

    def finish_inner(u):
        @pl.when(inner)
        def _():
            if u >= t_slots:
                outward(u - t_slots).wait_send()
                sent_home(u - t_slots, t.at[u % t_slots])
            across(u).wait_recv()
            add(s.at[u % s_slots], m_land.at[u % m_slots], t.at[u % t_slots])
            outward(u).start()
            send_home(u, t.at[u % t_slots])
            across(u).wait_send()

    def finish_outer(u):
        @pl.when(outer)
        def _():
            outward(u).wait_recv()
            send_home(u, b_land.at[u])

    def turn(u):
        if u + 2 < pieces:
            if u % 2 == 0:
                produce((u + 2) // 2)
            launch(u + 2)
        middle(u)
        if u >= 1:
            finish_inner(u - 1)
        if u >= 2:
            finish_outer(u - 2)

    set_a = (got_a, diag_a, hx_a, hy_a, ts_a, fx_a)
    set_b = (got_b, diag_b, hx_b, hy_b, ts_b, fx_b)
    gain2 = vec_all[3:4, :]

    loads[0].wait()
    loads[1].wait()
    produce(0)
    launch(0)
    launch(1)
    sums[...] = jnp.zeros_like(sums)
    turn(0)
    turn(1)
    turn(2)
    down_own.wait()
    for copy in down_recvs:
        copy.wait_recv()
    loads[9].start()
    loads[2].wait()
    loads[3].wait()
    turn(3)
    loads[9].wait()

    def upper_step(k, none):
        down, across_ = k // (units // CHUNK), k % (units // CHUNK)
        at, lanes = strip(down * rows, rows), strip(across_ * CHUNK, CHUNK)
        dup[at, lanes] = (dot_nt(cot[at, :], tot[lanes, :]) * dup[at, lanes].astype(f32)).astype(bf16)
        return none

    lax.fori_loop(0, (length // rows) * (units // CHUNK), upper_step, 0)
    turn(4)
    tiled_nt(dup, upw, part, dup.shape[1], 1024, 256)
    loads[6].start()
    first = reduce_steps(part, own_sum, *set_a, p_send, p_recv, 0)
    next(first)
    loads[4].wait()
    loads[5].wait()
    turn(5)
    next(first)
    next(first)
    turn(6)
    next(first, None)
    block(tot, col, side, core, rows, width)[...] = own_sum[...].astype(bf16)
    second = spread_steps(tot, rows, width, p_send, p_recv, 8)
    next(second)
    turn(7)
    next(second)
    next(second)
    turn(8)
    next(second, None)

    tile = 64

    def norm_step(k, none):
        at = strip(k * tile, tile)
        grad, standard, inverse = tot[at, :].astype(f32), std[at, :].astype(f32), stats[at, 0:1]
        scaled = grad * gain2
        mean_one = jnp.sum(scaled, axis=1, keepdims=True) / full
        mean_two = jnp.sum(scaled * standard, axis=1, keepdims=True) / full
        top = cot[at, :].astype(f32)
        low = (top + inverse * (scaled - mean_one - standard * mean_two)).astype(bf16)
        part[at, :] = low
        sums[0:1, :] += jnp.sum(grad * standard, axis=0, keepdims=True)
        sums[1:2, :] += jnp.sum(grad, axis=0, keepdims=True)
        sums[2:3, :] += jnp.sum(low.astype(f32), axis=0, keepdims=True)
        sums[3:4, :] += jnp.sum(top, axis=0, keepdims=True)

        @pl.when(k // (rows // tile) == col)
        def _():
            here = strip(row * width, width)
            own = tot[at, here].astype(f32) * vec_all[3:4, here]
            dres_own[strip(k % (rows // tile) * tile, tile), :] = cot[at, here].astype(f32) + inverse * (
                own - mean_one - std[at, here].astype(f32) * mean_two
            )

        return none

    lax.fori_loop(0, length // tile, norm_step, 0)
    loads[7].start()
    turn(9)
    tiled_nt(part, outw, d_att, full, 512, 256)

    heads = mixed.shape[1] // (3 * HEAD)
    factor = 1.0 / math.sqrt(HEAD)
    blocks = length // SPAN
    spots = (SPAN, SPAN)
    earlier = lax.broadcasted_iota(jnp.int32, spots, 1) <= lax.broadcasted_iota(jnp.int32, spots, 0)

    def head_step(head, none):
        base = head * 3 * HEAD
        at_q, at_k, at_v = strip(base, HEAD), strip(base + HEAD, HEAD), strip(base + 2 * HEAD, HEAD)
        at_o = strip(head * HEAD, HEAD)
        dk_acc[...] = jnp.zeros_like(dk_acc)
        dv_acc[...] = jnp.zeros_like(dv_acc)
        for k in range(blocks):
            here = pl.ds(k * SPAN, SPAN)
            seen = (k + 1) * SPAN
            query, dout = mixed[here, at_q], d_att[here, at_o]
            keys, values = mixed[:seen, at_k], mixed[:seen, at_v]
            scores = dot_nt(query, keys) * factor
            last = jnp.where(earlier | (marks[k : k + 1, :1] > 0), scores[:, seen - SPAN :], masked_score)
            scores = last if k == 0 else jnp.concatenate([scores[:, : seen - SPAN], last], axis=1)
            probs = jnp.exp(scores - stats[here, 1 + head : 2 + head])
            d_probs = dot_nt(dout, values)
            dots = jnp.sum(probs * d_probs, axis=1, keepdims=True)
            d_scores = (probs * (d_probs - dots)).astype(bf16)
            d_mix[here, at_q] = (jnp.dot(d_scores, keys, preferred_element_type=f32) * factor).astype(bf16)
            dk_acc[:seen] += dot_tn(d_scores, query)
            dv_acc[:seen] += dot_tn(probs.astype(bf16), dout)
        d_mix[:, at_k] = (dk_acc[...] * factor).astype(bf16)
        d_mix[:, at_v] = dv_acc[...].astype(bf16)
        return none

    for head in range(heads):
        head_step(head, 0)
        turn(10 + head)
    loads[6].wait()
    tiled_nt(d_mix, upw, cot, d_mix.shape[1], 1024, 256)
    third = reduce_steps(cot, own_sum, *set_b, p_send, p_recv, 16)
    next(third)
    next(third)
    turn(12)
    next(third)
    turn(13)
    loads[8].start()
    next(third, None)

    grad1, gain1 = own_sum, vec_all[0:1, strip(row * width, width)]
    scaled1 = grad1[...] * gain1
    first_sum = jnp.sum(scaled1, axis=1, keepdims=True)
    second_sum = jnp.sum(scaled1 * std1_own[...].astype(f32), axis=1, keepdims=True)
    lane = lax.broadcasted_iota(jnp.int32, (rows, 128), 1)
    pair = jnp.where(lane == 0, first_sum, jnp.where(lane == 1, second_sum, 0.0))
    stat_land[row] = pair.T[:8]
    stat_sends, stat_recvs = [], []
    for step in range(1, row_count):
        target, source = (row + step) % row_count, (row + row_count - step) % row_count
        stat_sends.append(put(stat_land.at[row], stat_land.at[row], p_send, p_recv, 35 + step - 1, {"row": target}))
        stat_recvs.append(
            put(stat_land.at[source], stat_land.at[source], p_send, p_recv, 35 + step - 1, {"row": source})
        )
        stat_sends[-1].start()
    small[...] = jnp.zeros_like(small)
    here = strip(row * width, width)
    small[0:1, :] = jnp.sum(grad1[...] * std1_own[...].astype(f32), axis=0, keepdims=True)
    small[1:2, :] = jnp.sum(grad1[...], axis=0, keepdims=True)
    small[2:6, :] = sums[0:4, here]
    uppers = jnp.sum(dup[...].astype(f32), axis=0, keepdims=True)
    for k in range(units // width):
        small[8 + k : 9 + k, :] = uppers[:, k * width : (k + 1) * width]
    mixes = jnp.sum(d_mix[...].astype(f32), axis=0, keepdims=True)
    spot = 8 + units // width
    picked = [mixes[:, (head * 3 + kind) * HEAD : (head * 3 + kind + 1) * HEAD] for head in range(heads) for kind in (0, 2)]
    small[spot : spot + 1, : 2 * heads * HEAD] = jnp.concatenate(picked, axis=1)
    to_x = partners()[0]
    x_copy = put(small.at[pl.ds(0, 8)], x_land, p_send, p_recv, 38, to_x)
    x_copy.start()
    turn(14)
    x_copy.wait_recv()
    x_copy.wait_send()
    small[0:2, :] += x_land[0:2, :]
    dp_sends, dp_recvs = [], []
    dp_land[plane] = small[...]
    for step in range(1, dp_count):
        target, source = (plane + step) % dp_count, (plane + dp_count - step) % dp_count
        dp_sends.append(put(dp_land.at[plane], dp_land.at[plane], p_send, p_recv, 39 + step - 1, {"dp": target}))
        dp_recvs.append(put(dp_land.at[source], dp_land.at[source], p_send, p_recv, 39 + step - 1, {"dp": source}))
        dp_sends[-1].start()
    for copy in stat_recvs:
        copy.wait_recv()
    both = stat_land[0]
    for k in range(1, row_count):
        both = both + stat_land[k]
    both = jnp.concatenate([both, jnp.zeros((120, rows), f32)], axis=0).T
    d_norm1 = inv1_own[...] * (
        scaled1 - both[:, 0:1] / full - std1_own[...].astype(f32) * (both[:, 1:2] / full)
    )
    tokens_block[...] = (dres_own[...] + d_norm1).astype(bf16)
    loads[10].start()
    loads[8].wait()
    tiled_nn(hid, n2, tot, 1024, 256)
    fourth = reduce_steps(tot, own_sum, *set_a, p_send, p_recv, 24)
    next(fourth)
    next(fourth)
    loads[7].wait()
    turn(15)
    turn(16)
    next(fourth)
    next(fourth, None)
    loads[10].wait()
    out_block[...] = (dres_own[...] + (own_sum[...] + down_bias[...])).astype(bf16)
    for copy in dp_recvs:
        copy.wait_recv()
    together = dp_land[0]
    for k in range(1, dp_count):
        together = together + dp_land[k]
    small_out[row] = together
    row_sends, row_recvs = [], []
    for step in range(1, row_count):
        target, source = (row + step) % row_count, (row + row_count - step) % row_count
        row_sends.append(put(small_out.at[row], small_out.at[row], p_send, p_recv, 42 + step - 1, {"row": target}))
        row_recvs.append(
            put(small_out.at[source], small_out.at[source], p_send, p_recv, 42 + step - 1, {"row": source})
        )
        row_sends[-1].start()
    for u in range(17, pieces):
        turn(u)
    finish_inner(pieces - 1)
    finish_outer(pieces - 2)
    finish_outer(pieces - 1)
    for copy in row_recvs:
        copy.wait_recv()
    for copy in down_sends + stat_sends + dp_sends + row_sends:
        copy.wait_send()

    @pl.when(outer)
    def _():
        for u in range(pieces - 2 * g_slots, pieces):
            inward(u).wait_send()
        for u in range(pieces):
            sent_home(u, b_land.at[u])

    @pl.when(inner)
    def _():
        for u in range(pieces - t_slots, pieces):
            outward(u).wait_send()
            sent_home(u, t.at[u % t_slots])

    for u in range(pieces):
        for step in range(1, row_count):
            source = (row + row_count - step) % row_count
            put(t.at[0, source], place(u, source), a_send, a_recv, 3 * u + step - 1, {"row": source}).wait_recv()


def backward_plane(
    cid, hid, cot, slope, n2, upw, std, n1, qkvw, down_nat, resid_own, attended, outw, mixed, stats, marks, vec_all, std1_own, inv1_own, down_bias
):
    f32, bf16 = jnp.float32, jnp.bfloat16
    length, full = cot.shape
    rows, width = length // lax.axis_size("col"), full // lax.axis_size("row")
    row_count, dp_count = full // width, lax.axis_size("dp")
    counts = (slope.shape[1] // CHUNK, slope.shape[1] // CHUNK, attended.shape[1] // CHUNK, mixed.shape[1] // CHUNK)
    total = sum(counts)
    unit = (row_count, CHUNK, CHUNK)
    shape = jax.ShapeDtypeStruct
    away, near = pl.BlockSpec(memory_space=pl.ANY), pl.BlockSpec(memory_space=pltpu.VMEM)
    vmem, dma = pltpu.VMEM, pltpu.SemaphoreType.DMA
    sets = [
        vmem((4, rows, width), bf16),
        vmem((rows, width), bf16),
        vmem((rows // 2, width), bf16),
        vmem((rows // 2, width), bf16),
        vmem((2, rows, width), bf16),
        vmem((2, rows, width), bf16),
    ]
    return pl.pallas_call(
        functools.partial(backward_kernel, counts),
        out_shape=[
            shape((row_count * counts[0], CHUNK, width), bf16),
            shape((2, CHUNK, row_count * counts[1] * CHUNK), bf16),
            shape((row_count * counts[2], CHUNK, width), bf16),
            shape((2, CHUNK, row_count * counts[3] * CHUNK), bf16),
            shape((2 * total,) + unit, bf16),
            shape((hid.shape[1], full), bf16),
            shape((rows, width), bf16),
            shape((rows, width), bf16),
            shape((row_count, 16, width), f32),
        ],
        in_specs=[away] * 10 + [near] * 9,
        out_specs=[away] * 6 + [near] * 3,
        scratch_shapes=[
            vmem((length, full), bf16),
            vmem((length, full), bf16),
            vmem((length, full), bf16),
            vmem((length, full), bf16),
            vmem((length, full), bf16),
            vmem(upw.shape, bf16),
            vmem(hid.shape, bf16),
            vmem(slope.shape, bf16),
            vmem(attended.shape, bf16),
            vmem(mixed.shape, bf16),
            vmem((length, HEAD), f32),
            vmem((length, HEAD), f32),
            vmem((2, row_count, width // CHUNK, CHUNK, CHUNK), bf16),
            vmem((2,) + unit, bf16),
            vmem((2,) + unit, bf16),
            vmem((3,) + unit, bf16),
            vmem((4,) + unit, bf16),
        ]
        + sets
        + sets
        + [
            vmem((rows, width), f32),
            vmem((rows, width), f32),
            vmem((8, full), f32),
            vmem((16, width), f32),
            vmem((8, width), f32),
            vmem((dp_count, 16, width), f32),
            vmem((row_count, 8, rows), f32),
            dma((11,)),
            pltpu.SemaphoreType.REGULAR,
            dma((2 * total + 1,)),
            dma((6 * total,)),
            dma((6 * total,)),
            dma((6 * total,)),
            dma((6 * total,)),
            dma((45,)),
            dma((45,)),
        ],
        compiler_params=pltpu.CompilerParams(
            collective_id=cid, has_side_effects=True, vmem_limit_bytes=64 * 1024 * 1024 - 65536
        ),
        cost_estimate=pl.CostEstimate(flops=40_000_000_000, bytes_accessed=100_000_000, transcendentals=4_000_000),
    )(hid, cot, slope, n2, upw, std, n1, qkvw, down_nat, resid_own, attended, outw, mixed, stats, marks, vec_all, std1_own, inv1_own, down_bias)


class Moves:
    def __init__(self, source, target, cut, parts, sends, recvs, base):
        row, plane = lax.axis_index("row"), lax.axis_index("dp")
        side, core = row // 2, row % 2
        parity = plane % 2
        other = {"dp": plane + 1 - 2 * parity}
        twin = side * 2 + 1 - core
        far = ((1 - side) * 2 + core, (1 - side) * 2 + 1 - core)
        self.sibling = put(source(twin), target(row), sends, recvs, base, {"row": twin})
        self.sibling_in = put(source(twin), target(twin), sends, recvs, base, {"row": twin})
        self.outs, self.ins, self.passes, self.gets = [], [], [], []
        at = base + 1
        for step in range(parts // 2):
            for k, device in enumerate(far):
                mine, theirs = 2 * step + parity, 2 * step + 1 - parity
                there, here = cut(target(row), mine), cut(target(device), mine)
                self.outs.append(put(cut(source(device), mine), there, sends, recvs, at, {"row": device}))
                self.ins.append(put(cut(source(device), mine), here, sends, recvs, at, {"row": device}))
                self.passes.append(put(here, here, sends, recvs, at + 1, other))
                lands = cut(target(device), theirs)
                self.gets.append(put(lands, lands, sends, recvs, at + 1, other))
                at += 2

    @staticmethod
    def count(parts):
        return 1 + 2 * parts

    def start(self):
        self.sibling.start()
        self.start_far()

    def start_far(self):
        for copy in self.outs:
            copy.start()

    def forward(self, begin=0, end=None):
        for came, passed in list(zip(self.ins, self.passes))[begin:end]:
            came.wait_recv()
            passed.start()

    def finish(self):
        self.sibling_in.wait_recv()
        for copy in self.gets:
            copy.wait_recv()

    def drain(self):
        self.sibling.wait_send()
        for copy in self.outs + self.passes:
            copy.wait_send()


FAR_PARTS = 4


def forward_kernel(
    tokens,
    cot_in,
    vecs,
    mixed_bias,
    up_bias,
    marks,
    qkv_in,
    out_nat,
    up_nat,
    cot_all,
    n1_out,
    n2_out,
    std_out,
    upw_out,
    qkvw_out,
    outw_out,
    mixed_out,
    attended_out,
    hid_out,
    slope_out,
    stats,
    vec_all,
    resid_own,
    std1_own,
    inv1_own,
    tok,
    n1,
    part,
    tot,
    qkvw,
    upw,
    outw,
    mixed,
    attended,
    hid,
    slope,
    own_sum,
    got,
    diag,
    hx,
    hy,
    ts,
    fx,
    qkv_raw,
    qkv_nat,
    local_sem,
    w_send,
    w_recv,
    p_send,
    p_recv,
):
    f32, bf16 = jnp.float32, jnp.bfloat16
    plane, row, col = lax.axis_index("dp"), lax.axis_index("row"), lax.axis_index("col")
    side, core = row // 2, row % 2
    rows, width = tokens.shape
    length, full = tok.shape
    row_count = full // width
    heads_width = attended.shape[1]
    units = hid.shape[1]

    barrier = pltpu.get_barrier_semaphore()
    twins = ({"row": (1 - side) * 2 + 1 - core}, {"dp": plane + 1 - 2 * (plane % 2)})
    for partner in partners() + twins:
        pl.semaphore_signal(barrier, inc=1, device_id=partner, device_id_type=MESH)
    pl.semaphore_wait(barrier, 5)

    def cut_rows(ref, part):
        count = ref.shape[0] // FAR_PARTS
        return ref.at[strip(part * count, count)]

    per = qkvw.shape[1]
    count = Moves.count(FAR_PARTS)
    qkv_moves = Moves(
        lambda r: qkv_nat.at[:, strip(r * per, per)],
        lambda r: qkvw.at[strip(r * width, width), :],
        cut_rows,
        FAR_PARTS,
        w_send,
        w_recv,
        0,
    )
    out_moves = Moves(
        lambda r: out_nat.at[strip(r * heads_width, heads_width), :],
        lambda r: outw.at[:, strip(r * width, width)],
        cut_rows,
        FAR_PARTS,
        w_send,
        w_recv,
        count,
    )
    up_moves = Moves(
        lambda r: up_nat.at[:, strip(r * units, units)],
        lambda r: upw.at[strip(r * width, width), :],
        cut_rows,
        FAR_PARTS,
        w_send,
        w_recv,
        2 * count,
    )
    locals_ = [
        (qkv_nat.at[:, strip(row * per, per)], qkvw.at[strip(row * width, width), :]),
        (out_nat.at[strip(row * heads_width, heads_width), :], outw.at[:, strip(row * width, width)]),
        (up_nat.at[:, strip(row * units, units)], upw.at[strip(row * width, width), :]),
        (cot_in, block(cot_all, col, side, core, rows, width)),
        (n1, n1_out),
        (part, n2_out),
        (n1, std_out),
        (upw, upw_out),
        (qkvw, qkvw_out),
        (outw, outw_out),
        (mixed, mixed_out),
        (attended, attended_out),
        (hid, hid_out),
        (slope, slope_out),
        (qkv_in, qkv_raw),
    ]
    local = [pltpu.make_async_copy(a, b, local_sem.at[k]) for k, (a, b) in enumerate(locals_)]
    local[14].start()
    for k in range(1, 4):
        local[k].start()

    block(tok, col, side, core, rows, width)[...] = tokens[...]
    gather = spread_steps(tok, rows, width, p_send, p_recv, 0)
    next(gather)
    vec_all[:, strip(row * width, width)] = vecs[...]
    vec_sends, vec_recvs = [], []
    for step in range(1, row_count):
        target, source = (row + step) % row_count, (row + row_count - step) % row_count
        here, there = vec_all.at[:, strip(row * width, width)], vec_all.at[:, strip(source * width, width)]
        vec_sends.append(put(here, here, p_send, p_recv, 8 + step - 1, {"row": target}))
        vec_recvs.append(put(there, there, p_send, p_recv, 8 + step - 1, {"row": source}))
        vec_sends[-1].start()
    out_moves.sibling.start()
    up_moves.sibling.start()
    local[14].wait()
    for kind in range(3):
        flat = qkv_raw[:, kind].reshape(width, qkv_raw.shape[2] * HEAD)
        for head in range(qkv_raw.shape[2]):
            qkv_nat[:, pl.ds((head * 3 + kind) * HEAD, HEAD)] = flat[:, head * HEAD : (head + 1) * HEAD]
    local[0].start()
    qkv_moves.sibling.start()
    next(gather)
    qkv_moves.start_far()
    next(gather)
    next(gather, None)
    for copy in vec_recvs:
        copy.wait_recv()

    tile = 64
    gain1, shift1 = vec_all[0:1, :], vec_all[1:2, :]

    def norm1_step(k, none):
        at = strip(k * tile, tile)
        values = tok[at, :].astype(f32)
        center = jnp.sum(values, axis=1, keepdims=True) / full
        inverse = lax.rsqrt(jnp.sum(values * values, axis=1, keepdims=True) / full - center * center + epsilon)
        n1[at, :] = ((values - center) * inverse * gain1 + shift1).astype(bf16)

        @pl.when(k // (rows // tile) == col)
        def _():
            here = strip(k % (rows // tile) * tile, tile)
            std1_own[here, :] = ((tok[at, strip(row * width, width)].astype(f32) - center) * inverse).astype(bf16)
            inv1_own[here, :] = inverse

        return none

    half_steps = length // tile // 2
    lax.fori_loop(0, half_steps, norm1_step, 0)
    qkv_moves.forward(0, 2)
    lax.fori_loop(half_steps, 2 * half_steps, norm1_step, 0)
    local[4].start()
    qkv_moves.forward(2, 4)
    out_moves.start_far()
    up_moves.start_far()
    qkv_moves.finish()
    local[0].wait()

    def mixed_step(k, none):
        down, across = k // (per // CHUNK), k % (per // CHUNK)
        at, lanes = strip(down * rows, rows), strip(across * CHUNK, CHUNK)
        value = jnp.dot(n1[at, :], qkvw[:, lanes], preferred_element_type=f32)
        mixed[at, lanes] = (value + mixed_bias[:, lanes]).astype(bf16)
        return none

    lax.fori_loop(0, (length // rows) * (per // CHUNK), mixed_step, 0)
    local[8].start()
    local[10].start()
    local[4].wait()

    heads = heads_width // HEAD
    factor = 1.0 / math.sqrt(HEAD)
    blocks = length // SPAN
    spots = (SPAN, SPAN)
    earlier = lax.broadcasted_iota(jnp.int32, spots, 1) <= lax.broadcasted_iota(jnp.int32, spots, 0)

    def head_step(head, none):
        base = head * 3 * HEAD
        at_q, at_k, at_v = strip(base, HEAD), strip(base + HEAD, HEAD), strip(base + 2 * HEAD, HEAD)
        for k in range(blocks):
            here = pl.ds(k * SPAN, SPAN)
            seen = (k + 1) * SPAN
            scores = dot_nt(mixed[here, at_q], mixed[:seen, at_k]) * factor
            last = jnp.where(earlier | (marks[k : k + 1, :1] > 0), scores[:, seen - SPAN :], masked_score)
            scores = last if k == 0 else jnp.concatenate([scores[:, : seen - SPAN], last], axis=1)
            highest = jnp.max(scores, axis=1, keepdims=True)
            weights = jnp.exp(scores - highest)
            weight_sum = jnp.sum(weights, axis=1, keepdims=True)
            stats[here, 1 + head : 2 + head] = highest + jnp.log(weight_sum)
            value = jnp.dot((weights / weight_sum).astype(bf16), mixed[:seen, at_v], preferred_element_type=f32)
            attended[here, strip(head * HEAD, HEAD)] = value.astype(bf16)
        return none

    for head in range(heads):
        head_step(head, 0)
    local[11].start()
    out_moves.forward()
    up_moves.forward(0, 4)
    out_moves.finish()
    local[1].wait()
    tiled_nn(attended, outw, part, rows, 512)
    local[9].start()
    add_up = reduce_steps(part, own_sum, got, diag, hx, hy, ts, fx, p_send, p_recv, 11)
    next(add_up)
    next(add_up)
    up_moves.forward(4, 8)
    next(add_up)
    next(add_up, None)
    block(tot, col, side, core, rows, width)[...] = own_sum[...].astype(bf16)
    again = spread_steps(tot, rows, width, p_send, p_recv, 19)
    for k in range(3):
        next(again)
    next(again, None)
    local[3].wait()
    cot_gather = spread_steps(cot_all, rows, width, p_send, p_recv, 27)
    next(cot_gather)

    gain2, shift2, out_bias = vec_all[3:4, :], vec_all[4:5, :], vec_all[2:3, :]

    def norm2_step(k, none):
        at = strip(k * tile, tile)
        values = tok[at, :].astype(f32) + (tot[at, :].astype(f32) + out_bias)
        center = jnp.sum(values, axis=1, keepdims=True) / full
        inverse = lax.rsqrt(jnp.sum(values * values, axis=1, keepdims=True) / full - center * center + epsilon)
        standard = (values - center) * inverse
        stats[at, 0:1] = inverse
        n1[at, :] = standard.astype(bf16)
        part[at, :] = (standard * gain2 + shift2).astype(bf16)

        @pl.when(k // (rows // tile) == col)
        def _():
            own = strip(row * width, width)
            here = strip(k % (rows // tile) * tile, tile)
            resid_own[here, :] = tok[at, own].astype(f32) + (tot[at, own].astype(f32) + vec_all[2:3, own])

        return none

    lax.fori_loop(0, 2 * half_steps, norm2_step, 0)
    local[5].start()
    local[6].start()
    next(cot_gather)
    up_moves.finish()
    local[2].wait()
    local[7].start()

    def up_step(k, none):
        down, across = k // (units // CHUNK), k % (units // CHUNK)
        at, lanes = strip(down * rows, rows), strip(across * CHUNK, CHUNK)
        u = jnp.dot(part[at, :], upw[:, lanes], preferred_element_type=f32) + up_bias[:, lanes]
        bent = jnp.tanh(0.7978845608028654 * (u + 0.044715 * u * u * u))
        hid[at, lanes] = (0.5 * u * (1.0 + bent)).astype(bf16)
        inside = 0.7978845608028654 * (1.0 + 3 * 0.044715 * u * u)
        slope[at, lanes] = (0.5 * (1.0 + bent) + 0.5 * u * (1.0 - bent * bent) * inside).astype(bf16)
        return none

    lax.fori_loop(0, (length // rows) * (units // CHUNK), up_step, 0)
    local[12].start()
    local[13].start()
    next(cot_gather)
    next(cot_gather, None)
    for k in range(5, 14):
        local[k].wait()
    for moves in (qkv_moves, out_moves, up_moves):
        moves.drain()
    for copy in vec_sends:
        copy.wait_send()


def forward_plane(cid, tokens, cot, vecs, mixed_bias, up_bias, marks, qkv_in, out_nat, up_nat):
    f32, bf16 = jnp.float32, jnp.bfloat16
    rows, width = tokens.shape
    row_count = lax.axis_size("row")
    length, full = rows * lax.axis_size("col"), width * row_count
    per, heads_width, units = qkv_in.shape[1] * qkv_in.shape[2] * HEAD // row_count, out_nat.shape[0] // row_count, up_nat.shape[1] // row_count
    shape = jax.ShapeDtypeStruct
    away, near = pl.BlockSpec(memory_space=pl.ANY), pl.BlockSpec(memory_space=pltpu.VMEM)
    vmem, dma = pltpu.VMEM, pltpu.SemaphoreType.DMA
    wide = shape((length, full), bf16)
    moved = 3 * Moves.count(FAR_PARTS)
    return pl.pallas_call(
        forward_kernel,
        out_shape=[
            wide,
            wide,
            wide,
            wide,
            shape((full, units), bf16),
            shape((full, per), bf16),
            shape((heads_width, full), bf16),
            shape((length, per), bf16),
            shape((length, heads_width), bf16),
            shape((length, units), bf16),
            shape((length, units), bf16),
            shape((length, 8), f32),
            shape((8, full), f32),
            shape((rows, width), f32),
            shape((rows, width), bf16),
            shape((rows, 1), f32),
        ],
        in_specs=[near] * 6 + [away] * 3,
        out_specs=[away] * 11 + [near] * 5,
        scratch_shapes=[
            vmem((length, full), bf16),
            vmem((length, full), bf16),
            vmem((length, full), bf16),
            vmem((length, full), bf16),
            vmem((full, per), bf16),
            vmem((full, units), bf16),
            vmem((heads_width, full), bf16),
            vmem((length, per), bf16),
            vmem((length, heads_width), bf16),
            vmem((length, units), bf16),
            vmem((length, units), bf16),
            vmem((rows, width), f32),
            vmem((4, rows, width), bf16),
            vmem((rows, width), bf16),
            vmem((rows // 2, width), bf16),
            vmem((rows // 2, width), bf16),
            vmem((2, rows, width), bf16),
            vmem((2, rows, width), bf16),
            vmem(qkv_in.shape, bf16),
            vmem((width, row_count * per), bf16),
            dma((15,)),
            dma((moved,)),
            dma((moved,)),
            dma((35,)),
            dma((35,)),
        ],
        compiler_params=pltpu.CompilerParams(
            collective_id=cid, has_side_effects=True, vmem_limit_bytes=60 * 1024 * 1024
        ),
        cost_estimate=pl.CostEstimate(flops=10_000_000_000, bytes_accessed=60_000_000, transcendentals=4_000_000),
    )(tokens, cot, vecs, mixed_bias, up_bias, marks, qkv_in, out_nat, up_nat)


def head_order_kernel(flat, result):
    for head in range(result.shape[2]):
        for kind in range(3):
            begin = (head * 3 + kind) * HEAD
            result[:, kind, head, :] = flat[:, begin : begin + HEAD].astype(jnp.float32)


def head_order(flat):
    rows, heads = flat.shape[0], flat.shape[1] // (3 * HEAD)
    tile = 128
    result = pl.pallas_call(
        head_order_kernel,
        grid=(rows // tile,),
        out_shape=jax.ShapeDtypeStruct((rows, 3, heads, HEAD), jnp.float32),
        in_specs=[pl.BlockSpec((tile, flat.shape[1]), lambda k: (k, 0))],
        out_specs=pl.BlockSpec((tile, 3, heads, HEAD), lambda k: (k, 0, 0, 0)),
    )(flat)
    return jnp.swapaxes(result, 1, 2)


def plane_plan(
    tokens,
    ln1_gain,
    ln1_shift,
    qkv_weight,
    qv_bias,
    out_weight,
    out_bias,
    ln2_gain,
    ln2_shift,
    up_weight,
    up_bias,
    down_weight,
    down_bias,
    span_starts,
    cotangent,
):
    f32 = jnp.float32
    rows, width = tokens.shape
    row_count = lax.axis_size("row")
    row = lax.axis_index("row")
    length = rows * lax.axis_size("col")
    heads = qkv_weight.shape[1] // row_count
    units = up_weight.shape[1] // row_count

    blank = jnp.zeros_like(ln1_gain)
    vecs = jnp.stack([ln1_gain, ln1_shift, out_bias, ln2_gain, ln2_shift, blank, blank, blank], axis=0)
    own_qv = lax.dynamic_slice_in_dim(qv_bias, row * heads, heads, 0)
    mixed_bias = jnp.stack([own_qv[:, 0], jnp.zeros_like(own_qv[:, 0]), own_qv[:, 1]], axis=1).reshape(1, -1)
    own_up_bias = lax.dynamic_slice_in_dim(up_bias, row * units, units, 0)[None]
    blocks = length // SPAN
    marked = jnp.any(span_starts[0][:, None] // SPAN == jnp.arange(blocks, dtype=jnp.int32)[None, :], axis=0)
    marks = jnp.broadcast_to(jnp.pad(marked.astype(f32), (0, -blocks % 8))[:, None], (blocks + -blocks % 8, 128))

    (
        cot_all, n1, n2, standard2, upw, qkvw, outw, mixed, attended, hidden, slope,
        stats, vec_all, residual_own, standard1_own, inverse1_own,
    ) = forward_plane(
        1,
        tokens,
        cotangent,
        vecs,
        mixed_bias,
        own_up_bias,
        marks,
        jnp.swapaxes(qkv_weight, 1, 2),
        out_weight.reshape(-1, width),
        up_weight,
    )
    down_grad, up_grad, out_grad, qkv_grad, _, _, output, tokens_grad, small = backward_plane(
        2, hidden, cot_all, slope, n2, upw, standard2, n1, qkvw, down_weight, residual_own, attended, outw, mixed, stats, marks,
        vec_all, standard1_own, inverse1_own, down_bias[None],
    )
    mine = lax.dynamic_index_in_dim(small, row, 0, keepdims=False)
    spot = 8 + units // width
    return (
        output,
        tokens_grad,
        mine[0],
        mine[1],
        head_order(qkv_grad.reshape(width, -1)),
        small[:, spot, : 2 * heads * HEAD].reshape(row_count * heads, 2, HEAD),
        out_grad.astype(f32).reshape(row_count * heads, HEAD, width),
        mine[4],
        mine[2],
        mine[3],
        up_grad.astype(f32).reshape(width, row_count * units),
        small[:, 8:spot].reshape(-1),
        down_grad.astype(f32).reshape(row_count * units, width),
        mine[5],
    )


def solution(mesh):
    sizes = dict(mesh.shape)
    flat = sizes == {"dp": 4, "row": 4, "col": 2}
    per_device = plane_plan if flat else general_plan
    placed = (
        P(("dp", "col"), "row"),
        P("row"),
        P("row"),
        P("row", "col", None, None),
        P("col", None, None),
        P("col", None, "row"),
        P("row"),
        P("row"),
        P("row"),
        P("row", "col"),
        P("col"),
        P("col", "row"),
        P("row"),
        P("dp", None),
        P(("dp", "col"), "row"),
    )
    return jax.shard_map(
        per_device,
        mesh=mesh,
        in_specs=placed,
        out_specs=(
            P(("dp", "col"), "row"),
            P(("dp", "col"), "row"),
            P("row"),
            P("row"),
            P("row", "col", None, None),
            P("col", None, None),
            P("col", None, "row"),
            P("row"),
            P("row"),
            P("row"),
            P("row", "col"),
            P("col"),
            P("col", "row"),
            P("row"),
        ),
        check_vma=False,
    )
```

```python
import functools
import math

import jax
import jax.numpy as jnp
from jax import lax
from jax.experimental import pallas as pl
from jax.experimental.pallas import tpu as pltpu
from jax.sharding import PartitionSpec as P

MESH = pl.DeviceIdType.MESH

D = 2048
HEAD = 128
SEQS = 1
SPAN = 256
BLOCK = 512


epsilon = 1e-05
masked_score = -1e30


def gelu_tanh(values):
    return (
        0.5
        * values
        * (1.0 + jnp.tanh(0.7978845608028654 * (values + 0.044715 * values * values * values)))
    )


def gather_columns(block_data):
    return lax.all_gather(block_data, "col", axis=0, tiled=True)


def gather_rows(block_data):
    return lax.all_gather(block_data, "row", axis=0, tiled=True)


def product(left_side, right_side, flipped):
    if flipped:
        return lax.dot_general(
            left_side, right_side, (((1,), (1,)), ((), ())), preferred_element_type=jnp.float32
        )
    return jnp.dot(left_side, right_side, preferred_element_type=jnp.float32)


def outer_sum(left_side, right_side):
    return lax.dot_general(
        left_side, right_side, (((0,), (0,)), ((), ())), preferred_element_type=jnp.float32
    )


def sum_rows(left_side, right_side, flipped):
    wide_left = lax.all_to_all(left_side, "row", split_axis=0, concat_axis=1, tiled=True)
    if flipped:
        wide_right = lax.all_gather(right_side, "row", axis=1, tiled=True)
    else:
        wide_right = lax.all_gather(right_side, "row", axis=0, tiled=True)
    return product(wide_left, wide_right, flipped)


def sum_columns(left_side, right_side, flipped):
    return lax.psum_scatter(
        product(left_side, right_side, flipped), "col", scatter_dimension=0, tiled=True
    )


def row_totals(first_sum, second_sum):
    return lax.psum((first_sum, second_sum), "row")


def norm_forward(values, gain_row, bias_row):
    totals, squares = row_totals(jnp.sum(values, axis=1), jnp.sum(values * values, axis=1))
    center = totals / D
    spread = squares / D - center * center
    inverse = lax.rsqrt(spread + epsilon)
    standard = (values - center[:, None]) * inverse[:, None]
    return (standard, inverse, (standard * gain_row + bias_row).astype(jnp.bfloat16))


def norm_backward(upstream, standard, inverse, gain_row):
    scaled = upstream * gain_row
    first_sum, second_sum = row_totals(jnp.sum(scaled, axis=1), jnp.sum(scaled * standard, axis=1))
    gradient = inverse[:, None] * (
        scaled - first_sum[:, None] / D - standard * (second_sum[:, None] / D)
    )
    return (gradient, jnp.sum(upstream * standard, axis=0), jnp.sum(upstream, axis=0))


def visible(query_pos, query_image, key_pos):
    earlier = key_pos[None, :] <= query_pos[:, None]
    same_span = (key_pos[None, :] // SPAN == query_pos[:, None] // SPAN) & (
        query_image[:, None] > 0
    )
    return earlier | same_span


def attention_forward(queries, key_value, token_image, row_offset, seq_length, block_rows):
    own_rows, head_count, width = queries.shape
    factor = 1.0 / math.sqrt(width)

    def block_forward(block_index):
        local = block_index * block_rows
        start_pos = row_offset + local
        query_block = lax.dynamic_slice_in_dim(queries, local, block_rows, 0)
        query_pos = start_pos + jnp.arange(block_rows, dtype=jnp.int32)
        query_image = lax.dynamic_slice_in_dim(token_image, start_pos, block_rows, 0)
        begin = start_pos // seq_length * seq_length // block_rows
        finish = start_pos // block_rows + 1

        def key_step(key_index, state_in):
            running, weight_sum, gathered = state_in
            key_begin = key_index * block_rows
            key_block = lax.dynamic_slice_in_dim(key_value, key_begin, block_rows, 0)
            key_pos = key_begin + jnp.arange(block_rows, dtype=jnp.int32)
            allowed = visible(query_pos, query_image, key_pos)
            scores = (
                jnp.einsum(
                    "qhd,khd->hqk",
                    query_block,
                    key_block[:, :, 0],
                    preferred_element_type=jnp.float32,
                )
                * factor
            )
            scores = jnp.where(allowed[None], scores, masked_score)
            highest = jnp.maximum(running, jnp.max(scores, axis=2))
            weights = jnp.exp(scores - highest[:, :, None])
            shrink = jnp.exp(running - highest)
            weight_sum = weight_sum * shrink + jnp.sum(weights, axis=2)
            gathered = gathered * shrink.T[:, :, None] + jnp.einsum(
                "hqk,khd->qhd",
                weights.astype(jnp.bfloat16),
                key_block[:, :, 1],
                preferred_element_type=jnp.float32,
            )
            return (highest, weight_sum, gathered)

        initial = (
            jnp.full((head_count, block_rows), masked_score, jnp.float32),
            jnp.zeros((head_count, block_rows), jnp.float32),
            jnp.zeros((block_rows, head_count, width), jnp.float32),
        )
        running, weight_sum, gathered = lax.fori_loop(begin, finish, key_step, initial)
        return (gathered / weight_sum.T[:, :, None], running + jnp.log(weight_sum))

    result, logsum = lax.map(block_forward, jnp.arange(own_rows // block_rows, dtype=jnp.int32))
    return (result.reshape(own_rows, head_count, width), logsum)


def attention_backward(
    queries,
    key_value,
    attended_full,
    logsum,
    d_attended,
    token_image,
    row_offset,
    seq_length,
    block_rows,
):
    own_rows, head_count, width = queries.shape
    factor = 1.0 / math.sqrt(width)
    row_dots = jnp.sum(d_attended.astype(jnp.float32) * attended_full, axis=2)

    def block_backward(block_index, state_out):
        d_queries, d_pairs = state_out
        local = block_index * block_rows
        start_pos = row_offset + local
        query_block = lax.dynamic_slice_in_dim(queries, local, block_rows, 0)
        dout_block = lax.dynamic_slice_in_dim(d_attended, local, block_rows, 0)
        dots_block = lax.dynamic_slice_in_dim(row_dots, local, block_rows, 0).T
        logsum_block = logsum[block_index]
        query_pos = start_pos + jnp.arange(block_rows, dtype=jnp.int32)
        query_image = lax.dynamic_slice_in_dim(token_image, start_pos, block_rows, 0)
        begin = start_pos // seq_length * seq_length // block_rows
        finish = start_pos // block_rows + 1

        def key_step(key_index, state_in):
            d_query, d_keys = state_in
            key_begin = key_index * block_rows
            key_block = lax.dynamic_slice_in_dim(key_value, key_begin, block_rows, 0)
            key_pos = key_begin + jnp.arange(block_rows, dtype=jnp.int32)
            allowed = visible(query_pos, query_image, key_pos)
            scores = (
                jnp.einsum(
                    "qhd,khd->hqk",
                    query_block,
                    key_block[:, :, 0],
                    preferred_element_type=jnp.float32,
                )
                * factor
            )
            scores = jnp.where(allowed[None], scores, masked_score)
            probabilities = jnp.exp(scores - logsum_block[:, :, None])
            d_probs = jnp.einsum(
                "qhd,khd->hqk", dout_block, key_block[:, :, 1], preferred_element_type=jnp.float32
            )
            d_scores = (probabilities * (d_probs - dots_block[:, :, None])).astype(jnp.bfloat16)
            d_query = d_query + jnp.einsum(
                "hqk,khd->qhd", d_scores, key_block[:, :, 0], preferred_element_type=jnp.float32
            )
            d_key = (
                jnp.einsum(
                    "hqk,qhd->khd", d_scores, query_block, preferred_element_type=jnp.float32
                )
                * factor
            )
            d_value = jnp.einsum(
                "hqk,qhd->khd",
                probabilities.astype(jnp.bfloat16),
                dout_block,
                preferred_element_type=jnp.float32,
            )
            previous = lax.dynamic_slice_in_dim(d_keys, key_begin, block_rows, 0)
            d_keys = lax.dynamic_update_slice_in_dim(
                d_keys, previous + jnp.stack([d_key, d_value], axis=2), key_begin, 0
            )
            return (d_query, d_keys)

        d_query, d_pairs = lax.fori_loop(
            begin,
            finish,
            key_step,
            (jnp.zeros((block_rows, head_count, width), jnp.float32), d_pairs),
        )
        d_queries = lax.dynamic_update_slice_in_dim(d_queries, d_query * factor, local, 0)
        return (d_queries, d_pairs)

    initial = (
        jnp.zeros((own_rows, head_count, width), jnp.float32),
        jnp.zeros((key_value.shape[0], head_count, 2, width), jnp.float32),
    )
    return lax.fori_loop(0, own_rows // block_rows, block_backward, initial)


def general_plan(
    tokens,
    ln1_gain,
    ln1_shift,
    qkv_weight,
    qv_bias,
    out_weight,
    out_bias,
    ln2_gain,
    ln2_shift,
    up_weight,
    up_bias,
    down_weight,
    down_bias,
    span_starts,
    cotangent,
):
    col_rows, row_width = tokens.shape
    group_rows = col_rows * lax.axis_size("col")
    own_rows = group_rows // lax.axis_size("row")
    head_count = qkv_weight.shape[1]
    seq_length = group_rows // SEQS
    block_rows = BLOCK - own_rows % BLOCK
    row_offset = lax.axis_index("row") * own_rows
    slot_count = seq_length // SPAN
    image_marks = jnp.sum(
        (
            span_starts[:, :, None] // SPAN
            == jnp.arange(slot_count, dtype=jnp.int32)[None, None, :]
        ).astype(jnp.int32),
        axis=1,
    )
    token_image = jnp.broadcast_to(
        image_marks.reshape(-1)[:, None], (group_rows // SPAN, SPAN)
    ).reshape(group_rows)
    qkv_flat = qkv_weight.reshape(row_width, head_count * 3 * HEAD)
    out_flat = out_weight.reshape(head_count * HEAD, row_width)
    inputs = tokens.astype(jnp.float32)
    standard1, inverse1, normed1 = norm_forward(inputs, ln1_gain, ln1_shift)
    normed1_all = gather_columns(normed1)
    mixed_sums = sum_rows(normed1_all, qkv_flat, False).reshape(own_rows, head_count, 3, HEAD)
    queries = (mixed_sums[:, :, 0] + qv_bias[:, 0]).astype(jnp.bfloat16)
    key_value_own = jnp.stack(
        [mixed_sums[:, :, 1], mixed_sums[:, :, 2] + qv_bias[:, 1]], axis=2
    ).astype(jnp.bfloat16)
    key_value = gather_rows(key_value_own)
    attended_full, logsum = attention_forward(
        queries, key_value, token_image, row_offset, seq_length, block_rows
    )
    attended = attended_full.astype(jnp.bfloat16).reshape(own_rows, head_count * HEAD)
    attended_all = gather_rows(attended)
    residual = inputs + (sum_columns(attended_all, out_flat, False) + out_bias)
    standard2, inverse2, normed2 = norm_forward(residual, ln2_gain, ln2_shift)
    normed2_all = gather_columns(normed2)
    up_sums = sum_rows(normed2_all, up_weight, False) + up_bias
    hidden = gelu_tanh(up_sums).astype(jnp.bfloat16)
    hidden_all = gather_rows(hidden)
    output = (residual + (sum_columns(hidden_all, down_weight, False) + down_bias)).astype(
        jnp.bfloat16
    )
    d_output = cotangent.astype(jnp.float32)
    d_output_all = gather_columns(cotangent)
    down_grad = outer_sum(hidden_all, d_output_all)
    down_bias_grad = jnp.sum(d_output_all, axis=0, dtype=jnp.float32)
    d_hidden = sum_rows(d_output_all, down_weight, True)
    d_upper = jax.vjp(gelu_tanh, up_sums)[1](d_hidden)[0].astype(jnp.bfloat16)
    d_upper_all = gather_rows(d_upper)
    normed2_use = gather_columns(normed2)
    up_grad = outer_sum(normed2_use, d_upper_all)
    up_bias_grad = jnp.sum(d_upper_all, axis=0, dtype=jnp.float32)
    d_normed2 = sum_columns(d_upper_all, up_weight, True)
    d_norm2, gain2_grad, shift2_grad = norm_backward(d_normed2, standard2, inverse2, ln2_gain)
    d_residual = d_output + d_norm2
    d_branch = d_residual.astype(jnp.bfloat16)
    d_branch_all = gather_columns(d_branch)
    out_grad = outer_sum(attended_all, d_branch_all)
    out_bias_grad = jnp.sum(d_branch_all, axis=0, dtype=jnp.float32)
    d_attended = (
        sum_rows(d_branch_all, out_flat, True)
        .astype(jnp.bfloat16)
        .reshape(own_rows, head_count, HEAD)
    )
    d_queries, d_pairs = attention_backward(
        queries,
        key_value,
        attended_full,
        logsum,
        d_attended,
        token_image,
        row_offset,
        seq_length,
        block_rows,
    )
    d_pairs_own = lax.psum_scatter(d_pairs, "row", scatter_dimension=0, tiled=True)
    d_mixed = jnp.concatenate([d_queries[:, :, None], d_pairs_own], axis=2).astype(jnp.bfloat16)
    d_mixed_all = gather_rows(d_mixed)
    normed1_use = gather_columns(normed1)
    d_mixed_flat = d_mixed_all.reshape(group_rows, head_count * 3 * HEAD)
    qkv_grad = outer_sum(normed1_use, d_mixed_flat)
    mixed_totals = jnp.sum(d_mixed_all, axis=0, dtype=jnp.float32)
    qv_bias_grad = jnp.stack([mixed_totals[:, 0], mixed_totals[:, 2]], axis=1)
    d_normed1 = sum_columns(d_mixed_flat, qkv_flat, True)
    d_norm1, gain1_grad, shift1_grad = norm_backward(d_normed1, standard1, inverse1, ln1_gain)
    tokens_grad = (d_residual + d_norm1).astype(jnp.bfloat16)
    norm_sums = lax.psum((gain1_grad, shift1_grad, gain2_grad, shift2_grad), ("dp", "col"))
    weight_sums = lax.psum(
        (
            qkv_grad,
            qv_bias_grad,
            out_grad,
            out_bias_grad,
            up_grad,
            up_bias_grad,
            down_grad,
            down_bias_grad,
        ),
        "dp",
    )
    return (
        output,
        tokens_grad,
        norm_sums[0],
        norm_sums[1],
        weight_sums[0].reshape(row_width, head_count, 3, HEAD),
        weight_sums[1],
        weight_sums[2].reshape(head_count, HEAD, row_width),
        weight_sums[3],
        norm_sums[2],
        norm_sums[3],
        weight_sums[4],
        weight_sums[5],
        weight_sums[6],
        weight_sums[7],
    )


def places():
    row, col = lax.axis_index("row"), lax.axis_index("col")
    return col, row // 2, row % 2


def partners():
    col, side, core = places()
    return ({"col": 1 - col}, {"row": (1 - side) * 2 + core}, {"row": side * 2 + 1 - core})


def block(ref, col, side, core, rows, width, part=None):
    begin, count = col * rows, rows
    if part is not None:
        begin, count = begin + part * (rows // 2), rows // 2
    return ref.at[strip(begin, count), strip((side * 2 + core) * width, width)]


def put(ref_from, ref_to, sends, recvs, at, partner):
    return pltpu.make_async_remote_copy(
        src_ref=ref_from,
        dst_ref=ref_to,
        send_sem=sends.at[at],
        recv_sem=recvs.at[at],
        device_id=partner,
        device_id_type=MESH,
    )


def strip(begin, count):
    return pl.ds(pl.multiple_of(begin, count), count)


def dot_nt(left, right):
    return lax.dot_general(left, right, (((1,), (1,)), ((), ())), preferred_element_type=jnp.float32)


def dot_tn(left, right):
    return lax.dot_general(left, right, (((0,), (0,)), ((), ())), preferred_element_type=jnp.float32)


def tiled_nt(left, right, target, inner, tile_rows, tile_cols):
    rows, cols = target.shape
    across = cols // tile_cols

    def step(at, none):
        down, side = at // across, at % across
        value = dot_nt(left[strip(down * tile_rows, tile_rows), :inner], right[strip(side * tile_cols, tile_cols), :inner])
        target[strip(down * tile_rows, tile_rows), strip(side * tile_cols, tile_cols)] = value.astype(target.dtype)
        return none

    lax.fori_loop(0, (rows // tile_rows) * across, step, 0)


def tiled_nn(left, right, target, tile_rows, tile_cols):
    rows, cols = target.shape
    across = cols // tile_cols

    def step(at, none):
        down, side = at // across, at % across
        value = jnp.dot(
            left[strip(down * tile_rows, tile_rows), :],
            right[:, strip(side * tile_cols, tile_cols)],
            preferred_element_type=jnp.float32,
        )
        target[strip(down * tile_rows, tile_rows), strip(side * tile_cols, tile_cols)] = value.astype(target.dtype)
        return none

    lax.fori_loop(0, (rows // tile_rows) * across, step, 0)


def reduce_steps(part, result, got, diag, half_x, half_y, to_send, from_xy, sends, recvs, base):
    f32 = jnp.float32
    rows, width = result.shape
    half = rows // 2
    low, high = pl.ds(0, half), pl.ds(half, half)
    col, side, core = places()
    to_x, to_y, to_core = partners()
    spots = ((1 - col, 1 - side), (col, 1 - side), (1 - col, side), (col, side))
    copies = [
        put(block(part, a, b, 1 - core, rows, width), got.at[k], sends, recvs, base + k, to_core)
        for k, (a, b) in enumerate(spots)
    ]
    for copy in copies:
        copy.start()
    mine = [block(part, a, b, core, rows, width) for a, b in spots]
    dx = put(diag.at[low], half_x, sends, recvs, base + 4, to_x)
    dy = put(diag.at[high], half_y, sends, recvs, base + 5, to_y)
    cy = put(to_send.at[0], from_xy.at[0], sends, recvs, base + 6, to_y)
    cx = put(to_send.at[1], from_xy.at[1], sends, recvs, base + 7, to_x)
    yield
    copies[0].wait_recv()
    diag[...] = (mine[0][...].astype(f32) + got[0].astype(f32)).astype(diag.dtype)
    dx.start()
    dy.start()
    copies[1].wait_recv()
    copies[2].wait_recv()
    to_send[0, high] = (mine[1][high].astype(f32) + got[1, high].astype(f32)).astype(diag.dtype)
    to_send[1, low] = (mine[2][low].astype(f32) + got[2, low].astype(f32)).astype(diag.dtype)
    copies[3].wait_recv()
    result[...] = mine[3][...].astype(f32) + got[3].astype(f32)
    yield
    dx.wait_recv()
    to_send[0, low] = (mine[1][low].astype(f32) + got[1, low].astype(f32) + half_x[...].astype(f32)).astype(diag.dtype)
    cy.start()
    dy.wait_recv()
    to_send[1, high] = (mine[2][high].astype(f32) + got[2, high].astype(f32) + half_y[...].astype(f32)).astype(
        diag.dtype
    )
    cx.start()
    yield
    cy.wait_recv()
    cx.wait_recv()
    result[...] = result[...] + from_xy[0].astype(f32) + from_xy[1].astype(f32)
    for copy in copies + [dx, dy, cy, cx]:
        copy.wait_send()


def spread_steps(out, rows, width, sends, recvs, base, mostly_x=False):
    col, side, core = places()
    to_x, to_y, to_core = partners()

    def copy_of(at, which, partner, part=None):
        ref = block(out, *which, rows, width, part)
        return put(ref, ref, sends, recvs, base + at, partner)

    own, ox, oy, od = (col, side, core), (1 - col, side, core), (col, 1 - side, core), (1 - col, 1 - side, core)
    plan = [
        copy_of(0, own, to_x),
        copy_of(1, own, to_y),
        copy_of(2, own, to_core),
        None if mostly_x else copy_of(3, ox, to_y, 0),
        copy_of(4, oy, to_x, None if mostly_x else 1),
        copy_of(5, ox, to_core),
        copy_of(6, oy, to_core),
        copy_of(7, od, to_core),
    ]
    for at in (0, 1, 2):
        plan[at].start()
    yield
    used = [at for at in range(8) if at != 3 or not mostly_x]
    plan[0].wait_recv()
    if not mostly_x:
        plan[3].start()
    plan[1].wait_recv()
    plan[4].start()
    plan[5].start()
    plan[6].start()
    yield
    if not mostly_x:
        plan[3].wait_recv()
    plan[4].wait_recv()
    plan[7].start()
    yield
    for at in (2, 5, 6, 7):
        plan[at].wait_recv()
    for at in used:
        plan[at].wait_send()


CHUNK = 256


def backward_kernel(
    counts,
    hid_h,
    cot_h,
    slope_h,
    n2_h,
    upw_h,
    std_h,
    n1_h,
    qkvw_h,
    down_nat,
    resid_h,
    attended_h,
    outw_h,
    mixed_h,
    std1_h,
    stats,
    marks,
    vec_all,
    inv1_own,
    down_bias,
    down_out,
    up_out,
    out_out,
    qkv_out,
    b_land,
    downw_land,
    out_block,
    tokens_block,
    small_out,
    cot,
    n2,
    std,
    part,
    tot,
    upw,
    hid,
    dup,
    attended,
    outw,
    mixed,
    std1_own,
    d_att,
    d_mix,
    dk_acc,
    dv_acc,
    g,
    s,
    t,
    r_land,
    m_land,
    got_a,
    diag_a,
    hx_a,
    hy_a,
    ts_a,
    fx_a,
    got_b,
    diag_b,
    hx_b,
    hy_b,
    ts_b,
    fx_b,
    dres_own,
    own_sum,
    sums,
    small,
    x_land,
    dp_land,
    stat_land,
    load_sem,
    credit,
    own_sem,
    z_send,
    z_recv,
    a_send,
    a_recv,
    p_send,
    p_recv,
):
    f32, bf16 = jnp.float32, jnp.bfloat16
    n_down, n_up, n_out, n_qkv = counts
    total = sum(counts)
    plane, row, col = lax.axis_index("dp"), lax.axis_index("row"), lax.axis_index("col")
    length, full = cot.shape
    rows, width = dres_own.shape
    row_count = full // width
    inner = (plane == 1) | (plane == 2)
    outer = jnp.logical_not(inner)
    to_inner = {"dp": plane // 3 + 1}
    to_middle = {"dp": 3 - plane}
    to_outer = {"dp": (plane - 1) * 3}
    side, core = row // 2, row % 2

    loads = [
        (hid_h, hid),
        (cot_h, cot),
        (slope_h, dup),
        (upw_h, upw),
        (n2_h, n2),
        (std_h, std),
        (qkvw_h, upw.at[:, : qkvw_h.shape[1]]),
        (n1_h, std),
        (downw_land, n2),
        (downw_land, tot),
        (resid_h, dres_own),
        (attended_h, attended),
        (outw_h, outw),
        (mixed_h, mixed),
        (std1_h, std1_own),
    ]
    loads = [pltpu.make_async_copy(a, b, load_sem.at[k]) for k, (a, b) in enumerate(loads)]
    for k in (0, 1, 2, 3, 4, 5, 11, 12, 13, 14):
        loads[k].start()

    dp_count = dp_land.shape[0]
    barrier = pltpu.get_barrier_semaphore()
    others = [{"row": (1 - side) * 2 + 1 - core}] + [{"dp": (plane + k) % dp_count} for k in range(1, dp_count)]
    for partner in partners() + tuple(others):
        pl.semaphore_signal(barrier, inc=1, device_id=partner, device_id_type=MESH)
    pl.semaphore_wait(barrier, 3 + len(others))

    units = hid.shape[1]
    down_sends, down_recvs = [], []
    for step in range(1, row_count):
        target, source = (row + step) % row_count, (row + row_count - step) % row_count
        here, there = downw_land.at[:, strip(row * width, width)], downw_land.at[:, strip(source * width, width)]
        piece = down_nat.at[strip(target * units, units), :]
        down_sends.append(put(piece, here, p_send, p_recv, 32 + step - 1, {"row": target}))
        down_recvs.append(put(piece, there, p_send, p_recv, 32 + step - 1, {"row": source}))
        down_sends[-1].start()
    down_own = pltpu.make_async_copy(
        down_nat.at[strip(row * units, units), :], downw_land.at[:, strip(row * width, width)], own_sem.at[2 * total]
    )
    down_own.start()

    def place(u, source):
        i, half = u // 2, u % 2
        if i < n_down:
            return down_out.at[source * n_down + i // 2 * 2 + half, :, pl.ds(i % 2 * CHUNK, CHUNK)]
        i -= n_down
        if i < n_up:
            return up_out.at[half, :, strip(source * n_up * CHUNK + i * CHUNK, CHUNK)]
        i -= n_up
        if i < n_out:
            return out_out.at[source * n_out + i, :, pl.ds(half * CHUNK, CHUNK)]
        i -= n_out
        return qkv_out.at[half, :, strip(source * n_qkv * CHUNK + i * CHUNK, CHUNK)]

    g_slots, s_slots, t_slots, r_slots, m_slots = g.shape[0], s.shape[0], t.shape[0], r_land.shape[0], m_land.shape[0]
    pieces = 2 * total

    def made(u):
        return g.at[u // 2 % g_slots, :, u % 2]

    def inward(u):
        return put(made(u), r_land.at[u % r_slots], z_send, z_recv, u, to_inner)

    def across(u):
        return put(s.at[u % s_slots], m_land.at[u % m_slots], z_send, z_recv, pieces + u, to_middle)

    def outward(u):
        return put(t.at[u % t_slots], b_land.at[u], z_send, z_recv, 2 * pieces + u, to_outer)

    def home(u, step, source):
        target = (row + step) % row_count
        return put(source.at[target], place(u, row), a_send, a_recv, 3 * u + step - 1, {"row": target})

    def home_own(u, source):
        return pltpu.make_async_copy(source.at[row], place(u, row), own_sem.at[u])

    def send_home(u, source):
        for step in range(1, row_count):
            home(u, step, source).start()
        home_own(u, source).start()

    def sent_home(u, source):
        for step in range(1, row_count):
            home(u, step, source).wait_send()
        home_own(u, source).wait()

    def produce(i):
        if i >= g_slots:

            @pl.when(outer)
            def _():
                inward(2 * (i - g_slots)).wait_send()
                inward(2 * (i - g_slots) + 1).wait_send()

        slot = g.at[i % g_slots]
        if i < n_down:
            begin, lane = i // 2 * 2 * CHUNK, i % 2 * CHUNK

            def step(k, none):
                value = dot_tn(hid[:, begin : begin + 2 * CHUNK], cot[:, strip(k * width + lane, CHUNK)]).astype(bf16)
                slot[k, 0] = value[:CHUNK]
                slot[k, 1] = value[CHUNK:]
                return none
        elif n_down + n_up <= i < n_down + n_up + n_out:
            left, begin, right = attended, (i - n_down - n_up) * CHUNK, part

            def step(k, none):
                value = dot_tn(left[:, begin : begin + CHUNK], right[:, strip(k * width, width)]).astype(bf16)
                slot[k, 0] = value[:, :CHUNK]
                slot[k, 1] = value[:, CHUNK:]
                return none
        else:
            if i < n_down + n_up:
                left, right, begin = n2, dup, (i - n_down) * CHUNK
            else:
                left, right, begin = std, d_mix, (i - n_down - n_up - n_out) * CHUNK

            def step(k, none):
                value = dot_tn(left[:, strip(k * width, width)], right[:, begin : begin + CHUNK]).astype(bf16)
                slot[k, 0] = value[:CHUNK]
                slot[k, 1] = value[CHUNK:]
                return none

        lax.fori_loop(0, row_count, step, 0)

    def launch(u):
        @pl.when(outer)
        def _():
            if u >= r_slots:
                pl.semaphore_wait(credit, 1)
            inward(u).start()

    def add(first, second, target):
        for k in range(row_count):
            target[k] = (first[k].astype(f32) + second[k].astype(f32)).astype(bf16)

    def middle(u):
        @pl.when(inner)
        def _():
            inward(u).wait_recv()
            add(made(u), r_land.at[u % r_slots], s.at[u % s_slots])
            across(u).start()
            if u + r_slots < pieces:
                pl.semaphore_signal(credit, inc=1, device_id=to_outer, device_id_type=MESH)

    def finish_inner(u):
        @pl.when(inner)
        def _():
            if u >= t_slots:
                outward(u - t_slots).wait_send()
                sent_home(u - t_slots, t.at[u % t_slots])
            across(u).wait_recv()
            add(s.at[u % s_slots], m_land.at[u % m_slots], t.at[u % t_slots])
            outward(u).start()
            send_home(u, t.at[u % t_slots])
            across(u).wait_send()

    def finish_outer(u):
        @pl.when(outer)
        def _():
            outward(u).wait_recv()
            send_home(u, b_land.at[u])

    def turn(u):
        middle(u)
        if u >= 1:
            finish_inner(u - 1)
        if u + 2 < pieces:
            if u % 2 == 0:
                produce((u + 2) // 2)
            launch(u + 2)
        if u >= 2:
            finish_outer(u - 2)

    set_a = (got_a, diag_a, hx_a, hy_a, ts_a, fx_a)
    set_b = (got_b, diag_b, hx_b, hy_b, ts_b, fx_b)
    gain2 = vec_all[3:4, :]

    loads[0].wait()
    loads[1].wait()
    produce(0)
    launch(0)
    launch(1)
    sums[...] = jnp.zeros_like(sums)
    turn(0)
    turn(1)
    turn(2)
    down_own.wait()
    for copy in down_recvs:
        copy.wait_recv()
    loads[9].start()
    loads[2].wait()
    loads[3].wait()
    loads[4].wait()
    turn(3)
    loads[9].wait()

    def upper_step(k, none):
        down, across_ = k // (units // CHUNK), k % (units // CHUNK)
        at, lanes = strip(down * rows, rows), strip(across_ * CHUNK, CHUNK)
        dup[at, lanes] = (dot_nt(cot[at, :], tot[lanes, :]) * dup[at, lanes].astype(f32)).astype(bf16)
        return none

    lax.fori_loop(0, (length // rows) * (units // CHUNK), upper_step, 0)
    turn(4)
    tiled_nt(dup, upw, part, dup.shape[1], 1024, 256)
    loads[6].start()
    first = reduce_steps(part, own_sum, *set_a, p_send, p_recv, 0)
    next(first)
    turn(5)
    next(first)
    turn(6)
    next(first)
    turn(7)
    for k in (5, 11, 12, 13, 14):
        loads[k].wait()
    next(first, None)
    block(tot, col, side, core, rows, width)[...] = own_sum[...].astype(bf16)
    second = spread_steps(tot, rows, width, p_send, p_recv, 8)
    next(second)
    turn(8)
    next(second)
    turn(9)
    next(second)
    turn(10)
    next(second, None)

    tile = 64

    def norm_step(k, none):
        at = strip(k * tile, tile)
        grad, standard, inverse = tot[at, :].astype(f32), std[at, :].astype(f32), stats[at, 0:1]
        scaled = grad * gain2
        mean_one = jnp.sum(scaled, axis=1, keepdims=True) / full
        mean_two = jnp.sum(scaled * standard, axis=1, keepdims=True) / full
        top = cot[at, :].astype(f32)
        low = (top + inverse * (scaled - mean_one - standard * mean_two)).astype(bf16)
        part[at, :] = low
        sums[0:1, :] += jnp.sum(grad * standard, axis=0, keepdims=True)
        sums[1:2, :] += jnp.sum(grad, axis=0, keepdims=True)
        sums[2:3, :] += jnp.sum(low.astype(f32), axis=0, keepdims=True)
        sums[3:4, :] += jnp.sum(top, axis=0, keepdims=True)

        @pl.when(k // (rows // tile) == col)
        def _():
            here = strip(row * width, width)
            own = tot[at, here].astype(f32) * vec_all[3:4, here]
            dres_own[strip(k % (rows // tile) * tile, tile), :] = cot[at, here].astype(f32) + inverse * (
                own - mean_one - std[at, here].astype(f32) * mean_two
            )

        return none

    lax.fori_loop(0, length // tile, norm_step, 0)
    loads[7].start()
    tiled_nt(part, outw, d_att, full, 512, 256)

    heads = mixed.shape[1] // (3 * HEAD)
    factor = 1.0 / math.sqrt(HEAD)
    blocks = length // SPAN
    spots = (SPAN, SPAN)
    earlier = lax.broadcasted_iota(jnp.int32, spots, 1) <= lax.broadcasted_iota(jnp.int32, spots, 0)

    def head_step(head, none):
        base = head * 3 * HEAD
        at_q, at_k, at_v = strip(base, HEAD), strip(base + HEAD, HEAD), strip(base + 2 * HEAD, HEAD)
        at_o = strip(head * HEAD, HEAD)
        dk_acc[...] = jnp.zeros_like(dk_acc)
        dv_acc[...] = jnp.zeros_like(dv_acc)
        for k in range(blocks):
            here = pl.ds(k * SPAN, SPAN)
            seen = (k + 1) * SPAN
            query, dout = mixed[here, at_q], d_att[here, at_o]
            keys, values = mixed[:seen, at_k], mixed[:seen, at_v]
            scores = dot_nt(query, keys) * factor
            last = jnp.where(earlier | (marks[k : k + 1, :1] > 0), scores[:, seen - SPAN :], masked_score)
            scores = last if k == 0 else jnp.concatenate([scores[:, : seen - SPAN], last], axis=1)
            probs = jnp.exp(scores - stats[here, 1 + head : 2 + head])
            d_probs = dot_nt(dout, values)
            dots = jnp.sum(probs * d_probs, axis=1, keepdims=True)
            d_scores = (probs * (d_probs - dots)).astype(bf16)
            d_mix[here, at_q] = (jnp.dot(d_scores, keys, preferred_element_type=f32) * factor).astype(bf16)
            dk_acc[:seen] += dot_tn(d_scores, query)
            dv_acc[:seen] += dot_tn(probs.astype(bf16), dout)
        d_mix[:, at_k] = (dk_acc[...] * factor).astype(bf16)
        d_mix[:, at_v] = dv_acc[...].astype(bf16)
        return none

    for head in range(heads):
        head_step(head, 0)
        turn(11 + head)
    loads[6].wait()
    tiled_nt(d_mix, upw, cot, d_mix.shape[1], 1024, 256)
    third = reduce_steps(cot, own_sum, *set_b, p_send, p_recv, 16)
    next(third)
    turn(11 + heads)
    next(third)
    loads[8].start()
    turn(12 + heads)
    next(third)
    loads[7].wait()
    turn(13 + heads)
    next(third, None)

    grad1, gain1 = own_sum, vec_all[0:1, strip(row * width, width)]
    scaled1 = grad1[...] * gain1
    first_sum = jnp.sum(scaled1, axis=1, keepdims=True)
    second_sum = jnp.sum(scaled1 * std1_own[...].astype(f32), axis=1, keepdims=True)
    lane = lax.broadcasted_iota(jnp.int32, (rows, 128), 1)
    pair = jnp.where(lane == 0, first_sum, jnp.where(lane == 1, second_sum, 0.0))
    stat_land[row] = pair.T[:8]
    stat_sends, stat_recvs = [], []
    for step in range(1, row_count):
        target, source = (row + step) % row_count, (row + row_count - step) % row_count
        stat_sends.append(put(stat_land.at[row], stat_land.at[row], p_send, p_recv, 35 + step - 1, {"row": target}))
        stat_recvs.append(
            put(stat_land.at[source], stat_land.at[source], p_send, p_recv, 35 + step - 1, {"row": source})
        )
        stat_sends[-1].start()
    small[...] = jnp.zeros_like(small)
    here = strip(row * width, width)
    small[0:1, :] = jnp.sum(grad1[...] * std1_own[...].astype(f32), axis=0, keepdims=True)
    small[1:2, :] = jnp.sum(grad1[...], axis=0, keepdims=True)
    small[2:6, :] = sums[0:4, here]
    uppers = jnp.sum(dup[...].astype(f32), axis=0, keepdims=True)
    for k in range(units // width):
        small[8 + k : 9 + k, :] = uppers[:, k * width : (k + 1) * width]
    mixes = jnp.sum(d_mix[...].astype(f32), axis=0, keepdims=True)
    spot = 8 + units // width
    picked = [mixes[:, (head * 3 + kind) * HEAD : (head * 3 + kind + 1) * HEAD] for head in range(heads) for kind in (0, 2)]
    small[spot : spot + 1, : 2 * heads * HEAD] = jnp.concatenate(picked, axis=1)
    to_x = partners()[0]
    x_copy = put(small.at[pl.ds(0, 8)], x_land, p_send, p_recv, 38, to_x)
    x_copy.start()
    turn(14 + heads)
    x_copy.wait_recv()
    x_copy.wait_send()
    small[0:2, :] += x_land[0:2, :]
    dp_sends, dp_recvs = [], []
    dp_land[plane] = small[...]
    for step in range(1, dp_count):
        target, source = (plane + step) % dp_count, (plane + dp_count - step) % dp_count
        dp_sends.append(put(dp_land.at[plane], dp_land.at[plane], p_send, p_recv, 39 + step - 1, {"dp": target}))
        dp_recvs.append(put(dp_land.at[source], dp_land.at[source], p_send, p_recv, 39 + step - 1, {"dp": source}))
        dp_sends[-1].start()
    for copy in stat_recvs:
        copy.wait_recv()
    both = stat_land[0]
    for k in range(1, row_count):
        both = both + stat_land[k]
    both = jnp.concatenate([both, jnp.zeros((120, rows), f32)], axis=0).T
    d_norm1 = inv1_own[...] * (
        scaled1 - both[:, 0:1] / full - std1_own[...].astype(f32) * (both[:, 1:2] / full)
    )
    tokens_block[...] = (dres_own[...] + d_norm1).astype(bf16)
    loads[10].start()
    loads[8].wait()
    tiled_nn(hid, n2, tot, 1024, 256)
    fourth = reduce_steps(tot, own_sum, *set_a, p_send, p_recv, 24)
    next(fourth)
    turn(15 + heads)
    next(fourth)
    turn(16 + heads)
    next(fourth)
    turn(17 + heads)
    next(fourth, None)
    loads[10].wait()
    out_block[...] = (dres_own[...] + (own_sum[...] + down_bias[...])).astype(bf16)
    for copy in dp_recvs:
        copy.wait_recv()
    together = dp_land[0]
    for k in range(1, dp_count):
        together = together + dp_land[k]
    small_out[row] = together
    row_sends, row_recvs = [], []
    for step in range(1, row_count):
        target, source = (row + step) % row_count, (row + row_count - step) % row_count
        row_sends.append(put(small_out.at[row], small_out.at[row], p_send, p_recv, 42 + step - 1, {"row": target}))
        row_recvs.append(
            put(small_out.at[source], small_out.at[source], p_send, p_recv, 42 + step - 1, {"row": source})
        )
        row_sends[-1].start()
    for u in range(18 + heads, pieces):
        turn(u)
    finish_inner(pieces - 1)
    finish_outer(pieces - 2)
    finish_outer(pieces - 1)
    for copy in row_recvs:
        copy.wait_recv()
    for copy in down_sends + stat_sends + dp_sends + row_sends:
        copy.wait_send()

    @pl.when(outer)
    def _():
        for u in range(pieces - 2 * g_slots, pieces):
            inward(u).wait_send()
        for u in range(pieces):
            sent_home(u, b_land.at[u])

    @pl.when(inner)
    def _():
        for u in range(pieces - t_slots, pieces):
            outward(u).wait_send()
            sent_home(u, t.at[u % t_slots])

    for u in range(pieces):
        for step in range(1, row_count):
            source = (row + row_count - step) % row_count
            put(t.at[0, source], place(u, source), a_send, a_recv, 3 * u + step - 1, {"row": source}).wait_recv()


def backward_plane(
    cid, hid, cot, slope, n2, upw, std, n1, qkvw, down_nat, resid_own, attended, outw, mixed, std1_own, stats, marks, vec_all, inv1_own, down_bias
):
    f32, bf16 = jnp.float32, jnp.bfloat16
    length, full = cot.shape
    rows, width = length // lax.axis_size("col"), full // lax.axis_size("row")
    row_count, dp_count = full // width, lax.axis_size("dp")
    counts = (slope.shape[1] // CHUNK, slope.shape[1] // CHUNK, attended.shape[1] // CHUNK, mixed.shape[1] // CHUNK)
    total = sum(counts)
    unit = (row_count, CHUNK, CHUNK)
    shape = jax.ShapeDtypeStruct
    away, near = pl.BlockSpec(memory_space=pl.ANY), pl.BlockSpec(memory_space=pltpu.VMEM)
    vmem, dma = pltpu.VMEM, pltpu.SemaphoreType.DMA
    sets = [
        vmem((4, rows, width), bf16),
        vmem((rows, width), bf16),
        vmem((rows // 2, width), bf16),
        vmem((rows // 2, width), bf16),
        vmem((2, rows, width), bf16),
        vmem((2, rows, width), bf16),
    ]
    return pl.pallas_call(
        functools.partial(backward_kernel, counts),
        out_shape=[
            shape((row_count * counts[0], CHUNK, width), bf16),
            shape((2, CHUNK, row_count * counts[1] * CHUNK), bf16),
            shape((row_count * counts[2], CHUNK, width), bf16),
            shape((2, CHUNK, row_count * counts[3] * CHUNK), bf16),
            shape((2 * total,) + unit, bf16),
            shape((hid.shape[1], full), bf16),
            shape((rows, width), bf16),
            shape((rows, width), bf16),
            shape((row_count, 16, width), f32),
        ],
        in_specs=[away] * 14 + [near] * 5,
        out_specs=[away] * 6 + [near] * 3,
        scratch_shapes=[
            vmem((length, full), bf16),
            vmem((length, full), bf16),
            vmem((length, full), bf16),
            vmem((length, full), bf16),
            vmem((length, full), bf16),
            vmem(upw.shape, bf16),
            vmem(hid.shape, bf16),
            vmem(slope.shape, bf16),
            vmem(attended.shape, bf16),
            vmem(outw.shape, bf16),
            vmem(mixed.shape, bf16),
            vmem(std1_own.shape, bf16),
            vmem(attended.shape, bf16),
            vmem(mixed.shape, bf16),
            vmem((length, HEAD), f32),
            vmem((length, HEAD), f32),
            vmem((2, row_count, width // CHUNK, CHUNK, CHUNK), bf16),
            vmem((2,) + unit, bf16),
            vmem((2,) + unit, bf16),
            vmem((3,) + unit, bf16),
            vmem((4,) + unit, bf16),
        ]
        + sets
        + sets
        + [
            vmem((rows, width), f32),
            vmem((rows, width), f32),
            vmem((8, full), f32),
            vmem((16, width), f32),
            vmem((8, width), f32),
            vmem((dp_count, 16, width), f32),
            vmem((row_count, 8, rows), f32),
            dma((15,)),
            pltpu.SemaphoreType.REGULAR,
            dma((2 * total + 1,)),
            dma((6 * total,)),
            dma((6 * total,)),
            dma((6 * total,)),
            dma((6 * total,)),
            dma((45,)),
            dma((45,)),
        ],
        compiler_params=pltpu.CompilerParams(
            collective_id=cid, has_side_effects=True, vmem_limit_bytes=64 * 1024 * 1024 - 65536
        ),
        cost_estimate=pl.CostEstimate(flops=40_000_000_000, bytes_accessed=100_000_000, transcendentals=4_000_000),
    )(hid, cot, slope, n2, upw, std, n1, qkvw, down_nat, resid_own, attended, outw, mixed, std1_own, stats, marks, vec_all, inv1_own, down_bias)


class Moves:
    def __init__(self, source, target, cut, parts, sends, recvs, base):
        row, plane = lax.axis_index("row"), lax.axis_index("dp")
        side, core = row // 2, row % 2
        parity = plane % 2
        other = {"dp": plane + 1 - 2 * parity}
        twin = side * 2 + 1 - core
        far = ((1 - side) * 2 + core, (1 - side) * 2 + 1 - core)
        self.sibling = put(source(twin), target(row), sends, recvs, base, {"row": twin})
        self.sibling_in = put(source(twin), target(twin), sends, recvs, base, {"row": twin})
        self.outs, self.ins, self.passes, self.gets = [], [], [], []
        at = base + 1
        for step in range(parts // 2):
            for k, device in enumerate(far):
                mine, theirs = 2 * step + parity, 2 * step + 1 - parity
                there, here = cut(target(row), mine), cut(target(device), mine)
                self.outs.append(put(cut(source(device), mine), there, sends, recvs, at, {"row": device}))
                self.ins.append(put(cut(source(device), mine), here, sends, recvs, at, {"row": device}))
                self.passes.append(put(here, here, sends, recvs, at + 1, other))
                lands = cut(target(device), theirs)
                self.gets.append(put(lands, lands, sends, recvs, at + 1, other))
                at += 2

    @staticmethod
    def count(parts):
        return 1 + 2 * parts

    def start(self):
        self.sibling.start()
        self.start_far()

    def start_far(self):
        for copy in self.outs:
            copy.start()

    def forward(self, begin=0, end=None):
        for came, passed in list(zip(self.ins, self.passes))[begin:end]:
            came.wait_recv()
            passed.start()

    def finish(self):
        self.sibling_in.wait_recv()
        for copy in self.gets:
            copy.wait_recv()

    def drain(self):
        self.sibling.wait_send()
        for copy in self.outs + self.passes:
            copy.wait_send()


FAR_PARTS = 4


def forward_kernel(
    tokens,
    cot_in,
    vecs,
    mixed_bias,
    up_bias,
    marks,
    qkv_in,
    out_nat,
    up_nat,
    cot_all,
    n1_out,
    n2_out,
    std_out,
    upw_out,
    qkvw_out,
    outw_out,
    mixed_out,
    attended_out,
    hid_out,
    slope_out,
    stats,
    vec_all,
    resid_own,
    std1_own,
    inv1_own,
    tok,
    n1,
    part,
    tot,
    qkvw,
    upw,
    outw,
    mixed,
    attended,
    hid,
    slope,
    own_sum,
    got,
    diag,
    hx,
    hy,
    ts,
    fx,
    qkv_raw,
    qkv_nat,
    local_sem,
    w_send,
    w_recv,
    p_send,
    p_recv,
):
    f32, bf16 = jnp.float32, jnp.bfloat16
    plane, row, col = lax.axis_index("dp"), lax.axis_index("row"), lax.axis_index("col")
    side, core = row // 2, row % 2
    rows, width = tokens.shape
    length, full = tok.shape
    row_count = full // width
    heads_width = attended.shape[1]
    units = hid.shape[1]

    barrier = pltpu.get_barrier_semaphore()
    twins = ({"row": (1 - side) * 2 + 1 - core}, {"dp": plane + 1 - 2 * (plane % 2)})
    for partner in partners() + twins:
        pl.semaphore_signal(barrier, inc=1, device_id=partner, device_id_type=MESH)
    pl.semaphore_wait(barrier, 5)

    def cut_rows(ref, part):
        count = ref.shape[0] // FAR_PARTS
        return ref.at[strip(part * count, count)]

    per = qkvw.shape[1]
    count = Moves.count(FAR_PARTS)
    qkv_moves = Moves(
        lambda r: qkv_nat.at[:, strip(r * per, per)],
        lambda r: qkvw.at[strip(r * width, width), :],
        cut_rows,
        FAR_PARTS,
        w_send,
        w_recv,
        0,
    )
    out_moves = Moves(
        lambda r: out_nat.at[strip(r * heads_width, heads_width), :],
        lambda r: outw.at[:, strip(r * width, width)],
        cut_rows,
        FAR_PARTS,
        w_send,
        w_recv,
        count,
    )
    up_moves = Moves(
        lambda r: up_nat.at[:, strip(r * units, units)],
        lambda r: upw.at[strip(r * width, width), :],
        cut_rows,
        FAR_PARTS,
        w_send,
        w_recv,
        2 * count,
    )
    locals_ = [
        (qkv_nat.at[:, strip(row * per, per)], qkvw.at[strip(row * width, width), :]),
        (out_nat.at[strip(row * heads_width, heads_width), :], outw.at[:, strip(row * width, width)]),
        (up_nat.at[:, strip(row * units, units)], upw.at[strip(row * width, width), :]),
        (cot_in, block(cot_all, col, side, core, rows, width)),
        (n1, n1_out),
        (part, n2_out),
        (n1, std_out),
        (upw, upw_out),
        (qkvw, qkvw_out),
        (outw, outw_out),
        (mixed, mixed_out),
        (attended, attended_out),
        (hid, hid_out),
        (slope, slope_out),
        (qkv_in, qkv_raw),
    ]
    local = [pltpu.make_async_copy(a, b, local_sem.at[k]) for k, (a, b) in enumerate(locals_)]
    local[14].start()
    for k in range(1, 4):
        local[k].start()

    block(tok, col, side, core, rows, width)[...] = tokens[...]
    gather = spread_steps(tok, rows, width, p_send, p_recv, 0)
    next(gather)
    vec_all[:, strip(row * width, width)] = vecs[...]
    vec_sends, vec_recvs = [], []
    for step in range(1, row_count):
        target, source = (row + step) % row_count, (row + row_count - step) % row_count
        here, there = vec_all.at[:, strip(row * width, width)], vec_all.at[:, strip(source * width, width)]
        vec_sends.append(put(here, here, p_send, p_recv, 8 + step - 1, {"row": target}))
        vec_recvs.append(put(there, there, p_send, p_recv, 8 + step - 1, {"row": source}))
        vec_sends[-1].start()
    out_moves.sibling.start()
    up_moves.sibling.start()
    local[14].wait()
    for kind in range(3):
        flat = qkv_raw[:, kind].reshape(width, qkv_raw.shape[2] * HEAD)
        for head in range(qkv_raw.shape[2]):
            qkv_nat[:, pl.ds((head * 3 + kind) * HEAD, HEAD)] = flat[:, head * HEAD : (head + 1) * HEAD]
    local[0].start()
    qkv_moves.sibling.start()
    next(gather)
    qkv_moves.start_far()
    next(gather)
    next(gather, None)
    for copy in vec_recvs:
        copy.wait_recv()

    tile = 64
    gain1, shift1 = vec_all[0:1, :], vec_all[1:2, :]

    def norm1_step(k, none):
        at = strip(k * tile, tile)
        values = tok[at, :].astype(f32)
        center = jnp.sum(values, axis=1, keepdims=True) / full
        inverse = lax.rsqrt(jnp.sum(values * values, axis=1, keepdims=True) / full - center * center + epsilon)
        n1[at, :] = ((values - center) * inverse * gain1 + shift1).astype(bf16)

        @pl.when(k // (rows // tile) == col)
        def _():
            here = strip(k % (rows // tile) * tile, tile)
            std1_own[here, :] = ((tok[at, strip(row * width, width)].astype(f32) - center) * inverse).astype(bf16)
            inv1_own[here, :] = inverse

        return none

    half_steps = length // tile // 2
    lax.fori_loop(0, half_steps, norm1_step, 0)
    qkv_moves.forward(0, 2)
    lax.fori_loop(half_steps, 2 * half_steps, norm1_step, 0)
    local[4].start()
    qkv_moves.forward(2, 4)
    out_moves.start_far()
    up_moves.start_far()
    qkv_moves.finish()
    local[0].wait()

    def mixed_step(k, none):
        down, across = k // (per // CHUNK), k % (per // CHUNK)
        at, lanes = strip(down * rows, rows), strip(across * CHUNK, CHUNK)
        value = jnp.dot(n1[at, :], qkvw[:, lanes], preferred_element_type=f32)
        mixed[at, lanes] = (value + mixed_bias[:, lanes]).astype(bf16)
        return none

    lax.fori_loop(0, (length // rows) * (per // CHUNK), mixed_step, 0)
    local[8].start()
    local[10].start()
    local[4].wait()

    heads = heads_width // HEAD
    factor = 1.0 / math.sqrt(HEAD)
    blocks = length // SPAN
    spots = (SPAN, SPAN)
    earlier = lax.broadcasted_iota(jnp.int32, spots, 1) <= lax.broadcasted_iota(jnp.int32, spots, 0)

    def head_step(head, none):
        base = head * 3 * HEAD
        at_q, at_k, at_v = strip(base, HEAD), strip(base + HEAD, HEAD), strip(base + 2 * HEAD, HEAD)
        for k in range(blocks):
            here = pl.ds(k * SPAN, SPAN)
            seen = (k + 1) * SPAN
            scores = dot_nt(mixed[here, at_q], mixed[:seen, at_k]) * factor
            last = jnp.where(earlier | (marks[k : k + 1, :1] > 0), scores[:, seen - SPAN :], masked_score)
            scores = last if k == 0 else jnp.concatenate([scores[:, : seen - SPAN], last], axis=1)
            highest = jnp.max(scores, axis=1, keepdims=True)
            weights = jnp.exp(scores - highest)
            weight_sum = jnp.sum(weights, axis=1, keepdims=True)
            stats[here, 1 + head : 2 + head] = highest + jnp.log(weight_sum)
            value = jnp.dot((weights / weight_sum).astype(bf16), mixed[:seen, at_v], preferred_element_type=f32)
            attended[here, strip(head * HEAD, HEAD)] = value.astype(bf16)
        return none

    for head in range(heads):
        head_step(head, 0)
    local[11].start()
    out_moves.forward()
    up_moves.forward(0, 4)
    out_moves.finish()
    local[1].wait()
    tiled_nn(attended, outw, part, rows, 512)
    local[9].start()
    add_up = reduce_steps(part, own_sum, got, diag, hx, hy, ts, fx, p_send, p_recv, 11)
    next(add_up)
    next(add_up)
    up_moves.forward(4, 8)
    next(add_up)
    next(add_up, None)
    block(tot, col, side, core, rows, width)[...] = own_sum[...].astype(bf16)
    again = spread_steps(tot, rows, width, p_send, p_recv, 19)
    for k in range(3):
        next(again)
    next(again, None)
    local[3].wait()
    cot_gather = spread_steps(cot_all, rows, width, p_send, p_recv, 27)
    next(cot_gather)

    gain2, shift2, out_bias = vec_all[3:4, :], vec_all[4:5, :], vec_all[2:3, :]

    def norm2_step(k, none):
        at = strip(k * tile, tile)
        values = tok[at, :].astype(f32) + (tot[at, :].astype(f32) + out_bias)
        center = jnp.sum(values, axis=1, keepdims=True) / full
        inverse = lax.rsqrt(jnp.sum(values * values, axis=1, keepdims=True) / full - center * center + epsilon)
        standard = (values - center) * inverse
        stats[at, 0:1] = inverse
        n1[at, :] = standard.astype(bf16)
        part[at, :] = (standard * gain2 + shift2).astype(bf16)

        @pl.when(k // (rows // tile) == col)
        def _():
            own = strip(row * width, width)
            here = strip(k % (rows // tile) * tile, tile)
            resid_own[here, :] = tok[at, own].astype(f32) + (tot[at, own].astype(f32) + vec_all[2:3, own])

        return none

    lax.fori_loop(0, 2 * half_steps, norm2_step, 0)
    local[5].start()
    local[6].start()
    next(cot_gather)
    up_moves.finish()
    local[2].wait()
    local[7].start()

    def up_step(k, none):
        down, across = k // (units // CHUNK), k % (units // CHUNK)
        at, lanes = strip(down * rows, rows), strip(across * CHUNK, CHUNK)
        u = jnp.dot(part[at, :], upw[:, lanes], preferred_element_type=f32) + up_bias[:, lanes]
        bent = jnp.tanh(0.7978845608028654 * (u + 0.044715 * u * u * u))
        hid[at, lanes] = (0.5 * u * (1.0 + bent)).astype(bf16)
        inside = 0.7978845608028654 * (1.0 + 3 * 0.044715 * u * u)
        slope[at, lanes] = (0.5 * (1.0 + bent) + 0.5 * u * (1.0 - bent * bent) * inside).astype(bf16)
        return none

    lax.fori_loop(0, (length // rows) * (units // CHUNK), up_step, 0)
    local[12].start()
    local[13].start()
    next(cot_gather)
    next(cot_gather, None)
    for k in range(5, 14):
        local[k].wait()
    for moves in (qkv_moves, out_moves, up_moves):
        moves.drain()
    for copy in vec_sends:
        copy.wait_send()


def forward_plane(cid, tokens, cot, vecs, mixed_bias, up_bias, marks, qkv_in, out_nat, up_nat):
    f32, bf16 = jnp.float32, jnp.bfloat16
    rows, width = tokens.shape
    row_count = lax.axis_size("row")
    length, full = rows * lax.axis_size("col"), width * row_count
    per, heads_width, units = qkv_in.shape[1] * qkv_in.shape[2] * HEAD // row_count, out_nat.shape[0] // row_count, up_nat.shape[1] // row_count
    shape = jax.ShapeDtypeStruct
    away, near = pl.BlockSpec(memory_space=pl.ANY), pl.BlockSpec(memory_space=pltpu.VMEM)
    vmem, dma = pltpu.VMEM, pltpu.SemaphoreType.DMA
    wide = shape((length, full), bf16)
    moved = 3 * Moves.count(FAR_PARTS)
    return pl.pallas_call(
        forward_kernel,
        out_shape=[
            wide,
            wide,
            wide,
            wide,
            shape((full, units), bf16),
            shape((full, per), bf16),
            shape((heads_width, full), bf16),
            shape((length, per), bf16),
            shape((length, heads_width), bf16),
            shape((length, units), bf16),
            shape((length, units), bf16),
            shape((length, 8), f32),
            shape((8, full), f32),
            shape((rows, width), f32),
            shape((rows, width), bf16),
            shape((rows, 1), f32),
        ],
        in_specs=[near] * 6 + [away] * 3,
        out_specs=[away] * 11 + [near] * 5,
        scratch_shapes=[
            vmem((length, full), bf16),
            vmem((length, full), bf16),
            vmem((length, full), bf16),
            vmem((length, full), bf16),
            vmem((full, per), bf16),
            vmem((full, units), bf16),
            vmem((heads_width, full), bf16),
            vmem((length, per), bf16),
            vmem((length, heads_width), bf16),
            vmem((length, units), bf16),
            vmem((length, units), bf16),
            vmem((rows, width), f32),
            vmem((4, rows, width), bf16),
            vmem((rows, width), bf16),
            vmem((rows // 2, width), bf16),
            vmem((rows // 2, width), bf16),
            vmem((2, rows, width), bf16),
            vmem((2, rows, width), bf16),
            vmem(qkv_in.shape, bf16),
            vmem((width, row_count * per), bf16),
            dma((15,)),
            dma((moved,)),
            dma((moved,)),
            dma((35,)),
            dma((35,)),
        ],
        compiler_params=pltpu.CompilerParams(
            collective_id=cid, has_side_effects=True, vmem_limit_bytes=60 * 1024 * 1024
        ),
        cost_estimate=pl.CostEstimate(flops=10_000_000_000, bytes_accessed=60_000_000, transcendentals=4_000_000),
    )(tokens, cot, vecs, mixed_bias, up_bias, marks, qkv_in, out_nat, up_nat)


def head_order_kernel(flat, result):
    for head in range(result.shape[2]):
        for kind in range(3):
            begin = (head * 3 + kind) * HEAD
            result[:, kind, head, :] = flat[:, begin : begin + HEAD].astype(jnp.float32)


def head_order(flat):
    rows, heads = flat.shape[0], flat.shape[1] // (3 * HEAD)
    tile = 128
    result = pl.pallas_call(
        head_order_kernel,
        grid=(rows // tile,),
        out_shape=jax.ShapeDtypeStruct((rows, 3, heads, HEAD), jnp.float32),
        in_specs=[pl.BlockSpec((tile, flat.shape[1]), lambda k: (k, 0))],
        out_specs=pl.BlockSpec((tile, 3, heads, HEAD), lambda k: (k, 0, 0, 0)),
    )(flat)
    return jnp.swapaxes(result, 1, 2)


def plane_plan(
    tokens,
    ln1_gain,
    ln1_shift,
    qkv_weight,
    qv_bias,
    out_weight,
    out_bias,
    ln2_gain,
    ln2_shift,
    up_weight,
    up_bias,
    down_weight,
    down_bias,
    span_starts,
    cotangent,
):
    f32 = jnp.float32
    rows, width = tokens.shape
    row_count = lax.axis_size("row")
    row = lax.axis_index("row")
    length = rows * lax.axis_size("col")
    heads = qkv_weight.shape[1] // row_count
    units = up_weight.shape[1] // row_count

    blank = jnp.zeros_like(ln1_gain)
    vecs = jnp.stack([ln1_gain, ln1_shift, out_bias, ln2_gain, ln2_shift, blank, blank, blank], axis=0)
    own_qv = lax.dynamic_slice_in_dim(qv_bias, row * heads, heads, 0)
    mixed_bias = jnp.stack([own_qv[:, 0], jnp.zeros_like(own_qv[:, 0]), own_qv[:, 1]], axis=1).reshape(1, -1)
    own_up_bias = lax.dynamic_slice_in_dim(up_bias, row * units, units, 0)[None]
    blocks = length // SPAN
    marked = jnp.any(span_starts[0][:, None] // SPAN == jnp.arange(blocks, dtype=jnp.int32)[None, :], axis=0)
    marks = jnp.broadcast_to(jnp.pad(marked.astype(f32), (0, -blocks % 8))[:, None], (blocks + -blocks % 8, 128))

    (
        cot_all, n1, n2, standard2, upw, qkvw, outw, mixed, attended, hidden, slope,
        stats, vec_all, residual_own, standard1_own, inverse1_own,
    ) = forward_plane(
        1,
        tokens,
        cotangent,
        vecs,
        mixed_bias,
        own_up_bias,
        marks,
        jnp.swapaxes(qkv_weight, 1, 2),
        out_weight.reshape(-1, width),
        up_weight,
    )
    down_grad, up_grad, out_grad, qkv_grad, _, _, output, tokens_grad, small = backward_plane(
        2, hidden, cot_all, slope, n2, upw, standard2, n1, qkvw, down_weight, residual_own, attended, outw, mixed, standard1_own,
        stats, marks, vec_all, inverse1_own, down_bias[None],
    )
    mine = lax.dynamic_index_in_dim(small, row, 0, keepdims=False)
    spot = 8 + units // width
    return (
        output,
        tokens_grad,
        mine[0],
        mine[1],
        head_order(qkv_grad.reshape(width, -1)),
        small[:, spot, : 2 * heads * HEAD].reshape(row_count * heads, 2, HEAD),
        out_grad.astype(f32).reshape(row_count * heads, HEAD, width),
        mine[4],
        mine[2],
        mine[3],
        up_grad.astype(f32).reshape(width, row_count * units),
        small[:, 8:spot].reshape(-1),
        down_grad.astype(f32).reshape(row_count * units, width),
        mine[5],
    )


def solution(mesh):
    sizes = dict(mesh.shape)
    flat = sizes == {"dp": 4, "row": 4, "col": 2}
    per_device = plane_plan if flat else general_plan
    placed = (
        P(("dp", "col"), "row"),
        P("row"),
        P("row"),
        P("row", "col", None, None),
        P("col", None, None),
        P("col", None, "row"),
        P("row"),
        P("row"),
        P("row"),
        P("row", "col"),
        P("col"),
        P("col", "row"),
        P("row"),
        P("dp", None),
        P(("dp", "col"), "row"),
    )
    return jax.shard_map(
        per_device,
        mesh=mesh,
        in_specs=placed,
        out_specs=(
            P(("dp", "col"), "row"),
            P(("dp", "col"), "row"),
            P("row"),
            P("row"),
            P("row", "col", None, None),
            P("col", None, None),
            P("col", None, "row"),
            P("row"),
            P("row"),
            P("row"),
            P("row", "col"),
            P("col"),
            P("col", "row"),
            P("row"),
        ),
        check_vma=False,
    )
```

```python
import functools
import math

import jax
import jax.numpy as jnp
from jax import lax
from jax.experimental import pallas as pl
from jax.experimental.pallas import tpu as pltpu
from jax.sharding import PartitionSpec as P

MESH = pl.DeviceIdType.MESH

D = 2048
HEAD = 128
SEQS = 1
SPAN = 256
BLOCK = 512


epsilon = 1e-05
masked_score = -1e30


def gelu_tanh(values):
    return (
        0.5
        * values
        * (1.0 + jnp.tanh(0.7978845608028654 * (values + 0.044715 * values * values * values)))
    )


def gather_columns(block_data):
    return lax.all_gather(block_data, "col", axis=0, tiled=True)


def gather_rows(block_data):
    return lax.all_gather(block_data, "row", axis=0, tiled=True)


def product(left_side, right_side, flipped):
    if flipped:
        return lax.dot_general(
            left_side, right_side, (((1,), (1,)), ((), ())), preferred_element_type=jnp.float32
        )
    return jnp.dot(left_side, right_side, preferred_element_type=jnp.float32)


def outer_sum(left_side, right_side):
    return lax.dot_general(
        left_side, right_side, (((0,), (0,)), ((), ())), preferred_element_type=jnp.float32
    )


def sum_rows(left_side, right_side, flipped):
    wide_left = lax.all_to_all(left_side, "row", split_axis=0, concat_axis=1, tiled=True)
    if flipped:
        wide_right = lax.all_gather(right_side, "row", axis=1, tiled=True)
    else:
        wide_right = lax.all_gather(right_side, "row", axis=0, tiled=True)
    return product(wide_left, wide_right, flipped)


def sum_columns(left_side, right_side, flipped):
    return lax.psum_scatter(
        product(left_side, right_side, flipped), "col", scatter_dimension=0, tiled=True
    )


def row_totals(first_sum, second_sum):
    return lax.psum((first_sum, second_sum), "row")


def norm_forward(values, gain_row, bias_row):
    totals, squares = row_totals(jnp.sum(values, axis=1), jnp.sum(values * values, axis=1))
    center = totals / D
    spread = squares / D - center * center
    inverse = lax.rsqrt(spread + epsilon)
    standard = (values - center[:, None]) * inverse[:, None]
    return (standard, inverse, (standard * gain_row + bias_row).astype(jnp.bfloat16))


def norm_backward(upstream, standard, inverse, gain_row):
    scaled = upstream * gain_row
    first_sum, second_sum = row_totals(jnp.sum(scaled, axis=1), jnp.sum(scaled * standard, axis=1))
    gradient = inverse[:, None] * (
        scaled - first_sum[:, None] / D - standard * (second_sum[:, None] / D)
    )
    return (gradient, jnp.sum(upstream * standard, axis=0), jnp.sum(upstream, axis=0))


def visible(query_pos, query_image, key_pos):
    earlier = key_pos[None, :] <= query_pos[:, None]
    same_span = (key_pos[None, :] // SPAN == query_pos[:, None] // SPAN) & (
        query_image[:, None] > 0
    )
    return earlier | same_span


def attention_forward(queries, key_value, token_image, row_offset, seq_length, block_rows):
    own_rows, head_count, width = queries.shape
    factor = 1.0 / math.sqrt(width)

    def block_forward(block_index):
        local = block_index * block_rows
        start_pos = row_offset + local
        query_block = lax.dynamic_slice_in_dim(queries, local, block_rows, 0)
        query_pos = start_pos + jnp.arange(block_rows, dtype=jnp.int32)
        query_image = lax.dynamic_slice_in_dim(token_image, start_pos, block_rows, 0)
        begin = start_pos // seq_length * seq_length // block_rows
        finish = start_pos // block_rows + 1

        def key_step(key_index, state_in):
            running, weight_sum, gathered = state_in
            key_begin = key_index * block_rows
            key_block = lax.dynamic_slice_in_dim(key_value, key_begin, block_rows, 0)
            key_pos = key_begin + jnp.arange(block_rows, dtype=jnp.int32)
            allowed = visible(query_pos, query_image, key_pos)
            scores = (
                jnp.einsum(
                    "qhd,khd->hqk",
                    query_block,
                    key_block[:, :, 0],
                    preferred_element_type=jnp.float32,
                )
                * factor
            )
            scores = jnp.where(allowed[None], scores, masked_score)
            highest = jnp.maximum(running, jnp.max(scores, axis=2))
            weights = jnp.exp(scores - highest[:, :, None])
            shrink = jnp.exp(running - highest)
            weight_sum = weight_sum * shrink + jnp.sum(weights, axis=2)
            gathered = gathered * shrink.T[:, :, None] + jnp.einsum(
                "hqk,khd->qhd",
                weights.astype(jnp.bfloat16),
                key_block[:, :, 1],
                preferred_element_type=jnp.float32,
            )
            return (highest, weight_sum, gathered)

        initial = (
            jnp.full((head_count, block_rows), masked_score, jnp.float32),
            jnp.zeros((head_count, block_rows), jnp.float32),
            jnp.zeros((block_rows, head_count, width), jnp.float32),
        )
        running, weight_sum, gathered = lax.fori_loop(begin, finish, key_step, initial)
        return (gathered / weight_sum.T[:, :, None], running + jnp.log(weight_sum))

    result, logsum = lax.map(block_forward, jnp.arange(own_rows // block_rows, dtype=jnp.int32))
    return (result.reshape(own_rows, head_count, width), logsum)


def attention_backward(
    queries,
    key_value,
    attended_full,
    logsum,
    d_attended,
    token_image,
    row_offset,
    seq_length,
    block_rows,
):
    own_rows, head_count, width = queries.shape
    factor = 1.0 / math.sqrt(width)
    row_dots = jnp.sum(d_attended.astype(jnp.float32) * attended_full, axis=2)

    def block_backward(block_index, state_out):
        d_queries, d_pairs = state_out
        local = block_index * block_rows
        start_pos = row_offset + local
        query_block = lax.dynamic_slice_in_dim(queries, local, block_rows, 0)
        dout_block = lax.dynamic_slice_in_dim(d_attended, local, block_rows, 0)
        dots_block = lax.dynamic_slice_in_dim(row_dots, local, block_rows, 0).T
        logsum_block = logsum[block_index]
        query_pos = start_pos + jnp.arange(block_rows, dtype=jnp.int32)
        query_image = lax.dynamic_slice_in_dim(token_image, start_pos, block_rows, 0)
        begin = start_pos // seq_length * seq_length // block_rows
        finish = start_pos // block_rows + 1

        def key_step(key_index, state_in):
            d_query, d_keys = state_in
            key_begin = key_index * block_rows
            key_block = lax.dynamic_slice_in_dim(key_value, key_begin, block_rows, 0)
            key_pos = key_begin + jnp.arange(block_rows, dtype=jnp.int32)
            allowed = visible(query_pos, query_image, key_pos)
            scores = (
                jnp.einsum(
                    "qhd,khd->hqk",
                    query_block,
                    key_block[:, :, 0],
                    preferred_element_type=jnp.float32,
                )
                * factor
            )
            scores = jnp.where(allowed[None], scores, masked_score)
            probabilities = jnp.exp(scores - logsum_block[:, :, None])
            d_probs = jnp.einsum(
                "qhd,khd->hqk", dout_block, key_block[:, :, 1], preferred_element_type=jnp.float32
            )
            d_scores = (probabilities * (d_probs - dots_block[:, :, None])).astype(jnp.bfloat16)
            d_query = d_query + jnp.einsum(
                "hqk,khd->qhd", d_scores, key_block[:, :, 0], preferred_element_type=jnp.float32
            )
            d_key = (
                jnp.einsum(
                    "hqk,qhd->khd", d_scores, query_block, preferred_element_type=jnp.float32
                )
                * factor
            )
            d_value = jnp.einsum(
                "hqk,qhd->khd",
                probabilities.astype(jnp.bfloat16),
                dout_block,
                preferred_element_type=jnp.float32,
            )
            previous = lax.dynamic_slice_in_dim(d_keys, key_begin, block_rows, 0)
            d_keys = lax.dynamic_update_slice_in_dim(
                d_keys, previous + jnp.stack([d_key, d_value], axis=2), key_begin, 0
            )
            return (d_query, d_keys)

        d_query, d_pairs = lax.fori_loop(
            begin,
            finish,
            key_step,
            (jnp.zeros((block_rows, head_count, width), jnp.float32), d_pairs),
        )
        d_queries = lax.dynamic_update_slice_in_dim(d_queries, d_query * factor, local, 0)
        return (d_queries, d_pairs)

    initial = (
        jnp.zeros((own_rows, head_count, width), jnp.float32),
        jnp.zeros((key_value.shape[0], head_count, 2, width), jnp.float32),
    )
    return lax.fori_loop(0, own_rows // block_rows, block_backward, initial)


def general_plan(
    tokens,
    ln1_gain,
    ln1_shift,
    qkv_weight,
    qv_bias,
    out_weight,
    out_bias,
    ln2_gain,
    ln2_shift,
    up_weight,
    up_bias,
    down_weight,
    down_bias,
    span_starts,
    cotangent,
):
    col_rows, row_width = tokens.shape
    group_rows = col_rows * lax.axis_size("col")
    own_rows = group_rows // lax.axis_size("row")
    head_count = qkv_weight.shape[1]
    seq_length = group_rows // SEQS
    block_rows = BLOCK - own_rows % BLOCK
    row_offset = lax.axis_index("row") * own_rows
    slot_count = seq_length // SPAN
    image_marks = jnp.sum(
        (
            span_starts[:, :, None] // SPAN
            == jnp.arange(slot_count, dtype=jnp.int32)[None, None, :]
        ).astype(jnp.int32),
        axis=1,
    )
    token_image = jnp.broadcast_to(
        image_marks.reshape(-1)[:, None], (group_rows // SPAN, SPAN)
    ).reshape(group_rows)
    qkv_flat = qkv_weight.reshape(row_width, head_count * 3 * HEAD)
    out_flat = out_weight.reshape(head_count * HEAD, row_width)
    inputs = tokens.astype(jnp.float32)
    standard1, inverse1, normed1 = norm_forward(inputs, ln1_gain, ln1_shift)
    normed1_all = gather_columns(normed1)
    mixed_sums = sum_rows(normed1_all, qkv_flat, False).reshape(own_rows, head_count, 3, HEAD)
    queries = (mixed_sums[:, :, 0] + qv_bias[:, 0]).astype(jnp.bfloat16)
    key_value_own = jnp.stack(
        [mixed_sums[:, :, 1], mixed_sums[:, :, 2] + qv_bias[:, 1]], axis=2
    ).astype(jnp.bfloat16)
    key_value = gather_rows(key_value_own)
    attended_full, logsum = attention_forward(
        queries, key_value, token_image, row_offset, seq_length, block_rows
    )
    attended = attended_full.astype(jnp.bfloat16).reshape(own_rows, head_count * HEAD)
    attended_all = gather_rows(attended)
    residual = inputs + (sum_columns(attended_all, out_flat, False) + out_bias)
    standard2, inverse2, normed2 = norm_forward(residual, ln2_gain, ln2_shift)
    normed2_all = gather_columns(normed2)
    up_sums = sum_rows(normed2_all, up_weight, False) + up_bias
    hidden = gelu_tanh(up_sums).astype(jnp.bfloat16)
    hidden_all = gather_rows(hidden)
    output = (residual + (sum_columns(hidden_all, down_weight, False) + down_bias)).astype(
        jnp.bfloat16
    )
    d_output = cotangent.astype(jnp.float32)
    d_output_all = gather_columns(cotangent)
    down_grad = outer_sum(hidden_all, d_output_all)
    down_bias_grad = jnp.sum(d_output_all, axis=0, dtype=jnp.float32)
    d_hidden = sum_rows(d_output_all, down_weight, True)
    d_upper = jax.vjp(gelu_tanh, up_sums)[1](d_hidden)[0].astype(jnp.bfloat16)
    d_upper_all = gather_rows(d_upper)
    normed2_use = gather_columns(normed2)
    up_grad = outer_sum(normed2_use, d_upper_all)
    up_bias_grad = jnp.sum(d_upper_all, axis=0, dtype=jnp.float32)
    d_normed2 = sum_columns(d_upper_all, up_weight, True)
    d_norm2, gain2_grad, shift2_grad = norm_backward(d_normed2, standard2, inverse2, ln2_gain)
    d_residual = d_output + d_norm2
    d_branch = d_residual.astype(jnp.bfloat16)
    d_branch_all = gather_columns(d_branch)
    out_grad = outer_sum(attended_all, d_branch_all)
    out_bias_grad = jnp.sum(d_branch_all, axis=0, dtype=jnp.float32)
    d_attended = (
        sum_rows(d_branch_all, out_flat, True)
        .astype(jnp.bfloat16)
        .reshape(own_rows, head_count, HEAD)
    )
    d_queries, d_pairs = attention_backward(
        queries,
        key_value,
        attended_full,
        logsum,
        d_attended,
        token_image,
        row_offset,
        seq_length,
        block_rows,
    )
    d_pairs_own = lax.psum_scatter(d_pairs, "row", scatter_dimension=0, tiled=True)
    d_mixed = jnp.concatenate([d_queries[:, :, None], d_pairs_own], axis=2).astype(jnp.bfloat16)
    d_mixed_all = gather_rows(d_mixed)
    normed1_use = gather_columns(normed1)
    d_mixed_flat = d_mixed_all.reshape(group_rows, head_count * 3 * HEAD)
    qkv_grad = outer_sum(normed1_use, d_mixed_flat)
    mixed_totals = jnp.sum(d_mixed_all, axis=0, dtype=jnp.float32)
    qv_bias_grad = jnp.stack([mixed_totals[:, 0], mixed_totals[:, 2]], axis=1)
    d_normed1 = sum_columns(d_mixed_flat, qkv_flat, True)
    d_norm1, gain1_grad, shift1_grad = norm_backward(d_normed1, standard1, inverse1, ln1_gain)
    tokens_grad = (d_residual + d_norm1).astype(jnp.bfloat16)
    norm_sums = lax.psum((gain1_grad, shift1_grad, gain2_grad, shift2_grad), ("dp", "col"))
    weight_sums = lax.psum(
        (
            qkv_grad,
            qv_bias_grad,
            out_grad,
            out_bias_grad,
            up_grad,
            up_bias_grad,
            down_grad,
            down_bias_grad,
        ),
        "dp",
    )
    return (
        output,
        tokens_grad,
        norm_sums[0],
        norm_sums[1],
        weight_sums[0].reshape(row_width, head_count, 3, HEAD),
        weight_sums[1],
        weight_sums[2].reshape(head_count, HEAD, row_width),
        weight_sums[3],
        norm_sums[2],
        norm_sums[3],
        weight_sums[4],
        weight_sums[5],
        weight_sums[6],
        weight_sums[7],
    )


def places():
    row, col = lax.axis_index("row"), lax.axis_index("col")
    return col, row // 2, row % 2


def partners():
    col, side, core = places()
    return ({"col": 1 - col}, {"row": (1 - side) * 2 + core}, {"row": side * 2 + 1 - core})


def block(ref, col, side, core, rows, width, part=None):
    begin, count = col * rows, rows
    if part is not None:
        begin, count = begin + part * (rows // 2), rows // 2
    return ref.at[strip(begin, count), strip((side * 2 + core) * width, width)]


def put(ref_from, ref_to, sends, recvs, at, partner):
    return pltpu.make_async_remote_copy(
        src_ref=ref_from,
        dst_ref=ref_to,
        send_sem=sends.at[at],
        recv_sem=recvs.at[at],
        device_id=partner,
        device_id_type=MESH,
    )


def strip(begin, count):
    return pl.ds(pl.multiple_of(begin, count), count)


def dot_nt(left, right):
    return lax.dot_general(left, right, (((1,), (1,)), ((), ())), preferred_element_type=jnp.float32)


def dot_tn(left, right):
    return lax.dot_general(left, right, (((0,), (0,)), ((), ())), preferred_element_type=jnp.float32)


def tiled_nt(left, right, target, inner, tile_rows, tile_cols):
    rows, cols = target.shape
    across = cols // tile_cols

    def step(at, none):
        down, side = at // across, at % across
        value = dot_nt(left[strip(down * tile_rows, tile_rows), :inner], right[strip(side * tile_cols, tile_cols), :inner])
        target[strip(down * tile_rows, tile_rows), strip(side * tile_cols, tile_cols)] = value.astype(target.dtype)
        return none

    lax.fori_loop(0, (rows // tile_rows) * across, step, 0)


def tiled_nn(left, right, target, tile_rows, tile_cols):
    rows, cols = target.shape
    across = cols // tile_cols

    def step(at, none):
        down, side = at // across, at % across
        value = jnp.dot(
            left[strip(down * tile_rows, tile_rows), :],
            right[:, strip(side * tile_cols, tile_cols)],
            preferred_element_type=jnp.float32,
        )
        target[strip(down * tile_rows, tile_rows), strip(side * tile_cols, tile_cols)] = value.astype(target.dtype)
        return none

    lax.fori_loop(0, (rows // tile_rows) * across, step, 0)


def reduce_steps(part, result, got, diag, half_x, half_y, to_send, from_xy, sends, recvs, base):
    f32 = jnp.float32
    rows, width = result.shape
    half = rows // 2
    low, high = pl.ds(0, half), pl.ds(half, half)
    col, side, core = places()
    to_x, to_y, to_core = partners()
    spots = ((1 - col, 1 - side), (col, 1 - side), (1 - col, side), (col, side))
    copies = [
        put(block(part, a, b, 1 - core, rows, width), got.at[k], sends, recvs, base + k, to_core)
        for k, (a, b) in enumerate(spots)
    ]
    for copy in copies:
        copy.start()
    mine = [block(part, a, b, core, rows, width) for a, b in spots]
    dx = put(diag.at[low], half_x, sends, recvs, base + 4, to_x)
    dy = put(diag.at[high], half_y, sends, recvs, base + 5, to_y)
    cy = put(to_send.at[0], from_xy.at[0], sends, recvs, base + 6, to_y)
    cx = put(to_send.at[1], from_xy.at[1], sends, recvs, base + 7, to_x)
    yield
    copies[0].wait_recv()
    diag[...] = (mine[0][...].astype(f32) + got[0].astype(f32)).astype(diag.dtype)
    dx.start()
    dy.start()
    copies[1].wait_recv()
    copies[2].wait_recv()
    to_send[0, high] = (mine[1][high].astype(f32) + got[1, high].astype(f32)).astype(diag.dtype)
    to_send[1, low] = (mine[2][low].astype(f32) + got[2, low].astype(f32)).astype(diag.dtype)
    copies[3].wait_recv()
    result[...] = mine[3][...].astype(f32) + got[3].astype(f32)
    yield
    dx.wait_recv()
    to_send[0, low] = (mine[1][low].astype(f32) + got[1, low].astype(f32) + half_x[...].astype(f32)).astype(diag.dtype)
    cy.start()
    dy.wait_recv()
    to_send[1, high] = (mine[2][high].astype(f32) + got[2, high].astype(f32) + half_y[...].astype(f32)).astype(
        diag.dtype
    )
    cx.start()
    yield
    cy.wait_recv()
    cx.wait_recv()
    result[...] = result[...] + from_xy[0].astype(f32) + from_xy[1].astype(f32)
    for copy in copies + [dx, dy, cy, cx]:
        copy.wait_send()


def spread_steps(out, rows, width, sends, recvs, base, mostly_x=False):
    col, side, core = places()
    to_x, to_y, to_core = partners()

    def copy_of(at, which, partner, part=None):
        ref = block(out, *which, rows, width, part)
        return put(ref, ref, sends, recvs, base + at, partner)

    own, ox, oy, od = (col, side, core), (1 - col, side, core), (col, 1 - side, core), (1 - col, 1 - side, core)
    plan = [
        copy_of(0, own, to_x),
        copy_of(1, own, to_y),
        copy_of(2, own, to_core),
        None if mostly_x else copy_of(3, ox, to_y, 0),
        copy_of(4, oy, to_x, None if mostly_x else 1),
        copy_of(5, ox, to_core),
        copy_of(6, oy, to_core),
        copy_of(7, od, to_core),
    ]
    for at in (0, 1, 2):
        plan[at].start()
    yield
    used = [at for at in range(8) if at != 3 or not mostly_x]
    plan[0].wait_recv()
    if not mostly_x:
        plan[3].start()
    plan[1].wait_recv()
    plan[4].start()
    plan[5].start()
    plan[6].start()
    yield
    if not mostly_x:
        plan[3].wait_recv()
    plan[4].wait_recv()
    plan[7].start()
    yield
    for at in (2, 5, 6, 7):
        plan[at].wait_recv()
    for at in used:
        plan[at].wait_send()


CHUNK = 256


def backward_kernel(
    counts,
    hid_h,
    cot_h,
    slope_h,
    n2_h,
    upw_h,
    std_h,
    n1_h,
    qkvw_h,
    down_nat,
    resid_h,
    attended_h,
    outw_h,
    mixed_h,
    std1_h,
    stats,
    marks,
    vec_all,
    inv1_own,
    down_bias,
    down_out,
    up_out,
    out_out,
    qkv_out,
    b_land,
    downw_land,
    out_block,
    tokens_block,
    small_out,
    cot,
    n2,
    std,
    part,
    tot,
    upw,
    hid,
    dup,
    attended,
    outw,
    mixed,
    std1_own,
    d_att,
    d_mix,
    dk_acc,
    dv_acc,
    g,
    s,
    t,
    r_land,
    m_land,
    got_a,
    diag_a,
    hx_a,
    hy_a,
    ts_a,
    fx_a,
    got_b,
    diag_b,
    hx_b,
    hy_b,
    ts_b,
    fx_b,
    dres_own,
    own_sum,
    sums,
    small,
    x_land,
    dp_land,
    stat_land,
    load_sem,
    credit,
    own_sem,
    z_send,
    z_recv,
    a_send,
    a_recv,
    p_send,
    p_recv,
):
    f32, bf16 = jnp.float32, jnp.bfloat16
    n_down, n_up, n_out, n_qkv = counts
    total = sum(counts)
    plane, row, col = lax.axis_index("dp"), lax.axis_index("row"), lax.axis_index("col")
    length, full = cot.shape
    rows, width = dres_own.shape
    row_count = full // width
    inner = (plane == 1) | (plane == 2)
    outer = jnp.logical_not(inner)
    to_inner = {"dp": plane // 3 + 1}
    to_middle = {"dp": 3 - plane}
    to_outer = {"dp": (plane - 1) * 3}
    side, core = row // 2, row % 2

    loads = [
        (hid_h, hid),
        (cot_h, cot),
        (slope_h, dup),
        (upw_h, upw),
        (n2_h, n2),
        (std_h, std),
        (qkvw_h, upw.at[:, : qkvw_h.shape[1]]),
        (n1_h, std),
        (downw_land, n2),
        (downw_land, tot),
        (resid_h, dres_own),
        (attended_h, attended),
        (outw_h, outw),
        (mixed_h, mixed),
        (std1_h, std1_own),
    ]
    loads = [pltpu.make_async_copy(a, b, load_sem.at[k]) for k, (a, b) in enumerate(loads)]
    for k in (0, 1, 2, 3, 4, 5, 11, 12, 13, 14):
        loads[k].start()

    dp_count = dp_land.shape[0]
    barrier = pltpu.get_barrier_semaphore()
    others = [{"row": (1 - side) * 2 + 1 - core}] + [{"dp": (plane + k) % dp_count} for k in range(1, dp_count)]
    for partner in partners() + tuple(others):
        pl.semaphore_signal(barrier, inc=1, device_id=partner, device_id_type=MESH)
    pl.semaphore_wait(barrier, 3 + len(others))

    units = hid.shape[1]
    down_sends, down_recvs = [], []
    for step in range(1, row_count):
        target, source = (row + step) % row_count, (row + row_count - step) % row_count
        here, there = downw_land.at[:, strip(row * width, width)], downw_land.at[:, strip(source * width, width)]
        piece = down_nat.at[strip(target * units, units), :]
        down_sends.append(put(piece, here, p_send, p_recv, 32 + step - 1, {"row": target}))
        down_recvs.append(put(piece, there, p_send, p_recv, 32 + step - 1, {"row": source}))
        down_sends[-1].start()
    down_own = pltpu.make_async_copy(
        down_nat.at[strip(row * units, units), :], downw_land.at[:, strip(row * width, width)], own_sem.at[2 * total]
    )
    down_own.start()

    def place(u, source):
        i, half = u // 2, u % 2
        if i < n_down:
            return down_out.at[source * n_down + i // 2 * 2 + half, :, pl.ds(i % 2 * CHUNK, CHUNK)]
        i -= n_down
        if i < n_up:
            return up_out.at[half, :, strip(source * n_up * CHUNK + i * CHUNK, CHUNK)]
        i -= n_up
        if i < n_out:
            return out_out.at[source * n_out + i, :, pl.ds(half * CHUNK, CHUNK)]
        i -= n_out
        return qkv_out.at[half, :, strip(source * n_qkv * CHUNK + i * CHUNK, CHUNK)]

    g_slots, s_slots, t_slots, r_slots, m_slots = g.shape[0], s.shape[0], t.shape[0], r_land.shape[0], m_land.shape[0]
    pieces = 2 * total

    def made(u):
        return g.at[u // 2 % g_slots, :, u % 2]

    def inward(u):
        return put(made(u), r_land.at[u % r_slots], z_send, z_recv, u, to_inner)

    def across(u):
        return put(s.at[u % s_slots], m_land.at[u % m_slots], z_send, z_recv, pieces + u, to_middle)

    def outward(u):
        return put(t.at[u % t_slots], b_land.at[u], z_send, z_recv, 2 * pieces + u, to_outer)

    def home(u, step, source):
        target = (row + step) % row_count
        return put(source.at[target], place(u, row), a_send, a_recv, 3 * u + step - 1, {"row": target})

    def home_own(u, source):
        return pltpu.make_async_copy(source.at[row], place(u, row), own_sem.at[u])

    def send_home(u, source):
        for step in range(1, row_count):
            home(u, step, source).start()
        home_own(u, source).start()

    def sent_home(u, source):
        for step in range(1, row_count):
            home(u, step, source).wait_send()
        home_own(u, source).wait()

    def produce(i):
        if i >= g_slots:

            @pl.when(outer)
            def _():
                inward(2 * (i - g_slots)).wait_send()
                inward(2 * (i - g_slots) + 1).wait_send()

        slot = g.at[i % g_slots]
        if i < n_down:
            begin, lane = i // 2 * 2 * CHUNK, i % 2 * CHUNK

            def step(k, none):
                value = dot_tn(hid[:, begin : begin + 2 * CHUNK], cot[:, strip(k * width + lane, CHUNK)]).astype(bf16)
                slot[k, 0] = value[:CHUNK]
                slot[k, 1] = value[CHUNK:]
                return none
        elif n_down + n_up <= i < n_down + n_up + n_out:
            left, begin, right = attended, (i - n_down - n_up) * CHUNK, part

            def step(k, none):
                value = dot_tn(left[:, begin : begin + CHUNK], right[:, strip(k * width, width)]).astype(bf16)
                slot[k, 0] = value[:, :CHUNK]
                slot[k, 1] = value[:, CHUNK:]
                return none
        else:
            if i < n_down + n_up:
                left, right, begin = n2, dup, (i - n_down) * CHUNK
            else:
                left, right, begin = std, d_mix, (i - n_down - n_up - n_out) * CHUNK

            def step(k, none):
                value = dot_tn(left[:, strip(k * width, width)], right[:, begin : begin + CHUNK]).astype(bf16)
                slot[k, 0] = value[:CHUNK]
                slot[k, 1] = value[CHUNK:]
                return none

        lax.fori_loop(0, row_count, step, 0)

    def launch(u):
        @pl.when(outer)
        def _():
            if u >= r_slots:
                pl.semaphore_wait(credit, 1)
            inward(u).start()

    def add(first, second, target):
        for k in range(row_count):
            target[k] = (first[k].astype(f32) + second[k].astype(f32)).astype(bf16)

    def middle(u):
        @pl.when(inner)
        def _():
            inward(u).wait_recv()
            add(made(u), r_land.at[u % r_slots], s.at[u % s_slots])
            across(u).start()
            if u + r_slots < pieces:
                pl.semaphore_signal(credit, inc=1, device_id=to_outer, device_id_type=MESH)

    def finish_inner(u):
        @pl.when(inner)
        def _():
            if u >= t_slots:
                outward(u - t_slots).wait_send()
                sent_home(u - t_slots, t.at[u % t_slots])
            across(u).wait_recv()
            add(s.at[u % s_slots], m_land.at[u % m_slots], t.at[u % t_slots])
            outward(u).start()
            send_home(u, t.at[u % t_slots])
            across(u).wait_send()

    def finish_outer(u):
        @pl.when(outer)
        def _():
            outward(u).wait_recv()
            send_home(u, b_land.at[u])

    def turn(u):
        middle(u)
        if u >= 1:
            finish_inner(u - 1)
        if u + 2 < pieces:
            if u % 2 == 0:
                produce((u + 2) // 2)
            launch(u + 2)
        if u >= 2:
            finish_outer(u - 2)

    set_a = (got_a, diag_a, hx_a, hy_a, ts_a, fx_a)
    set_b = (got_b, diag_b, hx_b, hy_b, ts_b, fx_b)
    gain2 = vec_all[3:4, :]

    loads[0].wait()
    loads[1].wait()
    produce(0)
    launch(0)
    launch(1)
    sums[...] = jnp.zeros_like(sums)
    turn(0)
    turn(1)
    turn(2)
    down_own.wait()
    for copy in down_recvs:
        copy.wait_recv()
    loads[9].start()
    loads[2].wait()
    loads[3].wait()
    loads[4].wait()
    turn(3)
    loads[9].wait()

    def upper_step(k, none):
        down, across_ = k // (units // CHUNK), k % (units // CHUNK)
        at, lanes = strip(down * rows, rows), strip(across_ * CHUNK, CHUNK)
        dup[at, lanes] = (dot_nt(cot[at, :], tot[lanes, :]) * dup[at, lanes].astype(f32)).astype(bf16)
        return none

    lax.fori_loop(0, (length // rows) * (units // CHUNK), upper_step, 0)
    turn(4)
    tiled_nt(dup, upw, part, dup.shape[1], 1024, 256)
    loads[6].start()
    first = reduce_steps(part, own_sum, *set_a, p_send, p_recv, 0)
    next(first)
    turn(5)
    next(first)
    turn(6)
    next(first)
    turn(7)
    for k in (5, 11, 12, 13, 14):
        loads[k].wait()
    next(first, None)
    block(tot, col, side, core, rows, width)[...] = own_sum[...].astype(bf16)
    second = spread_steps(tot, rows, width, p_send, p_recv, 8)
    next(second)
    turn(8)
    next(second)
    turn(9)
    next(second)
    turn(10)
    next(second, None)

    tile = 64

    def norm_step(k, none):
        at = strip(k * tile, tile)
        grad, standard, inverse = tot[at, :].astype(f32), std[at, :].astype(f32), stats[at, 0:1]
        scaled = grad * gain2
        mean_one = jnp.sum(scaled, axis=1, keepdims=True) / full
        mean_two = jnp.sum(scaled * standard, axis=1, keepdims=True) / full
        top = cot[at, :].astype(f32)
        low = (top + inverse * (scaled - mean_one - standard * mean_two)).astype(bf16)
        part[at, :] = low
        sums[0:1, :] += jnp.sum(grad * standard, axis=0, keepdims=True)
        sums[1:2, :] += jnp.sum(grad, axis=0, keepdims=True)
        sums[2:3, :] += jnp.sum(low.astype(f32), axis=0, keepdims=True)
        sums[3:4, :] += jnp.sum(top, axis=0, keepdims=True)

        @pl.when(k // (rows // tile) == col)
        def _():
            here = strip(row * width, width)
            own = tot[at, here].astype(f32) * vec_all[3:4, here]
            dres_own[strip(k % (rows // tile) * tile, tile), :] = cot[at, here].astype(f32) + inverse * (
                own - mean_one - std[at, here].astype(f32) * mean_two
            )

        return none

    lax.fori_loop(0, length // tile, norm_step, 0)
    loads[7].start()
    tiled_nt(part, outw, d_att, full, 512, 256)

    heads = mixed.shape[1] // (3 * HEAD)
    factor = 1.0 / math.sqrt(HEAD)
    blocks = length // SPAN
    spots = (SPAN, SPAN)
    earlier = lax.broadcasted_iota(jnp.int32, spots, 1) <= lax.broadcasted_iota(jnp.int32, spots, 0)

    def head_step(head, none):
        base = head * 3 * HEAD
        at_q, at_k, at_v = strip(base, HEAD), strip(base + HEAD, HEAD), strip(base + 2 * HEAD, HEAD)
        at_o = strip(head * HEAD, HEAD)
        dk_acc[...] = jnp.zeros_like(dk_acc)
        dv_acc[...] = jnp.zeros_like(dv_acc)
        for k in range(blocks):
            here = pl.ds(k * SPAN, SPAN)
            seen = (k + 1) * SPAN
            query, dout = mixed[here, at_q], d_att[here, at_o]
            keys, values = mixed[:seen, at_k], mixed[:seen, at_v]
            scores = dot_nt(query, keys) * factor
            last = jnp.where(earlier | (marks[k : k + 1, :1] > 0), scores[:, seen - SPAN :], masked_score)
            scores = last if k == 0 else jnp.concatenate([scores[:, : seen - SPAN], last], axis=1)
            probs = jnp.exp(scores - stats[here, 1 + head : 2 + head])
            d_probs = dot_nt(dout, values)
            dots = jnp.sum(probs * d_probs, axis=1, keepdims=True)
            d_scores = (probs * (d_probs - dots)).astype(bf16)
            d_mix[here, at_q] = (jnp.dot(d_scores, keys, preferred_element_type=f32) * factor).astype(bf16)
            dk_acc[:seen] += dot_tn(d_scores, query)
            dv_acc[:seen] += dot_tn(probs.astype(bf16), dout)
        d_mix[:, at_k] = (dk_acc[...] * factor).astype(bf16)
        d_mix[:, at_v] = dv_acc[...].astype(bf16)
        return none

    for head in range(heads):
        head_step(head, 0)
        turn(11 + head)
    loads[6].wait()
    tiled_nt(d_mix, upw, cot, d_mix.shape[1], 1024, 256)
    third = reduce_steps(cot, own_sum, *set_b, p_send, p_recv, 16)
    next(third)
    turn(11 + heads)
    next(third)
    loads[8].start()
    turn(12 + heads)
    next(third)
    loads[7].wait()
    turn(13 + heads)
    next(third, None)

    grad1, gain1 = own_sum, vec_all[0:1, strip(row * width, width)]
    scaled1 = grad1[...] * gain1
    first_sum = jnp.sum(scaled1, axis=1, keepdims=True)
    second_sum = jnp.sum(scaled1 * std1_own[...].astype(f32), axis=1, keepdims=True)
    lane = lax.broadcasted_iota(jnp.int32, (rows, 128), 1)
    pair = jnp.where(lane == 0, first_sum, jnp.where(lane == 1, second_sum, 0.0))
    stat_land[row] = pair.T[:8]
    stat_sends, stat_recvs = [], []
    for step in range(1, row_count):
        target, source = (row + step) % row_count, (row + row_count - step) % row_count
        stat_sends.append(put(stat_land.at[row], stat_land.at[row], p_send, p_recv, 35 + step - 1, {"row": target}))
        stat_recvs.append(
            put(stat_land.at[source], stat_land.at[source], p_send, p_recv, 35 + step - 1, {"row": source})
        )
        stat_sends[-1].start()
    small[...] = jnp.zeros_like(small)
    here = strip(row * width, width)
    small[0:1, :] = jnp.sum(grad1[...] * std1_own[...].astype(f32), axis=0, keepdims=True)
    small[1:2, :] = jnp.sum(grad1[...], axis=0, keepdims=True)
    small[2:6, :] = sums[0:4, here]
    uppers = jnp.sum(dup[...].astype(f32), axis=0, keepdims=True)
    for k in range(units // width):
        small[8 + k : 9 + k, :] = uppers[:, k * width : (k + 1) * width]
    mixes = jnp.sum(d_mix[...].astype(f32), axis=0, keepdims=True)
    spot = 8 + units // width
    picked = [mixes[:, (head * 3 + kind) * HEAD : (head * 3 + kind + 1) * HEAD] for head in range(heads) for kind in (0, 2)]
    small[spot : spot + 1, : 2 * heads * HEAD] = jnp.concatenate(picked, axis=1)
    to_x = partners()[0]
    x_copy = put(small.at[pl.ds(0, 8)], x_land, p_send, p_recv, 38, to_x)
    x_copy.start()
    turn(14 + heads)
    x_copy.wait_recv()
    x_copy.wait_send()
    small[0:2, :] += x_land[0:2, :]
    dp_sends, dp_recvs = [], []
    dp_land[plane] = small[...]
    for step in range(1, dp_count):
        target, source = (plane + step) % dp_count, (plane + dp_count - step) % dp_count
        dp_sends.append(put(dp_land.at[plane], dp_land.at[plane], p_send, p_recv, 39 + step - 1, {"dp": target}))
        dp_recvs.append(put(dp_land.at[source], dp_land.at[source], p_send, p_recv, 39 + step - 1, {"dp": source}))
        dp_sends[-1].start()
    for copy in stat_recvs:
        copy.wait_recv()
    both = stat_land[0]
    for k in range(1, row_count):
        both = both + stat_land[k]
    both = jnp.concatenate([both, jnp.zeros((120, rows), f32)], axis=0).T
    d_norm1 = inv1_own[...] * (
        scaled1 - both[:, 0:1] / full - std1_own[...].astype(f32) * (both[:, 1:2] / full)
    )
    tokens_block[...] = (dres_own[...] + d_norm1).astype(bf16)
    loads[10].start()
    loads[8].wait()
    tiled_nn(hid, n2, tot, 1024, 256)
    fourth = reduce_steps(tot, own_sum, *set_a, p_send, p_recv, 24)
    next(fourth)
    turn(15 + heads)
    next(fourth)
    turn(16 + heads)
    next(fourth)
    turn(17 + heads)
    next(fourth, None)
    loads[10].wait()
    out_block[...] = (dres_own[...] + (own_sum[...] + down_bias[...])).astype(bf16)
    for copy in dp_recvs:
        copy.wait_recv()
    together = dp_land[0]
    for k in range(1, dp_count):
        together = together + dp_land[k]
    small_out[row] = together
    row_sends, row_recvs = [], []
    for step in range(1, row_count):
        target, source = (row + step) % row_count, (row + row_count - step) % row_count
        row_sends.append(put(small_out.at[row], small_out.at[row], p_send, p_recv, 42 + step - 1, {"row": target}))
        row_recvs.append(
            put(small_out.at[source], small_out.at[source], p_send, p_recv, 42 + step - 1, {"row": source})
        )
        row_sends[-1].start()
    for u in range(18 + heads, pieces):
        turn(u)
    finish_inner(pieces - 1)
    finish_outer(pieces - 2)
    finish_outer(pieces - 1)
    for copy in row_recvs:
        copy.wait_recv()
    for copy in down_sends + stat_sends + dp_sends + row_sends:
        copy.wait_send()

    @pl.when(outer)
    def _():
        for u in range(pieces - 2 * g_slots, pieces):
            inward(u).wait_send()
        for u in range(pieces):
            sent_home(u, b_land.at[u])

    @pl.when(inner)
    def _():
        for u in range(pieces - t_slots, pieces):
            outward(u).wait_send()
            sent_home(u, t.at[u % t_slots])

    for u in range(pieces):
        for step in range(1, row_count):
            source = (row + row_count - step) % row_count
            put(t.at[0, source], place(u, source), a_send, a_recv, 3 * u + step - 1, {"row": source}).wait_recv()


def backward_plane(
    cid, hid, cot, slope, n2, upw, std, n1, qkvw, down_nat, resid_own, attended, outw, mixed, std1_own, stats, marks, vec_all, inv1_own, down_bias
):
    f32, bf16 = jnp.float32, jnp.bfloat16
    length, full = cot.shape
    rows, width = length // lax.axis_size("col"), full // lax.axis_size("row")
    row_count, dp_count = full // width, lax.axis_size("dp")
    counts = (slope.shape[1] // CHUNK, slope.shape[1] // CHUNK, attended.shape[1] // CHUNK, mixed.shape[1] // CHUNK)
    total = sum(counts)
    unit = (row_count, CHUNK, CHUNK)
    shape = jax.ShapeDtypeStruct
    away, near = pl.BlockSpec(memory_space=pl.ANY), pl.BlockSpec(memory_space=pltpu.VMEM)
    vmem, dma = pltpu.VMEM, pltpu.SemaphoreType.DMA
    sets = [
        vmem((4, rows, width), bf16),
        vmem((rows, width), bf16),
        vmem((rows // 2, width), bf16),
        vmem((rows // 2, width), bf16),
        vmem((2, rows, width), bf16),
        vmem((2, rows, width), bf16),
    ]
    return pl.pallas_call(
        functools.partial(backward_kernel, counts),
        out_shape=[
            shape((row_count * counts[0], CHUNK, width), bf16),
            shape((2, CHUNK, row_count * counts[1] * CHUNK), bf16),
            shape((row_count * counts[2], CHUNK, width), bf16),
            shape((2, CHUNK, row_count * counts[3] * CHUNK), bf16),
            shape((2 * total,) + unit, bf16),
            shape((hid.shape[1], full), bf16),
            shape((rows, width), bf16),
            shape((rows, width), bf16),
            shape((row_count, 16, width), f32),
        ],
        in_specs=[away] * 14 + [near] * 5,
        out_specs=[away] * 6 + [near] * 3,
        scratch_shapes=[
            vmem((length, full), bf16),
            vmem((length, full), bf16),
            vmem((length, full), bf16),
            vmem((length, full), bf16),
            vmem((length, full), bf16),
            vmem(upw.shape, bf16),
            vmem(hid.shape, bf16),
            vmem(slope.shape, bf16),
            vmem(attended.shape, bf16),
            vmem(outw.shape, bf16),
            vmem(mixed.shape, bf16),
            vmem(std1_own.shape, bf16),
            vmem(attended.shape, bf16),
            vmem(mixed.shape, bf16),
            vmem((length, HEAD), f32),
            vmem((length, HEAD), f32),
            vmem((2, row_count, width // CHUNK, CHUNK, CHUNK), bf16),
            vmem((2,) + unit, bf16),
            vmem((2,) + unit, bf16),
            vmem((3,) + unit, bf16),
            vmem((4,) + unit, bf16),
        ]
        + sets
        + sets
        + [
            vmem((rows, width), f32),
            vmem((rows, width), f32),
            vmem((8, full), f32),
            vmem((16, width), f32),
            vmem((8, width), f32),
            vmem((dp_count, 16, width), f32),
            vmem((row_count, 8, rows), f32),
            dma((15,)),
            pltpu.SemaphoreType.REGULAR,
            dma((2 * total + 1,)),
            dma((6 * total,)),
            dma((6 * total,)),
            dma((6 * total,)),
            dma((6 * total,)),
            dma((45,)),
            dma((45,)),
        ],
        compiler_params=pltpu.CompilerParams(
            collective_id=cid, has_side_effects=True, vmem_limit_bytes=64 * 1024 * 1024 - 65536
        ),
        cost_estimate=pl.CostEstimate(flops=40_000_000_000, bytes_accessed=100_000_000, transcendentals=4_000_000),
    )(hid, cot, slope, n2, upw, std, n1, qkvw, down_nat, resid_own, attended, outw, mixed, std1_own, stats, marks, vec_all, inv1_own, down_bias)


class Moves:
    def __init__(self, source, target, cut, parts, sends, recvs, base):
        row, plane = lax.axis_index("row"), lax.axis_index("dp")
        side, core = row // 2, row % 2
        parity = plane % 2
        other = {"dp": plane + 1 - 2 * parity}
        twin = side * 2 + 1 - core
        far = ((1 - side) * 2 + core, (1 - side) * 2 + 1 - core)
        self.sibling = put(source(twin), target(row), sends, recvs, base, {"row": twin})
        self.sibling_in = put(source(twin), target(twin), sends, recvs, base, {"row": twin})
        self.outs, self.ins, self.passes, self.gets = [], [], [], []
        at = base + 1
        for step in range(parts // 2):
            for k, device in enumerate(far):
                mine, theirs = 2 * step + parity, 2 * step + 1 - parity
                there, here = cut(target(row), mine), cut(target(device), mine)
                self.outs.append(put(cut(source(device), mine), there, sends, recvs, at, {"row": device}))
                self.ins.append(put(cut(source(device), mine), here, sends, recvs, at, {"row": device}))
                self.passes.append(put(here, here, sends, recvs, at + 1, other))
                lands = cut(target(device), theirs)
                self.gets.append(put(lands, lands, sends, recvs, at + 1, other))
                at += 2

    @staticmethod
    def count(parts):
        return 1 + 2 * parts

    def start(self):
        self.sibling.start()
        self.start_far()

    def start_far(self):
        for copy in self.outs:
            copy.start()

    def forward(self, begin=0, end=None):
        for came, passed in list(zip(self.ins, self.passes))[begin:end]:
            came.wait_recv()
            passed.start()

    def finish(self):
        self.sibling_in.wait_recv()
        for copy in self.gets:
            copy.wait_recv()

    def drain(self):
        self.sibling.wait_send()
        for copy in self.outs + self.passes:
            copy.wait_send()


FAR_PARTS = 4


def forward_kernel(
    tokens,
    cot_in,
    ln1_gain,
    ln1_shift,
    out_bias_in,
    ln2_gain,
    ln2_shift,
    qv_bias,
    up_bias_in,
    spans,
    qkv_in,
    out_nat,
    up_nat,
    cot_all,
    n1_out,
    n2_out,
    std_out,
    upw_out,
    qkvw_out,
    outw_out,
    mixed_out,
    attended_out,
    hid_out,
    slope_out,
    stats,
    marks,
    vec_all,
    resid_own,
    std1_own,
    inv1_own,
    tok,
    n1,
    part,
    tot,
    qkvw,
    upw,
    outw,
    mixed,
    attended,
    hid,
    slope,
    own_sum,
    got,
    diag,
    hx,
    hy,
    ts,
    fx,
    qkv_raw,
    qkv_nat,
    mixed_bias,
    local_sem,
    w_send,
    w_recv,
    p_send,
    p_recv,
):
    f32, bf16 = jnp.float32, jnp.bfloat16
    plane, row, col = lax.axis_index("dp"), lax.axis_index("row"), lax.axis_index("col")
    side, core = row // 2, row % 2
    rows, width = tokens.shape
    length, full = tok.shape
    row_count = full // width
    heads_width = attended.shape[1]
    units = hid.shape[1]

    barrier = pltpu.get_barrier_semaphore()
    twins = ({"row": (1 - side) * 2 + 1 - core}, {"dp": plane + 1 - 2 * (plane % 2)})
    for partner in partners() + twins:
        pl.semaphore_signal(barrier, inc=1, device_id=partner, device_id_type=MESH)
    pl.semaphore_wait(barrier, 5)

    def cut_rows(ref, part):
        count = ref.shape[0] // FAR_PARTS
        return ref.at[strip(part * count, count)]

    per = qkvw.shape[1]
    count = Moves.count(FAR_PARTS)
    qkv_moves = Moves(
        lambda r: qkv_nat.at[:, strip(r * per, per)],
        lambda r: qkvw.at[strip(r * width, width), :],
        cut_rows,
        FAR_PARTS,
        w_send,
        w_recv,
        0,
    )
    out_moves = Moves(
        lambda r: out_nat.at[strip(r * heads_width, heads_width), :],
        lambda r: outw.at[:, strip(r * width, width)],
        cut_rows,
        FAR_PARTS,
        w_send,
        w_recv,
        count,
    )
    up_moves = Moves(
        lambda r: up_nat.at[:, strip(r * units, units)],
        lambda r: upw.at[strip(r * width, width), :],
        cut_rows,
        FAR_PARTS,
        w_send,
        w_recv,
        2 * count,
    )
    locals_ = [
        (qkv_nat.at[:, strip(row * per, per)], qkvw.at[strip(row * width, width), :]),
        (out_nat.at[strip(row * heads_width, heads_width), :], outw.at[:, strip(row * width, width)]),
        (up_nat.at[:, strip(row * units, units)], upw.at[strip(row * width, width), :]),
        (cot_in, block(cot_all, col, side, core, rows, width)),
        (n1, n1_out),
        (part, n2_out),
        (n1, std_out),
        (upw, upw_out),
        (qkvw, qkvw_out),
        (outw, outw_out),
        (mixed, mixed_out),
        (attended, attended_out),
        (hid, hid_out),
        (slope, slope_out),
        (qkv_in, qkv_raw),
    ]
    local = [pltpu.make_async_copy(a, b, local_sem.at[k]) for k, (a, b) in enumerate(locals_)]
    local[14].start()
    for k in range(1, 4):
        local[k].start()

    block(tok, col, side, core, rows, width)[...] = tokens[...]
    gather = spread_steps(tok, rows, width, p_send, p_recv, 0)
    next(gather)
    here = strip(row * width, width)
    vec_all[:, here] = jnp.zeros((vec_all.shape[0], width), f32)
    for k, vector in enumerate((ln1_gain, ln1_shift, out_bias_in, ln2_gain, ln2_shift)):
        vec_all[k : k + 1, here] = vector[...]
    vec_sends, vec_recvs = [], []
    for step in range(1, row_count):
        target, source = (row + step) % row_count, (row + row_count - step) % row_count
        here, there = vec_all.at[:, strip(row * width, width)], vec_all.at[:, strip(source * width, width)]
        vec_sends.append(put(here, here, p_send, p_recv, 8 + step - 1, {"row": target}))
        vec_recvs.append(put(there, there, p_send, p_recv, 8 + step - 1, {"row": source}))
        vec_sends[-1].start()
    out_moves.sibling.start()
    up_moves.sibling.start()
    local[14].wait()
    for kind in range(3):
        flat = qkv_raw[:, kind].reshape(width, qkv_raw.shape[2] * HEAD)
        for head in range(qkv_raw.shape[2]):
            qkv_nat[:, pl.ds((head * 3 + kind) * HEAD, HEAD)] = flat[:, head * HEAD : (head + 1) * HEAD]
    local[0].start()
    qkv_moves.sibling.start()
    next(gather)
    qkv_moves.start_far()
    next(gather)
    next(gather, None)
    for copy in vec_recvs:
        copy.wait_recv()
    lines = lax.broadcasted_iota(jnp.int32, marks.shape, 0) * SPAN
    found = jnp.zeros(marks.shape, f32)
    for k in range(spans.shape[1]):
        found = jnp.where(lines == spans[0:1, k : k + 1] // SPAN * SPAN, 1.0, found)
    marks[...] = found

    tile = 64
    gain1, shift1 = vec_all[0:1, :], vec_all[1:2, :]

    def norm1_step(k, none):
        at = strip(k * tile, tile)
        values = tok[at, :].astype(f32)
        center = jnp.sum(values, axis=1, keepdims=True) / full
        inverse = lax.rsqrt(jnp.sum(values * values, axis=1, keepdims=True) / full - center * center + epsilon)
        n1[at, :] = ((values - center) * inverse * gain1 + shift1).astype(bf16)

        @pl.when(k // (rows // tile) == col)
        def _():
            here = strip(k % (rows // tile) * tile, tile)
            std1_own[here, :] = ((tok[at, strip(row * width, width)].astype(f32) - center) * inverse).astype(bf16)
            inv1_own[here, :] = inverse

        return none

    half_steps = length // tile // 2
    lax.fori_loop(0, half_steps, norm1_step, 0)
    qkv_moves.forward(0, 2)
    lax.fori_loop(half_steps, 2 * half_steps, norm1_step, 0)
    local[4].start()
    qkv_moves.forward(2, 4)
    out_moves.start_far()
    up_moves.start_far()
    qkv_moves.finish()
    local[0].wait()

    mixed_bias[...] = jnp.zeros_like(mixed_bias)
    for head in range(heads_width // HEAD):
        for k in range(2):
            lanes = pl.ds((head * 3 + 2 * k) * HEAD, HEAD)
            mixed_bias[:, lanes] = qv_bias[row * (heads_width // HEAD) + head, k : k + 1, :]
    up_bias = up_bias_in.at[:, strip(row * units, units)]

    def mixed_step(k, none):
        down, across = k // (per // CHUNK), k % (per // CHUNK)
        at, lanes = strip(down * rows, rows), strip(across * CHUNK, CHUNK)
        value = jnp.dot(n1[at, :], qkvw[:, lanes], preferred_element_type=f32)
        mixed[at, lanes] = (value + mixed_bias[:, lanes]).astype(bf16)
        return none

    lax.fori_loop(0, (length // rows) * (per // CHUNK), mixed_step, 0)
    local[8].start()
    local[10].start()
    local[4].wait()

    heads = heads_width // HEAD
    factor = 1.0 / math.sqrt(HEAD)
    blocks = length // SPAN
    spots = (SPAN, SPAN)
    earlier = lax.broadcasted_iota(jnp.int32, spots, 1) <= lax.broadcasted_iota(jnp.int32, spots, 0)

    def head_step(head, none):
        base = head * 3 * HEAD
        at_q, at_k, at_v = strip(base, HEAD), strip(base + HEAD, HEAD), strip(base + 2 * HEAD, HEAD)
        for k in range(blocks):
            here = pl.ds(k * SPAN, SPAN)
            seen = (k + 1) * SPAN
            scores = dot_nt(mixed[here, at_q], mixed[:seen, at_k]) * factor
            last = jnp.where(earlier | (marks[k : k + 1, :1] > 0), scores[:, seen - SPAN :], masked_score)
            scores = last if k == 0 else jnp.concatenate([scores[:, : seen - SPAN], last], axis=1)
            highest = jnp.max(scores, axis=1, keepdims=True)
            weights = jnp.exp(scores - highest)
            weight_sum = jnp.sum(weights, axis=1, keepdims=True)
            stats[here, 1 + head : 2 + head] = highest + jnp.log(weight_sum)
            value = jnp.dot((weights / weight_sum).astype(bf16), mixed[:seen, at_v], preferred_element_type=f32)
            attended[here, strip(head * HEAD, HEAD)] = value.astype(bf16)
        return none

    for head in range(heads):
        head_step(head, 0)
    local[11].start()
    out_moves.forward()
    up_moves.forward(0, 4)
    out_moves.finish()
    local[1].wait()
    tiled_nn(attended, outw, part, rows, 512)
    local[9].start()
    add_up = reduce_steps(part, own_sum, got, diag, hx, hy, ts, fx, p_send, p_recv, 11)
    next(add_up)
    next(add_up)
    up_moves.forward(4, 8)
    next(add_up)
    next(add_up, None)
    block(tot, col, side, core, rows, width)[...] = own_sum[...].astype(bf16)
    again = spread_steps(tot, rows, width, p_send, p_recv, 19)
    for k in range(3):
        next(again)
    next(again, None)
    local[3].wait()
    cot_gather = spread_steps(cot_all, rows, width, p_send, p_recv, 27)
    next(cot_gather)

    gain2, shift2, out_bias = vec_all[3:4, :], vec_all[4:5, :], vec_all[2:3, :]

    def norm2_step(k, none):
        at = strip(k * tile, tile)
        values = tok[at, :].astype(f32) + (tot[at, :].astype(f32) + out_bias)
        center = jnp.sum(values, axis=1, keepdims=True) / full
        inverse = lax.rsqrt(jnp.sum(values * values, axis=1, keepdims=True) / full - center * center + epsilon)
        standard = (values - center) * inverse
        stats[at, 0:1] = inverse
        n1[at, :] = standard.astype(bf16)
        part[at, :] = (standard * gain2 + shift2).astype(bf16)

        @pl.when(k // (rows // tile) == col)
        def _():
            own = strip(row * width, width)
            here = strip(k % (rows // tile) * tile, tile)
            resid_own[here, :] = tok[at, own].astype(f32) + (tot[at, own].astype(f32) + vec_all[2:3, own])

        return none

    lax.fori_loop(0, 2 * half_steps, norm2_step, 0)
    local[5].start()
    local[6].start()
    next(cot_gather)
    up_moves.finish()
    local[2].wait()
    local[7].start()

    def up_step(k, none):
        down, across = k // (units // CHUNK), k % (units // CHUNK)
        at, lanes = strip(down * rows, rows), strip(across * CHUNK, CHUNK)
        u = jnp.dot(part[at, :], upw[:, lanes], preferred_element_type=f32) + up_bias[:, lanes]
        bent = jnp.tanh(0.7978845608028654 * (u + 0.044715 * u * u * u))
        hid[at, lanes] = (0.5 * u * (1.0 + bent)).astype(bf16)
        inside = 0.7978845608028654 * (1.0 + 3 * 0.044715 * u * u)
        slope[at, lanes] = (0.5 * (1.0 + bent) + 0.5 * u * (1.0 - bent * bent) * inside).astype(bf16)
        return none

    lax.fori_loop(0, (length // rows) * (units // CHUNK), up_step, 0)
    local[12].start()
    local[13].start()
    next(cot_gather)
    next(cot_gather, None)
    for k in range(5, 14):
        local[k].wait()
    for moves in (qkv_moves, out_moves, up_moves):
        moves.drain()
    for copy in vec_sends:
        copy.wait_send()


def forward_plane(cid, tokens, cot, vectors, qv_bias, up_bias, spans, qkv_in, out_nat, up_nat):
    f32, bf16 = jnp.float32, jnp.bfloat16
    rows, width = tokens.shape
    row_count = lax.axis_size("row")
    length, full = rows * lax.axis_size("col"), width * row_count
    per, heads_width, units = qkv_in.shape[1] * qkv_in.shape[2] * HEAD // row_count, out_nat.shape[0] // row_count, up_nat.shape[1] // row_count
    shape = jax.ShapeDtypeStruct
    away, near = pl.BlockSpec(memory_space=pl.ANY), pl.BlockSpec(memory_space=pltpu.VMEM)
    vmem, dma = pltpu.VMEM, pltpu.SemaphoreType.DMA
    wide = shape((length, full), bf16)
    moved = 3 * Moves.count(FAR_PARTS)
    return pl.pallas_call(
        forward_kernel,
        out_shape=[
            wide,
            wide,
            wide,
            wide,
            shape((full, units), bf16),
            shape((full, per), bf16),
            shape((heads_width, full), bf16),
            shape((length, per), bf16),
            shape((length, heads_width), bf16),
            shape((length, units), bf16),
            shape((length, units), bf16),
            shape((length, 8), f32),
            shape((8, 128), f32),
            shape((8, full), f32),
            shape((rows, width), f32),
            shape((rows, width), bf16),
            shape((rows, 1), f32),
        ],
        in_specs=[near] * (5 + len(vectors)) + [away] * 3,
        out_specs=[away] * 11 + [near] * 6,
        scratch_shapes=[
            vmem((length, full), bf16),
            vmem((length, full), bf16),
            vmem((length, full), bf16),
            vmem((length, full), bf16),
            vmem((full, per), bf16),
            vmem((full, units), bf16),
            vmem((heads_width, full), bf16),
            vmem((length, per), bf16),
            vmem((length, heads_width), bf16),
            vmem((length, units), bf16),
            vmem((length, units), bf16),
            vmem((rows, width), f32),
            vmem((4, rows, width), bf16),
            vmem((rows, width), bf16),
            vmem((rows // 2, width), bf16),
            vmem((rows // 2, width), bf16),
            vmem((2, rows, width), bf16),
            vmem((2, rows, width), bf16),
            vmem(qkv_in.shape, bf16),
            vmem((width, row_count * per), bf16),
            vmem((1, per), f32),
            dma((15,)),
            dma((moved,)),
            dma((moved,)),
            dma((35,)),
            dma((35,)),
        ],
        compiler_params=pltpu.CompilerParams(
            collective_id=cid, has_side_effects=True, vmem_limit_bytes=60 * 1024 * 1024
        ),
        cost_estimate=pl.CostEstimate(flops=10_000_000_000, bytes_accessed=60_000_000, transcendentals=4_000_000),
    )(tokens, cot, *[vector[None] for vector in vectors], qv_bias, up_bias[None], spans, qkv_in, out_nat, up_nat)


def results_kernel(
    down, up, out, output, tokens, qkv, small, down_result, up_result, out_result, output_result, tokens_result, qkv_result, *vectors
):
    *sums, up_bias, qv_bias = vectors
    f32 = jnp.float32
    down_result[...] = down[...].astype(f32)
    up_result[...] = up[...].astype(f32)
    out_result[...] = out[...].astype(f32)
    output_result[...] = output[...]
    tokens_result[...] = tokens[...]
    for head in range(qkv_result.shape[2]):
        for kind in range(3):
            begin = (head * 3 + kind) * HEAD
            qkv_result[:, kind, head, :] = qkv[:, begin : begin + HEAD].astype(f32)

    @pl.when(pl.program_id(0) == 0)
    def _():
        row = lax.axis_index("row")
        for k, result in enumerate(sums):
            result[...] = small[row, k : k + 1, :]
        count, _, width = small.shape
        lines = up_bias.shape[1] // (count * width)
        heads = qv_bias.shape[0] // count
        for source in range(count):
            for k in range(lines):
                begin = (source * lines + k) * width
                up_bias[:, begin : begin + width] = small[source, 8 + k : 9 + k, :]
            for head in range(heads):
                for k in range(2):
                    begin = (head * 2 + k) * HEAD
                    line = small[source, 8 + lines : 9 + lines, begin : begin + HEAD]
                    qv_bias[source * heads + head, k : k + 1, :] = line


def results(down, up, out, output, tokens, qkv, small):
    f32 = jnp.float32
    shape = jax.ShapeDtypeStruct
    rows, heads = qkv.shape[0], qkv.shape[1] // (3 * HEAD)
    width, units = small.shape[2], up.shape[1]
    steps = 8

    def cut(array):
        return pl.BlockSpec((array.shape[0] // steps, array.shape[1]), lambda k: (k, 0))

    def whole(*dims):
        return pl.BlockSpec(dims, lambda k: (0,) * len(dims))

    line = whole(1, width)
    *made, up_bias, qv_bias = pl.pallas_call(
        results_kernel,
        grid=(steps,),
        out_shape=[shape(a.shape, f32) for a in (down, up, out)]
        + [shape(a.shape, a.dtype) for a in (output, tokens)]
        + [shape((rows, 3, heads, HEAD), f32)]
        + [shape((1, width), f32)] * 6
        + [shape((1, units), f32), shape((heads, 2, HEAD), f32)],
        in_specs=[cut(a) for a in (down, up, out, output, tokens, qkv)] + [whole(*small.shape)],
        out_specs=[cut(a) for a in (down, up, out, output, tokens)]
        + [pl.BlockSpec((rows // steps, 3, heads, HEAD), lambda k: (k, 0, 0, 0))]
        + [line] * 6
        + [whole(1, units), whole(heads, 2, HEAD)],
        compiler_params=pltpu.CompilerParams(vmem_limit_bytes=63 * 1024 * 1024),
    )(down, up, out, output, tokens, qkv, small)
    made[5] = jnp.swapaxes(made[5], 1, 2)
    return made[:6], [sums[0] for sums in made[6:]], up_bias[0], qv_bias


def plane_plan(
    tokens,
    ln1_gain,
    ln1_shift,
    qkv_weight,
    qv_bias,
    out_weight,
    out_bias,
    ln2_gain,
    ln2_shift,
    up_weight,
    up_bias,
    down_weight,
    down_bias,
    span_starts,
    cotangent,
):
    width = tokens.shape[1]
    (
        cot_all, n1, n2, standard2, upw, qkvw, outw, mixed, attended, hidden, slope,
        stats, marks, vec_all, residual_own, standard1_own, inverse1_own,
    ) = forward_plane(
        1,
        tokens,
        cotangent,
        (ln1_gain, ln1_shift, out_bias, ln2_gain, ln2_shift),
        qv_bias,
        up_bias,
        span_starts,
        jnp.swapaxes(qkv_weight, 1, 2),
        out_weight.reshape(-1, width),
        up_weight,
    )
    down_grad, up_grad, out_grad, qkv_grad, _, _, output, tokens_grad, small = backward_plane(
        2, hidden, cot_all, slope, n2, upw, standard2, n1, qkvw, down_weight, residual_own, attended, outw, mixed, standard1_own,
        stats, marks, vec_all, inverse1_own, down_bias[None],
    )
    grads, sums, up_bias_grad, qv_bias_grad = results(
        down_grad.reshape(-1, width), up_grad.reshape(width, -1), out_grad.reshape(-1, width), output, tokens_grad,
        qkv_grad.reshape(width, -1), small
    )
    return (
        grads[3],
        grads[4],
        sums[0],
        sums[1],
        grads[5],
        qv_bias_grad,
        grads[2].reshape(out_weight.shape),
        sums[4],
        sums[2],
        sums[3],
        grads[1],
        up_bias_grad,
        grads[0],
        sums[5],
    )


def solution(mesh):
    sizes = dict(mesh.shape)
    flat = sizes == {"dp": 4, "row": 4, "col": 2}
    per_device = plane_plan if flat else general_plan
    placed = (
        P(("dp", "col"), "row"),
        P("row"),
        P("row"),
        P("row", "col", None, None),
        P("col", None, None),
        P("col", None, "row"),
        P("row"),
        P("row"),
        P("row"),
        P("row", "col"),
        P("col"),
        P("col", "row"),
        P("row"),
        P("dp", None),
        P(("dp", "col"), "row"),
    )
    return jax.shard_map(
        per_device,
        mesh=mesh,
        in_specs=placed,
        out_specs=(
            P(("dp", "col"), "row"),
            P(("dp", "col"), "row"),
            P("row"),
            P("row"),
            P("row", "col", None, None),
            P("col", None, None),
            P("col", None, "row"),
            P("row"),
            P("row"),
            P("row"),
            P("row", "col"),
            P("col"),
            P("col", "row"),
            P("row"),
        ),
        check_vma=False,
    )
```

```python
import functools
import math

import jax
import jax.numpy as jnp
from jax import lax
from jax.experimental import pallas as pl
from jax.experimental.pallas import tpu as pltpu
from jax.sharding import PartitionSpec as P

MESH = pl.DeviceIdType.MESH

D = 2048
HEAD = 128
SEQS = 1
SPAN = 256
BLOCK = 512


epsilon = 1e-05
masked_score = -1e30


def gelu_tanh(values):
    return (
        0.5
        * values
        * (1.0 + jnp.tanh(0.7978845608028654 * (values + 0.044715 * values * values * values)))
    )


def gather_columns(block_data):
    return lax.all_gather(block_data, "col", axis=0, tiled=True)


def gather_rows(block_data):
    return lax.all_gather(block_data, "row", axis=0, tiled=True)


def product(left_side, right_side, flipped):
    if flipped:
        return lax.dot_general(
            left_side, right_side, (((1,), (1,)), ((), ())), preferred_element_type=jnp.float32
        )
    return jnp.dot(left_side, right_side, preferred_element_type=jnp.float32)


def outer_sum(left_side, right_side):
    return lax.dot_general(
        left_side, right_side, (((0,), (0,)), ((), ())), preferred_element_type=jnp.float32
    )


def sum_rows(left_side, right_side, flipped):
    wide_left = lax.all_to_all(left_side, "row", split_axis=0, concat_axis=1, tiled=True)
    if flipped:
        wide_right = lax.all_gather(right_side, "row", axis=1, tiled=True)
    else:
        wide_right = lax.all_gather(right_side, "row", axis=0, tiled=True)
    return product(wide_left, wide_right, flipped)


def sum_columns(left_side, right_side, flipped):
    return lax.psum_scatter(
        product(left_side, right_side, flipped), "col", scatter_dimension=0, tiled=True
    )


def row_totals(first_sum, second_sum):
    return lax.psum((first_sum, second_sum), "row")


def norm_forward(values, gain_row, bias_row):
    totals, squares = row_totals(jnp.sum(values, axis=1), jnp.sum(values * values, axis=1))
    center = totals / D
    spread = squares / D - center * center
    inverse = lax.rsqrt(spread + epsilon)
    standard = (values - center[:, None]) * inverse[:, None]
    return (standard, inverse, (standard * gain_row + bias_row).astype(jnp.bfloat16))


def norm_backward(upstream, standard, inverse, gain_row):
    scaled = upstream * gain_row
    first_sum, second_sum = row_totals(jnp.sum(scaled, axis=1), jnp.sum(scaled * standard, axis=1))
    gradient = inverse[:, None] * (
        scaled - first_sum[:, None] / D - standard * (second_sum[:, None] / D)
    )
    return (gradient, jnp.sum(upstream * standard, axis=0), jnp.sum(upstream, axis=0))


def visible(query_pos, query_image, key_pos):
    earlier = key_pos[None, :] <= query_pos[:, None]
    same_span = (key_pos[None, :] // SPAN == query_pos[:, None] // SPAN) & (
        query_image[:, None] > 0
    )
    return earlier | same_span


def attention_forward(queries, key_value, token_image, row_offset, seq_length, block_rows):
    own_rows, head_count, width = queries.shape
    factor = 1.0 / math.sqrt(width)

    def block_forward(block_index):
        local = block_index * block_rows
        start_pos = row_offset + local
        query_block = lax.dynamic_slice_in_dim(queries, local, block_rows, 0)
        query_pos = start_pos + jnp.arange(block_rows, dtype=jnp.int32)
        query_image = lax.dynamic_slice_in_dim(token_image, start_pos, block_rows, 0)
        begin = start_pos // seq_length * seq_length // block_rows
        finish = start_pos // block_rows + 1

        def key_step(key_index, state_in):
            running, weight_sum, gathered = state_in
            key_begin = key_index * block_rows
            key_block = lax.dynamic_slice_in_dim(key_value, key_begin, block_rows, 0)
            key_pos = key_begin + jnp.arange(block_rows, dtype=jnp.int32)
            allowed = visible(query_pos, query_image, key_pos)
            scores = (
                jnp.einsum(
                    "qhd,khd->hqk",
                    query_block,
                    key_block[:, :, 0],
                    preferred_element_type=jnp.float32,
                )
                * factor
            )
            scores = jnp.where(allowed[None], scores, masked_score)
            highest = jnp.maximum(running, jnp.max(scores, axis=2))
            weights = jnp.exp(scores - highest[:, :, None])
            shrink = jnp.exp(running - highest)
            weight_sum = weight_sum * shrink + jnp.sum(weights, axis=2)
            gathered = gathered * shrink.T[:, :, None] + jnp.einsum(
                "hqk,khd->qhd",
                weights.astype(jnp.bfloat16),
                key_block[:, :, 1],
                preferred_element_type=jnp.float32,
            )
            return (highest, weight_sum, gathered)

        initial = (
            jnp.full((head_count, block_rows), masked_score, jnp.float32),
            jnp.zeros((head_count, block_rows), jnp.float32),
            jnp.zeros((block_rows, head_count, width), jnp.float32),
        )
        running, weight_sum, gathered = lax.fori_loop(begin, finish, key_step, initial)
        return (gathered / weight_sum.T[:, :, None], running + jnp.log(weight_sum))

    result, logsum = lax.map(block_forward, jnp.arange(own_rows // block_rows, dtype=jnp.int32))
    return (result.reshape(own_rows, head_count, width), logsum)


def attention_backward(
    queries,
    key_value,
    attended_full,
    logsum,
    d_attended,
    token_image,
    row_offset,
    seq_length,
    block_rows,
):
    own_rows, head_count, width = queries.shape
    factor = 1.0 / math.sqrt(width)
    row_dots = jnp.sum(d_attended.astype(jnp.float32) * attended_full, axis=2)

    def block_backward(block_index, state_out):
        d_queries, d_pairs = state_out
        local = block_index * block_rows
        start_pos = row_offset + local
        query_block = lax.dynamic_slice_in_dim(queries, local, block_rows, 0)
        dout_block = lax.dynamic_slice_in_dim(d_attended, local, block_rows, 0)
        dots_block = lax.dynamic_slice_in_dim(row_dots, local, block_rows, 0).T
        logsum_block = logsum[block_index]
        query_pos = start_pos + jnp.arange(block_rows, dtype=jnp.int32)
        query_image = lax.dynamic_slice_in_dim(token_image, start_pos, block_rows, 0)
        begin = start_pos // seq_length * seq_length // block_rows
        finish = start_pos // block_rows + 1

        def key_step(key_index, state_in):
            d_query, d_keys = state_in
            key_begin = key_index * block_rows
            key_block = lax.dynamic_slice_in_dim(key_value, key_begin, block_rows, 0)
            key_pos = key_begin + jnp.arange(block_rows, dtype=jnp.int32)
            allowed = visible(query_pos, query_image, key_pos)
            scores = (
                jnp.einsum(
                    "qhd,khd->hqk",
                    query_block,
                    key_block[:, :, 0],
                    preferred_element_type=jnp.float32,
                )
                * factor
            )
            scores = jnp.where(allowed[None], scores, masked_score)
            probabilities = jnp.exp(scores - logsum_block[:, :, None])
            d_probs = jnp.einsum(
                "qhd,khd->hqk", dout_block, key_block[:, :, 1], preferred_element_type=jnp.float32
            )
            d_scores = (probabilities * (d_probs - dots_block[:, :, None])).astype(jnp.bfloat16)
            d_query = d_query + jnp.einsum(
                "hqk,khd->qhd", d_scores, key_block[:, :, 0], preferred_element_type=jnp.float32
            )
            d_key = (
                jnp.einsum(
                    "hqk,qhd->khd", d_scores, query_block, preferred_element_type=jnp.float32
                )
                * factor
            )
            d_value = jnp.einsum(
                "hqk,qhd->khd",
                probabilities.astype(jnp.bfloat16),
                dout_block,
                preferred_element_type=jnp.float32,
            )
            previous = lax.dynamic_slice_in_dim(d_keys, key_begin, block_rows, 0)
            d_keys = lax.dynamic_update_slice_in_dim(
                d_keys, previous + jnp.stack([d_key, d_value], axis=2), key_begin, 0
            )
            return (d_query, d_keys)

        d_query, d_pairs = lax.fori_loop(
            begin,
            finish,
            key_step,
            (jnp.zeros((block_rows, head_count, width), jnp.float32), d_pairs),
        )
        d_queries = lax.dynamic_update_slice_in_dim(d_queries, d_query * factor, local, 0)
        return (d_queries, d_pairs)

    initial = (
        jnp.zeros((own_rows, head_count, width), jnp.float32),
        jnp.zeros((key_value.shape[0], head_count, 2, width), jnp.float32),
    )
    return lax.fori_loop(0, own_rows // block_rows, block_backward, initial)


def general_plan(
    tokens,
    ln1_gain,
    ln1_shift,
    qkv_weight,
    qv_bias,
    out_weight,
    out_bias,
    ln2_gain,
    ln2_shift,
    up_weight,
    up_bias,
    down_weight,
    down_bias,
    span_starts,
    cotangent,
):
    col_rows, row_width = tokens.shape
    group_rows = col_rows * lax.axis_size("col")
    own_rows = group_rows // lax.axis_size("row")
    head_count = qkv_weight.shape[1]
    seq_length = group_rows // SEQS
    block_rows = BLOCK - own_rows % BLOCK
    row_offset = lax.axis_index("row") * own_rows
    slot_count = seq_length // SPAN
    image_marks = jnp.sum(
        (
            span_starts[:, :, None] // SPAN
            == jnp.arange(slot_count, dtype=jnp.int32)[None, None, :]
        ).astype(jnp.int32),
        axis=1,
    )
    token_image = jnp.broadcast_to(
        image_marks.reshape(-1)[:, None], (group_rows // SPAN, SPAN)
    ).reshape(group_rows)
    qkv_flat = qkv_weight.reshape(row_width, head_count * 3 * HEAD)
    out_flat = out_weight.reshape(head_count * HEAD, row_width)
    inputs = tokens.astype(jnp.float32)
    standard1, inverse1, normed1 = norm_forward(inputs, ln1_gain, ln1_shift)
    normed1_all = gather_columns(normed1)
    mixed_sums = sum_rows(normed1_all, qkv_flat, False).reshape(own_rows, head_count, 3, HEAD)
    queries = (mixed_sums[:, :, 0] + qv_bias[:, 0]).astype(jnp.bfloat16)
    key_value_own = jnp.stack(
        [mixed_sums[:, :, 1], mixed_sums[:, :, 2] + qv_bias[:, 1]], axis=2
    ).astype(jnp.bfloat16)
    key_value = gather_rows(key_value_own)
    attended_full, logsum = attention_forward(
        queries, key_value, token_image, row_offset, seq_length, block_rows
    )
    attended = attended_full.astype(jnp.bfloat16).reshape(own_rows, head_count * HEAD)
    attended_all = gather_rows(attended)
    residual = inputs + (sum_columns(attended_all, out_flat, False) + out_bias)
    standard2, inverse2, normed2 = norm_forward(residual, ln2_gain, ln2_shift)
    normed2_all = gather_columns(normed2)
    up_sums = sum_rows(normed2_all, up_weight, False) + up_bias
    hidden = gelu_tanh(up_sums).astype(jnp.bfloat16)
    hidden_all = gather_rows(hidden)
    output = (residual + (sum_columns(hidden_all, down_weight, False) + down_bias)).astype(
        jnp.bfloat16
    )
    d_output = cotangent.astype(jnp.float32)
    d_output_all = gather_columns(cotangent)
    down_grad = outer_sum(hidden_all, d_output_all)
    down_bias_grad = jnp.sum(d_output_all, axis=0, dtype=jnp.float32)
    d_hidden = sum_rows(d_output_all, down_weight, True)
    d_upper = jax.vjp(gelu_tanh, up_sums)[1](d_hidden)[0].astype(jnp.bfloat16)
    d_upper_all = gather_rows(d_upper)
    normed2_use = gather_columns(normed2)
    up_grad = outer_sum(normed2_use, d_upper_all)
    up_bias_grad = jnp.sum(d_upper_all, axis=0, dtype=jnp.float32)
    d_normed2 = sum_columns(d_upper_all, up_weight, True)
    d_norm2, gain2_grad, shift2_grad = norm_backward(d_normed2, standard2, inverse2, ln2_gain)
    d_residual = d_output + d_norm2
    d_branch = d_residual.astype(jnp.bfloat16)
    d_branch_all = gather_columns(d_branch)
    out_grad = outer_sum(attended_all, d_branch_all)
    out_bias_grad = jnp.sum(d_branch_all, axis=0, dtype=jnp.float32)
    d_attended = (
        sum_rows(d_branch_all, out_flat, True)
        .astype(jnp.bfloat16)
        .reshape(own_rows, head_count, HEAD)
    )
    d_queries, d_pairs = attention_backward(
        queries,
        key_value,
        attended_full,
        logsum,
        d_attended,
        token_image,
        row_offset,
        seq_length,
        block_rows,
    )
    d_pairs_own = lax.psum_scatter(d_pairs, "row", scatter_dimension=0, tiled=True)
    d_mixed = jnp.concatenate([d_queries[:, :, None], d_pairs_own], axis=2).astype(jnp.bfloat16)
    d_mixed_all = gather_rows(d_mixed)
    normed1_use = gather_columns(normed1)
    d_mixed_flat = d_mixed_all.reshape(group_rows, head_count * 3 * HEAD)
    qkv_grad = outer_sum(normed1_use, d_mixed_flat)
    mixed_totals = jnp.sum(d_mixed_all, axis=0, dtype=jnp.float32)
    qv_bias_grad = jnp.stack([mixed_totals[:, 0], mixed_totals[:, 2]], axis=1)
    d_normed1 = sum_columns(d_mixed_flat, qkv_flat, True)
    d_norm1, gain1_grad, shift1_grad = norm_backward(d_normed1, standard1, inverse1, ln1_gain)
    tokens_grad = (d_residual + d_norm1).astype(jnp.bfloat16)
    norm_sums = lax.psum((gain1_grad, shift1_grad, gain2_grad, shift2_grad), ("dp", "col"))
    weight_sums = lax.psum(
        (
            qkv_grad,
            qv_bias_grad,
            out_grad,
            out_bias_grad,
            up_grad,
            up_bias_grad,
            down_grad,
            down_bias_grad,
        ),
        "dp",
    )
    return (
        output,
        tokens_grad,
        norm_sums[0],
        norm_sums[1],
        weight_sums[0].reshape(row_width, head_count, 3, HEAD),
        weight_sums[1],
        weight_sums[2].reshape(head_count, HEAD, row_width),
        weight_sums[3],
        norm_sums[2],
        norm_sums[3],
        weight_sums[4],
        weight_sums[5],
        weight_sums[6],
        weight_sums[7],
    )


def places():
    row, col = lax.axis_index("row"), lax.axis_index("col")
    return col, row // 2, row % 2


def partners():
    col, side, core = places()
    return ({"col": 1 - col}, {"row": (1 - side) * 2 + core}, {"row": side * 2 + 1 - core})


def block(ref, col, side, core, rows, width, part=None):
    begin, count = col * rows, rows
    if part is not None:
        begin, count = begin + part * (rows // 2), rows // 2
    return ref.at[strip(begin, count), strip((side * 2 + core) * width, width)]


def put(ref_from, ref_to, sends, recvs, at, partner):
    return pltpu.make_async_remote_copy(
        src_ref=ref_from,
        dst_ref=ref_to,
        send_sem=sends.at[at],
        recv_sem=recvs.at[at],
        device_id=partner,
        device_id_type=MESH,
    )


def strip(begin, count):
    return pl.ds(pl.multiple_of(begin, count), count)


def dot_nt(left, right):
    return lax.dot_general(left, right, (((1,), (1,)), ((), ())), preferred_element_type=jnp.float32)


def dot_tn(left, right):
    return lax.dot_general(left, right, (((0,), (0,)), ((), ())), preferred_element_type=jnp.float32)


def tiled_nt(left, right, target, inner, tile_rows, tile_cols, span=(0, 1, 1)):
    rows, cols = target.shape
    across = cols // tile_cols

    def step(at, none):
        down, side = at // across, at % across
        value = dot_nt(left[strip(down * tile_rows, tile_rows), :inner], right[strip(side * tile_cols, tile_cols), :inner])
        target[strip(down * tile_rows, tile_rows), strip(side * tile_cols, tile_cols)] = value.astype(target.dtype)
        return none

    count = (rows // tile_rows) * across
    lax.fori_loop(span[0] * count // span[2], span[1] * count // span[2], step, 0)


def tiled_nn(left, right, target, tile_rows, tile_cols, span=(0, 1, 1)):
    rows, cols = target.shape
    across = cols // tile_cols

    def step(at, none):
        down, side = at // across, at % across
        value = jnp.dot(
            left[strip(down * tile_rows, tile_rows), :],
            right[:, strip(side * tile_cols, tile_cols)],
            preferred_element_type=jnp.float32,
        )
        target[strip(down * tile_rows, tile_rows), strip(side * tile_cols, tile_cols)] = value.astype(target.dtype)
        return none

    count = (rows // tile_rows) * across
    lax.fori_loop(span[0] * count // span[2], span[1] * count // span[2], step, 0)


def reduce_steps(part, result, got, diag, half_x, half_y, to_send, from_xy, sends, recvs, base, mostly_x=False):
    f32 = jnp.float32
    rows, width = result.shape
    half = rows // 2
    low, high = pl.ds(0, half), pl.ds(half, half)
    col, side, core = places()
    to_x, to_y, to_core = partners()
    spots = ((1 - col, 1 - side), (col, 1 - side), (1 - col, side), (col, side))
    copies = [
        put(block(part, a, b, 1 - core, rows, width), got.at[k], sends, recvs, base + k, to_core)
        for k, (a, b) in enumerate(spots)
    ]
    for copy in copies:
        copy.start()
    mine = [block(part, a, b, core, rows, width) for a, b in spots]
    dx = put(diag.at[low], half_x, sends, recvs, base + 4, to_x)
    dy = put(diag.at[high], half_y, sends, recvs, base + 5, to_x if mostly_x else to_y)

    def onward(k, span, at, partner):
        return put(to_send.at[k, span], from_xy.at[k, span], sends, recvs, base + at, partner)

    y_high, x_low = onward(0, high, 6, to_y), onward(1, low, 7, to_x)
    y_low, x_high = onward(0, low, 8, to_y), onward(1, high, 9, to_x)

    def pair(k, span):
        return mine[k][span].astype(f32) + got[k, span].astype(f32)

    yield
    copies[0].wait_recv()
    diag[...] = (mine[0][...].astype(f32) + got[0].astype(f32)).astype(diag.dtype)
    dx.start()
    dy.start()
    copies[1].wait_recv()
    if not mostly_x:
        to_send[0, high] = pair(1, high).astype(diag.dtype)
        y_high.start()
    copies[2].wait_recv()
    to_send[1, low] = pair(2, low).astype(diag.dtype)
    x_low.start()
    if mostly_x:
        to_send[1, high] = pair(2, high).astype(diag.dtype)
        x_high.start()
    copies[3].wait_recv()
    yield
    dx.wait_recv()
    to_send[0, low] = (pair(1, low) + half_x[...].astype(f32)).astype(diag.dtype)
    y_low.start()
    dy.wait_recv()
    if mostly_x:
        to_send[0, high] = (pair(1, high) + half_y[...].astype(f32)).astype(diag.dtype)
        y_high.start()
    else:
        to_send[1, high] = (pair(2, high) + half_y[...].astype(f32)).astype(diag.dtype)
        x_high.start()
    yield
    for copy in (y_high, x_low, y_low, x_high):
        copy.wait_recv()
    near = mine[3][...].astype(f32) + got[3].astype(f32)
    result[...] = near + from_xy[0].astype(f32) + from_xy[1].astype(f32)
    for copy in copies + [dx, dy, y_high, x_low, y_low, x_high]:
        copy.wait_send()


def spread_steps(out, rows, width, sends, recvs, base, mostly_x=False):
    col, side, core = places()
    to_x, to_y, to_core = partners()

    def copy_of(at, which, partner, part=None):
        ref = block(out, *which, rows, width, part)
        return put(ref, ref, sends, recvs, base + at, partner)

    own, ox, oy, od = (col, side, core), (1 - col, side, core), (col, 1 - side, core), (1 - col, 1 - side, core)
    plan = [
        copy_of(0, own, to_x, 0),
        copy_of(1, own, to_y, 1),
        copy_of(2, own, to_x, 1),
        copy_of(3, own, to_y, 0),
        copy_of(4, own, to_core),
        copy_of(5, oy, to_x, 0) if mostly_x else copy_of(5, ox, to_y, 0),
        copy_of(6, oy, to_x, 1),
        copy_of(7, ox, to_core),
        copy_of(8, oy, to_core),
        copy_of(9, od, to_core),
    ]
    for at in range(5):
        plan[at].start()
    yield
    plan[0].wait_recv()
    if not mostly_x:
        plan[5].start()
    plan[1].wait_recv()
    plan[6].start()
    plan[2].wait_recv()
    plan[7].start()
    plan[3].wait_recv()
    plan[8].start()
    if mostly_x:
        plan[5].start()
    yield
    plan[5].wait_recv()
    plan[6].wait_recv()
    plan[9].start()
    yield
    for at in (4, 7, 8, 9):
        plan[at].wait_recv()
    for copy in plan:
        copy.wait_send()


CHUNK = 256
LINES = CHUNK // 2


def backward_kernel(
    counts,
    hid_h,
    cot_h,
    slope_h,
    n2_h,
    upw_h,
    std_h,
    n1_h,
    qkvw_h,
    down_nat,
    resid_h,
    attended_h,
    outw_h,
    mixed_h,
    std1_h,
    stats,
    marks,
    vec_all,
    inv1_own,
    down_bias,
    down_out,
    up_out,
    out_out,
    qkv_out,
    b_land,
    downw_land,
    out_block,
    tokens_block,
    small_out,
    cot,
    n2,
    std,
    part,
    tot,
    upw,
    hid,
    dup,
    attended,
    outw,
    mixed,
    std1_own,
    d_att,
    d_mix,
    dk_acc,
    dv_acc,
    g,
    s,
    t,
    r_land,
    m_land,
    got_a,
    diag_a,
    hx_a,
    hy_a,
    ts_a,
    fx_a,
    got_b,
    diag_b,
    hx_b,
    hy_b,
    ts_b,
    fx_b,
    dres_own,
    own_sum,
    sums,
    small,
    x_land,
    dp_land,
    stat_land,
    load_sem,
    credit,
    own_sem,
    z_send,
    z_recv,
    a_send,
    a_recv,
    p_send,
    p_recv,
):
    f32, bf16 = jnp.float32, jnp.bfloat16
    n_down, n_up, n_out, n_qkv = counts
    total = sum(counts)
    plane, row, col = lax.axis_index("dp"), lax.axis_index("row"), lax.axis_index("col")
    length, full = cot.shape
    rows, width = dres_own.shape
    row_count = full // width
    inner = (plane == 1) | (plane == 2)
    outer = jnp.logical_not(inner)
    to_inner = {"dp": plane // 3 + 1}
    to_middle = {"dp": 3 - plane}
    to_outer = {"dp": (plane - 1) * 3}
    side, core = row // 2, row % 2

    loads = [
        (hid_h, hid),
        (cot_h, cot),
        (slope_h, dup),
        (upw_h, upw),
        (n2_h, n2),
        (std_h, std),
        (qkvw_h, upw.at[:, : qkvw_h.shape[1]]),
        (n1_h, std),
        (downw_land, n2),
        (downw_land, tot),
        (resid_h, dres_own),
        (attended_h, attended),
        (outw_h, outw),
        (mixed_h, mixed),
        (std1_h, std1_own),
    ]
    loads = [pltpu.make_async_copy(a, b, load_sem.at[k]) for k, (a, b) in enumerate(loads)]
    for k in (0, 1, 2, 3, 4, 5, 11, 12, 13, 14):
        loads[k].start()

    dp_count = dp_land.shape[0]
    barrier = pltpu.get_barrier_semaphore()
    others = [{"row": (1 - side) * 2 + 1 - core}] + [{"dp": (plane + k) % dp_count} for k in range(1, dp_count)]
    for partner in partners() + tuple(others):
        pl.semaphore_signal(barrier, inc=1, device_id=partner, device_id_type=MESH)
    pl.semaphore_wait(barrier, 3 + len(others))

    units = hid.shape[1]
    down_sends, down_recvs = [], []
    for step in range(1, row_count):
        target, source = (row + step) % row_count, (row + row_count - step) % row_count
        here, there = downw_land.at[:, strip(row * width, width)], downw_land.at[:, strip(source * width, width)]
        piece = down_nat.at[strip(target * units, units), :]
        down_sends.append(put(piece, here, p_send, p_recv, 40 + step - 1, {"row": target}))
        down_recvs.append(put(piece, there, p_send, p_recv, 40 + step - 1, {"row": source}))
        down_sends[-1].start()
    down_own = pltpu.make_async_copy(
        down_nat.at[strip(row * units, units), :], downw_land.at[:, strip(row * width, width)], own_sem.at[4 * total]
    )
    down_own.start()

    def place(u, source):
        i, half, quarter = u // 4, u // 2 % 2, pl.ds(u % 2 * LINES, LINES)
        if i < n_down:
            return down_out.at[source * n_down + i // 2 * 2 + half, quarter, pl.ds(i % 2 * CHUNK, CHUNK)]
        i -= n_down
        if i < n_up:
            return up_out.at[half, quarter, strip(source * n_up * CHUNK + i * CHUNK, CHUNK)]
        i -= n_up
        if i < n_out:
            return out_out.at[source * n_out + i, quarter, pl.ds(half * CHUNK, CHUNK)]
        i -= n_out
        return qkv_out.at[half, quarter, strip(source * n_qkv * CHUNK + i * CHUNK, CHUNK)]

    g_slots, s_slots, t_slots, r_slots, m_slots = g.shape[0], s.shape[0], t.shape[0], r_land.shape[0], m_land.shape[0]
    pieces = 4 * total

    def made(u):
        return g.at[u // 4 % g_slots, :, u // 2 % 2, pl.ds(u % 2 * LINES, LINES)]

    def inward(u):
        return put(made(u), r_land.at[u % r_slots], z_send, z_recv, u, to_inner)

    def across(u):
        return put(s.at[u % s_slots], m_land.at[u % m_slots], z_send, z_recv, pieces + u, to_middle)

    def outward(u):
        return put(t.at[u % t_slots], b_land.at[u], z_send, z_recv, 2 * pieces + u, to_outer)

    def home(u, step, source):
        target = (row + step) % row_count
        return put(source.at[target], place(u, row), a_send, a_recv, 3 * u + step - 1, {"row": target})

    def home_own(u, source):
        return pltpu.make_async_copy(source.at[row], place(u, row), own_sem.at[u])

    def send_home(u, source):
        for step in range(1, row_count):
            home(u, step, source).start()
        home_own(u, source).start()

    def sent_home(u, source):
        for step in range(1, row_count):
            home(u, step, source).wait_send()
        home_own(u, source).wait()

    def produce(i):
        if i >= g_slots:

            @pl.when(outer)
            def _():
                for k in range(4):
                    inward(4 * (i - g_slots) + k).wait_send()

        slot = g.at[i % g_slots]
        if i < n_down:
            begin, lane = i // 2 * 2 * CHUNK, i % 2 * CHUNK

            def step(k, none):
                value = dot_tn(hid[:, begin : begin + 2 * CHUNK], cot[:, strip(k * width + lane, CHUNK)]).astype(bf16)
                slot[k, 0] = value[:CHUNK]
                slot[k, 1] = value[CHUNK:]
                return none
        elif n_down + n_up <= i < n_down + n_up + n_out:
            left, begin, right = attended, (i - n_down - n_up) * CHUNK, part

            def step(k, none):
                value = dot_tn(left[:, begin : begin + CHUNK], right[:, strip(k * width, width)]).astype(bf16)
                slot[k, 0] = value[:, :CHUNK]
                slot[k, 1] = value[:, CHUNK:]
                return none
        else:
            if i < n_down + n_up:
                left, right, begin = n2, dup, (i - n_down) * CHUNK
            else:
                left, right, begin = std, d_mix, (i - n_down - n_up - n_out) * CHUNK

            def step(k, none):
                value = dot_tn(left[:, strip(k * width, width)], right[:, begin : begin + CHUNK]).astype(bf16)
                slot[k, 0] = value[:CHUNK]
                slot[k, 1] = value[CHUNK:]
                return none

        lax.fori_loop(0, row_count, step, 0)

    def launch(u):
        @pl.when(outer)
        def _():
            if u >= r_slots:
                pl.semaphore_wait(credit, 1)
            inward(u).start()

    def add(first, second, target):
        for k in range(row_count):
            target[k] = (first[k].astype(f32) + second[k].astype(f32)).astype(bf16)

    def middle(u):
        @pl.when(inner)
        def _():
            inward(u).wait_recv()
            add(made(u), r_land.at[u % r_slots], s.at[u % s_slots])
            across(u).start()
            if u + r_slots < pieces:
                pl.semaphore_signal(credit, inc=1, device_id=to_outer, device_id_type=MESH)

    def finish_inner(u):
        @pl.when(inner)
        def _():
            if u >= t_slots:
                outward(u - t_slots).wait_send()
                sent_home(u - t_slots, t.at[u % t_slots])
            across(u).wait_recv()
            add(s.at[u % s_slots], m_land.at[u % m_slots], t.at[u % t_slots])
            outward(u).start()
            send_home(u, t.at[u % t_slots])
            across(u).wait_send()

    def finish_outer(u):
        @pl.when(outer)
        def _():
            outward(u).wait_recv()
            send_home(u, b_land.at[u])

    ahead = 4

    def pass_on(u):
        middle(u)
        if u >= 2:
            finish_inner(u - 2)
        if u + ahead < pieces:
            if u % 4 == 0:
                produce((u + ahead) // 4)
            launch(u + ahead)
        if u >= 3:
            finish_outer(u - 3)

    set_a = (got_a, diag_a, hx_a, hy_a, ts_a, fx_a)
    set_b = (got_b, diag_b, hx_b, hy_b, ts_b, fx_b)
    gain2 = vec_all[3:4, :]
    heads = mixed.shape[1] // (3 * HEAD)
    here = strip(row * width, width)
    tile = 64
    first = reduce_steps(part, own_sum, *set_a, p_send, p_recv, 0, mostly_x=True)
    second = spread_steps(tot, rows, width, p_send, p_recv, 10, mostly_x=True)
    third = reduce_steps(cot, own_sum, *set_b, p_send, p_recv, 20, mostly_x=True)
    fourth = reduce_steps(tot, own_sum, *set_a, p_send, p_recv, 30, mostly_x=True)

    def down_here():
        down_own.wait()
        for copy in down_recvs:
            copy.wait_recv()
        loads[9].start()

    def upper_step(k, none):
        down, across_ = k // (units // CHUNK), k % (units // CHUNK)
        at, lanes = strip(down * rows, rows), strip(across_ * CHUNK, CHUNK)
        dup[at, lanes] = (dot_nt(cot[at, :], tot[lanes, :]) * dup[at, lanes].astype(f32)).astype(bf16)
        return none

    def uppers(part_of):
        if part_of == 0:
            for k in (2, 3, 4, 9):
                loads[k].wait()
        count = (length // rows) * (units // CHUNK) // 2
        lax.fori_loop(part_of * count, (part_of + 1) * count, upper_step, 0)

    def d_normed2(part_of):
        tiled_nt(dup, upw, part, units, 1024, 256, (part_of, part_of + 1, 2))
        if part_of == 1:
            loads[6].start()
            next(first)

    def gather_start():
        next(first, None)
        block(tot, col, side, core, rows, width)[...] = own_sum[...].astype(bf16)
        next(second)

    def norm_step(k, none):
        at = strip(k * tile, tile)
        grad, standard, inverse = tot[at, :].astype(f32), std[at, :].astype(f32), stats[at, 0:1]
        scaled = grad * gain2
        mean_one = jnp.sum(scaled, axis=1, keepdims=True) / full
        mean_two = jnp.sum(scaled * standard, axis=1, keepdims=True) / full
        top = cot[at, :].astype(f32)
        low = (top + inverse * (scaled - mean_one - standard * mean_two)).astype(bf16)
        part[at, :] = low
        sums[0:1, :] += jnp.sum(grad * standard, axis=0, keepdims=True)
        sums[1:2, :] += jnp.sum(grad, axis=0, keepdims=True)
        sums[2:3, :] += jnp.sum(low.astype(f32), axis=0, keepdims=True)
        sums[3:4, :] += jnp.sum(top, axis=0, keepdims=True)

        @pl.when(k // (rows // tile) == col)
        def _():
            own = tot[at, here].astype(f32) * vec_all[3:4, here]
            dres_own[strip(k % (rows // tile) * tile, tile), :] = cot[at, here].astype(f32) + inverse * (
                own - mean_one - std[at, here].astype(f32) * mean_two
            )

        return none

    def norm_back(part_of):
        if part_of == 0:
            for k in (5, 11, 12, 13, 14):
                loads[k].wait()
        count = length // tile // 2
        lax.fori_loop(part_of * count, (part_of + 1) * count, norm_step, 0)
        if part_of == 1:
            loads[7].start()

    def d_attended():
        tiled_nt(part, outw, d_att, full, 512, 256)

    factor = 1.0 / math.sqrt(HEAD)
    blocks = length // SPAN
    spots = (SPAN, SPAN)
    earlier = lax.broadcasted_iota(jnp.int32, spots, 1) <= lax.broadcasted_iota(jnp.int32, spots, 0)

    def attention_back(head, begin, end):
        base = head * 3 * HEAD
        at_q, at_k, at_v = pl.ds(base, HEAD), pl.ds(base + HEAD, HEAD), pl.ds(base + 2 * HEAD, HEAD)
        at_o = pl.ds(head * HEAD, HEAD)
        if begin == 0:
            dk_acc[...] = jnp.zeros_like(dk_acc)
            dv_acc[...] = jnp.zeros_like(dv_acc)
        for k in range(begin, end):
            now = pl.ds(k * SPAN, SPAN)
            seen = (k + 1) * SPAN
            query, dout = mixed[now, at_q], d_att[now, at_o]
            keys, values = mixed[:seen, at_k], mixed[:seen, at_v]
            scores = dot_nt(query, keys) * factor
            last = jnp.where(earlier | (marks[k : k + 1, :1] > 0), scores[:, seen - SPAN :], masked_score)
            scores = last if k == 0 else jnp.concatenate([scores[:, : seen - SPAN], last], axis=1)
            probs = jnp.exp(scores - stats[now, 1 + head : 2 + head])
            d_probs = dot_nt(dout, values)
            dots = jnp.sum(probs * d_probs, axis=1, keepdims=True)
            d_scores = (probs * (d_probs - dots)).astype(bf16)
            d_mix[now, at_q] = (jnp.dot(d_scores, keys, preferred_element_type=f32) * factor).astype(bf16)
            dk_acc[:seen] += dot_tn(d_scores, query)
            dv_acc[:seen] += dot_tn(probs.astype(bf16), dout)
        if end == blocks:
            d_mix[:, at_k] = (dk_acc[...] * factor).astype(bf16)
            d_mix[:, at_v] = dv_acc[...].astype(bf16)

    def d_normed1(part_of):
        if part_of == 0:
            loads[6].wait()
        tiled_nt(d_mix, upw, cot, d_mix.shape[1], 1024, 256, (part_of, part_of + 1, 2))
        if part_of == 1:
            next(third)

    def output_sums(part_of):
        if part_of == 0:
            loads[8].wait()
        tiled_nn(hid, n2, tot, 1024, 256, (part_of, part_of + 1, 2))
        if part_of == 1:
            next(fourth)

    grad1 = own_sum
    stat_sends, stat_recvs, dp_sends, dp_recvs, row_sends, row_recvs = [], [], [], [], [], []
    for step in range(1, row_count):
        target, source = (row + step) % row_count, (row + row_count - step) % row_count
        to, since = {"row": target}, {"row": source}
        stat_sends.append(put(stat_land.at[row], stat_land.at[row], p_send, p_recv, 43 + step - 1, to))
        stat_recvs.append(put(stat_land.at[source], stat_land.at[source], p_send, p_recv, 43 + step - 1, since))
        row_sends.append(put(small_out.at[row], small_out.at[row], p_send, p_recv, 50 + step - 1, to))
        row_recvs.append(put(small_out.at[source], small_out.at[source], p_send, p_recv, 50 + step - 1, since))
    for step in range(1, dp_count):
        target, source = (plane + step) % dp_count, (plane + dp_count - step) % dp_count
        dp_sends.append(put(dp_land.at[plane], dp_land.at[plane], p_send, p_recv, 47 + step - 1, {"dp": target}))
        dp_recvs.append(put(dp_land.at[source], dp_land.at[source], p_send, p_recv, 47 + step - 1, {"dp": source}))
    x_copy = put(small.at[pl.ds(0, 8)], x_land, p_send, p_recv, 46, partners()[0])

    def row_stats():
        next(third, None)
        scaled = grad1[...] * vec_all[0:1, here]
        first_sum = jnp.sum(scaled, axis=1, keepdims=True)
        second_sum = jnp.sum(scaled * std1_own[...].astype(f32), axis=1, keepdims=True)
        lane = lax.broadcasted_iota(jnp.int32, (rows, 128), 1)
        pair = jnp.where(lane == 0, first_sum, jnp.where(lane == 1, second_sum, 0.0))
        stat_land[row] = pair.T[:8]
        for copy in stat_sends:
            copy.start()

    def small_sums():
        small[...] = jnp.zeros_like(small)
        small[0:1, :] = jnp.sum(grad1[...] * std1_own[...].astype(f32), axis=0, keepdims=True)
        small[1:2, :] = jnp.sum(grad1[...], axis=0, keepdims=True)
        small[2:6, :] = sums[0:4, here]
        totals = jnp.sum(dup[...].astype(f32), axis=0, keepdims=True)
        for k in range(units // width):
            small[8 + k : 9 + k, :] = totals[:, k * width : (k + 1) * width]
        mixes = jnp.sum(d_mix[...].astype(f32), axis=0, keepdims=True)
        spot = 8 + units // width
        picked = [
            mixes[:, (head * 3 + kind) * HEAD : (head * 3 + kind + 1) * HEAD] for head in range(heads) for kind in (0, 2)
        ]
        small[spot : spot + 1, : 2 * heads * HEAD] = jnp.concatenate(picked, axis=1)
        x_copy.start()

    def tokens_out():
        for copy in stat_recvs:
            copy.wait_recv()
        both = stat_land[0]
        for k in range(1, row_count):
            both = both + stat_land[k]
        both = jnp.concatenate([both, jnp.zeros((120, rows), f32)], axis=0).T
        scaled = grad1[...] * vec_all[0:1, here]
        d_norm1 = inv1_own[...] * (
            scaled - both[:, 0:1] / full - std1_own[...].astype(f32) * (both[:, 1:2] / full)
        )
        tokens_block[...] = (dres_own[...] + d_norm1).astype(bf16)
        loads[10].start()

    def dp_start():
        x_copy.wait_recv()
        x_copy.wait_send()
        small[0:2, :] += x_land[0:2, :]
        dp_land[plane] = small[...]
        for copy in dp_sends:
            copy.start()

    def output_out():
        next(fourth, None)
        loads[10].wait()
        out_block[...] = (dres_own[...] + (own_sum[...] + down_bias[...])).astype(bf16)

    def rows_start():
        for copy in dp_recvs:
            copy.wait_recv()
        together = dp_land[0]
        for k in range(1, dp_count):
            together = together + dp_land[k]
        small_out[row] = together
        for copy in row_sends:
            copy.start()

    tasks = {
        6: [down_here],
        8: [lambda: uppers(0)],
        9: [lambda: uppers(1)],
        10: [lambda: d_normed2(0)],
        11: [lambda: d_normed2(1)],
        13: [lambda: next(first)],
        16: [lambda: next(first)],
        19: [gather_start],
        22: [lambda: next(second)],
        24: [lambda: next(second)],
        25: [lambda: next(second, None), loads[8].start],
        26: [lambda: norm_back(0)],
        27: [lambda: norm_back(1)],
        28: [d_attended],
        29: [lambda: attention_back(0, 0, blocks)],
        30: [lambda: attention_back(1, 0, blocks)],
        31: [lambda: output_sums(0), loads[7].wait],
        32: [lambda: d_normed1(0)],
        33: [lambda: d_normed1(1)],
        34: [lambda: next(third)],
        35: [lambda: output_sums(1)],
        36: [lambda: next(fourth)],
        37: [lambda: next(third)],
        39: [lambda: next(fourth)],
        40: [row_stats],
        41: [small_sums],
        42: [tokens_out],
        43: [dp_start],
        44: [output_out],
        45: [rows_start],
    }
    sums[...] = jnp.zeros_like(sums)
    loads[0].wait()
    loads[1].wait()
    produce(0)
    for k in range(ahead):
        launch(k)
    for u in range(pieces):
        pass_on(u)
        for task in tasks.get(u, ()):
            task()
    finish_inner(pieces - 2)
    finish_inner(pieces - 1)
    finish_outer(pieces - 3)
    finish_outer(pieces - 2)
    finish_outer(pieces - 1)
    for copy in row_recvs:
        copy.wait_recv()
    for copy in down_sends + stat_sends + dp_sends + row_sends:
        copy.wait_send()

    @pl.when(outer)
    def _():
        for u in range(pieces - 4 * g_slots, pieces):
            inward(u).wait_send()
        for u in range(pieces):
            sent_home(u, b_land.at[u])

    @pl.when(inner)
    def _():
        for u in range(pieces - t_slots, pieces):
            outward(u).wait_send()
            sent_home(u, t.at[u % t_slots])

    for u in range(pieces):
        for step in range(1, row_count):
            source = (row + row_count - step) % row_count
            put(t.at[0, source], place(u, source), a_send, a_recv, 3 * u + step - 1, {"row": source}).wait_recv()


def backward_plane(
    cid, hid, cot, slope, n2, upw, std, n1, qkvw, down_nat, resid_own, attended, outw, mixed, std1_own, stats, marks, vec_all, inv1_own, down_bias
):
    f32, bf16 = jnp.float32, jnp.bfloat16
    length, full = cot.shape
    rows, width = length // lax.axis_size("col"), full // lax.axis_size("row")
    row_count, dp_count = full // width, lax.axis_size("dp")
    counts = (slope.shape[1] // CHUNK, slope.shape[1] // CHUNK, attended.shape[1] // CHUNK, mixed.shape[1] // CHUNK)
    total = sum(counts)
    unit = (row_count, LINES, CHUNK)
    shape = jax.ShapeDtypeStruct
    away, near = pl.BlockSpec(memory_space=pl.ANY), pl.BlockSpec(memory_space=pltpu.VMEM)
    vmem, dma = pltpu.VMEM, pltpu.SemaphoreType.DMA
    sets = [
        vmem((4, rows, width), bf16),
        vmem((rows, width), bf16),
        vmem((rows // 2, width), bf16),
        vmem((rows // 2, width), bf16),
        vmem((2, rows, width), bf16),
        vmem((2, rows, width), bf16),
    ]
    return pl.pallas_call(
        functools.partial(backward_kernel, counts),
        out_shape=[
            shape((row_count * counts[0], CHUNK, width), bf16),
            shape((2, CHUNK, row_count * counts[1] * CHUNK), bf16),
            shape((row_count * counts[2], CHUNK, width), bf16),
            shape((2, CHUNK, row_count * counts[3] * CHUNK), bf16),
            shape((4 * total,) + unit, bf16),
            shape((hid.shape[1], full), bf16),
            shape((rows, width), bf16),
            shape((rows, width), bf16),
            shape((row_count, 16, width), f32),
        ],
        in_specs=[away] * 14 + [near] * 5,
        out_specs=[away] * 6 + [near] * 3,
        scratch_shapes=[
            vmem((length, full), bf16),
            vmem((length, full), bf16),
            vmem((length, full), bf16),
            vmem((length, full), bf16),
            vmem((length, full), bf16),
            vmem(upw.shape, bf16),
            vmem(hid.shape, bf16),
            vmem(slope.shape, bf16),
            vmem(attended.shape, bf16),
            vmem(outw.shape, bf16),
            vmem(mixed.shape, bf16),
            vmem(std1_own.shape, bf16),
            vmem(attended.shape, bf16),
            vmem(mixed.shape, bf16),
            vmem((length, HEAD), f32),
            vmem((length, HEAD), f32),
            vmem((2, row_count, width // CHUNK, CHUNK, CHUNK), bf16),
            vmem((3,) + unit, bf16),
            vmem((4,) + unit, bf16),
            vmem((6,) + unit, bf16),
            vmem((6,) + unit, bf16),
        ]
        + sets
        + sets
        + [
            vmem((rows, width), f32),
            vmem((rows, width), f32),
            vmem((8, full), f32),
            vmem((16, width), f32),
            vmem((8, width), f32),
            vmem((dp_count, 16, width), f32),
            vmem((row_count, 8, rows), f32),
            dma((15,)),
            pltpu.SemaphoreType.REGULAR,
            dma((4 * total + 1,)),
            dma((12 * total,)),
            dma((12 * total,)),
            dma((12 * total,)),
            dma((12 * total,)),
            dma((53,)),
            dma((53,)),
        ],
        compiler_params=pltpu.CompilerParams(
            collective_id=cid, has_side_effects=True, vmem_limit_bytes=64 * 1024 * 1024 - 65536
        ),
        cost_estimate=pl.CostEstimate(flops=40_000_000_000, bytes_accessed=100_000_000, transcendentals=4_000_000),
    )(hid, cot, slope, n2, upw, std, n1, qkvw, down_nat, resid_own, attended, outw, mixed, std1_own, stats, marks, vec_all, inv1_own, down_bias)


class Moves:
    def __init__(self, source, target, cut, parts, sends, recvs, base):
        row, plane = lax.axis_index("row"), lax.axis_index("dp")
        side, core = row // 2, row % 2
        parity = plane % 2
        other = {"dp": plane + 1 - 2 * parity}
        twin = side * 2 + 1 - core
        far = ((1 - side) * 2 + core, (1 - side) * 2 + 1 - core)
        self.sibling = put(source(twin), target(row), sends, recvs, base, {"row": twin})
        self.sibling_in = put(source(twin), target(twin), sends, recvs, base, {"row": twin})
        self.outs, self.ins, self.passes, self.gets = [], [], [], []
        at = base + 1
        for step in range(parts // 2):
            for k, device in enumerate(far):
                mine, theirs = 2 * step + parity, 2 * step + 1 - parity
                there, here = cut(target(row), mine), cut(target(device), mine)
                self.outs.append(put(cut(source(device), mine), there, sends, recvs, at, {"row": device}))
                self.ins.append(put(cut(source(device), mine), here, sends, recvs, at, {"row": device}))
                self.passes.append(put(here, here, sends, recvs, at + 1, other))
                lands = cut(target(device), theirs)
                self.gets.append(put(lands, lands, sends, recvs, at + 1, other))
                at += 2

    @staticmethod
    def count(parts):
        return 1 + 2 * parts

    def start(self):
        self.sibling.start()
        self.start_far()

    def start_far(self):
        for copy in self.outs:
            copy.start()

    def forward(self, begin=0, end=None):
        for came, passed in list(zip(self.ins, self.passes))[begin:end]:
            came.wait_recv()
            passed.start()

    def finish(self):
        self.sibling_in.wait_recv()
        for copy in self.gets:
            copy.wait_recv()

    def drain(self):
        self.sibling.wait_send()
        for copy in self.outs + self.passes:
            copy.wait_send()


FAR_PARTS = 4


def forward_kernel(
    tokens,
    cot_in,
    ln1_gain,
    ln1_shift,
    out_bias_in,
    ln2_gain,
    ln2_shift,
    qv_bias,
    up_bias_in,
    spans,
    qkv_in,
    out_nat,
    up_nat,
    cot_all,
    n1_out,
    n2_out,
    std_out,
    upw_out,
    qkvw_out,
    outw_out,
    mixed_out,
    attended_out,
    hid_out,
    slope_out,
    stats,
    marks,
    vec_all,
    resid_own,
    std1_own,
    inv1_own,
    tok,
    n1,
    part,
    tot,
    qkvw,
    upw,
    outw,
    mixed,
    attended,
    hid,
    slope,
    own_sum,
    got,
    diag,
    hx,
    hy,
    ts,
    fx,
    qkv_raw,
    qkv_nat,
    mixed_bias,
    local_sem,
    w_send,
    w_recv,
    p_send,
    p_recv,
):
    f32, bf16 = jnp.float32, jnp.bfloat16
    plane, row, col = lax.axis_index("dp"), lax.axis_index("row"), lax.axis_index("col")
    side, core = row // 2, row % 2
    rows, width = tokens.shape
    length, full = tok.shape
    row_count = full // width
    heads_width = attended.shape[1]
    units = hid.shape[1]

    barrier = pltpu.get_barrier_semaphore()
    twins = ({"row": (1 - side) * 2 + 1 - core}, {"dp": plane + 1 - 2 * (plane % 2)})
    for partner in partners() + twins:
        pl.semaphore_signal(barrier, inc=1, device_id=partner, device_id_type=MESH)
    pl.semaphore_wait(barrier, 5)

    def cut_rows(ref, part):
        count = ref.shape[0] // FAR_PARTS
        return ref.at[strip(part * count, count)]

    per = qkvw.shape[1]
    count = Moves.count(FAR_PARTS)
    qkv_moves = Moves(
        lambda r: qkv_nat.at[:, strip(r * per, per)],
        lambda r: qkvw.at[strip(r * width, width), :],
        cut_rows,
        FAR_PARTS,
        w_send,
        w_recv,
        0,
    )
    out_moves = Moves(
        lambda r: out_nat.at[strip(r * heads_width, heads_width), :],
        lambda r: outw.at[:, strip(r * width, width)],
        cut_rows,
        FAR_PARTS,
        w_send,
        w_recv,
        count,
    )
    up_moves = Moves(
        lambda r: up_nat.at[:, strip(r * units, units)],
        lambda r: upw.at[strip(r * width, width), :],
        cut_rows,
        FAR_PARTS,
        w_send,
        w_recv,
        2 * count,
    )
    locals_ = [
        (qkv_nat.at[:, strip(row * per, per)], qkvw.at[strip(row * width, width), :]),
        (out_nat.at[strip(row * heads_width, heads_width), :], outw.at[:, strip(row * width, width)]),
        (up_nat.at[:, strip(row * units, units)], upw.at[strip(row * width, width), :]),
        (cot_in, block(cot_all, col, side, core, rows, width)),
        (n1, n1_out),
        (part, n2_out),
        (n1, std_out),
        (upw, upw_out),
        (qkvw, qkvw_out),
        (outw, outw_out),
        (mixed, mixed_out),
        (attended, attended_out),
        (hid, hid_out),
        (slope, slope_out),
        (qkv_in, qkv_raw),
    ]
    local = [pltpu.make_async_copy(a, b, local_sem.at[k]) for k, (a, b) in enumerate(locals_)]
    local[14].start()
    for k in range(1, 4):
        local[k].start()

    block(tok, col, side, core, rows, width)[...] = tokens[...]
    gather = spread_steps(tok, rows, width, p_send, p_recv, 0)
    next(gather)
    here = strip(row * width, width)
    vec_all[:, here] = jnp.zeros((vec_all.shape[0], width), f32)
    for k, vector in enumerate((ln1_gain, ln1_shift, out_bias_in, ln2_gain, ln2_shift)):
        vec_all[k : k + 1, here] = vector[...]
    vec_sends, vec_recvs = [], []
    for step in range(1, row_count):
        target, source = (row + step) % row_count, (row + row_count - step) % row_count
        here, there = vec_all.at[:, strip(row * width, width)], vec_all.at[:, strip(source * width, width)]
        vec_sends.append(put(here, here, p_send, p_recv, 10 + step - 1, {"row": target}))
        vec_recvs.append(put(there, there, p_send, p_recv, 10 + step - 1, {"row": source}))
        vec_sends[-1].start()
    out_moves.sibling.start()
    up_moves.sibling.start()
    local[14].wait()
    for kind in range(3):
        flat = qkv_raw[:, kind].reshape(width, qkv_raw.shape[2] * HEAD)
        for head in range(qkv_raw.shape[2]):
            qkv_nat[:, pl.ds((head * 3 + kind) * HEAD, HEAD)] = flat[:, head * HEAD : (head + 1) * HEAD]
    local[0].start()
    qkv_moves.sibling.start()
    next(gather)
    qkv_moves.start_far()
    next(gather)
    next(gather, None)
    for copy in vec_recvs:
        copy.wait_recv()
    lines = lax.broadcasted_iota(jnp.int32, marks.shape, 0) * SPAN
    found = jnp.zeros(marks.shape, f32)
    for k in range(spans.shape[1]):
        found = jnp.where(lines == spans[0:1, k : k + 1] // SPAN * SPAN, 1.0, found)
    marks[...] = found

    tile = 64
    gain1, shift1 = vec_all[0:1, :], vec_all[1:2, :]

    def norm1_step(k, none):
        at = strip(k * tile, tile)
        values = tok[at, :].astype(f32)
        center = jnp.sum(values, axis=1, keepdims=True) / full
        inverse = lax.rsqrt(jnp.sum(values * values, axis=1, keepdims=True) / full - center * center + epsilon)
        n1[at, :] = ((values - center) * inverse * gain1 + shift1).astype(bf16)

        @pl.when(k // (rows // tile) == col)
        def _():
            here = strip(k % (rows // tile) * tile, tile)
            std1_own[here, :] = ((tok[at, strip(row * width, width)].astype(f32) - center) * inverse).astype(bf16)
            inv1_own[here, :] = inverse

        return none

    half_steps = length // tile // 2
    lax.fori_loop(0, half_steps, norm1_step, 0)
    qkv_moves.forward(0, 2)
    lax.fori_loop(half_steps, 2 * half_steps, norm1_step, 0)
    local[4].start()
    qkv_moves.forward(2, 4)
    out_moves.start_far()
    up_moves.start_far()
    qkv_moves.finish()
    local[0].wait()

    mixed_bias[...] = jnp.zeros_like(mixed_bias)
    for head in range(heads_width // HEAD):
        for k in range(2):
            lanes = pl.ds((head * 3 + 2 * k) * HEAD, HEAD)
            mixed_bias[:, lanes] = qv_bias[row * (heads_width // HEAD) + head, k : k + 1, :]
    up_bias = up_bias_in.at[:, strip(row * units, units)]

    def mixed_step(k, none):
        down, across = k // (per // CHUNK), k % (per // CHUNK)
        at, lanes = strip(down * rows, rows), strip(across * CHUNK, CHUNK)
        value = jnp.dot(n1[at, :], qkvw[:, lanes], preferred_element_type=f32)
        mixed[at, lanes] = (value + mixed_bias[:, lanes]).astype(bf16)
        return none

    lax.fori_loop(0, (length // rows) * (per // CHUNK), mixed_step, 0)
    local[8].start()
    local[10].start()
    local[4].wait()

    heads = heads_width // HEAD
    factor = 1.0 / math.sqrt(HEAD)
    blocks = length // SPAN
    spots = (SPAN, SPAN)
    earlier = lax.broadcasted_iota(jnp.int32, spots, 1) <= lax.broadcasted_iota(jnp.int32, spots, 0)

    def head_step(head, none):
        base = head * 3 * HEAD
        at_q, at_k, at_v = strip(base, HEAD), strip(base + HEAD, HEAD), strip(base + 2 * HEAD, HEAD)
        for k in range(blocks):
            here = pl.ds(k * SPAN, SPAN)
            seen = (k + 1) * SPAN
            scores = dot_nt(mixed[here, at_q], mixed[:seen, at_k]) * factor
            last = jnp.where(earlier | (marks[k : k + 1, :1] > 0), scores[:, seen - SPAN :], masked_score)
            scores = last if k == 0 else jnp.concatenate([scores[:, : seen - SPAN], last], axis=1)
            highest = jnp.max(scores, axis=1, keepdims=True)
            weights = jnp.exp(scores - highest)
            weight_sum = jnp.sum(weights, axis=1, keepdims=True)
            stats[here, 1 + head : 2 + head] = highest + jnp.log(weight_sum)
            value = jnp.dot((weights / weight_sum).astype(bf16), mixed[:seen, at_v], preferred_element_type=f32)
            attended[here, strip(head * HEAD, HEAD)] = value.astype(bf16)
        return none

    for head in range(heads):
        head_step(head, 0)
    local[11].start()
    out_moves.forward()
    up_moves.forward(0, 4)
    out_moves.finish()
    local[1].wait()
    tiled_nn(attended, outw, part, rows, 512)
    local[9].start()
    add_up = reduce_steps(part, own_sum, got, diag, hx, hy, ts, fx, p_send, p_recv, 13)
    next(add_up)
    next(add_up)
    up_moves.forward(4, 8)
    next(add_up)
    next(add_up, None)
    block(tot, col, side, core, rows, width)[...] = own_sum[...].astype(bf16)
    again = spread_steps(tot, rows, width, p_send, p_recv, 23)
    for k in range(3):
        next(again)
    next(again, None)
    local[3].wait()
    cot_gather = spread_steps(cot_all, rows, width, p_send, p_recv, 33)
    next(cot_gather)

    gain2, shift2, out_bias = vec_all[3:4, :], vec_all[4:5, :], vec_all[2:3, :]

    def norm2_step(k, none):
        at = strip(k * tile, tile)
        values = tok[at, :].astype(f32) + (tot[at, :].astype(f32) + out_bias)
        center = jnp.sum(values, axis=1, keepdims=True) / full
        inverse = lax.rsqrt(jnp.sum(values * values, axis=1, keepdims=True) / full - center * center + epsilon)
        standard = (values - center) * inverse
        stats[at, 0:1] = inverse
        n1[at, :] = standard.astype(bf16)
        part[at, :] = (standard * gain2 + shift2).astype(bf16)

        @pl.when(k // (rows // tile) == col)
        def _():
            own = strip(row * width, width)
            here = strip(k % (rows // tile) * tile, tile)
            resid_own[here, :] = tok[at, own].astype(f32) + (tot[at, own].astype(f32) + vec_all[2:3, own])

        return none

    lax.fori_loop(0, 2 * half_steps, norm2_step, 0)
    local[5].start()
    local[6].start()
    next(cot_gather)
    up_moves.finish()
    local[2].wait()
    local[7].start()

    def up_step(k, none):
        down, across = k // (units // CHUNK), k % (units // CHUNK)
        at, lanes = strip(down * rows, rows), strip(across * CHUNK, CHUNK)
        u = jnp.dot(part[at, :], upw[:, lanes], preferred_element_type=f32) + up_bias[:, lanes]
        bent = jnp.tanh(0.7978845608028654 * (u + 0.044715 * u * u * u))
        hid[at, lanes] = (0.5 * u * (1.0 + bent)).astype(bf16)
        inside = 0.7978845608028654 * (1.0 + 3 * 0.044715 * u * u)
        slope[at, lanes] = (0.5 * (1.0 + bent) + 0.5 * u * (1.0 - bent * bent) * inside).astype(bf16)
        return none

    lax.fori_loop(0, (length // rows) * (units // CHUNK), up_step, 0)
    local[12].start()
    local[13].start()
    next(cot_gather)
    next(cot_gather, None)
    for k in range(5, 14):
        local[k].wait()
    for moves in (qkv_moves, out_moves, up_moves):
        moves.drain()
    for copy in vec_sends:
        copy.wait_send()


def forward_plane(cid, tokens, cot, vectors, qv_bias, up_bias, spans, qkv_in, out_nat, up_nat):
    f32, bf16 = jnp.float32, jnp.bfloat16
    rows, width = tokens.shape
    row_count = lax.axis_size("row")
    length, full = rows * lax.axis_size("col"), width * row_count
    per, heads_width, units = qkv_in.shape[1] * qkv_in.shape[2] * HEAD // row_count, out_nat.shape[0] // row_count, up_nat.shape[1] // row_count
    shape = jax.ShapeDtypeStruct
    away, near = pl.BlockSpec(memory_space=pl.ANY), pl.BlockSpec(memory_space=pltpu.VMEM)
    vmem, dma = pltpu.VMEM, pltpu.SemaphoreType.DMA
    wide = shape((length, full), bf16)
    moved = 3 * Moves.count(FAR_PARTS)
    return pl.pallas_call(
        forward_kernel,
        out_shape=[
            wide,
            wide,
            wide,
            wide,
            shape((full, units), bf16),
            shape((full, per), bf16),
            shape((heads_width, full), bf16),
            shape((length, per), bf16),
            shape((length, heads_width), bf16),
            shape((length, units), bf16),
            shape((length, units), bf16),
            shape((length, 8), f32),
            shape((8, 128), f32),
            shape((8, full), f32),
            shape((rows, width), f32),
            shape((rows, width), bf16),
            shape((rows, 1), f32),
        ],
        in_specs=[near] * (5 + len(vectors)) + [away] * 3,
        out_specs=[away] * 11 + [near] * 6,
        scratch_shapes=[
            vmem((length, full), bf16),
            vmem((length, full), bf16),
            vmem((length, full), bf16),
            vmem((length, full), bf16),
            vmem((full, per), bf16),
            vmem((full, units), bf16),
            vmem((heads_width, full), bf16),
            vmem((length, per), bf16),
            vmem((length, heads_width), bf16),
            vmem((length, units), bf16),
            vmem((length, units), bf16),
            vmem((rows, width), f32),
            vmem((4, rows, width), bf16),
            vmem((rows, width), bf16),
            vmem((rows // 2, width), bf16),
            vmem((rows // 2, width), bf16),
            vmem((2, rows, width), bf16),
            vmem((2, rows, width), bf16),
            vmem(qkv_in.shape, bf16),
            vmem((width, row_count * per), bf16),
            vmem((1, per), f32),
            dma((15,)),
            dma((moved,)),
            dma((moved,)),
            dma((43,)),
            dma((43,)),
        ],
        compiler_params=pltpu.CompilerParams(
            collective_id=cid, has_side_effects=True, vmem_limit_bytes=60 * 1024 * 1024
        ),
        cost_estimate=pl.CostEstimate(flops=10_000_000_000, bytes_accessed=60_000_000, transcendentals=4_000_000),
    )(tokens, cot, *[vector[None] for vector in vectors], qv_bias, up_bias[None], spans, qkv_in, out_nat, up_nat)


def results_kernel(
    down, up, out, output, tokens, qkv, small, down_result, up_result, out_result, output_result, tokens_result, qkv_result, *vectors
):
    *sums, up_bias, qv_bias = vectors
    f32 = jnp.float32
    down_result[...] = down[...].astype(f32)
    up_result[...] = up[...].astype(f32)
    out_result[...] = out[...].astype(f32)
    output_result[...] = output[...]
    tokens_result[...] = tokens[...]
    for head in range(qkv_result.shape[2]):
        for kind in range(3):
            begin = (head * 3 + kind) * HEAD
            qkv_result[:, kind, head, :] = qkv[:, begin : begin + HEAD].astype(f32)

    @pl.when(pl.program_id(0) == 0)
    def _():
        row = lax.axis_index("row")
        for k, result in enumerate(sums):
            result[...] = small[row, k : k + 1, :]
        count, _, width = small.shape
        lines = up_bias.shape[1] // (count * width)
        heads = qv_bias.shape[0] // count
        for source in range(count):
            for k in range(lines):
                begin = (source * lines + k) * width
                up_bias[:, begin : begin + width] = small[source, 8 + k : 9 + k, :]
            for head in range(heads):
                for k in range(2):
                    begin = (head * 2 + k) * HEAD
                    line = small[source, 8 + lines : 9 + lines, begin : begin + HEAD]
                    qv_bias[source * heads + head, k : k + 1, :] = line


def results(down, up, out, output, tokens, qkv, small):
    f32 = jnp.float32
    shape = jax.ShapeDtypeStruct
    rows, heads = qkv.shape[0], qkv.shape[1] // (3 * HEAD)
    width, units = small.shape[2], up.shape[1]
    steps = 8

    def cut(array):
        return pl.BlockSpec((array.shape[0] // steps, array.shape[1]), lambda k: (k, 0))

    def whole(*dims):
        return pl.BlockSpec(dims, lambda k: (0,) * len(dims))

    line = whole(1, width)
    *made, up_bias, qv_bias = pl.pallas_call(
        results_kernel,
        grid=(steps,),
        out_shape=[shape(a.shape, f32) for a in (down, up, out)]
        + [shape(a.shape, a.dtype) for a in (output, tokens)]
        + [shape((rows, 3, heads, HEAD), f32)]
        + [shape((1, width), f32)] * 6
        + [shape((1, units), f32), shape((heads, 2, HEAD), f32)],
        in_specs=[cut(a) for a in (down, up, out, output, tokens, qkv)] + [whole(*small.shape)],
        out_specs=[cut(a) for a in (down, up, out, output, tokens)]
        + [pl.BlockSpec((rows // steps, 3, heads, HEAD), lambda k: (k, 0, 0, 0))]
        + [line] * 6
        + [whole(1, units), whole(heads, 2, HEAD)],
        compiler_params=pltpu.CompilerParams(vmem_limit_bytes=63 * 1024 * 1024),
    )(down, up, out, output, tokens, qkv, small)
    made[5] = jnp.swapaxes(made[5], 1, 2)
    return made[:6], [sums[0] for sums in made[6:]], up_bias[0], qv_bias


def plane_plan(
    tokens,
    ln1_gain,
    ln1_shift,
    qkv_weight,
    qv_bias,
    out_weight,
    out_bias,
    ln2_gain,
    ln2_shift,
    up_weight,
    up_bias,
    down_weight,
    down_bias,
    span_starts,
    cotangent,
):
    width = tokens.shape[1]
    (
        cot_all, n1, n2, standard2, upw, qkvw, outw, mixed, attended, hidden, slope,
        stats, marks, vec_all, residual_own, standard1_own, inverse1_own,
    ) = forward_plane(
        1,
        tokens,
        cotangent,
        (ln1_gain, ln1_shift, out_bias, ln2_gain, ln2_shift),
        qv_bias,
        up_bias,
        span_starts,
        jnp.swapaxes(qkv_weight, 1, 2),
        out_weight.reshape(-1, width),
        up_weight,
    )
    down_grad, up_grad, out_grad, qkv_grad, _, _, output, tokens_grad, small = backward_plane(
        2, hidden, cot_all, slope, n2, upw, standard2, n1, qkvw, down_weight, residual_own, attended, outw, mixed, standard1_own,
        stats, marks, vec_all, inverse1_own, down_bias[None],
    )
    grads, sums, up_bias_grad, qv_bias_grad = results(
        down_grad.reshape(-1, width), up_grad.reshape(width, -1), out_grad.reshape(-1, width), output, tokens_grad,
        qkv_grad.reshape(width, -1), small
    )
    return (
        grads[3],
        grads[4],
        sums[0],
        sums[1],
        grads[5],
        qv_bias_grad,
        grads[2].reshape(out_weight.shape),
        sums[4],
        sums[2],
        sums[3],
        grads[1],
        up_bias_grad,
        grads[0],
        sums[5],
    )


def solution(mesh):
    sizes = dict(mesh.shape)
    flat = sizes == {"dp": 4, "row": 4, "col": 2}
    per_device = plane_plan if flat else general_plan
    placed = (
        P(("dp", "col"), "row"),
        P("row"),
        P("row"),
        P("row", "col", None, None),
        P("col", None, None),
        P("col", None, "row"),
        P("row"),
        P("row"),
        P("row"),
        P("row", "col"),
        P("col"),
        P("col", "row"),
        P("row"),
        P("dp", None),
        P(("dp", "col"), "row"),
    )
    return jax.shard_map(
        per_device,
        mesh=mesh,
        in_specs=placed,
        out_specs=(
            P(("dp", "col"), "row"),
            P(("dp", "col"), "row"),
            P("row"),
            P("row"),
            P("row", "col", None, None),
            P("col", None, None),
            P("col", None, "row"),
            P("row"),
            P("row"),
            P("row"),
            P("row", "col"),
            P("col"),
            P("col", "row"),
            P("row"),
        ),
        check_vma=False,
    )
```

```python
import functools
import math

import jax
import jax.numpy as jnp
from jax import lax
from jax.experimental import pallas as pl
from jax.experimental.pallas import tpu as pltpu
from jax.sharding import PartitionSpec as P

MESH = pl.DeviceIdType.MESH

D = 2048
HEAD = 128
SEQS = 1
SPAN = 256
BLOCK = 512


epsilon = 1e-05
masked_score = -1e30


def gelu_tanh(values):
    return (
        0.5
        * values
        * (1.0 + jnp.tanh(0.7978845608028654 * (values + 0.044715 * values * values * values)))
    )


def gather_columns(block_data):
    return lax.all_gather(block_data, "col", axis=0, tiled=True)


def gather_rows(block_data):
    return lax.all_gather(block_data, "row", axis=0, tiled=True)


def product(left_side, right_side, flipped):
    if flipped:
        return lax.dot_general(
            left_side, right_side, (((1,), (1,)), ((), ())), preferred_element_type=jnp.float32
        )
    return jnp.dot(left_side, right_side, preferred_element_type=jnp.float32)


def outer_sum(left_side, right_side):
    return lax.dot_general(
        left_side, right_side, (((0,), (0,)), ((), ())), preferred_element_type=jnp.float32
    )


def sum_rows(left_side, right_side, flipped):
    wide_left = lax.all_to_all(left_side, "row", split_axis=0, concat_axis=1, tiled=True)
    if flipped:
        wide_right = lax.all_gather(right_side, "row", axis=1, tiled=True)
    else:
        wide_right = lax.all_gather(right_side, "row", axis=0, tiled=True)
    return product(wide_left, wide_right, flipped)


def sum_columns(left_side, right_side, flipped):
    return lax.psum_scatter(
        product(left_side, right_side, flipped), "col", scatter_dimension=0, tiled=True
    )


def row_totals(first_sum, second_sum):
    return lax.psum((first_sum, second_sum), "row")


def norm_forward(values, gain_row, bias_row):
    totals, squares = row_totals(jnp.sum(values, axis=1), jnp.sum(values * values, axis=1))
    center = totals / D
    spread = squares / D - center * center
    inverse = lax.rsqrt(spread + epsilon)
    standard = (values - center[:, None]) * inverse[:, None]
    return (standard, inverse, (standard * gain_row + bias_row).astype(jnp.bfloat16))


def norm_backward(upstream, standard, inverse, gain_row):
    scaled = upstream * gain_row
    first_sum, second_sum = row_totals(jnp.sum(scaled, axis=1), jnp.sum(scaled * standard, axis=1))
    gradient = inverse[:, None] * (
        scaled - first_sum[:, None] / D - standard * (second_sum[:, None] / D)
    )
    return (gradient, jnp.sum(upstream * standard, axis=0), jnp.sum(upstream, axis=0))


def visible(query_pos, query_image, key_pos):
    earlier = key_pos[None, :] <= query_pos[:, None]
    same_span = (key_pos[None, :] // SPAN == query_pos[:, None] // SPAN) & (
        query_image[:, None] > 0
    )
    return earlier | same_span


def attention_forward(queries, key_value, token_image, row_offset, seq_length, block_rows):
    own_rows, head_count, width = queries.shape
    factor = 1.0 / math.sqrt(width)

    def block_forward(block_index):
        local = block_index * block_rows
        start_pos = row_offset + local
        query_block = lax.dynamic_slice_in_dim(queries, local, block_rows, 0)
        query_pos = start_pos + jnp.arange(block_rows, dtype=jnp.int32)
        query_image = lax.dynamic_slice_in_dim(token_image, start_pos, block_rows, 0)
        begin = start_pos // seq_length * seq_length // block_rows
        finish = start_pos // block_rows + 1

        def key_step(key_index, state_in):
            running, weight_sum, gathered = state_in
            key_begin = key_index * block_rows
            key_block = lax.dynamic_slice_in_dim(key_value, key_begin, block_rows, 0)
            key_pos = key_begin + jnp.arange(block_rows, dtype=jnp.int32)
            allowed = visible(query_pos, query_image, key_pos)
            scores = (
                jnp.einsum(
                    "qhd,khd->hqk",
                    query_block,
                    key_block[:, :, 0],
                    preferred_element_type=jnp.float32,
                )
                * factor
            )
            scores = jnp.where(allowed[None], scores, masked_score)
            highest = jnp.maximum(running, jnp.max(scores, axis=2))
            weights = jnp.exp(scores - highest[:, :, None])
            shrink = jnp.exp(running - highest)
            weight_sum = weight_sum * shrink + jnp.sum(weights, axis=2)
            gathered = gathered * shrink.T[:, :, None] + jnp.einsum(
                "hqk,khd->qhd",
                weights.astype(jnp.bfloat16),
                key_block[:, :, 1],
                preferred_element_type=jnp.float32,
            )
            return (highest, weight_sum, gathered)

        initial = (
            jnp.full((head_count, block_rows), masked_score, jnp.float32),
            jnp.zeros((head_count, block_rows), jnp.float32),
            jnp.zeros((block_rows, head_count, width), jnp.float32),
        )
        running, weight_sum, gathered = lax.fori_loop(begin, finish, key_step, initial)
        return (gathered / weight_sum.T[:, :, None], running + jnp.log(weight_sum))

    result, logsum = lax.map(block_forward, jnp.arange(own_rows // block_rows, dtype=jnp.int32))
    return (result.reshape(own_rows, head_count, width), logsum)


def attention_backward(
    queries,
    key_value,
    attended_full,
    logsum,
    d_attended,
    token_image,
    row_offset,
    seq_length,
    block_rows,
):
    own_rows, head_count, width = queries.shape
    factor = 1.0 / math.sqrt(width)
    row_dots = jnp.sum(d_attended.astype(jnp.float32) * attended_full, axis=2)

    def block_backward(block_index, state_out):
        d_queries, d_pairs = state_out
        local = block_index * block_rows
        start_pos = row_offset + local
        query_block = lax.dynamic_slice_in_dim(queries, local, block_rows, 0)
        dout_block = lax.dynamic_slice_in_dim(d_attended, local, block_rows, 0)
        dots_block = lax.dynamic_slice_in_dim(row_dots, local, block_rows, 0).T
        logsum_block = logsum[block_index]
        query_pos = start_pos + jnp.arange(block_rows, dtype=jnp.int32)
        query_image = lax.dynamic_slice_in_dim(token_image, start_pos, block_rows, 0)
        begin = start_pos // seq_length * seq_length // block_rows
        finish = start_pos // block_rows + 1

        def key_step(key_index, state_in):
            d_query, d_keys = state_in
            key_begin = key_index * block_rows
            key_block = lax.dynamic_slice_in_dim(key_value, key_begin, block_rows, 0)
            key_pos = key_begin + jnp.arange(block_rows, dtype=jnp.int32)
            allowed = visible(query_pos, query_image, key_pos)
            scores = (
                jnp.einsum(
                    "qhd,khd->hqk",
                    query_block,
                    key_block[:, :, 0],
                    preferred_element_type=jnp.float32,
                )
                * factor
            )
            scores = jnp.where(allowed[None], scores, masked_score)
            probabilities = jnp.exp(scores - logsum_block[:, :, None])
            d_probs = jnp.einsum(
                "qhd,khd->hqk", dout_block, key_block[:, :, 1], preferred_element_type=jnp.float32
            )
            d_scores = (probabilities * (d_probs - dots_block[:, :, None])).astype(jnp.bfloat16)
            d_query = d_query + jnp.einsum(
                "hqk,khd->qhd", d_scores, key_block[:, :, 0], preferred_element_type=jnp.float32
            )
            d_key = (
                jnp.einsum(
                    "hqk,qhd->khd", d_scores, query_block, preferred_element_type=jnp.float32
                )
                * factor
            )
            d_value = jnp.einsum(
                "hqk,qhd->khd",
                probabilities.astype(jnp.bfloat16),
                dout_block,
                preferred_element_type=jnp.float32,
            )
            previous = lax.dynamic_slice_in_dim(d_keys, key_begin, block_rows, 0)
            d_keys = lax.dynamic_update_slice_in_dim(
                d_keys, previous + jnp.stack([d_key, d_value], axis=2), key_begin, 0
            )
            return (d_query, d_keys)

        d_query, d_pairs = lax.fori_loop(
            begin,
            finish,
            key_step,
            (jnp.zeros((block_rows, head_count, width), jnp.float32), d_pairs),
        )
        d_queries = lax.dynamic_update_slice_in_dim(d_queries, d_query * factor, local, 0)
        return (d_queries, d_pairs)

    initial = (
        jnp.zeros((own_rows, head_count, width), jnp.float32),
        jnp.zeros((key_value.shape[0], head_count, 2, width), jnp.float32),
    )
    return lax.fori_loop(0, own_rows // block_rows, block_backward, initial)


def general_plan(
    tokens,
    ln1_gain,
    ln1_shift,
    qkv_weight,
    qv_bias,
    out_weight,
    out_bias,
    ln2_gain,
    ln2_shift,
    up_weight,
    up_bias,
    down_weight,
    down_bias,
    span_starts,
    cotangent,
):
    col_rows, row_width = tokens.shape
    group_rows = col_rows * lax.axis_size("col")
    own_rows = group_rows // lax.axis_size("row")
    head_count = qkv_weight.shape[1]
    seq_length = group_rows // SEQS
    block_rows = BLOCK - own_rows % BLOCK
    row_offset = lax.axis_index("row") * own_rows
    slot_count = seq_length // SPAN
    image_marks = jnp.sum(
        (
            span_starts[:, :, None] // SPAN
            == jnp.arange(slot_count, dtype=jnp.int32)[None, None, :]
        ).astype(jnp.int32),
        axis=1,
    )
    token_image = jnp.broadcast_to(
        image_marks.reshape(-1)[:, None], (group_rows // SPAN, SPAN)
    ).reshape(group_rows)
    qkv_flat = qkv_weight.reshape(row_width, head_count * 3 * HEAD)
    out_flat = out_weight.reshape(head_count * HEAD, row_width)
    inputs = tokens.astype(jnp.float32)
    standard1, inverse1, normed1 = norm_forward(inputs, ln1_gain, ln1_shift)
    normed1_all = gather_columns(normed1)
    mixed_sums = sum_rows(normed1_all, qkv_flat, False).reshape(own_rows, head_count, 3, HEAD)
    queries = (mixed_sums[:, :, 0] + qv_bias[:, 0]).astype(jnp.bfloat16)
    key_value_own = jnp.stack(
        [mixed_sums[:, :, 1], mixed_sums[:, :, 2] + qv_bias[:, 1]], axis=2
    ).astype(jnp.bfloat16)
    key_value = gather_rows(key_value_own)
    attended_full, logsum = attention_forward(
        queries, key_value, token_image, row_offset, seq_length, block_rows
    )
    attended = attended_full.astype(jnp.bfloat16).reshape(own_rows, head_count * HEAD)
    attended_all = gather_rows(attended)
    residual = inputs + (sum_columns(attended_all, out_flat, False) + out_bias)
    standard2, inverse2, normed2 = norm_forward(residual, ln2_gain, ln2_shift)
    normed2_all = gather_columns(normed2)
    up_sums = sum_rows(normed2_all, up_weight, False) + up_bias
    hidden = gelu_tanh(up_sums).astype(jnp.bfloat16)
    hidden_all = gather_rows(hidden)
    output = (residual + (sum_columns(hidden_all, down_weight, False) + down_bias)).astype(
        jnp.bfloat16
    )
    d_output = cotangent.astype(jnp.float32)
    d_output_all = gather_columns(cotangent)
    down_grad = outer_sum(hidden_all, d_output_all)
    down_bias_grad = jnp.sum(d_output_all, axis=0, dtype=jnp.float32)
    d_hidden = sum_rows(d_output_all, down_weight, True)
    d_upper = jax.vjp(gelu_tanh, up_sums)[1](d_hidden)[0].astype(jnp.bfloat16)
    d_upper_all = gather_rows(d_upper)
    normed2_use = gather_columns(normed2)
    up_grad = outer_sum(normed2_use, d_upper_all)
    up_bias_grad = jnp.sum(d_upper_all, axis=0, dtype=jnp.float32)
    d_normed2 = sum_columns(d_upper_all, up_weight, True)
    d_norm2, gain2_grad, shift2_grad = norm_backward(d_normed2, standard2, inverse2, ln2_gain)
    d_residual = d_output + d_norm2
    d_branch = d_residual.astype(jnp.bfloat16)
    d_branch_all = gather_columns(d_branch)
    out_grad = outer_sum(attended_all, d_branch_all)
    out_bias_grad = jnp.sum(d_branch_all, axis=0, dtype=jnp.float32)
    d_attended = (
        sum_rows(d_branch_all, out_flat, True)
        .astype(jnp.bfloat16)
        .reshape(own_rows, head_count, HEAD)
    )
    d_queries, d_pairs = attention_backward(
        queries,
        key_value,
        attended_full,
        logsum,
        d_attended,
        token_image,
        row_offset,
        seq_length,
        block_rows,
    )
    d_pairs_own = lax.psum_scatter(d_pairs, "row", scatter_dimension=0, tiled=True)
    d_mixed = jnp.concatenate([d_queries[:, :, None], d_pairs_own], axis=2).astype(jnp.bfloat16)
    d_mixed_all = gather_rows(d_mixed)
    normed1_use = gather_columns(normed1)
    d_mixed_flat = d_mixed_all.reshape(group_rows, head_count * 3 * HEAD)
    qkv_grad = outer_sum(normed1_use, d_mixed_flat)
    mixed_totals = jnp.sum(d_mixed_all, axis=0, dtype=jnp.float32)
    qv_bias_grad = jnp.stack([mixed_totals[:, 0], mixed_totals[:, 2]], axis=1)
    d_normed1 = sum_columns(d_mixed_flat, qkv_flat, True)
    d_norm1, gain1_grad, shift1_grad = norm_backward(d_normed1, standard1, inverse1, ln1_gain)
    tokens_grad = (d_residual + d_norm1).astype(jnp.bfloat16)
    norm_sums = lax.psum((gain1_grad, shift1_grad, gain2_grad, shift2_grad), ("dp", "col"))
    weight_sums = lax.psum(
        (
            qkv_grad,
            qv_bias_grad,
            out_grad,
            out_bias_grad,
            up_grad,
            up_bias_grad,
            down_grad,
            down_bias_grad,
        ),
        "dp",
    )
    return (
        output,
        tokens_grad,
        norm_sums[0],
        norm_sums[1],
        weight_sums[0].reshape(row_width, head_count, 3, HEAD),
        weight_sums[1],
        weight_sums[2].reshape(head_count, HEAD, row_width),
        weight_sums[3],
        norm_sums[2],
        norm_sums[3],
        weight_sums[4],
        weight_sums[5],
        weight_sums[6],
        weight_sums[7],
    )


def places():
    row, col = lax.axis_index("row"), lax.axis_index("col")
    return col, row // 2, row % 2


def partners():
    col, side, core = places()
    return ({"col": 1 - col}, {"row": (1 - side) * 2 + core}, {"row": side * 2 + 1 - core})


def block(ref, col, side, core, rows, width, part=None):
    begin, count = col * rows, rows
    if part is not None:
        begin, count = begin + part * (rows // 2), rows // 2
    return ref.at[strip(begin, count), strip((side * 2 + core) * width, width)]


def put(ref_from, ref_to, sends, recvs, at, partner):
    return pltpu.make_async_remote_copy(
        src_ref=ref_from,
        dst_ref=ref_to,
        send_sem=sends.at[at],
        recv_sem=recvs.at[at],
        device_id=partner,
        device_id_type=MESH,
    )


def strip(begin, count):
    return pl.ds(pl.multiple_of(begin, count), count)


def dot_nt(left, right):
    return lax.dot_general(left, right, (((1,), (1,)), ((), ())), preferred_element_type=jnp.float32)


def dot_tn(left, right):
    return lax.dot_general(left, right, (((0,), (0,)), ((), ())), preferred_element_type=jnp.float32)


def tiled_nt(left, right, target, inner, tile_rows, tile_cols, span=(0, 1, 1)):
    rows, cols = target.shape
    across = cols // tile_cols

    def step(at, none):
        down, side = at // across, at % across
        value = dot_nt(left[strip(down * tile_rows, tile_rows), :inner], right[strip(side * tile_cols, tile_cols), :inner])
        target[strip(down * tile_rows, tile_rows), strip(side * tile_cols, tile_cols)] = value.astype(target.dtype)
        return none

    count = (rows // tile_rows) * across
    lax.fori_loop(span[0] * count // span[2], span[1] * count // span[2], step, 0)


def tiled_nn(left, right, target, tile_rows, tile_cols, span=(0, 1, 1)):
    rows, cols = target.shape
    across = cols // tile_cols

    def step(at, none):
        down, side = at // across, at % across
        value = jnp.dot(
            left[strip(down * tile_rows, tile_rows), :],
            right[:, strip(side * tile_cols, tile_cols)],
            preferred_element_type=jnp.float32,
        )
        target[strip(down * tile_rows, tile_rows), strip(side * tile_cols, tile_cols)] = value.astype(target.dtype)
        return none

    count = (rows // tile_rows) * across
    lax.fori_loop(span[0] * count // span[2], span[1] * count // span[2], step, 0)


def reduce_steps(part, result, got, diag, half_x, half_y, to_send, from_xy, sends, recvs, base, mostly_x=False):
    f32 = jnp.float32
    rows, width = result.shape
    half = rows // 2
    low, high = pl.ds(0, half), pl.ds(half, half)
    col, side, core = places()
    to_x, to_y, to_core = partners()
    spots = ((1 - col, 1 - side), (col, 1 - side), (1 - col, side), (col, side))
    copies = [
        put(block(part, a, b, 1 - core, rows, width), got.at[k], sends, recvs, base + k, to_core)
        for k, (a, b) in enumerate(spots)
    ]
    for copy in copies:
        copy.start()
    mine = [block(part, a, b, core, rows, width) for a, b in spots]
    dx = put(diag.at[low], half_x, sends, recvs, base + 4, to_x)
    dy = put(diag.at[high], half_y, sends, recvs, base + 5, to_x if mostly_x else to_y)

    def onward(k, span, at, partner):
        return put(to_send.at[k, span], from_xy.at[k, span], sends, recvs, base + at, partner)

    y_high, x_low = onward(0, high, 6, to_y), onward(1, low, 7, to_x)
    y_low, x_high = onward(0, low, 8, to_y), onward(1, high, 9, to_x)

    def pair(k, span):
        return mine[k][span].astype(f32) + got[k, span].astype(f32)

    yield
    copies[0].wait_recv()
    diag[...] = (mine[0][...].astype(f32) + got[0].astype(f32)).astype(diag.dtype)
    dx.start()
    dy.start()
    copies[1].wait_recv()
    if not mostly_x:
        to_send[0, high] = pair(1, high).astype(diag.dtype)
        y_high.start()
    copies[2].wait_recv()
    to_send[1, low] = pair(2, low).astype(diag.dtype)
    x_low.start()
    if mostly_x:
        to_send[1, high] = pair(2, high).astype(diag.dtype)
        x_high.start()
    copies[3].wait_recv()
    yield
    dx.wait_recv()
    to_send[0, low] = (pair(1, low) + half_x[...].astype(f32)).astype(diag.dtype)
    y_low.start()
    dy.wait_recv()
    if mostly_x:
        to_send[0, high] = (pair(1, high) + half_y[...].astype(f32)).astype(diag.dtype)
        y_high.start()
    else:
        to_send[1, high] = (pair(2, high) + half_y[...].astype(f32)).astype(diag.dtype)
        x_high.start()
    yield
    for copy in (y_high, x_low, y_low, x_high):
        copy.wait_recv()
    near = mine[3][...].astype(f32) + got[3].astype(f32)
    result[...] = near + from_xy[0].astype(f32) + from_xy[1].astype(f32)
    for copy in copies + [dx, dy, y_high, x_low, y_low, x_high]:
        copy.wait_send()


def spread_steps(out, rows, width, sends, recvs, base, mostly_x=False):
    col, side, core = places()
    to_x, to_y, to_core = partners()

    def copy_of(at, which, partner, part=None):
        ref = block(out, *which, rows, width, part)
        return put(ref, ref, sends, recvs, base + at, partner)

    own, ox, oy, od = (col, side, core), (1 - col, side, core), (col, 1 - side, core), (1 - col, 1 - side, core)
    plan = [
        copy_of(0, own, to_x, 0),
        copy_of(1, own, to_y, 1),
        copy_of(2, own, to_x, 1),
        copy_of(3, own, to_y, 0),
        copy_of(4, own, to_core),
        copy_of(5, oy, to_x, 0) if mostly_x else copy_of(5, ox, to_y, 0),
        copy_of(6, oy, to_x, 1),
        copy_of(7, ox, to_core),
        copy_of(8, oy, to_core),
        copy_of(9, od, to_core),
    ]
    for at in range(5):
        plan[at].start()
    yield
    plan[0].wait_recv()
    if not mostly_x:
        plan[5].start()
    plan[1].wait_recv()
    plan[6].start()
    plan[2].wait_recv()
    plan[7].start()
    plan[3].wait_recv()
    plan[8].start()
    if mostly_x:
        plan[5].start()
    yield
    plan[5].wait_recv()
    plan[6].wait_recv()
    plan[9].start()
    yield
    for at in (4, 7, 8, 9):
        plan[at].wait_recv()
    for copy in plan:
        copy.wait_send()


CHUNK = 256
LINES = CHUNK // 2


def backward_kernel(
    counts,
    hid_h,
    cot_h,
    slope_h,
    n2_h,
    upw_h,
    std_h,
    n1_h,
    qkvw_h,
    down_nat,
    resid_h,
    attended_h,
    outw_h,
    mixed_h,
    std1_h,
    stats,
    marks,
    vec_all,
    inv1_own,
    down_bias,
    down_out,
    up_out,
    out_out,
    qkv_out,
    b_land,
    downw_land,
    out_block,
    tokens_block,
    small_out,
    cot,
    n2,
    std,
    part,
    tot,
    upw,
    hid,
    dup,
    attended,
    outw,
    mixed,
    std1_own,
    d_att,
    d_mix,
    dk_acc,
    dv_acc,
    g,
    s,
    t,
    r_land,
    m_land,
    got_a,
    diag_a,
    hx_a,
    hy_a,
    ts_a,
    fx_a,
    got_b,
    diag_b,
    hx_b,
    hy_b,
    ts_b,
    fx_b,
    dres_own,
    own_sum,
    sums,
    small,
    x_land,
    dp_land,
    stat_land,
    load_sem,
    credit,
    own_sem,
    z_send,
    z_recv,
    a_send,
    a_recv,
    p_send,
    p_recv,
):
    f32, bf16 = jnp.float32, jnp.bfloat16
    n_down, n_up, n_out, n_qkv = counts
    total = sum(counts)
    plane, row, col = lax.axis_index("dp"), lax.axis_index("row"), lax.axis_index("col")
    length, full = cot.shape
    rows, width = dres_own.shape
    row_count = full // width
    inner = (plane == 1) | (plane == 2)
    outer = jnp.logical_not(inner)
    to_inner = {"dp": plane // 3 + 1}
    to_middle = {"dp": 3 - plane}
    to_outer = {"dp": (plane - 1) * 3}
    side, core = row // 2, row % 2

    loads = [
        (hid_h, hid),
        (cot_h, cot),
        (slope_h, dup),
        (upw_h, upw),
        (n2_h, n2),
        (std_h, std),
        (qkvw_h, upw.at[:, : qkvw_h.shape[1]]),
        (n1_h, std),
        (downw_land, n2),
        (downw_land, tot),
        (resid_h, dres_own),
        (attended_h, attended),
        (outw_h, outw),
        (mixed_h, mixed),
        (std1_h, std1_own),
    ]
    loads = [pltpu.make_async_copy(a, b, load_sem.at[k]) for k, (a, b) in enumerate(loads)]
    for k in (0, 1, 2, 3, 4, 5, 11, 12, 13, 14):
        loads[k].start()

    dp_count = dp_land.shape[0]
    barrier = pltpu.get_barrier_semaphore()
    others = [{"row": (1 - side) * 2 + 1 - core}] + [{"dp": (plane + k) % dp_count} for k in range(1, dp_count)]
    for partner in partners() + tuple(others):
        pl.semaphore_signal(barrier, inc=1, device_id=partner, device_id_type=MESH)
    pl.semaphore_wait(barrier, 3 + len(others))

    units = hid.shape[1]
    down_sends, down_recvs = [], []
    for step in range(1, row_count):
        target, source = (row + step) % row_count, (row + row_count - step) % row_count
        here, there = downw_land.at[:, strip(row * width, width)], downw_land.at[:, strip(source * width, width)]
        piece = down_nat.at[strip(target * units, units), :]
        down_sends.append(put(piece, here, p_send, p_recv, 40 + step - 1, {"row": target}))
        down_recvs.append(put(piece, there, p_send, p_recv, 40 + step - 1, {"row": source}))
        down_sends[-1].start()
    down_own = pltpu.make_async_copy(
        down_nat.at[strip(row * units, units), :], downw_land.at[:, strip(row * width, width)], own_sem.at[4 * total]
    )
    down_own.start()

    def place(u, source):
        i, half, quarter = u // 4, u // 2 % 2, pl.ds(u % 2 * LINES, LINES)
        if i < n_down:
            return down_out.at[source * n_down + i // 2 * 2 + half, quarter, pl.ds(i % 2 * CHUNK, CHUNK)]
        i -= n_down
        if i < n_up:
            return up_out.at[half, quarter, strip(source * n_up * CHUNK + i * CHUNK, CHUNK)]
        i -= n_up
        if i < n_out:
            return out_out.at[source * n_out + i, quarter, pl.ds(half * CHUNK, CHUNK)]
        i -= n_out
        return qkv_out.at[half, quarter, strip(source * n_qkv * CHUNK + i * CHUNK, CHUNK)]

    g_slots, s_slots, t_slots, r_slots, m_slots = g.shape[0], s.shape[0], t.shape[0], r_land.shape[0], m_land.shape[0]
    pieces = 4 * total

    def made(u):
        return g.at[u // 4 % g_slots, :, u // 2 % 2, pl.ds(u % 2 * LINES, LINES)]

    def inward(u):
        return put(made(u), r_land.at[u % r_slots], z_send, z_recv, u, to_inner)

    def across(u):
        return put(s.at[u % s_slots], m_land.at[u % m_slots], z_send, z_recv, pieces + u, to_middle)

    def outward(u):
        return put(t.at[u % t_slots], b_land.at[u], z_send, z_recv, 2 * pieces + u, to_outer)

    def home(u, step, source):
        target = (row + step) % row_count
        return put(source.at[target], place(u, row), a_send, a_recv, 3 * u + step - 1, {"row": target})

    def home_own(u, source):
        return pltpu.make_async_copy(source.at[row], place(u, row), own_sem.at[u])

    def send_home(u, source):
        for step in range(1, row_count):
            home(u, step, source).start()
        home_own(u, source).start()

    def sent_home(u, source):
        for step in range(1, row_count):
            home(u, step, source).wait_send()
        home_own(u, source).wait()

    def produce(i):
        if i >= g_slots:

            @pl.when(outer)
            def _():
                for k in range(4):
                    inward(4 * (i - g_slots) + k).wait_send()

        slot = g.at[i % g_slots]
        if i < n_down:
            begin, lane = i // 2 * 2 * CHUNK, i % 2 * CHUNK

            def step(k, none):
                value = dot_tn(hid[:, begin : begin + 2 * CHUNK], cot[:, strip(k * width + lane, CHUNK)]).astype(bf16)
                slot[k, 0] = value[:CHUNK]
                slot[k, 1] = value[CHUNK:]
                return none
        elif n_down + n_up <= i < n_down + n_up + n_out:
            left, begin, right = attended, (i - n_down - n_up) * CHUNK, part

            def step(k, none):
                value = dot_tn(left[:, begin : begin + CHUNK], right[:, strip(k * width, width)]).astype(bf16)
                slot[k, 0] = value[:, :CHUNK]
                slot[k, 1] = value[:, CHUNK:]
                return none
        else:
            if i < n_down + n_up:
                left, right, begin = n2, dup, (i - n_down) * CHUNK
            else:
                left, right, begin = std, d_mix, (i - n_down - n_up - n_out) * CHUNK

            def step(k, none):
                value = dot_tn(left[:, strip(k * width, width)], right[:, begin : begin + CHUNK]).astype(bf16)
                slot[k, 0] = value[:CHUNK]
                slot[k, 1] = value[CHUNK:]
                return none

        lax.fori_loop(0, row_count, step, 0)

    def launch(u):
        @pl.when(outer)
        def _():
            if u >= r_slots:
                pl.semaphore_wait(credit, 1)
            inward(u).start()

    def add(first, second, target):
        for k in range(row_count):
            target[k] = (first[k].astype(f32) + second[k].astype(f32)).astype(bf16)

    def middle(u):
        @pl.when(inner)
        def _():
            inward(u).wait_recv()
            add(made(u), r_land.at[u % r_slots], s.at[u % s_slots])
            across(u).start()
            if u + r_slots < pieces:
                pl.semaphore_signal(credit, inc=1, device_id=to_outer, device_id_type=MESH)

    def finish_inner(u):
        @pl.when(inner)
        def _():
            if u >= t_slots:
                outward(u - t_slots).wait_send()
                sent_home(u - t_slots, t.at[u % t_slots])
            across(u).wait_recv()
            add(s.at[u % s_slots], m_land.at[u % m_slots], t.at[u % t_slots])
            outward(u).start()
            send_home(u, t.at[u % t_slots])
            across(u).wait_send()

    def finish_outer(u):
        @pl.when(outer)
        def _():
            outward(u).wait_recv()
            send_home(u, b_land.at[u])

    ahead = 4

    def pass_on(u):
        middle(u)
        if u >= 2:
            finish_inner(u - 2)
        if u + ahead < pieces:
            if u % 4 == 0:
                produce((u + ahead) // 4)
            launch(u + ahead)
        if u >= 3:
            finish_outer(u - 3)

    set_a = (got_a, diag_a, hx_a, hy_a, ts_a, fx_a)
    set_b = (got_b, diag_b, hx_b, hy_b, ts_b, fx_b)
    gain2 = vec_all[3:4, :]
    heads = mixed.shape[1] // (3 * HEAD)
    here = strip(row * width, width)
    tile = 64
    first = reduce_steps(part, own_sum, *set_a, p_send, p_recv, 0, mostly_x=True)
    second = spread_steps(tot, rows, width, p_send, p_recv, 10, mostly_x=True)
    third = reduce_steps(cot, own_sum, *set_b, p_send, p_recv, 20, mostly_x=True)
    fourth = reduce_steps(tot, own_sum, *set_a, p_send, p_recv, 30, mostly_x=True)

    def down_here():
        down_own.wait()
        for copy in down_recvs:
            copy.wait_recv()
        loads[9].start()

    def upper_step(k, none):
        down, across_ = k // (units // CHUNK), k % (units // CHUNK)
        at, lanes = strip(down * rows, rows), strip(across_ * CHUNK, CHUNK)
        dup[at, lanes] = (dot_nt(cot[at, :], tot[lanes, :]) * dup[at, lanes].astype(f32)).astype(bf16)
        return none

    def uppers(part_of):
        if part_of == 0:
            for k in (2, 3, 4, 9):
                loads[k].wait()
        count = (length // rows) * (units // CHUNK) // 2
        lax.fori_loop(part_of * count, (part_of + 1) * count, upper_step, 0)

    def d_normed2(part_of):
        tiled_nt(dup, upw, part, units, 1024, 256, (part_of, part_of + 1, 2))
        if part_of == 1:
            loads[6].start()
            next(first)

    def gather_start():
        next(first, None)
        block(tot, col, side, core, rows, width)[...] = own_sum[...].astype(bf16)
        next(second)

    def norm_step(k, none):
        at = strip(k * tile, tile)
        grad, standard, inverse = tot[at, :].astype(f32), std[at, :].astype(f32), stats[at, 0:1]
        scaled = grad * gain2
        mean_one = jnp.sum(scaled, axis=1, keepdims=True) / full
        mean_two = jnp.sum(scaled * standard, axis=1, keepdims=True) / full
        top = cot[at, :].astype(f32)
        low = (top + inverse * (scaled - mean_one - standard * mean_two)).astype(bf16)
        part[at, :] = low
        sums[0:1, :] += jnp.sum(grad * standard, axis=0, keepdims=True)
        sums[1:2, :] += jnp.sum(grad, axis=0, keepdims=True)
        sums[2:3, :] += jnp.sum(low.astype(f32), axis=0, keepdims=True)
        sums[3:4, :] += jnp.sum(top, axis=0, keepdims=True)

        @pl.when(k // (rows // tile) == col)
        def _():
            own = tot[at, here].astype(f32) * vec_all[3:4, here]
            dres_own[strip(k % (rows // tile) * tile, tile), :] = cot[at, here].astype(f32) + inverse * (
                own - mean_one - std[at, here].astype(f32) * mean_two
            )

        return none

    def norm_back(part_of):
        if part_of == 0:
            for k in (5, 11, 12, 13, 14):
                loads[k].wait()
        count = length // tile // 2
        lax.fori_loop(part_of * count, (part_of + 1) * count, norm_step, 0)
        if part_of == 1:
            loads[7].start()

    def d_attended():
        tiled_nt(part, outw, d_att, full, 512, 256)

    factor = 1.0 / math.sqrt(HEAD)
    blocks = length // SPAN
    spots = (SPAN, SPAN)
    earlier = lax.broadcasted_iota(jnp.int32, spots, 1) <= lax.broadcasted_iota(jnp.int32, spots, 0)

    def attention_back(head, begin, end):
        base = head * 3 * HEAD
        at_q, at_k, at_v = pl.ds(base, HEAD), pl.ds(base + HEAD, HEAD), pl.ds(base + 2 * HEAD, HEAD)
        at_o = pl.ds(head * HEAD, HEAD)
        if begin == 0:
            dk_acc[...] = jnp.zeros_like(dk_acc)
            dv_acc[...] = jnp.zeros_like(dv_acc)
        for k in range(begin, end):
            now = pl.ds(k * SPAN, SPAN)
            seen = (k + 1) * SPAN
            query, dout = mixed[now, at_q], d_att[now, at_o]
            keys, values = mixed[:seen, at_k], mixed[:seen, at_v]
            scores = dot_nt(query, keys) * factor
            last = jnp.where(earlier | (marks[k : k + 1, :1] > 0), scores[:, seen - SPAN :], masked_score)
            scores = last if k == 0 else jnp.concatenate([scores[:, : seen - SPAN], last], axis=1)
            probs = jnp.exp(scores - stats[now, 1 + head : 2 + head])
            d_probs = dot_nt(dout, values)
            dots = jnp.sum(probs * d_probs, axis=1, keepdims=True)
            d_scores = (probs * (d_probs - dots)).astype(bf16)
            d_mix[now, at_q] = (jnp.dot(d_scores, keys, preferred_element_type=f32) * factor).astype(bf16)
            dk_acc[:seen] += dot_tn(d_scores, query)
            dv_acc[:seen] += dot_tn(probs.astype(bf16), dout)
        if end == blocks:
            d_mix[:, at_k] = (dk_acc[...] * factor).astype(bf16)
            d_mix[:, at_v] = dv_acc[...].astype(bf16)

    def d_normed1(part_of):
        if part_of == 0:
            loads[6].wait()
        tiled_nt(d_mix, upw, cot, d_mix.shape[1], 1024, 256, (part_of, part_of + 1, 2))
        if part_of == 1:
            next(third)

    def output_sums(part_of):
        if part_of == 0:
            loads[8].wait()
        tiled_nn(hid, n2, tot, 1024, 256, (part_of, part_of + 1, 2))
        if part_of == 1:
            next(fourth)

    grad1 = own_sum
    stat_sends, stat_recvs, dp_sends, dp_recvs, row_sends, row_recvs = [], [], [], [], [], []
    for step in range(1, row_count):
        target, source = (row + step) % row_count, (row + row_count - step) % row_count
        to, since = {"row": target}, {"row": source}
        stat_sends.append(put(stat_land.at[row], stat_land.at[row], p_send, p_recv, 43 + step - 1, to))
        stat_recvs.append(put(stat_land.at[source], stat_land.at[source], p_send, p_recv, 43 + step - 1, since))
        row_sends.append(put(small_out.at[row], small_out.at[row], p_send, p_recv, 50 + step - 1, to))
        row_recvs.append(put(small_out.at[source], small_out.at[source], p_send, p_recv, 50 + step - 1, since))
    for step in range(1, dp_count):
        target, source = (plane + step) % dp_count, (plane + dp_count - step) % dp_count
        dp_sends.append(put(dp_land.at[plane], dp_land.at[plane], p_send, p_recv, 47 + step - 1, {"dp": target}))
        dp_recvs.append(put(dp_land.at[source], dp_land.at[source], p_send, p_recv, 47 + step - 1, {"dp": source}))
    x_copy = put(small.at[pl.ds(0, 8)], x_land, p_send, p_recv, 46, partners()[0])

    def row_stats():
        next(third, None)
        scaled = grad1[...] * vec_all[0:1, here]
        first_sum = jnp.sum(scaled, axis=1, keepdims=True)
        second_sum = jnp.sum(scaled * std1_own[...].astype(f32), axis=1, keepdims=True)
        lane = lax.broadcasted_iota(jnp.int32, (rows, 128), 1)
        pair = jnp.where(lane == 0, first_sum, jnp.where(lane == 1, second_sum, 0.0))
        stat_land[row] = pair.T[:8]
        for copy in stat_sends:
            copy.start()

    def small_sums():
        small[...] = jnp.zeros_like(small)
        small[0:1, :] = jnp.sum(grad1[...] * std1_own[...].astype(f32), axis=0, keepdims=True)
        small[1:2, :] = jnp.sum(grad1[...], axis=0, keepdims=True)
        small[2:6, :] = sums[0:4, here]
        totals = jnp.sum(dup[...].astype(f32), axis=0, keepdims=True)
        for k in range(units // width):
            small[8 + k : 9 + k, :] = totals[:, k * width : (k + 1) * width]
        mixes = jnp.sum(d_mix[...].astype(f32), axis=0, keepdims=True)
        spot = 8 + units // width
        picked = [
            mixes[:, (head * 3 + kind) * HEAD : (head * 3 + kind + 1) * HEAD] for head in range(heads) for kind in (0, 2)
        ]
        small[spot : spot + 1, : 2 * heads * HEAD] = jnp.concatenate(picked, axis=1)
        x_copy.start()

    def tokens_out():
        for copy in stat_recvs:
            copy.wait_recv()
        both = stat_land[0]
        for k in range(1, row_count):
            both = both + stat_land[k]
        both = jnp.concatenate([both, jnp.zeros((120, rows), f32)], axis=0).T
        scaled = grad1[...] * vec_all[0:1, here]
        d_norm1 = inv1_own[...] * (
            scaled - both[:, 0:1] / full - std1_own[...].astype(f32) * (both[:, 1:2] / full)
        )
        tokens_block[...] = (dres_own[...] + d_norm1).astype(bf16)
        loads[10].start()

    def dp_start():
        x_copy.wait_recv()
        x_copy.wait_send()
        small[0:2, :] += x_land[0:2, :]
        dp_land[plane] = small[...]
        for copy in dp_sends:
            copy.start()

    def output_out():
        next(fourth, None)
        loads[10].wait()
        out_block[...] = (dres_own[...] + (own_sum[...] + down_bias[...])).astype(bf16)

    def rows_start():
        for copy in dp_recvs:
            copy.wait_recv()
        together = dp_land[0]
        for k in range(1, dp_count):
            together = together + dp_land[k]
        small_out[row] = together
        for copy in row_sends:
            copy.start()

    tasks = {
        6: [down_here],
        8: [lambda: uppers(0)],
        9: [lambda: uppers(1)],
        10: [lambda: d_normed2(0)],
        11: [lambda: d_normed2(1)],
        13: [lambda: next(first)],
        16: [lambda: next(first)],
        19: [gather_start],
        22: [lambda: next(second)],
        24: [lambda: next(second)],
        25: [lambda: next(second, None), loads[8].start],
        26: [lambda: norm_back(0)],
        27: [lambda: norm_back(1)],
        28: [d_attended],
        29: [lambda: attention_back(0, 0, blocks)],
        30: [lambda: attention_back(1, 0, blocks)],
        31: [lambda: output_sums(0), loads[7].wait],
        32: [lambda: d_normed1(0)],
        33: [lambda: d_normed1(1)],
        34: [lambda: next(third)],
        35: [lambda: output_sums(1)],
        36: [lambda: next(fourth)],
        37: [lambda: next(third)],
        39: [lambda: next(fourth)],
        40: [row_stats],
        41: [small_sums],
        42: [tokens_out],
        43: [dp_start],
        44: [output_out],
        45: [rows_start],
    }
    sums[...] = jnp.zeros_like(sums)
    loads[0].wait()
    loads[1].wait()
    produce(0)
    for k in range(ahead):
        launch(k)
    for u in range(pieces):
        pass_on(u)
        for task in tasks.get(u, ()):
            task()
    finish_inner(pieces - 2)
    finish_inner(pieces - 1)
    finish_outer(pieces - 3)
    finish_outer(pieces - 2)
    finish_outer(pieces - 1)
    for copy in row_recvs:
        copy.wait_recv()
    for copy in down_sends + stat_sends + dp_sends + row_sends:
        copy.wait_send()

    @pl.when(outer)
    def _():
        for u in range(pieces - 4 * g_slots, pieces):
            inward(u).wait_send()
        for u in range(pieces):
            sent_home(u, b_land.at[u])

    @pl.when(inner)
    def _():
        for u in range(pieces - t_slots, pieces):
            outward(u).wait_send()
            sent_home(u, t.at[u % t_slots])

    for u in range(pieces):
        for step in range(1, row_count):
            source = (row + row_count - step) % row_count
            put(t.at[0, source], place(u, source), a_send, a_recv, 3 * u + step - 1, {"row": source}).wait_recv()


def backward_plane(
    cid, hid, cot, slope, n2, upw, std, n1, qkvw, down_nat, resid_own, attended, outw, mixed, std1_own, stats, marks, vec_all, inv1_own, down_bias
):
    f32, bf16 = jnp.float32, jnp.bfloat16
    length, full = cot.shape
    rows, width = length // lax.axis_size("col"), full // lax.axis_size("row")
    row_count, dp_count = full // width, lax.axis_size("dp")
    counts = (slope.shape[1] // CHUNK, slope.shape[1] // CHUNK, attended.shape[1] // CHUNK, mixed.shape[1] // CHUNK)
    total = sum(counts)
    unit = (row_count, LINES, CHUNK)
    shape = jax.ShapeDtypeStruct
    away, near = pl.BlockSpec(memory_space=pl.ANY), pl.BlockSpec(memory_space=pltpu.VMEM)
    vmem, dma = pltpu.VMEM, pltpu.SemaphoreType.DMA
    sets = [
        vmem((4, rows, width), bf16),
        vmem((rows, width), bf16),
        vmem((rows // 2, width), bf16),
        vmem((rows // 2, width), bf16),
        vmem((2, rows, width), bf16),
        vmem((2, rows, width), bf16),
    ]
    return pl.pallas_call(
        functools.partial(backward_kernel, counts),
        out_shape=[
            shape((row_count * counts[0], CHUNK, width), bf16),
            shape((2, CHUNK, row_count * counts[1] * CHUNK), bf16),
            shape((row_count * counts[2], CHUNK, width), bf16),
            shape((2, CHUNK, row_count * counts[3] * CHUNK), bf16),
            shape((4 * total,) + unit, bf16),
            shape((hid.shape[1], full), bf16),
            shape((rows, width), bf16),
            shape((rows, width), bf16),
            shape((row_count, 16, width), f32),
        ],
        in_specs=[away] * 14 + [near] * 5,
        out_specs=[away] * 6 + [near] * 3,
        scratch_shapes=[
            vmem((length, full), bf16),
            vmem((length, full), bf16),
            vmem((length, full), bf16),
            vmem((length, full), bf16),
            vmem((length, full), bf16),
            vmem(upw.shape, bf16),
            vmem(hid.shape, bf16),
            vmem(slope.shape, bf16),
            vmem(attended.shape, bf16),
            vmem(outw.shape, bf16),
            vmem(mixed.shape, bf16),
            vmem(std1_own.shape, bf16),
            vmem(attended.shape, bf16),
            vmem(mixed.shape, bf16),
            vmem((length, HEAD), f32),
            vmem((length, HEAD), f32),
            vmem((2, row_count, width // CHUNK, CHUNK, CHUNK), bf16),
            vmem((3,) + unit, bf16),
            vmem((4,) + unit, bf16),
            vmem((6,) + unit, bf16),
            vmem((6,) + unit, bf16),
        ]
        + sets
        + sets
        + [
            vmem((rows, width), f32),
            vmem((rows, width), f32),
            vmem((8, full), f32),
            vmem((16, width), f32),
            vmem((8, width), f32),
            vmem((dp_count, 16, width), f32),
            vmem((row_count, 8, rows), f32),
            dma((15,)),
            pltpu.SemaphoreType.REGULAR,
            dma((4 * total + 1,)),
            dma((12 * total,)),
            dma((12 * total,)),
            dma((12 * total,)),
            dma((12 * total,)),
            dma((53,)),
            dma((53,)),
        ],
        compiler_params=pltpu.CompilerParams(
            collective_id=cid, has_side_effects=True, vmem_limit_bytes=64 * 1024 * 1024 - 65536
        ),
        cost_estimate=pl.CostEstimate(flops=40_000_000_000, bytes_accessed=100_000_000, transcendentals=4_000_000),
    )(hid, cot, slope, n2, upw, std, n1, qkvw, down_nat, resid_own, attended, outw, mixed, std1_own, stats, marks, vec_all, inv1_own, down_bias)


class Moves:
    def __init__(self, source, target, cut, parts, sends, recvs, base):
        row, plane = lax.axis_index("row"), lax.axis_index("dp")
        side, core = row // 2, row % 2
        parity = plane % 2
        other = {"dp": plane + 1 - 2 * parity}
        twin = side * 2 + 1 - core
        far = ((1 - side) * 2 + core, (1 - side) * 2 + 1 - core)
        self.sibling = put(source(twin), target(row), sends, recvs, base, {"row": twin})
        self.sibling_in = put(source(twin), target(twin), sends, recvs, base, {"row": twin})
        self.outs, self.ins, self.passes, self.gets = [], [], [], []
        at = base + 1
        for step in range(parts // 2):
            for k, device in enumerate(far):
                mine, theirs = 2 * step + parity, 2 * step + 1 - parity
                there, here = cut(target(row), mine), cut(target(device), mine)
                self.outs.append(put(cut(source(device), mine), there, sends, recvs, at, {"row": device}))
                self.ins.append(put(cut(source(device), mine), here, sends, recvs, at, {"row": device}))
                self.passes.append(put(here, here, sends, recvs, at + 1, other))
                lands = cut(target(device), theirs)
                self.gets.append(put(lands, lands, sends, recvs, at + 1, other))
                at += 2

    @staticmethod
    def count(parts):
        return 1 + 2 * parts

    def start(self):
        self.sibling.start()
        self.start_far()

    def start_far(self):
        for copy in self.outs:
            copy.start()

    def forward(self, begin=0, end=None):
        for came, passed in list(zip(self.ins, self.passes))[begin:end]:
            came.wait_recv()
            passed.start()

    def finish(self):
        self.sibling_in.wait_recv()
        for copy in self.gets:
            copy.wait_recv()

    def drain(self):
        self.sibling.wait_send()
        for copy in self.outs + self.passes:
            copy.wait_send()


FAR_PARTS = 8


def forward_kernel(
    tokens,
    cot_in,
    ln1_gain,
    ln1_shift,
    out_bias_in,
    ln2_gain,
    ln2_shift,
    qv_bias,
    up_bias_in,
    spans,
    qkv_in,
    out_nat,
    up_nat,
    cot_all,
    n1_out,
    n2_out,
    std_out,
    upw_out,
    qkvw_out,
    outw_out,
    mixed_out,
    attended_out,
    hid_out,
    slope_out,
    stats,
    marks,
    vec_all,
    resid_own,
    std1_own,
    inv1_own,
    tok,
    n1,
    part,
    tot,
    qkvw,
    upw,
    outw,
    mixed,
    attended,
    hid,
    slope,
    own_sum,
    got,
    diag,
    hx,
    hy,
    ts,
    fx,
    qkv_raw,
    qkv_nat,
    mixed_bias,
    local_sem,
    w_send,
    w_recv,
    p_send,
    p_recv,
):
    f32, bf16 = jnp.float32, jnp.bfloat16
    plane, row, col = lax.axis_index("dp"), lax.axis_index("row"), lax.axis_index("col")
    side, core = row // 2, row % 2
    rows, width = tokens.shape
    length, full = tok.shape
    row_count = full // width
    heads_width = attended.shape[1]
    units = hid.shape[1]

    barrier = pltpu.get_barrier_semaphore()
    twins = ({"row": (1 - side) * 2 + 1 - core}, {"dp": plane + 1 - 2 * (plane % 2)})
    for partner in partners() + twins:
        pl.semaphore_signal(barrier, inc=1, device_id=partner, device_id_type=MESH)
    pl.semaphore_wait(barrier, 5)

    def cut_rows(ref, part):
        count = ref.shape[0] // FAR_PARTS
        return ref.at[strip(part * count, count)]

    per = qkvw.shape[1]
    count = Moves.count(FAR_PARTS)
    qkv_moves = Moves(
        lambda r: qkv_nat.at[:, strip(r * per, per)],
        lambda r: qkvw.at[strip(r * width, width), :],
        cut_rows,
        FAR_PARTS,
        w_send,
        w_recv,
        0,
    )
    out_moves = Moves(
        lambda r: out_nat.at[strip(r * heads_width, heads_width), :],
        lambda r: outw.at[:, strip(r * width, width)],
        cut_rows,
        FAR_PARTS,
        w_send,
        w_recv,
        count,
    )
    up_moves = Moves(
        lambda r: up_nat.at[:, strip(r * units, units)],
        lambda r: upw.at[strip(r * width, width), :],
        cut_rows,
        FAR_PARTS,
        w_send,
        w_recv,
        2 * count,
    )
    locals_ = [
        (qkv_nat.at[:, strip(row * per, per)], qkvw.at[strip(row * width, width), :]),
        (out_nat.at[strip(row * heads_width, heads_width), :], outw.at[:, strip(row * width, width)]),
        (up_nat.at[:, strip(row * units, units)], upw.at[strip(row * width, width), :]),
        (cot_in, block(cot_all, col, side, core, rows, width)),
        (n1, n1_out),
        (part, n2_out),
        (n1, std_out),
        (upw, upw_out),
        (qkvw, qkvw_out),
        (outw, outw_out),
        (mixed, mixed_out),
        (attended, attended_out),
        (hid, hid_out),
        (slope, slope_out),
        (qkv_in, qkv_raw),
    ]
    local = [pltpu.make_async_copy(a, b, local_sem.at[k]) for k, (a, b) in enumerate(locals_)]
    local[14].start()
    for k in range(1, 4):
        local[k].start()

    block(tok, col, side, core, rows, width)[...] = tokens[...]
    gather = spread_steps(tok, rows, width, p_send, p_recv, 0, mostly_x=True)
    next(gather)
    here = strip(row * width, width)
    vec_all[:, here] = jnp.zeros((vec_all.shape[0], width), f32)
    for k, vector in enumerate((ln1_gain, ln1_shift, out_bias_in, ln2_gain, ln2_shift)):
        vec_all[k : k + 1, here] = vector[...]
    vec_sends, vec_recvs = [], []
    for step in range(1, row_count):
        target, source = (row + step) % row_count, (row + row_count - step) % row_count
        here, there = vec_all.at[:, strip(row * width, width)], vec_all.at[:, strip(source * width, width)]
        vec_sends.append(put(here, here, p_send, p_recv, 10 + step - 1, {"row": target}))
        vec_recvs.append(put(there, there, p_send, p_recv, 10 + step - 1, {"row": source}))
        vec_sends[-1].start()
    out_moves.sibling.start()
    up_moves.sibling.start()
    local[14].wait()
    for kind in range(3):
        flat = qkv_raw[:, kind].reshape(width, qkv_raw.shape[2] * HEAD)
        for head in range(qkv_raw.shape[2]):
            qkv_nat[:, pl.ds((head * 3 + kind) * HEAD, HEAD)] = flat[:, head * HEAD : (head + 1) * HEAD]
    local[0].start()
    qkv_moves.sibling.start()
    qkv_moves.start_far()
    next(gather)
    next(gather)
    next(gather, None)
    for copy in vec_recvs:
        copy.wait_recv()
    lines = lax.broadcasted_iota(jnp.int32, marks.shape, 0) * SPAN
    found = jnp.zeros(marks.shape, f32)
    for k in range(spans.shape[1]):
        found = jnp.where(lines == spans[0:1, k : k + 1] // SPAN * SPAN, 1.0, found)
    marks[...] = found

    tile = 64
    gain1, shift1 = vec_all[0:1, :], vec_all[1:2, :]

    def norm1_step(k, none):
        at = strip(k * tile, tile)
        values = tok[at, :].astype(f32)
        center = jnp.sum(values, axis=1, keepdims=True) / full
        inverse = lax.rsqrt(jnp.sum(values * values, axis=1, keepdims=True) / full - center * center + epsilon)
        n1[at, :] = ((values - center) * inverse * gain1 + shift1).astype(bf16)

        @pl.when(k // (rows // tile) == col)
        def _():
            here = strip(k % (rows // tile) * tile, tile)
            std1_own[here, :] = ((tok[at, strip(row * width, width)].astype(f32) - center) * inverse).astype(bf16)
            inv1_own[here, :] = inverse

        return none

    half_steps = length // tile // 2
    quarter = half_steps // 2
    for k in range(4):
        qkv_moves.forward(2 * k, 2 * k + 1)
        lax.fori_loop(k * quarter, (k + 1) * quarter, norm1_step, 0)
        qkv_moves.forward(2 * k + 1, 2 * k + 2)
    local[4].start()
    out_moves.start_far()
    up_moves.start_far()
    qkv_moves.finish()
    local[0].wait()

    mixed_bias[...] = jnp.zeros_like(mixed_bias)
    for head in range(heads_width // HEAD):
        for k in range(2):
            lanes = pl.ds((head * 3 + 2 * k) * HEAD, HEAD)
            mixed_bias[:, lanes] = qv_bias[row * (heads_width // HEAD) + head, k : k + 1, :]
    up_bias = up_bias_in.at[:, strip(row * units, units)]

    def mixed_step(k, none):
        down, across = k // (per // CHUNK), k % (per // CHUNK)
        at, lanes = strip(down * rows, rows), strip(across * CHUNK, CHUNK)
        value = jnp.dot(n1[at, :], qkvw[:, lanes], preferred_element_type=f32)
        mixed[at, lanes] = (value + mixed_bias[:, lanes]).astype(bf16)
        return none

    lax.fori_loop(0, (length // rows) * (per // CHUNK), mixed_step, 0)
    local[8].start()
    local[10].start()
    local[4].wait()

    heads = heads_width // HEAD
    factor = 1.0 / math.sqrt(HEAD)
    blocks = length // SPAN
    spots = (SPAN, SPAN)
    earlier = lax.broadcasted_iota(jnp.int32, spots, 1) <= lax.broadcasted_iota(jnp.int32, spots, 0)

    def head_step(head, none):
        base = head * 3 * HEAD
        at_q, at_k, at_v = strip(base, HEAD), strip(base + HEAD, HEAD), strip(base + 2 * HEAD, HEAD)
        for k in range(blocks):
            here = pl.ds(k * SPAN, SPAN)
            seen = (k + 1) * SPAN
            scores = dot_nt(mixed[here, at_q], mixed[:seen, at_k]) * factor
            last = jnp.where(earlier | (marks[k : k + 1, :1] > 0), scores[:, seen - SPAN :], masked_score)
            scores = last if k == 0 else jnp.concatenate([scores[:, : seen - SPAN], last], axis=1)
            highest = jnp.max(scores, axis=1, keepdims=True)
            weights = jnp.exp(scores - highest)
            weight_sum = jnp.sum(weights, axis=1, keepdims=True)
            stats[here, 1 + head : 2 + head] = highest + jnp.log(weight_sum)
            value = jnp.dot((weights / weight_sum).astype(bf16), mixed[:seen, at_v], preferred_element_type=f32)
            attended[here, strip(head * HEAD, HEAD)] = value.astype(bf16)
        return none

    for head in range(heads):
        head_step(head, 0)
    local[11].start()
    out_moves.forward()
    up_moves.forward(0, 4)
    out_moves.finish()
    local[1].wait()
    tiled_nn(attended, outw, part, rows, 512)
    local[9].start()
    add_up = reduce_steps(part, own_sum, got, diag, hx, hy, ts, fx, p_send, p_recv, 13)
    next(add_up)
    next(add_up)
    up_moves.forward(4, 8)
    next(add_up)
    next(add_up, None)
    block(tot, col, side, core, rows, width)[...] = own_sum[...].astype(bf16)
    again = spread_steps(tot, rows, width, p_send, p_recv, 23)
    next(again)
    next(again)
    local[3].wait()
    cot_gather = spread_steps(cot_all, rows, width, p_send, p_recv, 33)
    next(cot_gather)
    next(again)
    next(again, None)

    gain2, shift2, out_bias = vec_all[3:4, :], vec_all[4:5, :], vec_all[2:3, :]

    def norm2_step(k, none):
        at = strip(k * tile, tile)
        values = tok[at, :].astype(f32) + (tot[at, :].astype(f32) + out_bias)
        center = jnp.sum(values, axis=1, keepdims=True) / full
        inverse = lax.rsqrt(jnp.sum(values * values, axis=1, keepdims=True) / full - center * center + epsilon)
        standard = (values - center) * inverse
        stats[at, 0:1] = inverse
        n1[at, :] = standard.astype(bf16)
        part[at, :] = (standard * gain2 + shift2).astype(bf16)

        @pl.when(k // (rows // tile) == col)
        def _():
            own = strip(row * width, width)
            here = strip(k % (rows // tile) * tile, tile)
            resid_own[here, :] = tok[at, own].astype(f32) + (tot[at, own].astype(f32) + vec_all[2:3, own])

        return none

    lax.fori_loop(0, 2 * half_steps, norm2_step, 0)
    local[5].start()
    local[6].start()
    next(cot_gather)
    up_moves.finish()
    local[2].wait()
    local[7].start()

    def up_step(k, none):
        down, across = k // (units // CHUNK), k % (units // CHUNK)
        at, lanes = strip(down * rows, rows), strip(across * CHUNK, CHUNK)
        u = jnp.dot(part[at, :], upw[:, lanes], preferred_element_type=f32) + up_bias[:, lanes]
        bent = jnp.tanh(0.7978845608028654 * (u + 0.044715 * u * u * u))
        hid[at, lanes] = (0.5 * u * (1.0 + bent)).astype(bf16)
        inside = 0.7978845608028654 * (1.0 + 3 * 0.044715 * u * u)
        slope[at, lanes] = (0.5 * (1.0 + bent) + 0.5 * u * (1.0 - bent * bent) * inside).astype(bf16)
        return none

    lax.fori_loop(0, (length // rows) * (units // CHUNK), up_step, 0)
    local[12].start()
    local[13].start()
    next(cot_gather)
    next(cot_gather, None)
    for k in range(5, 14):
        local[k].wait()
    for moves in (qkv_moves, out_moves, up_moves):
        moves.drain()
    for copy in vec_sends:
        copy.wait_send()


def forward_plane(cid, tokens, cot, vectors, qv_bias, up_bias, spans, qkv_in, out_nat, up_nat):
    f32, bf16 = jnp.float32, jnp.bfloat16
    rows, width = tokens.shape
    row_count = lax.axis_size("row")
    length, full = rows * lax.axis_size("col"), width * row_count
    per, heads_width, units = qkv_in.shape[1] * qkv_in.shape[2] * HEAD // row_count, out_nat.shape[0] // row_count, up_nat.shape[1] // row_count
    shape = jax.ShapeDtypeStruct
    away, near = pl.BlockSpec(memory_space=pl.ANY), pl.BlockSpec(memory_space=pltpu.VMEM)
    vmem, dma = pltpu.VMEM, pltpu.SemaphoreType.DMA
    wide = shape((length, full), bf16)
    moved = 3 * Moves.count(FAR_PARTS)
    return pl.pallas_call(
        forward_kernel,
        out_shape=[
            wide,
            wide,
            wide,
            wide,
            shape((full, units), bf16),
            shape((full, per), bf16),
            shape((heads_width, full), bf16),
            shape((length, per), bf16),
            shape((length, heads_width), bf16),
            shape((length, units), bf16),
            shape((length, units), bf16),
            shape((length, 8), f32),
            shape((8, 128), f32),
            shape((8, full), f32),
            shape((rows, width), f32),
            shape((rows, width), bf16),
            shape((rows, 1), f32),
        ],
        in_specs=[near] * (5 + len(vectors)) + [away] * 3,
        out_specs=[away] * 11 + [near] * 6,
        scratch_shapes=[
            vmem((length, full), bf16),
            vmem((length, full), bf16),
            vmem((length, full), bf16),
            vmem((length, full), bf16),
            vmem((full, per), bf16),
            vmem((full, units), bf16),
            vmem((heads_width, full), bf16),
            vmem((length, per), bf16),
            vmem((length, heads_width), bf16),
            vmem((length, units), bf16),
            vmem((length, units), bf16),
            vmem((rows, width), f32),
            vmem((4, rows, width), bf16),
            vmem((rows, width), bf16),
            vmem((rows // 2, width), bf16),
            vmem((rows // 2, width), bf16),
            vmem((2, rows, width), bf16),
            vmem((2, rows, width), bf16),
            vmem(qkv_in.shape, bf16),
            vmem((width, row_count * per), bf16),
            vmem((1, per), f32),
            dma((15,)),
            dma((moved,)),
            dma((moved,)),
            dma((43,)),
            dma((43,)),
        ],
        compiler_params=pltpu.CompilerParams(
            collective_id=cid, has_side_effects=True, vmem_limit_bytes=60 * 1024 * 1024
        ),
        cost_estimate=pl.CostEstimate(flops=10_000_000_000, bytes_accessed=60_000_000, transcendentals=4_000_000),
    )(tokens, cot, *[vector[None] for vector in vectors], qv_bias, up_bias[None], spans, qkv_in, out_nat, up_nat)


def results_kernel(
    down, up, out, output, tokens, qkv, small, down_result, up_result, out_result, output_result, tokens_result, qkv_result, *vectors
):
    *sums, up_bias, qv_bias = vectors
    f32 = jnp.float32
    down_result[...] = down[...].astype(f32)
    up_result[...] = up[...].astype(f32)
    out_result[...] = out[...].astype(f32)
    output_result[...] = output[...]
    tokens_result[...] = tokens[...]
    for head in range(qkv_result.shape[2]):
        for kind in range(3):
            begin = (head * 3 + kind) * HEAD
            qkv_result[:, kind, head, :] = qkv[:, begin : begin + HEAD].astype(f32)

    @pl.when(pl.program_id(0) == 0)
    def _():
        row = lax.axis_index("row")
        for k, result in enumerate(sums):
            result[...] = small[row, k : k + 1, :]
        count, _, width = small.shape
        lines = up_bias.shape[1] // (count * width)
        heads = qv_bias.shape[0] // count
        for source in range(count):
            for k in range(lines):
                begin = (source * lines + k) * width
                up_bias[:, begin : begin + width] = small[source, 8 + k : 9 + k, :]
            for head in range(heads):
                for k in range(2):
                    begin = (head * 2 + k) * HEAD
                    line = small[source, 8 + lines : 9 + lines, begin : begin + HEAD]
                    qv_bias[source * heads + head, k : k + 1, :] = line


def results(down, up, out, output, tokens, qkv, small):
    f32 = jnp.float32
    shape = jax.ShapeDtypeStruct
    rows, heads = qkv.shape[0], qkv.shape[1] // (3 * HEAD)
    width, units = small.shape[2], up.shape[1]
    steps = 8

    def cut(array):
        return pl.BlockSpec((array.shape[0] // steps, array.shape[1]), lambda k: (k, 0))

    def whole(*dims):
        return pl.BlockSpec(dims, lambda k: (0,) * len(dims))

    line = whole(1, width)
    *made, up_bias, qv_bias = pl.pallas_call(
        results_kernel,
        grid=(steps,),
        out_shape=[shape(a.shape, f32) for a in (down, up, out)]
        + [shape(a.shape, a.dtype) for a in (output, tokens)]
        + [shape((rows, 3, heads, HEAD), f32)]
        + [shape((1, width), f32)] * 6
        + [shape((1, units), f32), shape((heads, 2, HEAD), f32)],
        in_specs=[cut(a) for a in (down, up, out, output, tokens, qkv)] + [whole(*small.shape)],
        out_specs=[cut(a) for a in (down, up, out, output, tokens)]
        + [pl.BlockSpec((rows // steps, 3, heads, HEAD), lambda k: (k, 0, 0, 0))]
        + [line] * 6
        + [whole(1, units), whole(heads, 2, HEAD)],
        compiler_params=pltpu.CompilerParams(vmem_limit_bytes=63 * 1024 * 1024),
    )(down, up, out, output, tokens, qkv, small)
    made[5] = jnp.swapaxes(made[5], 1, 2)
    return made[:6], [sums[0] for sums in made[6:]], up_bias[0], qv_bias


def plane_plan(
    tokens,
    ln1_gain,
    ln1_shift,
    qkv_weight,
    qv_bias,
    out_weight,
    out_bias,
    ln2_gain,
    ln2_shift,
    up_weight,
    up_bias,
    down_weight,
    down_bias,
    span_starts,
    cotangent,
):
    width = tokens.shape[1]
    (
        cot_all, n1, n2, standard2, upw, qkvw, outw, mixed, attended, hidden, slope,
        stats, marks, vec_all, residual_own, standard1_own, inverse1_own,
    ) = forward_plane(
        1,
        tokens,
        cotangent,
        (ln1_gain, ln1_shift, out_bias, ln2_gain, ln2_shift),
        qv_bias,
        up_bias,
        span_starts,
        jnp.swapaxes(qkv_weight, 1, 2),
        out_weight.reshape(-1, width),
        up_weight,
    )
    down_grad, up_grad, out_grad, qkv_grad, _, _, output, tokens_grad, small = backward_plane(
        2, hidden, cot_all, slope, n2, upw, standard2, n1, qkvw, down_weight, residual_own, attended, outw, mixed, standard1_own,
        stats, marks, vec_all, inverse1_own, down_bias[None],
    )
    grads, sums, up_bias_grad, qv_bias_grad = results(
        down_grad.reshape(-1, width), up_grad.reshape(width, -1), out_grad.reshape(-1, width), output, tokens_grad,
        qkv_grad.reshape(width, -1), small
    )
    return (
        grads[3],
        grads[4],
        sums[0],
        sums[1],
        grads[5],
        qv_bias_grad,
        grads[2].reshape(out_weight.shape),
        sums[4],
        sums[2],
        sums[3],
        grads[1],
        up_bias_grad,
        grads[0],
        sums[5],
    )


def solution(mesh):
    sizes = dict(mesh.shape)
    flat = sizes == {"dp": 4, "row": 4, "col": 2}
    per_device = plane_plan if flat else general_plan
    placed = (
        P(("dp", "col"), "row"),
        P("row"),
        P("row"),
        P("row", "col", None, None),
        P("col", None, None),
        P("col", None, "row"),
        P("row"),
        P("row"),
        P("row"),
        P("row", "col"),
        P("col"),
        P("col", "row"),
        P("row"),
        P("dp", None),
        P(("dp", "col"), "row"),
    )
    return jax.shard_map(
        per_device,
        mesh=mesh,
        in_specs=placed,
        out_specs=(
            P(("dp", "col"), "row"),
            P(("dp", "col"), "row"),
            P("row"),
            P("row"),
            P("row", "col", None, None),
            P("col", None, None),
            P("col", None, "row"),
            P("row"),
            P("row"),
            P("row"),
            P("row", "col"),
            P("col"),
            P("col", "row"),
            P("row"),
        ),
        check_vma=False,
    )
```

```python
import functools
import math

import jax
import jax.numpy as jnp
from jax import lax
from jax.experimental import pallas as pl
from jax.experimental.pallas import tpu as pltpu
from jax.sharding import PartitionSpec as P

MESH = pl.DeviceIdType.MESH

D = 2048
HEAD = 128
SEQS = 1
SPAN = 256
BLOCK = 512


epsilon = 1e-05
masked_score = -1e30


def gelu_tanh(values):
    return (
        0.5
        * values
        * (1.0 + jnp.tanh(0.7978845608028654 * (values + 0.044715 * values * values * values)))
    )


def gather_columns(block_data):
    return lax.all_gather(block_data, "col", axis=0, tiled=True)


def gather_rows(block_data):
    return lax.all_gather(block_data, "row", axis=0, tiled=True)


def product(left_side, right_side, flipped):
    if flipped:
        return lax.dot_general(
            left_side, right_side, (((1,), (1,)), ((), ())), preferred_element_type=jnp.float32
        )
    return jnp.dot(left_side, right_side, preferred_element_type=jnp.float32)


def outer_sum(left_side, right_side):
    return lax.dot_general(
        left_side, right_side, (((0,), (0,)), ((), ())), preferred_element_type=jnp.float32
    )


def sum_rows(left_side, right_side, flipped):
    wide_left = lax.all_to_all(left_side, "row", split_axis=0, concat_axis=1, tiled=True)
    if flipped:
        wide_right = lax.all_gather(right_side, "row", axis=1, tiled=True)
    else:
        wide_right = lax.all_gather(right_side, "row", axis=0, tiled=True)
    return product(wide_left, wide_right, flipped)


def sum_columns(left_side, right_side, flipped):
    return lax.psum_scatter(
        product(left_side, right_side, flipped), "col", scatter_dimension=0, tiled=True
    )


def row_totals(first_sum, second_sum):
    return lax.psum((first_sum, second_sum), "row")


def norm_forward(values, gain_row, bias_row):
    totals, squares = row_totals(jnp.sum(values, axis=1), jnp.sum(values * values, axis=1))
    center = totals / D
    spread = squares / D - center * center
    inverse = lax.rsqrt(spread + epsilon)
    standard = (values - center[:, None]) * inverse[:, None]
    return (standard, inverse, (standard * gain_row + bias_row).astype(jnp.bfloat16))


def norm_backward(upstream, standard, inverse, gain_row):
    scaled = upstream * gain_row
    first_sum, second_sum = row_totals(jnp.sum(scaled, axis=1), jnp.sum(scaled * standard, axis=1))
    gradient = inverse[:, None] * (
        scaled - first_sum[:, None] / D - standard * (second_sum[:, None] / D)
    )
    return (gradient, jnp.sum(upstream * standard, axis=0), jnp.sum(upstream, axis=0))


def visible(query_pos, query_image, key_pos):
    earlier = key_pos[None, :] <= query_pos[:, None]
    same_span = (key_pos[None, :] // SPAN == query_pos[:, None] // SPAN) & (
        query_image[:, None] > 0
    )
    return earlier | same_span


def attention_forward(queries, key_value, token_image, row_offset, seq_length, block_rows):
    own_rows, head_count, width = queries.shape
    factor = 1.0 / math.sqrt(width)

    def block_forward(block_index):
        local = block_index * block_rows
        start_pos = row_offset + local
        query_block = lax.dynamic_slice_in_dim(queries, local, block_rows, 0)
        query_pos = start_pos + jnp.arange(block_rows, dtype=jnp.int32)
        query_image = lax.dynamic_slice_in_dim(token_image, start_pos, block_rows, 0)
        begin = start_pos // seq_length * seq_length // block_rows
        finish = start_pos // block_rows + 1

        def key_step(key_index, state_in):
            running, weight_sum, gathered = state_in
            key_begin = key_index * block_rows
            key_block = lax.dynamic_slice_in_dim(key_value, key_begin, block_rows, 0)
            key_pos = key_begin + jnp.arange(block_rows, dtype=jnp.int32)
            allowed = visible(query_pos, query_image, key_pos)
            scores = (
                jnp.einsum(
                    "qhd,khd->hqk",
                    query_block,
                    key_block[:, :, 0],
                    preferred_element_type=jnp.float32,
                )
                * factor
            )
            scores = jnp.where(allowed[None], scores, masked_score)
            highest = jnp.maximum(running, jnp.max(scores, axis=2))
            weights = jnp.exp(scores - highest[:, :, None])
            shrink = jnp.exp(running - highest)
            weight_sum = weight_sum * shrink + jnp.sum(weights, axis=2)
            gathered = gathered * shrink.T[:, :, None] + jnp.einsum(
                "hqk,khd->qhd",
                weights.astype(jnp.bfloat16),
                key_block[:, :, 1],
                preferred_element_type=jnp.float32,
            )
            return (highest, weight_sum, gathered)

        initial = (
            jnp.full((head_count, block_rows), masked_score, jnp.float32),
            jnp.zeros((head_count, block_rows), jnp.float32),
            jnp.zeros((block_rows, head_count, width), jnp.float32),
        )
        running, weight_sum, gathered = lax.fori_loop(begin, finish, key_step, initial)
        return (gathered / weight_sum.T[:, :, None], running + jnp.log(weight_sum))

    result, logsum = lax.map(block_forward, jnp.arange(own_rows // block_rows, dtype=jnp.int32))
    return (result.reshape(own_rows, head_count, width), logsum)


def attention_backward(
    queries,
    key_value,
    attended_full,
    logsum,
    d_attended,
    token_image,
    row_offset,
    seq_length,
    block_rows,
):
    own_rows, head_count, width = queries.shape
    factor = 1.0 / math.sqrt(width)
    row_dots = jnp.sum(d_attended.astype(jnp.float32) * attended_full, axis=2)

    def block_backward(block_index, state_out):
        d_queries, d_pairs = state_out
        local = block_index * block_rows
        start_pos = row_offset + local
        query_block = lax.dynamic_slice_in_dim(queries, local, block_rows, 0)
        dout_block = lax.dynamic_slice_in_dim(d_attended, local, block_rows, 0)
        dots_block = lax.dynamic_slice_in_dim(row_dots, local, block_rows, 0).T
        logsum_block = logsum[block_index]
        query_pos = start_pos + jnp.arange(block_rows, dtype=jnp.int32)
        query_image = lax.dynamic_slice_in_dim(token_image, start_pos, block_rows, 0)
        begin = start_pos // seq_length * seq_length // block_rows
        finish = start_pos // block_rows + 1

        def key_step(key_index, state_in):
            d_query, d_keys = state_in
            key_begin = key_index * block_rows
            key_block = lax.dynamic_slice_in_dim(key_value, key_begin, block_rows, 0)
            key_pos = key_begin + jnp.arange(block_rows, dtype=jnp.int32)
            allowed = visible(query_pos, query_image, key_pos)
            scores = (
                jnp.einsum(
                    "qhd,khd->hqk",
                    query_block,
                    key_block[:, :, 0],
                    preferred_element_type=jnp.float32,
                )
                * factor
            )
            scores = jnp.where(allowed[None], scores, masked_score)
            probabilities = jnp.exp(scores - logsum_block[:, :, None])
            d_probs = jnp.einsum(
                "qhd,khd->hqk", dout_block, key_block[:, :, 1], preferred_element_type=jnp.float32
            )
            d_scores = (probabilities * (d_probs - dots_block[:, :, None])).astype(jnp.bfloat16)
            d_query = d_query + jnp.einsum(
                "hqk,khd->qhd", d_scores, key_block[:, :, 0], preferred_element_type=jnp.float32
            )
            d_key = (
                jnp.einsum(
                    "hqk,qhd->khd", d_scores, query_block, preferred_element_type=jnp.float32
                )
                * factor
            )
            d_value = jnp.einsum(
                "hqk,qhd->khd",
                probabilities.astype(jnp.bfloat16),
                dout_block,
                preferred_element_type=jnp.float32,
            )
            previous = lax.dynamic_slice_in_dim(d_keys, key_begin, block_rows, 0)
            d_keys = lax.dynamic_update_slice_in_dim(
                d_keys, previous + jnp.stack([d_key, d_value], axis=2), key_begin, 0
            )
            return (d_query, d_keys)

        d_query, d_pairs = lax.fori_loop(
            begin,
            finish,
            key_step,
            (jnp.zeros((block_rows, head_count, width), jnp.float32), d_pairs),
        )
        d_queries = lax.dynamic_update_slice_in_dim(d_queries, d_query * factor, local, 0)
        return (d_queries, d_pairs)

    initial = (
        jnp.zeros((own_rows, head_count, width), jnp.float32),
        jnp.zeros((key_value.shape[0], head_count, 2, width), jnp.float32),
    )
    return lax.fori_loop(0, own_rows // block_rows, block_backward, initial)


def general_plan(
    tokens,
    ln1_gain,
    ln1_shift,
    qkv_weight,
    qv_bias,
    out_weight,
    out_bias,
    ln2_gain,
    ln2_shift,
    up_weight,
    up_bias,
    down_weight,
    down_bias,
    span_starts,
    cotangent,
):
    col_rows, row_width = tokens.shape
    group_rows = col_rows * lax.axis_size("col")
    own_rows = group_rows // lax.axis_size("row")
    head_count = qkv_weight.shape[1]
    seq_length = group_rows // SEQS
    block_rows = BLOCK - own_rows % BLOCK
    row_offset = lax.axis_index("row") * own_rows
    slot_count = seq_length // SPAN
    image_marks = jnp.sum(
        (
            span_starts[:, :, None] // SPAN
            == jnp.arange(slot_count, dtype=jnp.int32)[None, None, :]
        ).astype(jnp.int32),
        axis=1,
    )
    token_image = jnp.broadcast_to(
        image_marks.reshape(-1)[:, None], (group_rows // SPAN, SPAN)
    ).reshape(group_rows)
    qkv_flat = qkv_weight.reshape(row_width, head_count * 3 * HEAD)
    out_flat = out_weight.reshape(head_count * HEAD, row_width)
    inputs = tokens.astype(jnp.float32)
    standard1, inverse1, normed1 = norm_forward(inputs, ln1_gain, ln1_shift)
    normed1_all = gather_columns(normed1)
    mixed_sums = sum_rows(normed1_all, qkv_flat, False).reshape(own_rows, head_count, 3, HEAD)
    queries = (mixed_sums[:, :, 0] + qv_bias[:, 0]).astype(jnp.bfloat16)
    key_value_own = jnp.stack(
        [mixed_sums[:, :, 1], mixed_sums[:, :, 2] + qv_bias[:, 1]], axis=2
    ).astype(jnp.bfloat16)
    key_value = gather_rows(key_value_own)
    attended_full, logsum = attention_forward(
        queries, key_value, token_image, row_offset, seq_length, block_rows
    )
    attended = attended_full.astype(jnp.bfloat16).reshape(own_rows, head_count * HEAD)
    attended_all = gather_rows(attended)
    residual = inputs + (sum_columns(attended_all, out_flat, False) + out_bias)
    standard2, inverse2, normed2 = norm_forward(residual, ln2_gain, ln2_shift)
    normed2_all = gather_columns(normed2)
    up_sums = sum_rows(normed2_all, up_weight, False) + up_bias
    hidden = gelu_tanh(up_sums).astype(jnp.bfloat16)
    hidden_all = gather_rows(hidden)
    output = (residual + (sum_columns(hidden_all, down_weight, False) + down_bias)).astype(
        jnp.bfloat16
    )
    d_output = cotangent.astype(jnp.float32)
    d_output_all = gather_columns(cotangent)
    down_grad = outer_sum(hidden_all, d_output_all)
    down_bias_grad = jnp.sum(d_output_all, axis=0, dtype=jnp.float32)
    d_hidden = sum_rows(d_output_all, down_weight, True)
    d_upper = jax.vjp(gelu_tanh, up_sums)[1](d_hidden)[0].astype(jnp.bfloat16)
    d_upper_all = gather_rows(d_upper)
    normed2_use = gather_columns(normed2)
    up_grad = outer_sum(normed2_use, d_upper_all)
    up_bias_grad = jnp.sum(d_upper_all, axis=0, dtype=jnp.float32)
    d_normed2 = sum_columns(d_upper_all, up_weight, True)
    d_norm2, gain2_grad, shift2_grad = norm_backward(d_normed2, standard2, inverse2, ln2_gain)
    d_residual = d_output + d_norm2
    d_branch = d_residual.astype(jnp.bfloat16)
    d_branch_all = gather_columns(d_branch)
    out_grad = outer_sum(attended_all, d_branch_all)
    out_bias_grad = jnp.sum(d_branch_all, axis=0, dtype=jnp.float32)
    d_attended = (
        sum_rows(d_branch_all, out_flat, True)
        .astype(jnp.bfloat16)
        .reshape(own_rows, head_count, HEAD)
    )
    d_queries, d_pairs = attention_backward(
        queries,
        key_value,
        attended_full,
        logsum,
        d_attended,
        token_image,
        row_offset,
        seq_length,
        block_rows,
    )
    d_pairs_own = lax.psum_scatter(d_pairs, "row", scatter_dimension=0, tiled=True)
    d_mixed = jnp.concatenate([d_queries[:, :, None], d_pairs_own], axis=2).astype(jnp.bfloat16)
    d_mixed_all = gather_rows(d_mixed)
    normed1_use = gather_columns(normed1)
    d_mixed_flat = d_mixed_all.reshape(group_rows, head_count * 3 * HEAD)
    qkv_grad = outer_sum(normed1_use, d_mixed_flat)
    mixed_totals = jnp.sum(d_mixed_all, axis=0, dtype=jnp.float32)
    qv_bias_grad = jnp.stack([mixed_totals[:, 0], mixed_totals[:, 2]], axis=1)
    d_normed1 = sum_columns(d_mixed_flat, qkv_flat, True)
    d_norm1, gain1_grad, shift1_grad = norm_backward(d_normed1, standard1, inverse1, ln1_gain)
    tokens_grad = (d_residual + d_norm1).astype(jnp.bfloat16)
    norm_sums = lax.psum((gain1_grad, shift1_grad, gain2_grad, shift2_grad), ("dp", "col"))
    weight_sums = lax.psum(
        (
            qkv_grad,
            qv_bias_grad,
            out_grad,
            out_bias_grad,
            up_grad,
            up_bias_grad,
            down_grad,
            down_bias_grad,
        ),
        "dp",
    )
    return (
        output,
        tokens_grad,
        norm_sums[0],
        norm_sums[1],
        weight_sums[0].reshape(row_width, head_count, 3, HEAD),
        weight_sums[1],
        weight_sums[2].reshape(head_count, HEAD, row_width),
        weight_sums[3],
        norm_sums[2],
        norm_sums[3],
        weight_sums[4],
        weight_sums[5],
        weight_sums[6],
        weight_sums[7],
    )


def places():
    row, col = lax.axis_index("row"), lax.axis_index("col")
    return col, row // 2, row % 2


def partners():
    col, side, core = places()
    return ({"col": 1 - col}, {"row": (1 - side) * 2 + core}, {"row": side * 2 + 1 - core})


def block(ref, col, side, core, rows, width, part=None):
    begin, count = col * rows, rows
    if part is not None:
        begin, count = begin + part * (rows // 2), rows // 2
    return ref.at[strip(begin, count), strip((side * 2 + core) * width, width)]


def put(ref_from, ref_to, sends, recvs, at, partner):
    return pltpu.make_async_remote_copy(
        src_ref=ref_from,
        dst_ref=ref_to,
        send_sem=sends.at[at],
        recv_sem=recvs.at[at],
        device_id=partner,
        device_id_type=MESH,
    )


def strip(begin, count):
    return pl.ds(pl.multiple_of(begin, count), count)


def dot_nt(left, right):
    return lax.dot_general(left, right, (((1,), (1,)), ((), ())), preferred_element_type=jnp.float32)


def dot_tn(left, right):
    return lax.dot_general(left, right, (((0,), (0,)), ((), ())), preferred_element_type=jnp.float32)


def tiled_nt(left, right, target, inner, tile_rows, tile_cols, span=(0, 1, 1)):
    rows, cols = target.shape
    across = cols // tile_cols

    def step(at, none):
        down, side = at // across, at % across
        value = dot_nt(left[strip(down * tile_rows, tile_rows), :inner], right[strip(side * tile_cols, tile_cols), :inner])
        target[strip(down * tile_rows, tile_rows), strip(side * tile_cols, tile_cols)] = value.astype(target.dtype)
        return none

    count = (rows // tile_rows) * across
    lax.fori_loop(span[0] * count // span[2], span[1] * count // span[2], step, 0)


def tiled_nn(left, right, target, tile_rows, tile_cols, span=(0, 1, 1)):
    rows, cols = target.shape
    across = cols // tile_cols

    def step(at, none):
        down, side = at // across, at % across
        value = jnp.dot(
            left[strip(down * tile_rows, tile_rows), :],
            right[:, strip(side * tile_cols, tile_cols)],
            preferred_element_type=jnp.float32,
        )
        target[strip(down * tile_rows, tile_rows), strip(side * tile_cols, tile_cols)] = value.astype(target.dtype)
        return none

    count = (rows // tile_rows) * across
    lax.fori_loop(span[0] * count // span[2], span[1] * count // span[2], step, 0)


def reduce_steps(part, result, got, diag, half_x, half_y, to_send, from_xy, sends, recvs, base, mostly_x=False):
    f32 = jnp.float32
    rows, width = result.shape
    half = rows // 2
    low, high = pl.ds(0, half), pl.ds(half, half)
    col, side, core = places()
    to_x, to_y, to_core = partners()
    spots = ((1 - col, 1 - side), (col, 1 - side), (1 - col, side), (col, side))
    copies = [
        put(block(part, a, b, 1 - core, rows, width), got.at[k], sends, recvs, base + k, to_core)
        for k, (a, b) in enumerate(spots)
    ]
    for copy in copies:
        copy.start()
    mine = [block(part, a, b, core, rows, width) for a, b in spots]
    dx = put(diag.at[low], half_x, sends, recvs, base + 4, to_x)
    dy = put(diag.at[high], half_y, sends, recvs, base + 5, to_x if mostly_x else to_y)

    def onward(k, span, at, partner):
        return put(to_send.at[k, span], from_xy.at[k, span], sends, recvs, base + at, partner)

    y_high, x_low = onward(0, high, 6, to_y), onward(1, low, 7, to_x)
    y_low, x_high = onward(0, low, 8, to_y), onward(1, high, 9, to_x)

    def pair(k, span):
        return mine[k][span].astype(f32) + got[k, span].astype(f32)

    yield
    copies[0].wait_recv()
    diag[...] = (mine[0][...].astype(f32) + got[0].astype(f32)).astype(diag.dtype)
    dx.start()
    dy.start()
    copies[1].wait_recv()
    if not mostly_x:
        to_send[0, high] = pair(1, high).astype(diag.dtype)
        y_high.start()
    copies[2].wait_recv()
    to_send[1, low] = pair(2, low).astype(diag.dtype)
    x_low.start()
    if mostly_x:
        to_send[1, high] = pair(2, high).astype(diag.dtype)
        x_high.start()
    copies[3].wait_recv()
    yield
    dx.wait_recv()
    to_send[0, low] = (pair(1, low) + half_x[...].astype(f32)).astype(diag.dtype)
    y_low.start()
    dy.wait_recv()
    if mostly_x:
        to_send[0, high] = (pair(1, high) + half_y[...].astype(f32)).astype(diag.dtype)
        y_high.start()
    else:
        to_send[1, high] = (pair(2, high) + half_y[...].astype(f32)).astype(diag.dtype)
        x_high.start()
    yield
    for copy in (y_high, x_low, y_low, x_high):
        copy.wait_recv()
    near = mine[3][...].astype(f32) + got[3].astype(f32)
    result[...] = near + from_xy[0].astype(f32) + from_xy[1].astype(f32)
    for copy in copies + [dx, dy, y_high, x_low, y_low, x_high]:
        copy.wait_send()


def spread_steps(out, rows, width, sends, recvs, base, mostly_x=False):
    col, side, core = places()
    to_x, to_y, to_core = partners()

    def copy_of(at, which, partner, part=None):
        ref = block(out, *which, rows, width, part)
        return put(ref, ref, sends, recvs, base + at, partner)

    own, ox, oy, od = (col, side, core), (1 - col, side, core), (col, 1 - side, core), (1 - col, 1 - side, core)
    plan = [
        copy_of(0, own, to_x, 0),
        copy_of(1, own, to_y, 1),
        copy_of(2, own, to_x, 1),
        copy_of(3, own, to_y, 0),
        copy_of(4, own, to_core),
        copy_of(5, oy, to_x, 0) if mostly_x else copy_of(5, ox, to_y, 0),
        copy_of(6, oy, to_x, 1),
        copy_of(7, ox, to_core),
        copy_of(8, oy, to_core),
        copy_of(9, od, to_core),
    ]
    for at in range(5):
        plan[at].start()
    yield
    plan[0].wait_recv()
    if not mostly_x:
        plan[5].start()
    plan[1].wait_recv()
    plan[6].start()
    plan[2].wait_recv()
    plan[7].start()
    plan[3].wait_recv()
    plan[8].start()
    if mostly_x:
        plan[5].start()
    yield
    plan[5].wait_recv()
    plan[6].wait_recv()
    plan[9].start()
    yield
    for at in (4, 7, 8, 9):
        plan[at].wait_recv()
    for copy in plan:
        copy.wait_send()


CHUNK = 256
LINES = CHUNK // 2


def backward_kernel(
    counts,
    hid_h,
    cot_h,
    slope_h,
    n2_h,
    upw_h,
    std_h,
    n1_h,
    qkvw_h,
    down_nat,
    resid_h,
    attended_h,
    outw_h,
    mixed_h,
    std1_h,
    stats,
    marks,
    vec_all,
    inv1_own,
    down_bias,
    down_out,
    up_out,
    out_out,
    qkv_out,
    b_land,
    downw_land,
    out_block,
    tokens_block,
    small_out,
    cot,
    n2,
    std,
    part,
    tot,
    upw,
    hid,
    dup,
    attended,
    outw,
    mixed,
    std1_own,
    d_att,
    d_mix,
    dk_acc,
    dv_acc,
    g,
    s,
    t,
    r_land,
    m_land,
    got_a,
    diag_a,
    hx_a,
    hy_a,
    ts_a,
    fx_a,
    got_b,
    diag_b,
    hx_b,
    hy_b,
    ts_b,
    fx_b,
    dres_own,
    own_sum,
    sums,
    small,
    x_land,
    dp_land,
    stat_land,
    load_sem,
    credit,
    own_sem,
    z_send,
    z_recv,
    a_send,
    a_recv,
    p_send,
    p_recv,
):
    f32, bf16 = jnp.float32, jnp.bfloat16
    n_down, n_up, n_out, n_qkv = counts
    total = sum(counts)
    plane, row, col = lax.axis_index("dp"), lax.axis_index("row"), lax.axis_index("col")
    length, full = cot.shape
    rows, width = dres_own.shape
    row_count = full // width
    inner = (plane == 1) | (plane == 2)
    outer = jnp.logical_not(inner)
    to_inner = {"dp": plane // 3 + 1}
    to_middle = {"dp": 3 - plane}
    to_outer = {"dp": (plane - 1) * 3}
    side, core = row // 2, row % 2

    loads = [
        (hid_h, hid),
        (cot_h, cot),
        (slope_h, dup),
        (upw_h, upw),
        (n2_h, n2),
        (std_h, std),
        (qkvw_h, upw.at[:, : qkvw_h.shape[1]]),
        (n1_h, std),
        (downw_land, n2),
        (downw_land, tot),
        (resid_h, dres_own),
        (attended_h, attended),
        (outw_h, outw),
        (mixed_h, mixed),
        (std1_h, std1_own),
    ]
    loads = [pltpu.make_async_copy(a, b, load_sem.at[k]) for k, (a, b) in enumerate(loads)]
    for k in (0, 1, 2, 3, 4, 5, 11, 12, 13, 14):
        loads[k].start()

    dp_count = dp_land.shape[0]
    barrier = pltpu.get_barrier_semaphore()
    others = [{"row": (1 - side) * 2 + 1 - core}] + [{"dp": (plane + k) % dp_count} for k in range(1, dp_count)]
    for partner in partners() + tuple(others):
        pl.semaphore_signal(barrier, inc=1, device_id=partner, device_id_type=MESH)
    pl.semaphore_wait(barrier, 3 + len(others))

    units = hid.shape[1]
    down_sends, down_recvs = [], []
    for step in range(1, row_count):
        target, source = (row + step) % row_count, (row + row_count - step) % row_count
        here, there = downw_land.at[:, strip(row * width, width)], downw_land.at[:, strip(source * width, width)]
        piece = down_nat.at[strip(target * units, units), :]
        down_sends.append(put(piece, here, p_send, p_recv, 40 + step - 1, {"row": target}))
        down_recvs.append(put(piece, there, p_send, p_recv, 40 + step - 1, {"row": source}))
        down_sends[-1].start()
    down_own = pltpu.make_async_copy(
        down_nat.at[strip(row * units, units), :], downw_land.at[:, strip(row * width, width)], own_sem.at[4 * total]
    )
    down_own.start()

    def place(u, source):
        i, half, quarter = u // 4, u // 2 % 2, pl.ds(u % 2 * LINES, LINES)
        if i < n_down:
            return down_out.at[source * n_down + i // 2 * 2 + half, quarter, pl.ds(i % 2 * CHUNK, CHUNK)]
        i -= n_down
        if i < n_up:
            return up_out.at[half, quarter, strip(source * n_up * CHUNK + i * CHUNK, CHUNK)]
        i -= n_up
        if i < n_out:
            return out_out.at[source * n_out + i, quarter, pl.ds(half * CHUNK, CHUNK)]
        i -= n_out
        return qkv_out.at[half, quarter, strip(source * n_qkv * CHUNK + i * CHUNK, CHUNK)]

    g_slots, s_slots, t_slots, r_slots, m_slots = g.shape[0], s.shape[0], t.shape[0], r_land.shape[0], m_land.shape[0]
    pieces = 4 * total

    def made(u):
        return g.at[u // 4 % g_slots, :, u // 2 % 2, pl.ds(u % 2 * LINES, LINES)]

    def inward(u):
        return put(made(u), r_land.at[u % r_slots], z_send, z_recv, u, to_inner)

    def across(u):
        return put(s.at[u % s_slots], m_land.at[u % m_slots], z_send, z_recv, pieces + u, to_middle)

    def outward(u):
        return put(t.at[u % t_slots], b_land.at[u], z_send, z_recv, 2 * pieces + u, to_outer)

    def home(u, step, source):
        target = (row + step) % row_count
        return put(source.at[target], place(u, row), a_send, a_recv, 3 * u + step - 1, {"row": target})

    def home_own(u, source):
        return pltpu.make_async_copy(source.at[row], place(u, row), own_sem.at[u])

    def send_home(u, source):
        for step in range(1, row_count):
            home(u, step, source).start()
        home_own(u, source).start()

    def sent_home(u, source):
        for step in range(1, row_count):
            home(u, step, source).wait_send()
        home_own(u, source).wait()

    def produce(i):
        if i >= g_slots:

            @pl.when(outer)
            def _():
                for k in range(4):
                    inward(4 * (i - g_slots) + k).wait_send()

        slot = g.at[i % g_slots]
        if i < n_down:
            begin, lane = i // 2 * 2 * CHUNK, i % 2 * CHUNK

            def step(k, none):
                value = dot_tn(hid[:, begin : begin + 2 * CHUNK], cot[:, strip(k * width + lane, CHUNK)]).astype(bf16)
                slot[k, 0] = value[:CHUNK]
                slot[k, 1] = value[CHUNK:]
                return none
        elif n_down + n_up <= i < n_down + n_up + n_out:
            left, begin, right = attended, (i - n_down - n_up) * CHUNK, part

            def step(k, none):
                value = dot_tn(left[:, begin : begin + CHUNK], right[:, strip(k * width, width)]).astype(bf16)
                slot[k, 0] = value[:, :CHUNK]
                slot[k, 1] = value[:, CHUNK:]
                return none
        else:
            if i < n_down + n_up:
                left, right, begin = n2, dup, (i - n_down) * CHUNK
            else:
                left, right, begin = std, d_mix, (i - n_down - n_up - n_out) * CHUNK

            def step(k, none):
                value = dot_tn(left[:, strip(k * width, width)], right[:, begin : begin + CHUNK]).astype(bf16)
                slot[k, 0] = value[:CHUNK]
                slot[k, 1] = value[CHUNK:]
                return none

        lax.fori_loop(0, row_count, step, 0)

    def launch(u):
        @pl.when(outer)
        def _():
            if u >= r_slots:
                pl.semaphore_wait(credit, 1)
            inward(u).start()

    def add(first, second, target):
        for k in range(row_count):
            target[k] = (first[k].astype(f32) + second[k].astype(f32)).astype(bf16)

    def middle(u):
        @pl.when(inner)
        def _():
            inward(u).wait_recv()
            add(made(u), r_land.at[u % r_slots], s.at[u % s_slots])
            across(u).start()
            if u + r_slots < pieces:
                pl.semaphore_signal(credit, inc=1, device_id=to_outer, device_id_type=MESH)

    def finish_inner(u):
        @pl.when(inner)
        def _():
            if u >= t_slots:
                outward(u - t_slots).wait_send()
                sent_home(u - t_slots, t.at[u % t_slots])
            across(u).wait_recv()
            add(s.at[u % s_slots], m_land.at[u % m_slots], t.at[u % t_slots])
            outward(u).start()
            send_home(u, t.at[u % t_slots])
            across(u).wait_send()

    def finish_outer(u):
        @pl.when(outer)
        def _():
            outward(u).wait_recv()
            send_home(u, b_land.at[u])

    ahead = 4

    def pass_on(u):
        middle(u)
        if u >= 2:
            finish_inner(u - 2)
        if u + ahead < pieces:
            if u % 4 == 0:
                produce((u + ahead) // 4)
            launch(u + ahead)
        if u >= 3:
            finish_outer(u - 3)

    set_a = (got_a, diag_a, hx_a, hy_a, ts_a, fx_a)
    set_b = (got_b, diag_b, hx_b, hy_b, ts_b, fx_b)
    gain2 = vec_all[3:4, :]
    heads = mixed.shape[1] // (3 * HEAD)
    here = strip(row * width, width)
    tile = 64
    first = reduce_steps(part, own_sum, *set_a, p_send, p_recv, 0, mostly_x=True)
    second = spread_steps(tot, rows, width, p_send, p_recv, 10, mostly_x=True)
    third = reduce_steps(cot, own_sum, *set_b, p_send, p_recv, 20, mostly_x=True)
    fourth = reduce_steps(tot, own_sum, *set_a, p_send, p_recv, 30, mostly_x=True)

    def down_here():
        down_own.wait()
        for copy in down_recvs:
            copy.wait_recv()
        loads[9].start()

    def upper_step(k, none):
        down, across_ = k // (units // CHUNK), k % (units // CHUNK)
        at, lanes = strip(down * rows, rows), strip(across_ * CHUNK, CHUNK)
        dup[at, lanes] = (dot_nt(cot[at, :], tot[lanes, :]) * dup[at, lanes].astype(f32)).astype(bf16)
        return none

    def uppers(part_of):
        if part_of == 0:
            for k in (2, 3, 4, 9):
                loads[k].wait()
        count = (length // rows) * (units // CHUNK) // 2
        lax.fori_loop(part_of * count, (part_of + 1) * count, upper_step, 0)

    def d_normed2(part_of):
        tiled_nt(dup, upw, part, units, 1024, 256, (part_of, part_of + 1, 2))
        if part_of == 1:
            loads[6].start()
            next(first)

    def gather_start():
        next(first, None)
        block(tot, col, side, core, rows, width)[...] = own_sum[...].astype(bf16)
        next(second)

    def norm_step(k, none):
        at = strip(k * tile, tile)
        grad, standard, inverse = tot[at, :].astype(f32), std[at, :].astype(f32), stats[at, 0:1]
        scaled = grad * gain2
        mean_one = jnp.sum(scaled, axis=1, keepdims=True) / full
        mean_two = jnp.sum(scaled * standard, axis=1, keepdims=True) / full
        top = cot[at, :].astype(f32)
        low = (top + inverse * (scaled - mean_one - standard * mean_two)).astype(bf16)
        part[at, :] = low
        sums[0:1, :] += jnp.sum(grad * standard, axis=0, keepdims=True)
        sums[1:2, :] += jnp.sum(grad, axis=0, keepdims=True)
        sums[2:3, :] += jnp.sum(low.astype(f32), axis=0, keepdims=True)
        sums[3:4, :] += jnp.sum(top, axis=0, keepdims=True)

        @pl.when(k // (rows // tile) == col)
        def _():
            own = tot[at, here].astype(f32) * vec_all[3:4, here]
            dres_own[strip(k % (rows // tile) * tile, tile), :] = cot[at, here].astype(f32) + inverse * (
                own - mean_one - std[at, here].astype(f32) * mean_two
            )

        return none

    def norm_back(part_of):
        if part_of == 0:
            for k in (5, 11, 12, 13, 14):
                loads[k].wait()
        count = length // tile // 2
        lax.fori_loop(part_of * count, (part_of + 1) * count, norm_step, 0)
        if part_of == 1:
            loads[7].start()

    def d_attended():
        tiled_nt(part, outw, d_att, full, 512, 256)

    factor = 1.0 / math.sqrt(HEAD)
    blocks = length // SPAN
    spots = (SPAN, SPAN)
    earlier = lax.broadcasted_iota(jnp.int32, spots, 1) <= lax.broadcasted_iota(jnp.int32, spots, 0)

    def attention_back(head, begin, end):
        base = head * 3 * HEAD
        at_q, at_k, at_v = pl.ds(base, HEAD), pl.ds(base + HEAD, HEAD), pl.ds(base + 2 * HEAD, HEAD)
        at_o = pl.ds(head * HEAD, HEAD)
        if begin == 0:
            dk_acc[...] = jnp.zeros_like(dk_acc)
            dv_acc[...] = jnp.zeros_like(dv_acc)
        for k in range(begin, end):
            now = pl.ds(k * SPAN, SPAN)
            seen = (k + 1) * SPAN
            query, dout = mixed[now, at_q], d_att[now, at_o]
            keys, values = mixed[:seen, at_k], mixed[:seen, at_v]
            scores = dot_nt(query, keys) * factor
            last = jnp.where(earlier | (marks[k : k + 1, :1] > 0), scores[:, seen - SPAN :], masked_score)
            scores = last if k == 0 else jnp.concatenate([scores[:, : seen - SPAN], last], axis=1)
            probs = jnp.exp(scores - stats[now, 1 + head : 2 + head])
            d_probs = dot_nt(dout, values)
            dots = jnp.sum(probs * d_probs, axis=1, keepdims=True)
            d_scores = (probs * (d_probs - dots)).astype(bf16)
            d_mix[now, at_q] = (jnp.dot(d_scores, keys, preferred_element_type=f32) * factor).astype(bf16)
            dk_acc[:seen] += dot_tn(d_scores, query)
            dv_acc[:seen] += dot_tn(probs.astype(bf16), dout)
        if end == blocks:
            d_mix[:, at_k] = (dk_acc[...] * factor).astype(bf16)
            d_mix[:, at_v] = dv_acc[...].astype(bf16)

    def d_normed1(part_of):
        if part_of == 0:
            loads[6].wait()
        tiled_nt(d_mix, upw, cot, d_mix.shape[1], 1024, 256, (part_of, part_of + 1, 2))
        if part_of == 1:
            next(third)

    def output_sums(part_of):
        if part_of == 0:
            loads[8].wait()
        tiled_nn(hid, n2, tot, 1024, 256, (part_of, part_of + 1, 2))
        if part_of == 1:
            next(fourth)

    grad1 = own_sum
    stat_sends, stat_recvs, dp_sends, dp_recvs, row_sends, row_recvs = [], [], [], [], [], []
    for step in range(1, row_count):
        target, source = (row + step) % row_count, (row + row_count - step) % row_count
        to, since = {"row": target}, {"row": source}
        stat_sends.append(put(stat_land.at[row], stat_land.at[row], p_send, p_recv, 43 + step - 1, to))
        stat_recvs.append(put(stat_land.at[source], stat_land.at[source], p_send, p_recv, 43 + step - 1, since))
        row_sends.append(put(small_out.at[row], small_out.at[row], p_send, p_recv, 50 + step - 1, to))
        row_recvs.append(put(small_out.at[source], small_out.at[source], p_send, p_recv, 50 + step - 1, since))
    for step in range(1, dp_count):
        target, source = (plane + step) % dp_count, (plane + dp_count - step) % dp_count
        dp_sends.append(put(dp_land.at[plane], dp_land.at[plane], p_send, p_recv, 47 + step - 1, {"dp": target}))
        dp_recvs.append(put(dp_land.at[source], dp_land.at[source], p_send, p_recv, 47 + step - 1, {"dp": source}))
    x_copy = put(small.at[pl.ds(0, 8)], x_land, p_send, p_recv, 46, partners()[0])

    def row_stats():
        next(third, None)
        scaled = grad1[...] * vec_all[0:1, here]
        first_sum = jnp.sum(scaled, axis=1, keepdims=True)
        second_sum = jnp.sum(scaled * std1_own[...].astype(f32), axis=1, keepdims=True)
        lane = lax.broadcasted_iota(jnp.int32, (rows, 128), 1)
        pair = jnp.where(lane == 0, first_sum, jnp.where(lane == 1, second_sum, 0.0))
        stat_land[row] = pair.T[:8]
        for copy in stat_sends:
            copy.start()

    def small_sums():
        small[...] = jnp.zeros_like(small)
        small[0:1, :] = jnp.sum(grad1[...] * std1_own[...].astype(f32), axis=0, keepdims=True)
        small[1:2, :] = jnp.sum(grad1[...], axis=0, keepdims=True)
        small[2:6, :] = sums[0:4, here]
        totals = jnp.sum(dup[...].astype(f32), axis=0, keepdims=True)
        for k in range(units // width):
            small[8 + k : 9 + k, :] = totals[:, k * width : (k + 1) * width]
        mixes = jnp.sum(d_mix[...].astype(f32), axis=0, keepdims=True)
        spot = 8 + units // width
        picked = [
            mixes[:, (head * 3 + kind) * HEAD : (head * 3 + kind + 1) * HEAD] for head in range(heads) for kind in (0, 2)
        ]
        small[spot : spot + 1, : 2 * heads * HEAD] = jnp.concatenate(picked, axis=1)
        x_copy.start()

    def tokens_out():
        for copy in stat_recvs:
            copy.wait_recv()
        both = stat_land[0]
        for k in range(1, row_count):
            both = both + stat_land[k]
        both = jnp.concatenate([both, jnp.zeros((120, rows), f32)], axis=0).T
        scaled = grad1[...] * vec_all[0:1, here]
        d_norm1 = inv1_own[...] * (
            scaled - both[:, 0:1] / full - std1_own[...].astype(f32) * (both[:, 1:2] / full)
        )
        tokens_block[...] = (dres_own[...] + d_norm1).astype(bf16)
        loads[10].start()

    def dp_start():
        x_copy.wait_recv()
        x_copy.wait_send()
        small[0:2, :] += x_land[0:2, :]
        dp_land[plane] = small[...]
        for copy in dp_sends:
            copy.start()

    def output_out():
        next(fourth, None)
        loads[10].wait()
        out_block[...] = (dres_own[...] + (own_sum[...] + down_bias[...])).astype(bf16)

    def rows_start():
        for copy in dp_recvs:
            copy.wait_recv()
        together = dp_land[0]
        for k in range(1, dp_count):
            together = together + dp_land[k]
        small_out[row] = together
        for copy in row_sends:
            copy.start()

    tasks = {
        6: [down_here],
        8: [lambda: uppers(0)],
        9: [lambda: uppers(1)],
        10: [lambda: d_normed2(0)],
        11: [lambda: d_normed2(1)],
        13: [lambda: next(first)],
        16: [lambda: next(first)],
        19: [gather_start],
        22: [lambda: next(second)],
        24: [lambda: next(second)],
        25: [lambda: next(second, None), loads[8].start],
        26: [lambda: norm_back(0)],
        27: [lambda: norm_back(1)],
        28: [d_attended],
        29: [lambda: attention_back(0, 0, blocks)],
        30: [lambda: attention_back(1, 0, blocks)],
        31: [lambda: output_sums(0), loads[7].wait],
        32: [lambda: d_normed1(0)],
        33: [lambda: d_normed1(1)],
        34: [lambda: next(third)],
        35: [lambda: output_sums(1)],
        36: [lambda: next(fourth)],
        37: [lambda: next(third)],
        39: [lambda: next(fourth)],
        40: [row_stats],
        41: [small_sums],
        42: [tokens_out],
        43: [dp_start],
        44: [output_out],
        45: [rows_start],
    }
    sums[...] = jnp.zeros_like(sums)
    loads[0].wait()
    loads[1].wait()
    produce(0)
    for k in range(ahead):
        launch(k)
    for u in range(pieces):
        pass_on(u)
        for task in tasks.get(u, ()):
            task()
    finish_inner(pieces - 2)
    finish_inner(pieces - 1)
    finish_outer(pieces - 3)
    finish_outer(pieces - 2)
    finish_outer(pieces - 1)
    for copy in row_recvs:
        copy.wait_recv()
    for copy in down_sends + stat_sends + dp_sends + row_sends:
        copy.wait_send()

    @pl.when(outer)
    def _():
        for u in range(pieces - 4 * g_slots, pieces):
            inward(u).wait_send()
        for u in range(pieces):
            sent_home(u, b_land.at[u])

    @pl.when(inner)
    def _():
        for u in range(pieces - t_slots, pieces):
            outward(u).wait_send()
            sent_home(u, t.at[u % t_slots])

    for u in range(pieces):
        for step in range(1, row_count):
            source = (row + row_count - step) % row_count
            put(t.at[0, source], place(u, source), a_send, a_recv, 3 * u + step - 1, {"row": source}).wait_recv()


def backward_plane(
    cid, hid, cot, slope, n2, upw, std, n1, qkvw, down_nat, resid_own, attended, outw, mixed, std1_own, stats, marks, vec_all, inv1_own, down_bias
):
    f32, bf16 = jnp.float32, jnp.bfloat16
    length, full = cot.shape
    rows, width = length // lax.axis_size("col"), full // lax.axis_size("row")
    row_count, dp_count = full // width, lax.axis_size("dp")
    counts = (slope.shape[1] // CHUNK, slope.shape[1] // CHUNK, attended.shape[1] // CHUNK, mixed.shape[1] // CHUNK)
    total = sum(counts)
    unit = (row_count, LINES, CHUNK)
    shape = jax.ShapeDtypeStruct
    away, near = pl.BlockSpec(memory_space=pl.ANY), pl.BlockSpec(memory_space=pltpu.VMEM)
    vmem, dma = pltpu.VMEM, pltpu.SemaphoreType.DMA
    sets = [
        vmem((4, rows, width), bf16),
        vmem((rows, width), bf16),
        vmem((rows // 2, width), bf16),
        vmem((rows // 2, width), bf16),
        vmem((2, rows, width), bf16),
        vmem((2, rows, width), bf16),
    ]
    return pl.pallas_call(
        functools.partial(backward_kernel, counts),
        out_shape=[
            shape((row_count * counts[0], CHUNK, width), bf16),
            shape((2, CHUNK, row_count * counts[1] * CHUNK), bf16),
            shape((row_count * counts[2], CHUNK, width), bf16),
            shape((2, CHUNK, row_count * counts[3] * CHUNK), bf16),
            shape((4 * total,) + unit, bf16),
            shape((hid.shape[1], full), bf16),
            shape((rows, width), bf16),
            shape((rows, width), bf16),
            shape((row_count, 16, width), f32),
        ],
        in_specs=[away] * 14 + [near] * 5,
        out_specs=[away] * 6 + [near] * 3,
        scratch_shapes=[
            vmem((length, full), bf16),
            vmem((length, full), bf16),
            vmem((length, full), bf16),
            vmem((length, full), bf16),
            vmem((length, full), bf16),
            vmem(upw.shape, bf16),
            vmem(hid.shape, bf16),
            vmem(slope.shape, bf16),
            vmem(attended.shape, bf16),
            vmem(outw.shape, bf16),
            vmem(mixed.shape, bf16),
            vmem(std1_own.shape, bf16),
            vmem(attended.shape, bf16),
            vmem(mixed.shape, bf16),
            vmem((length, HEAD), f32),
            vmem((length, HEAD), f32),
            vmem((2, row_count, width // CHUNK, CHUNK, CHUNK), bf16),
            vmem((3,) + unit, bf16),
            vmem((4,) + unit, bf16),
            vmem((6,) + unit, bf16),
            vmem((6,) + unit, bf16),
        ]
        + sets
        + sets
        + [
            vmem((rows, width), f32),
            vmem((rows, width), f32),
            vmem((8, full), f32),
            vmem((16, width), f32),
            vmem((8, width), f32),
            vmem((dp_count, 16, width), f32),
            vmem((row_count, 8, rows), f32),
            dma((15,)),
            pltpu.SemaphoreType.REGULAR,
            dma((4 * total + 1,)),
            dma((12 * total,)),
            dma((12 * total,)),
            dma((12 * total,)),
            dma((12 * total,)),
            dma((53,)),
            dma((53,)),
        ],
        compiler_params=pltpu.CompilerParams(
            collective_id=cid, has_side_effects=True, vmem_limit_bytes=64 * 1024 * 1024 - 65536
        ),
        cost_estimate=pl.CostEstimate(flops=40_000_000_000, bytes_accessed=100_000_000, transcendentals=4_000_000),
    )(hid, cot, slope, n2, upw, std, n1, qkvw, down_nat, resid_own, attended, outw, mixed, std1_own, stats, marks, vec_all, inv1_own, down_bias)


class Moves:
    def __init__(self, source, target, cut, parts, sends, recvs, base):
        row, plane = lax.axis_index("row"), lax.axis_index("dp")
        side, core = row // 2, row % 2
        parity = plane % 2
        other = {"dp": plane + 1 - 2 * parity}
        twin = side * 2 + 1 - core
        far = ((1 - side) * 2 + core, (1 - side) * 2 + 1 - core)
        self.sibling = put(source(twin), target(row), sends, recvs, base, {"row": twin})
        self.sibling_in = put(source(twin), target(twin), sends, recvs, base, {"row": twin})
        self.outs, self.ins, self.passes, self.gets = [], [], [], []
        at = base + 1
        for step in range(parts // 2):
            for k, device in enumerate(far):
                mine, theirs = 2 * step + parity, 2 * step + 1 - parity
                there, here = cut(target(row), mine), cut(target(device), mine)
                self.outs.append(put(cut(source(device), mine), there, sends, recvs, at, {"row": device}))
                self.ins.append(put(cut(source(device), mine), here, sends, recvs, at, {"row": device}))
                self.passes.append(put(here, here, sends, recvs, at + 1, other))
                lands = cut(target(device), theirs)
                self.gets.append(put(lands, lands, sends, recvs, at + 1, other))
                at += 2

    @staticmethod
    def count(parts):
        return 1 + 2 * parts

    def start(self):
        self.sibling.start()
        self.start_far()

    def start_far(self):
        for copy in self.outs:
            copy.start()

    def forward(self, begin=0, end=None):
        for came, passed in list(zip(self.ins, self.passes))[begin:end]:
            came.wait_recv()
            passed.start()

    def finish(self):
        self.sibling_in.wait_recv()
        for copy in self.gets:
            copy.wait_recv()

    def drain(self):
        self.sibling.wait_send()
        for copy in self.outs + self.passes:
            copy.wait_send()


FAR_PARTS = 8


def forward_kernel(
    tokens,
    cot_in,
    ln1_gain,
    ln1_shift,
    out_bias_in,
    ln2_gain,
    ln2_shift,
    qv_bias,
    up_bias_in,
    spans,
    qkv_in,
    out_nat,
    up_nat,
    cot_all,
    n1_out,
    n2_out,
    std_out,
    upw_out,
    qkvw_out,
    outw_out,
    mixed_out,
    attended_out,
    hid_out,
    slope_out,
    stats,
    marks,
    vec_all,
    resid_own,
    std1_own,
    inv1_own,
    tok,
    n1,
    part,
    tot,
    qkvw,
    upw,
    outw,
    mixed,
    attended,
    hid,
    slope,
    own_sum,
    got,
    diag,
    hx,
    hy,
    ts,
    fx,
    qkv_raw,
    qkv_nat,
    mixed_bias,
    local_sem,
    w_send,
    w_recv,
    p_send,
    p_recv,
):
    f32, bf16 = jnp.float32, jnp.bfloat16
    plane, row, col = lax.axis_index("dp"), lax.axis_index("row"), lax.axis_index("col")
    side, core = row // 2, row % 2
    rows, width = tokens.shape
    length, full = tok.shape
    row_count = full // width
    heads_width = attended.shape[1]
    units = hid.shape[1]

    barrier = pltpu.get_barrier_semaphore()
    twins = ({"row": (1 - side) * 2 + 1 - core}, {"dp": plane + 1 - 2 * (plane % 2)})
    for partner in partners() + twins:
        pl.semaphore_signal(barrier, inc=1, device_id=partner, device_id_type=MESH)
    pl.semaphore_wait(barrier, 5)

    def cut_rows(ref, part):
        count = ref.shape[0] // FAR_PARTS
        return ref.at[strip(part * count, count)]

    per = qkvw.shape[1]
    count = Moves.count(FAR_PARTS)
    qkv_moves = Moves(
        lambda r: qkv_nat.at[:, strip(r * per, per)],
        lambda r: qkvw.at[strip(r * width, width), :],
        cut_rows,
        FAR_PARTS,
        w_send,
        w_recv,
        0,
    )
    out_moves = Moves(
        lambda r: out_nat.at[strip(r * heads_width, heads_width), :],
        lambda r: outw.at[:, strip(r * width, width)],
        cut_rows,
        FAR_PARTS,
        w_send,
        w_recv,
        count,
    )
    up_moves = Moves(
        lambda r: up_nat.at[:, strip(r * units, units)],
        lambda r: upw.at[strip(r * width, width), :],
        cut_rows,
        FAR_PARTS,
        w_send,
        w_recv,
        2 * count,
    )
    locals_ = [
        (qkv_nat.at[:, strip(row * per, per)], qkvw.at[strip(row * width, width), :]),
        (out_nat.at[strip(row * heads_width, heads_width), :], outw.at[:, strip(row * width, width)]),
        (up_nat.at[:, strip(row * units, units)], upw.at[strip(row * width, width), :]),
        (cot_in, block(cot_all, col, side, core, rows, width)),
        (n1, n1_out),
        (part, n2_out),
        (n1, std_out),
        (upw, upw_out),
        (qkvw, qkvw_out),
        (outw, outw_out),
        (mixed, mixed_out),
        (attended, attended_out),
        (hid, hid_out),
        (slope, slope_out),
        (qkv_in, qkv_raw),
    ]
    local = [pltpu.make_async_copy(a, b, local_sem.at[k]) for k, (a, b) in enumerate(locals_)]
    local[14].start()
    for k in range(1, 4):
        local[k].start()

    block(tok, col, side, core, rows, width)[...] = tokens[...]
    gather = spread_steps(tok, rows, width, p_send, p_recv, 0, mostly_x=True)
    next(gather)
    here = strip(row * width, width)
    vec_all[:, here] = jnp.zeros((vec_all.shape[0], width), f32)
    for k, vector in enumerate((ln1_gain, ln1_shift, out_bias_in, ln2_gain, ln2_shift)):
        vec_all[k : k + 1, here] = vector[...]
    vec_sends, vec_recvs = [], []
    for step in range(1, row_count):
        target, source = (row + step) % row_count, (row + row_count - step) % row_count
        here, there = vec_all.at[:, strip(row * width, width)], vec_all.at[:, strip(source * width, width)]
        vec_sends.append(put(here, here, p_send, p_recv, 10 + step - 1, {"row": target}))
        vec_recvs.append(put(there, there, p_send, p_recv, 10 + step - 1, {"row": source}))
        vec_sends[-1].start()
    out_moves.sibling.start()
    up_moves.sibling.start()
    local[14].wait()
    for kind in range(3):
        flat = qkv_raw[:, kind].reshape(width, qkv_raw.shape[2] * HEAD)
        for head in range(qkv_raw.shape[2]):
            qkv_nat[:, pl.ds((head * 3 + kind) * HEAD, HEAD)] = flat[:, head * HEAD : (head + 1) * HEAD]
    local[0].start()
    qkv_moves.sibling.start()
    qkv_moves.start_far()
    next(gather)
    next(gather)
    next(gather, None)
    for copy in vec_recvs:
        copy.wait_recv()
    lines = lax.broadcasted_iota(jnp.int32, marks.shape, 0) * SPAN
    found = jnp.zeros(marks.shape, f32)
    for k in range(spans.shape[1]):
        found = jnp.where(lines == spans[0:1, k : k + 1] // SPAN * SPAN, 1.0, found)
    marks[...] = found

    tile = 64
    gain1, shift1 = vec_all[0:1, :], vec_all[1:2, :]

    def norm1_step(k, none):
        at = strip(k * tile, tile)
        values = tok[at, :].astype(f32)
        center = jnp.sum(values, axis=1, keepdims=True) / full
        inverse = lax.rsqrt(jnp.sum(values * values, axis=1, keepdims=True) / full - center * center + epsilon)
        n1[at, :] = ((values - center) * inverse * gain1 + shift1).astype(bf16)

        @pl.when(k // (rows // tile) == col)
        def _():
            here = strip(k % (rows // tile) * tile, tile)
            std1_own[here, :] = ((tok[at, strip(row * width, width)].astype(f32) - center) * inverse).astype(bf16)
            inv1_own[here, :] = inverse

        return none

    half_steps = length // tile // 2
    quarter = half_steps // 2
    for k in range(4):
        qkv_moves.forward(2 * k, 2 * k + 1)
        lax.fori_loop(k * quarter, (k + 1) * quarter, norm1_step, 0)
        qkv_moves.forward(2 * k + 1, 2 * k + 2)
    local[4].start()
    out_moves.start_far()
    up_moves.start_far()
    qkv_moves.finish()
    local[0].wait()

    mixed_bias[...] = jnp.zeros_like(mixed_bias)
    for head in range(heads_width // HEAD):
        for k in range(2):
            lanes = pl.ds((head * 3 + 2 * k) * HEAD, HEAD)
            mixed_bias[:, lanes] = qv_bias[row * (heads_width // HEAD) + head, k : k + 1, :]
    up_bias = up_bias_in.at[:, strip(row * units, units)]

    def mixed_step(k, none):
        down, across = k // (per // CHUNK), k % (per // CHUNK)
        at, lanes = strip(down * rows, rows), strip(across * CHUNK, CHUNK)
        value = jnp.dot(n1[at, :], qkvw[:, lanes], preferred_element_type=f32)
        mixed[at, lanes] = (value + mixed_bias[:, lanes]).astype(bf16)
        return none

    lax.fori_loop(0, (length // rows) * (per // CHUNK), mixed_step, 0)
    local[8].start()
    local[10].start()
    local[4].wait()

    heads = heads_width // HEAD
    factor = 1.0 / math.sqrt(HEAD)
    blocks = length // SPAN
    spots = (SPAN, SPAN)
    earlier = lax.broadcasted_iota(jnp.int32, spots, 1) <= lax.broadcasted_iota(jnp.int32, spots, 0)

    def head_step(head, none):
        base = head * 3 * HEAD
        at_q, at_k, at_v = strip(base, HEAD), strip(base + HEAD, HEAD), strip(base + 2 * HEAD, HEAD)
        for k in range(blocks):
            here = pl.ds(k * SPAN, SPAN)
            seen = (k + 1) * SPAN
            scores = dot_nt(mixed[here, at_q], mixed[:seen, at_k]) * factor
            last = jnp.where(earlier | (marks[k : k + 1, :1] > 0), scores[:, seen - SPAN :], masked_score)
            scores = last if k == 0 else jnp.concatenate([scores[:, : seen - SPAN], last], axis=1)
            highest = jnp.max(scores, axis=1, keepdims=True)
            weights = jnp.exp(scores - highest)
            weight_sum = jnp.sum(weights, axis=1, keepdims=True)
            stats[here, 1 + head : 2 + head] = highest + jnp.log(weight_sum)
            value = jnp.dot((weights / weight_sum).astype(bf16), mixed[:seen, at_v], preferred_element_type=f32)
            attended[here, strip(head * HEAD, HEAD)] = value.astype(bf16)
        return none

    for head in range(heads):
        head_step(head, 0)
        if head == 0:
            out_moves.forward()
    local[11].start()
    up_moves.forward(0, 4)
    out_moves.finish()
    local[1].wait()
    tiled_nn(attended, outw, part, rows, 512)
    local[9].start()
    add_up = reduce_steps(part, own_sum, got, diag, hx, hy, ts, fx, p_send, p_recv, 13)
    next(add_up)
    next(add_up)
    next(add_up)
    up_moves.forward(4, 8)
    next(add_up, None)
    block(tot, col, side, core, rows, width)[...] = own_sum[...].astype(bf16)
    again = spread_steps(tot, rows, width, p_send, p_recv, 23)
    next(again)
    next(again)
    local[3].wait()
    cot_gather = spread_steps(cot_all, rows, width, p_send, p_recv, 33)
    next(cot_gather)
    next(again)
    next(again, None)

    gain2, shift2, out_bias = vec_all[3:4, :], vec_all[4:5, :], vec_all[2:3, :]

    def norm2_step(k, none):
        at = strip(k * tile, tile)
        values = tok[at, :].astype(f32) + (tot[at, :].astype(f32) + out_bias)
        center = jnp.sum(values, axis=1, keepdims=True) / full
        inverse = lax.rsqrt(jnp.sum(values * values, axis=1, keepdims=True) / full - center * center + epsilon)
        standard = (values - center) * inverse
        stats[at, 0:1] = inverse
        n1[at, :] = standard.astype(bf16)
        part[at, :] = (standard * gain2 + shift2).astype(bf16)

        @pl.when(k // (rows // tile) == col)
        def _():
            own = strip(row * width, width)
            here = strip(k % (rows // tile) * tile, tile)
            resid_own[here, :] = tok[at, own].astype(f32) + (tot[at, own].astype(f32) + vec_all[2:3, own])

        return none

    lax.fori_loop(0, 2 * half_steps, norm2_step, 0)
    local[5].start()
    local[6].start()
    next(cot_gather)
    up_moves.finish()
    local[2].wait()
    local[7].start()

    def up_step(k, none):
        down, across = k // (units // CHUNK), k % (units // CHUNK)
        at, lanes = strip(down * rows, rows), strip(across * CHUNK, CHUNK)
        u = jnp.dot(part[at, :], upw[:, lanes], preferred_element_type=f32) + up_bias[:, lanes]
        bent = jnp.tanh(0.7978845608028654 * (u + 0.044715 * u * u * u))
        hid[at, lanes] = (0.5 * u * (1.0 + bent)).astype(bf16)
        inside = 0.7978845608028654 * (1.0 + 3 * 0.044715 * u * u)
        slope[at, lanes] = (0.5 * (1.0 + bent) + 0.5 * u * (1.0 - bent * bent) * inside).astype(bf16)
        return none

    lax.fori_loop(0, (length // rows) * (units // CHUNK), up_step, 0)
    local[12].start()
    local[13].start()
    next(cot_gather)
    next(cot_gather, None)
    for k in range(5, 14):
        local[k].wait()
    for moves in (qkv_moves, out_moves, up_moves):
        moves.drain()
    for copy in vec_sends:
        copy.wait_send()


def forward_plane(cid, tokens, cot, vectors, qv_bias, up_bias, spans, qkv_in, out_nat, up_nat):
    f32, bf16 = jnp.float32, jnp.bfloat16
    rows, width = tokens.shape
    row_count = lax.axis_size("row")
    length, full = rows * lax.axis_size("col"), width * row_count
    per, heads_width, units = qkv_in.shape[1] * qkv_in.shape[2] * HEAD // row_count, out_nat.shape[0] // row_count, up_nat.shape[1] // row_count
    shape = jax.ShapeDtypeStruct
    away, near = pl.BlockSpec(memory_space=pl.ANY), pl.BlockSpec(memory_space=pltpu.VMEM)
    vmem, dma = pltpu.VMEM, pltpu.SemaphoreType.DMA
    wide = shape((length, full), bf16)
    moved = 3 * Moves.count(FAR_PARTS)
    return pl.pallas_call(
        forward_kernel,
        out_shape=[
            wide,
            wide,
            wide,
            wide,
            shape((full, units), bf16),
            shape((full, per), bf16),
            shape((heads_width, full), bf16),
            shape((length, per), bf16),
            shape((length, heads_width), bf16),
            shape((length, units), bf16),
            shape((length, units), bf16),
            shape((length, 8), f32),
            shape((8, 128), f32),
            shape((8, full), f32),
            shape((rows, width), f32),
            shape((rows, width), bf16),
            shape((rows, 1), f32),
        ],
        in_specs=[near] * (5 + len(vectors)) + [away] * 3,
        out_specs=[away] * 11 + [near] * 6,
        scratch_shapes=[
            vmem((length, full), bf16),
            vmem((length, full), bf16),
            vmem((length, full), bf16),
            vmem((length, full), bf16),
            vmem((full, per), bf16),
            vmem((full, units), bf16),
            vmem((heads_width, full), bf16),
            vmem((length, per), bf16),
            vmem((length, heads_width), bf16),
            vmem((length, units), bf16),
            vmem((length, units), bf16),
            vmem((rows, width), f32),
            vmem((4, rows, width), bf16),
            vmem((rows, width), bf16),
            vmem((rows // 2, width), bf16),
            vmem((rows // 2, width), bf16),
            vmem((2, rows, width), bf16),
            vmem((2, rows, width), bf16),
            vmem(qkv_in.shape, bf16),
            vmem((width, row_count * per), bf16),
            vmem((1, per), f32),
            dma((15,)),
            dma((moved,)),
            dma((moved,)),
            dma((43,)),
            dma((43,)),
        ],
        compiler_params=pltpu.CompilerParams(
            collective_id=cid, has_side_effects=True, vmem_limit_bytes=60 * 1024 * 1024
        ),
        cost_estimate=pl.CostEstimate(flops=10_000_000_000, bytes_accessed=60_000_000, transcendentals=4_000_000),
    )(tokens, cot, *[vector[None] for vector in vectors], qv_bias, up_bias[None], spans, qkv_in, out_nat, up_nat)


def results_kernel(
    down, up, out, output, tokens, qkv, small, down_result, up_result, out_result, output_result, tokens_result, qkv_result, *vectors
):
    *sums, up_bias, qv_bias = vectors
    f32 = jnp.float32
    down_result[...] = down[...].astype(f32)
    up_result[...] = up[...].astype(f32)
    out_result[...] = out[...].astype(f32)
    output_result[...] = output[...]
    tokens_result[...] = tokens[...]
    for head in range(qkv_result.shape[2]):
        for kind in range(3):
            begin = (head * 3 + kind) * HEAD
            qkv_result[:, kind, head, :] = qkv[:, begin : begin + HEAD].astype(f32)

    @pl.when(pl.program_id(0) == 0)
    def _():
        row = lax.axis_index("row")
        for k, result in enumerate(sums):
            result[...] = small[row, k : k + 1, :]
        count, _, width = small.shape
        lines = up_bias.shape[1] // (count * width)
        heads = qv_bias.shape[0] // count
        for source in range(count):
            for k in range(lines):
                begin = (source * lines + k) * width
                up_bias[:, begin : begin + width] = small[source, 8 + k : 9 + k, :]
            for head in range(heads):
                for k in range(2):
                    begin = (head * 2 + k) * HEAD
                    line = small[source, 8 + lines : 9 + lines, begin : begin + HEAD]
                    qv_bias[source * heads + head, k : k + 1, :] = line


def results(down, up, out, output, tokens, qkv, small):
    f32 = jnp.float32
    shape = jax.ShapeDtypeStruct
    rows, heads = qkv.shape[0], qkv.shape[1] // (3 * HEAD)
    width, units = small.shape[2], up.shape[1]
    steps = 8

    def cut(array):
        return pl.BlockSpec((array.shape[0] // steps, array.shape[1]), lambda k: (k, 0))

    def whole(*dims):
        return pl.BlockSpec(dims, lambda k: (0,) * len(dims))

    line = whole(1, width)
    *made, up_bias, qv_bias = pl.pallas_call(
        results_kernel,
        grid=(steps,),
        out_shape=[shape(a.shape, f32) for a in (down, up, out)]
        + [shape(a.shape, a.dtype) for a in (output, tokens)]
        + [shape((rows, 3, heads, HEAD), f32)]
        + [shape((1, width), f32)] * 6
        + [shape((1, units), f32), shape((heads, 2, HEAD), f32)],
        in_specs=[cut(a) for a in (down, up, out, output, tokens, qkv)] + [whole(*small.shape)],
        out_specs=[cut(a) for a in (down, up, out, output, tokens)]
        + [pl.BlockSpec((rows // steps, 3, heads, HEAD), lambda k: (k, 0, 0, 0))]
        + [line] * 6
        + [whole(1, units), whole(heads, 2, HEAD)],
        compiler_params=pltpu.CompilerParams(vmem_limit_bytes=63 * 1024 * 1024),
    )(down, up, out, output, tokens, qkv, small)
    made[5] = jnp.swapaxes(made[5], 1, 2)
    return made[:6], [sums[0] for sums in made[6:]], up_bias[0], qv_bias


def plane_plan(
    tokens,
    ln1_gain,
    ln1_shift,
    qkv_weight,
    qv_bias,
    out_weight,
    out_bias,
    ln2_gain,
    ln2_shift,
    up_weight,
    up_bias,
    down_weight,
    down_bias,
    span_starts,
    cotangent,
):
    width = tokens.shape[1]
    (
        cot_all, n1, n2, standard2, upw, qkvw, outw, mixed, attended, hidden, slope,
        stats, marks, vec_all, residual_own, standard1_own, inverse1_own,
    ) = forward_plane(
        1,
        tokens,
        cotangent,
        (ln1_gain, ln1_shift, out_bias, ln2_gain, ln2_shift),
        qv_bias,
        up_bias,
        span_starts,
        jnp.swapaxes(qkv_weight, 1, 2),
        out_weight.reshape(-1, width),
        up_weight,
    )
    down_grad, up_grad, out_grad, qkv_grad, _, _, output, tokens_grad, small = backward_plane(
        2, hidden, cot_all, slope, n2, upw, standard2, n1, qkvw, down_weight, residual_own, attended, outw, mixed, standard1_own,
        stats, marks, vec_all, inverse1_own, down_bias[None],
    )
    grads, sums, up_bias_grad, qv_bias_grad = results(
        down_grad.reshape(-1, width), up_grad.reshape(width, -1), out_grad.reshape(-1, width), output, tokens_grad,
        qkv_grad.reshape(width, -1), small
    )
    return (
        grads[3],
        grads[4],
        sums[0],
        sums[1],
        grads[5],
        qv_bias_grad,
        grads[2].reshape(out_weight.shape),
        sums[4],
        sums[2],
        sums[3],
        grads[1],
        up_bias_grad,
        grads[0],
        sums[5],
    )


def solution(mesh):
    sizes = dict(mesh.shape)
    flat = sizes == {"dp": 4, "row": 4, "col": 2}
    per_device = plane_plan if flat else general_plan
    placed = (
        P(("dp", "col"), "row"),
        P("row"),
        P("row"),
        P("row", "col", None, None),
        P("col", None, None),
        P("col", None, "row"),
        P("row"),
        P("row"),
        P("row"),
        P("row", "col"),
        P("col"),
        P("col", "row"),
        P("row"),
        P("dp", None),
        P(("dp", "col"), "row"),
    )
    return jax.shard_map(
        per_device,
        mesh=mesh,
        in_specs=placed,
        out_specs=(
            P(("dp", "col"), "row"),
            P(("dp", "col"), "row"),
            P("row"),
            P("row"),
            P("row", "col", None, None),
            P("col", None, None),
            P("col", None, "row"),
            P("row"),
            P("row"),
            P("row"),
            P("row", "col"),
            P("col"),
            P("col", "row"),
            P("row"),
        ),
        check_vma=False,
    )
```

```python
import functools
import math

import jax
import jax.numpy as jnp
from jax import lax
from jax.experimental import pallas as pl
from jax.experimental.pallas import tpu as pltpu
from jax.sharding import PartitionSpec as P

MESH = pl.DeviceIdType.MESH

D = 2048
HEAD = 128
SEQS = 1
SPAN = 256
BLOCK = 512


epsilon = 1e-05
masked_score = -1e30


def gelu_tanh(values):
    return (
        0.5
        * values
        * (1.0 + jnp.tanh(0.7978845608028654 * (values + 0.044715 * values * values * values)))
    )


def gather_columns(block_data):
    return lax.all_gather(block_data, "col", axis=0, tiled=True)


def gather_rows(block_data):
    return lax.all_gather(block_data, "row", axis=0, tiled=True)


def product(left_side, right_side, flipped):
    if flipped:
        return lax.dot_general(
            left_side, right_side, (((1,), (1,)), ((), ())), preferred_element_type=jnp.float32
        )
    return jnp.dot(left_side, right_side, preferred_element_type=jnp.float32)


def outer_sum(left_side, right_side):
    return lax.dot_general(
        left_side, right_side, (((0,), (0,)), ((), ())), preferred_element_type=jnp.float32
    )


def sum_rows(left_side, right_side, flipped):
    wide_left = lax.all_to_all(left_side, "row", split_axis=0, concat_axis=1, tiled=True)
    if flipped:
        wide_right = lax.all_gather(right_side, "row", axis=1, tiled=True)
    else:
        wide_right = lax.all_gather(right_side, "row", axis=0, tiled=True)
    return product(wide_left, wide_right, flipped)


def sum_columns(left_side, right_side, flipped):
    return lax.psum_scatter(
        product(left_side, right_side, flipped), "col", scatter_dimension=0, tiled=True
    )


def row_totals(first_sum, second_sum):
    return lax.psum((first_sum, second_sum), "row")


def norm_forward(values, gain_row, bias_row):
    totals, squares = row_totals(jnp.sum(values, axis=1), jnp.sum(values * values, axis=1))
    center = totals / D
    spread = squares / D - center * center
    inverse = lax.rsqrt(spread + epsilon)
    standard = (values - center[:, None]) * inverse[:, None]
    return (standard, inverse, (standard * gain_row + bias_row).astype(jnp.bfloat16))


def norm_backward(upstream, standard, inverse, gain_row):
    scaled = upstream * gain_row
    first_sum, second_sum = row_totals(jnp.sum(scaled, axis=1), jnp.sum(scaled * standard, axis=1))
    gradient = inverse[:, None] * (
        scaled - first_sum[:, None] / D - standard * (second_sum[:, None] / D)
    )
    return (gradient, jnp.sum(upstream * standard, axis=0), jnp.sum(upstream, axis=0))


def visible(query_pos, query_image, key_pos):
    earlier = key_pos[None, :] <= query_pos[:, None]
    same_span = (key_pos[None, :] // SPAN == query_pos[:, None] // SPAN) & (
        query_image[:, None] > 0
    )
    return earlier | same_span


def attention_forward(queries, key_value, token_image, row_offset, seq_length, block_rows):
    own_rows, head_count, width = queries.shape
    factor = 1.0 / math.sqrt(width)

    def block_forward(block_index):
        local = block_index * block_rows
        start_pos = row_offset + local
        query_block = lax.dynamic_slice_in_dim(queries, local, block_rows, 0)
        query_pos = start_pos + jnp.arange(block_rows, dtype=jnp.int32)
        query_image = lax.dynamic_slice_in_dim(token_image, start_pos, block_rows, 0)
        begin = start_pos // seq_length * seq_length // block_rows
        finish = start_pos // block_rows + 1

        def key_step(key_index, state_in):
            running, weight_sum, gathered = state_in
            key_begin = key_index * block_rows
            key_block = lax.dynamic_slice_in_dim(key_value, key_begin, block_rows, 0)
            key_pos = key_begin + jnp.arange(block_rows, dtype=jnp.int32)
            allowed = visible(query_pos, query_image, key_pos)
            scores = (
                jnp.einsum(
                    "qhd,khd->hqk",
                    query_block,
                    key_block[:, :, 0],
                    preferred_element_type=jnp.float32,
                )
                * factor
            )
            scores = jnp.where(allowed[None], scores, masked_score)
            highest = jnp.maximum(running, jnp.max(scores, axis=2))
            weights = jnp.exp(scores - highest[:, :, None])
            shrink = jnp.exp(running - highest)
            weight_sum = weight_sum * shrink + jnp.sum(weights, axis=2)
            gathered = gathered * shrink.T[:, :, None] + jnp.einsum(
                "hqk,khd->qhd",
                weights.astype(jnp.bfloat16),
                key_block[:, :, 1],
                preferred_element_type=jnp.float32,
            )
            return (highest, weight_sum, gathered)

        initial = (
            jnp.full((head_count, block_rows), masked_score, jnp.float32),
            jnp.zeros((head_count, block_rows), jnp.float32),
            jnp.zeros((block_rows, head_count, width), jnp.float32),
        )
        running, weight_sum, gathered = lax.fori_loop(begin, finish, key_step, initial)
        return (gathered / weight_sum.T[:, :, None], running + jnp.log(weight_sum))

    result, logsum = lax.map(block_forward, jnp.arange(own_rows // block_rows, dtype=jnp.int32))
    return (result.reshape(own_rows, head_count, width), logsum)


def attention_backward(
    queries,
    key_value,
    attended_full,
    logsum,
    d_attended,
    token_image,
    row_offset,
    seq_length,
    block_rows,
):
    own_rows, head_count, width = queries.shape
    factor = 1.0 / math.sqrt(width)
    row_dots = jnp.sum(d_attended.astype(jnp.float32) * attended_full, axis=2)

    def block_backward(block_index, state_out):
        d_queries, d_pairs = state_out
        local = block_index * block_rows
        start_pos = row_offset + local
        query_block = lax.dynamic_slice_in_dim(queries, local, block_rows, 0)
        dout_block = lax.dynamic_slice_in_dim(d_attended, local, block_rows, 0)
        dots_block = lax.dynamic_slice_in_dim(row_dots, local, block_rows, 0).T
        logsum_block = logsum[block_index]
        query_pos = start_pos + jnp.arange(block_rows, dtype=jnp.int32)
        query_image = lax.dynamic_slice_in_dim(token_image, start_pos, block_rows, 0)
        begin = start_pos // seq_length * seq_length // block_rows
        finish = start_pos // block_rows + 1

        def key_step(key_index, state_in):
            d_query, d_keys = state_in
            key_begin = key_index * block_rows
            key_block = lax.dynamic_slice_in_dim(key_value, key_begin, block_rows, 0)
            key_pos = key_begin + jnp.arange(block_rows, dtype=jnp.int32)
            allowed = visible(query_pos, query_image, key_pos)
            scores = (
                jnp.einsum(
                    "qhd,khd->hqk",
                    query_block,
                    key_block[:, :, 0],
                    preferred_element_type=jnp.float32,
                )
                * factor
            )
            scores = jnp.where(allowed[None], scores, masked_score)
            probabilities = jnp.exp(scores - logsum_block[:, :, None])
            d_probs = jnp.einsum(
                "qhd,khd->hqk", dout_block, key_block[:, :, 1], preferred_element_type=jnp.float32
            )
            d_scores = (probabilities * (d_probs - dots_block[:, :, None])).astype(jnp.bfloat16)
            d_query = d_query + jnp.einsum(
                "hqk,khd->qhd", d_scores, key_block[:, :, 0], preferred_element_type=jnp.float32
            )
            d_key = (
                jnp.einsum(
                    "hqk,qhd->khd", d_scores, query_block, preferred_element_type=jnp.float32
                )
                * factor
            )
            d_value = jnp.einsum(
                "hqk,qhd->khd",
                probabilities.astype(jnp.bfloat16),
                dout_block,
                preferred_element_type=jnp.float32,
            )
            previous = lax.dynamic_slice_in_dim(d_keys, key_begin, block_rows, 0)
            d_keys = lax.dynamic_update_slice_in_dim(
                d_keys, previous + jnp.stack([d_key, d_value], axis=2), key_begin, 0
            )
            return (d_query, d_keys)

        d_query, d_pairs = lax.fori_loop(
            begin,
            finish,
            key_step,
            (jnp.zeros((block_rows, head_count, width), jnp.float32), d_pairs),
        )
        d_queries = lax.dynamic_update_slice_in_dim(d_queries, d_query * factor, local, 0)
        return (d_queries, d_pairs)

    initial = (
        jnp.zeros((own_rows, head_count, width), jnp.float32),
        jnp.zeros((key_value.shape[0], head_count, 2, width), jnp.float32),
    )
    return lax.fori_loop(0, own_rows // block_rows, block_backward, initial)


def general_plan(
    tokens,
    ln1_gain,
    ln1_shift,
    qkv_weight,
    qv_bias,
    out_weight,
    out_bias,
    ln2_gain,
    ln2_shift,
    up_weight,
    up_bias,
    down_weight,
    down_bias,
    span_starts,
    cotangent,
):
    col_rows, row_width = tokens.shape
    group_rows = col_rows * lax.axis_size("col")
    own_rows = group_rows // lax.axis_size("row")
    head_count = qkv_weight.shape[1]
    seq_length = group_rows // SEQS
    block_rows = BLOCK - own_rows % BLOCK
    row_offset = lax.axis_index("row") * own_rows
    slot_count = seq_length // SPAN
    image_marks = jnp.sum(
        (
            span_starts[:, :, None] // SPAN
            == jnp.arange(slot_count, dtype=jnp.int32)[None, None, :]
        ).astype(jnp.int32),
        axis=1,
    )
    token_image = jnp.broadcast_to(
        image_marks.reshape(-1)[:, None], (group_rows // SPAN, SPAN)
    ).reshape(group_rows)
    qkv_flat = qkv_weight.reshape(row_width, head_count * 3 * HEAD)
    out_flat = out_weight.reshape(head_count * HEAD, row_width)
    inputs = tokens.astype(jnp.float32)
    standard1, inverse1, normed1 = norm_forward(inputs, ln1_gain, ln1_shift)
    normed1_all = gather_columns(normed1)
    mixed_sums = sum_rows(normed1_all, qkv_flat, False).reshape(own_rows, head_count, 3, HEAD)
    queries = (mixed_sums[:, :, 0] + qv_bias[:, 0]).astype(jnp.bfloat16)
    key_value_own = jnp.stack(
        [mixed_sums[:, :, 1], mixed_sums[:, :, 2] + qv_bias[:, 1]], axis=2
    ).astype(jnp.bfloat16)
    key_value = gather_rows(key_value_own)
    attended_full, logsum = attention_forward(
        queries, key_value, token_image, row_offset, seq_length, block_rows
    )
    attended = attended_full.astype(jnp.bfloat16).reshape(own_rows, head_count * HEAD)
    attended_all = gather_rows(attended)
    residual = inputs + (sum_columns(attended_all, out_flat, False) + out_bias)
    standard2, inverse2, normed2 = norm_forward(residual, ln2_gain, ln2_shift)
    normed2_all = gather_columns(normed2)
    up_sums = sum_rows(normed2_all, up_weight, False) + up_bias
    hidden = gelu_tanh(up_sums).astype(jnp.bfloat16)
    hidden_all = gather_rows(hidden)
    output = (residual + (sum_columns(hidden_all, down_weight, False) + down_bias)).astype(
        jnp.bfloat16
    )
    d_output = cotangent.astype(jnp.float32)
    d_output_all = gather_columns(cotangent)
    down_grad = outer_sum(hidden_all, d_output_all)
    down_bias_grad = jnp.sum(d_output_all, axis=0, dtype=jnp.float32)
    d_hidden = sum_rows(d_output_all, down_weight, True)
    d_upper = jax.vjp(gelu_tanh, up_sums)[1](d_hidden)[0].astype(jnp.bfloat16)
    d_upper_all = gather_rows(d_upper)
    normed2_use = gather_columns(normed2)
    up_grad = outer_sum(normed2_use, d_upper_all)
    up_bias_grad = jnp.sum(d_upper_all, axis=0, dtype=jnp.float32)
    d_normed2 = sum_columns(d_upper_all, up_weight, True)
    d_norm2, gain2_grad, shift2_grad = norm_backward(d_normed2, standard2, inverse2, ln2_gain)
    d_residual = d_output + d_norm2
    d_branch = d_residual.astype(jnp.bfloat16)
    d_branch_all = gather_columns(d_branch)
    out_grad = outer_sum(attended_all, d_branch_all)
    out_bias_grad = jnp.sum(d_branch_all, axis=0, dtype=jnp.float32)
    d_attended = (
        sum_rows(d_branch_all, out_flat, True)
        .astype(jnp.bfloat16)
        .reshape(own_rows, head_count, HEAD)
    )
    d_queries, d_pairs = attention_backward(
        queries,
        key_value,
        attended_full,
        logsum,
        d_attended,
        token_image,
        row_offset,
        seq_length,
        block_rows,
    )
    d_pairs_own = lax.psum_scatter(d_pairs, "row", scatter_dimension=0, tiled=True)
    d_mixed = jnp.concatenate([d_queries[:, :, None], d_pairs_own], axis=2).astype(jnp.bfloat16)
    d_mixed_all = gather_rows(d_mixed)
    normed1_use = gather_columns(normed1)
    d_mixed_flat = d_mixed_all.reshape(group_rows, head_count * 3 * HEAD)
    qkv_grad = outer_sum(normed1_use, d_mixed_flat)
    mixed_totals = jnp.sum(d_mixed_all, axis=0, dtype=jnp.float32)
    qv_bias_grad = jnp.stack([mixed_totals[:, 0], mixed_totals[:, 2]], axis=1)
    d_normed1 = sum_columns(d_mixed_flat, qkv_flat, True)
    d_norm1, gain1_grad, shift1_grad = norm_backward(d_normed1, standard1, inverse1, ln1_gain)
    tokens_grad = (d_residual + d_norm1).astype(jnp.bfloat16)
    norm_sums = lax.psum((gain1_grad, shift1_grad, gain2_grad, shift2_grad), ("dp", "col"))
    weight_sums = lax.psum(
        (
            qkv_grad,
            qv_bias_grad,
            out_grad,
            out_bias_grad,
            up_grad,
            up_bias_grad,
            down_grad,
            down_bias_grad,
        ),
        "dp",
    )
    return (
        output,
        tokens_grad,
        norm_sums[0],
        norm_sums[1],
        weight_sums[0].reshape(row_width, head_count, 3, HEAD),
        weight_sums[1],
        weight_sums[2].reshape(head_count, HEAD, row_width),
        weight_sums[3],
        norm_sums[2],
        norm_sums[3],
        weight_sums[4],
        weight_sums[5],
        weight_sums[6],
        weight_sums[7],
    )


def places():
    row, col = lax.axis_index("row"), lax.axis_index("col")
    return col, row // 2, row % 2


def partners():
    col, side, core = places()
    return ({"col": 1 - col}, {"row": (1 - side) * 2 + core}, {"row": side * 2 + 1 - core})


def block(ref, col, side, core, rows, width, part=None):
    begin, count = col * rows, rows
    if part is not None:
        begin, count = begin + part * (rows // 2), rows // 2
    return ref.at[strip(begin, count), strip((side * 2 + core) * width, width)]


def put(ref_from, ref_to, sends, recvs, at, partner):
    return pltpu.make_async_remote_copy(
        src_ref=ref_from,
        dst_ref=ref_to,
        send_sem=sends.at[at],
        recv_sem=recvs.at[at],
        device_id=partner,
        device_id_type=MESH,
    )


def strip(begin, count):
    return pl.ds(pl.multiple_of(begin, count), count)


def dot_nt(left, right):
    return lax.dot_general(left, right, (((1,), (1,)), ((), ())), preferred_element_type=jnp.float32)


def dot_tn(left, right):
    return lax.dot_general(left, right, (((0,), (0,)), ((), ())), preferred_element_type=jnp.float32)


def tiled_nt(left, right, target, inner, tile_rows, tile_cols, span=(0, 1, 1)):
    rows, cols = target.shape
    across = cols // tile_cols

    def step(at, none):
        down, side = at // across, at % across
        value = dot_nt(left[strip(down * tile_rows, tile_rows), :inner], right[strip(side * tile_cols, tile_cols), :inner])
        target[strip(down * tile_rows, tile_rows), strip(side * tile_cols, tile_cols)] = value.astype(target.dtype)
        return none

    count = (rows // tile_rows) * across
    lax.fori_loop(span[0] * count // span[2], span[1] * count // span[2], step, 0)


def tiled_nn(left, right, target, tile_rows, tile_cols, span=(0, 1, 1)):
    rows, cols = target.shape
    across = cols // tile_cols

    def step(at, none):
        down, side = at // across, at % across
        value = jnp.dot(
            left[strip(down * tile_rows, tile_rows), :],
            right[:, strip(side * tile_cols, tile_cols)],
            preferred_element_type=jnp.float32,
        )
        target[strip(down * tile_rows, tile_rows), strip(side * tile_cols, tile_cols)] = value.astype(target.dtype)
        return none

    count = (rows // tile_rows) * across
    lax.fori_loop(span[0] * count // span[2], span[1] * count // span[2], step, 0)


def reduce_steps(part, result, got, diag, half_x, half_y, to_send, from_xy, sends, recvs, base, mostly_x=False):
    f32 = jnp.float32
    rows, width = result.shape
    half = rows // 2
    low, high = pl.ds(0, half), pl.ds(half, half)
    col, side, core = places()
    to_x, to_y, to_core = partners()
    spots = ((1 - col, 1 - side), (col, 1 - side), (1 - col, side), (col, side))
    copies = [
        put(block(part, a, b, 1 - core, rows, width), got.at[k], sends, recvs, base + k, to_core)
        for k, (a, b) in enumerate(spots)
    ]
    for copy in copies:
        copy.start()
    mine = [block(part, a, b, core, rows, width) for a, b in spots]
    dx = put(diag.at[low], half_x, sends, recvs, base + 4, to_x)
    dy = put(diag.at[high], half_y, sends, recvs, base + 5, to_x if mostly_x else to_y)

    def onward(k, span, at, partner):
        return put(to_send.at[k, span], from_xy.at[k, span], sends, recvs, base + at, partner)

    y_high, x_low = onward(0, high, 6, to_y), onward(1, low, 7, to_x)
    y_low, x_high = onward(0, low, 8, to_y), onward(1, high, 9, to_x)

    def pair(k, span):
        return mine[k][span].astype(f32) + got[k, span].astype(f32)

    yield
    copies[0].wait_recv()
    diag[...] = (mine[0][...].astype(f32) + got[0].astype(f32)).astype(diag.dtype)
    dx.start()
    dy.start()
    copies[1].wait_recv()
    if not mostly_x:
        to_send[0, high] = pair(1, high).astype(diag.dtype)
        y_high.start()
    copies[2].wait_recv()
    to_send[1, low] = pair(2, low).astype(diag.dtype)
    x_low.start()
    if mostly_x:
        to_send[1, high] = pair(2, high).astype(diag.dtype)
        x_high.start()
    copies[3].wait_recv()
    yield
    dx.wait_recv()
    to_send[0, low] = (pair(1, low) + half_x[...].astype(f32)).astype(diag.dtype)
    y_low.start()
    dy.wait_recv()
    if mostly_x:
        to_send[0, high] = (pair(1, high) + half_y[...].astype(f32)).astype(diag.dtype)
        y_high.start()
    else:
        to_send[1, high] = (pair(2, high) + half_y[...].astype(f32)).astype(diag.dtype)
        x_high.start()
    yield
    for copy in (y_high, x_low, y_low, x_high):
        copy.wait_recv()
    near = mine[3][...].astype(f32) + got[3].astype(f32)
    result[...] = near + from_xy[0].astype(f32) + from_xy[1].astype(f32)
    for copy in copies + [dx, dy, y_high, x_low, y_low, x_high]:
        copy.wait_send()


def spread_steps(out, rows, width, sends, recvs, base, mostly_x=False):
    col, side, core = places()
    to_x, to_y, to_core = partners()

    def copy_of(at, which, partner, part=None):
        ref = block(out, *which, rows, width, part)
        return put(ref, ref, sends, recvs, base + at, partner)

    own, ox, oy, od = (col, side, core), (1 - col, side, core), (col, 1 - side, core), (1 - col, 1 - side, core)
    plan = [
        copy_of(0, own, to_x, 0),
        copy_of(1, own, to_y, 1),
        copy_of(2, own, to_x, 1),
        copy_of(3, own, to_y, 0),
        copy_of(4, own, to_core),
        copy_of(5, oy, to_x, 0) if mostly_x else copy_of(5, ox, to_y, 0),
        copy_of(6, oy, to_x, 1),
        copy_of(7, ox, to_core),
        copy_of(8, oy, to_core),
        copy_of(9, od, to_core),
    ]
    for at in range(5):
        plan[at].start()
    yield
    plan[0].wait_recv()
    if not mostly_x:
        plan[5].start()
    plan[1].wait_recv()
    plan[6].start()
    plan[2].wait_recv()
    plan[7].start()
    plan[3].wait_recv()
    plan[8].start()
    if mostly_x:
        plan[5].start()
    yield
    plan[5].wait_recv()
    plan[6].wait_recv()
    plan[9].start()
    yield
    for at in (4, 7, 8, 9):
        plan[at].wait_recv()
    for copy in plan:
        copy.wait_send()


CHUNK = 256
LINES = CHUNK // 2


def backward_kernel(
    counts,
    hid_h,
    cot_h,
    slope_h,
    n2_h,
    upw_h,
    std_h,
    n1_h,
    qkvw_h,
    down_nat,
    resid_h,
    attended_h,
    outw_h,
    mixed_h,
    std1_h,
    stats,
    marks,
    vec_all,
    inv1_own,
    down_bias,
    down_out,
    up_out,
    out_out,
    qkv_out,
    b_land,
    downw_land,
    out_block,
    tokens_block,
    small_out,
    cot,
    n2,
    std,
    part,
    tot,
    upw,
    hid,
    dup,
    attended,
    outw,
    mixed,
    std1_own,
    d_att,
    d_mix,
    dk_acc,
    dv_acc,
    g,
    s,
    t,
    r_land,
    m_land,
    got_a,
    diag_a,
    hx_a,
    hy_a,
    ts_a,
    fx_a,
    got_b,
    diag_b,
    hx_b,
    hy_b,
    ts_b,
    fx_b,
    dres_own,
    own_sum,
    sums,
    small,
    x_land,
    dp_land,
    stat_land,
    load_sem,
    credit,
    own_sem,
    z_send,
    z_recv,
    a_send,
    a_recv,
    p_send,
    p_recv,
):
    f32, bf16 = jnp.float32, jnp.bfloat16
    n_down, n_up, n_out, n_qkv = counts
    total = sum(counts)
    plane, row, col = lax.axis_index("dp"), lax.axis_index("row"), lax.axis_index("col")
    length, full = cot.shape
    rows, width = dres_own.shape
    row_count = full // width
    inner = (plane == 1) | (plane == 2)
    outer = jnp.logical_not(inner)
    to_inner = {"dp": plane // 3 + 1}
    to_middle = {"dp": 3 - plane}
    to_outer = {"dp": (plane - 1) * 3}
    side, core = row // 2, row % 2

    loads = [
        (hid_h, hid),
        (cot_h, cot),
        (slope_h, dup),
        (upw_h, upw),
        (n2_h, n2),
        (std_h, std),
        (qkvw_h, upw.at[:, : qkvw_h.shape[1]]),
        (n1_h, std),
        (downw_land, n2),
        (downw_land, tot),
        (resid_h, dres_own),
        (attended_h, attended),
        (outw_h, outw),
        (mixed_h, mixed),
        (std1_h, std1_own),
    ]
    loads = [pltpu.make_async_copy(a, b, load_sem.at[k]) for k, (a, b) in enumerate(loads)]
    for k in (0, 1, 2, 3, 4, 5, 11, 12, 13, 14):
        loads[k].start()

    dp_count = dp_land.shape[0]
    barrier = pltpu.get_barrier_semaphore()
    others = [{"row": (1 - side) * 2 + 1 - core}] + [{"dp": (plane + k) % dp_count} for k in range(1, dp_count)]
    for partner in partners() + tuple(others):
        pl.semaphore_signal(barrier, inc=1, device_id=partner, device_id_type=MESH)
    pl.semaphore_wait(barrier, 3 + len(others))

    units = hid.shape[1]
    down_sends, down_recvs = [], []
    for step in range(1, row_count):
        target, source = (row + step) % row_count, (row + row_count - step) % row_count
        here, there = downw_land.at[:, strip(row * width, width)], downw_land.at[:, strip(source * width, width)]
        piece = down_nat.at[strip(target * units, units), :]
        down_sends.append(put(piece, here, p_send, p_recv, 40 + step - 1, {"row": target}))
        down_recvs.append(put(piece, there, p_send, p_recv, 40 + step - 1, {"row": source}))
        down_sends[-1].start()
    down_own = pltpu.make_async_copy(
        down_nat.at[strip(row * units, units), :], downw_land.at[:, strip(row * width, width)], own_sem.at[4 * total]
    )
    down_own.start()

    def place(u, source):
        i, half, quarter = u // 4, u // 2 % 2, pl.ds(u % 2 * LINES, LINES)
        if i < n_down:
            return down_out.at[source * n_down + i // 2 * 2 + half, quarter, pl.ds(i % 2 * CHUNK, CHUNK)]
        i -= n_down
        if i < n_up:
            return up_out.at[half, quarter, strip(source * n_up * CHUNK + i * CHUNK, CHUNK)]
        i -= n_up
        if i < n_out:
            return out_out.at[source * n_out + i, quarter, pl.ds(half * CHUNK, CHUNK)]
        i -= n_out
        return qkv_out.at[half, quarter, strip(source * n_qkv * CHUNK + i * CHUNK, CHUNK)]

    g_slots, s_slots, t_slots, r_slots, m_slots = g.shape[0], s.shape[0], t.shape[0], r_land.shape[0], m_land.shape[0]
    pieces = 4 * total

    def made(u):
        return g.at[u // 4 % g_slots, :, u // 2 % 2, pl.ds(u % 2 * LINES, LINES)]

    def inward(u):
        return put(made(u), r_land.at[u % r_slots], z_send, z_recv, u, to_inner)

    def across(u):
        return put(s.at[u % s_slots], m_land.at[u % m_slots], z_send, z_recv, pieces + u, to_middle)

    def outward(u):
        return put(t.at[u % t_slots], b_land.at[u], z_send, z_recv, 2 * pieces + u, to_outer)

    def home(u, step, source):
        target = (row + step) % row_count
        return put(source.at[target], place(u, row), a_send, a_recv, 3 * u + step - 1, {"row": target})

    def home_own(u, source):
        return pltpu.make_async_copy(source.at[row], place(u, row), own_sem.at[u])

    def send_home(u, source):
        for step in range(1, row_count):
            home(u, step, source).start()
        home_own(u, source).start()

    def sent_home(u, source):
        for step in range(1, row_count):
            home(u, step, source).wait_send()
        home_own(u, source).wait()

    def produce(i):
        if i >= g_slots:

            @pl.when(outer)
            def _():
                for k in range(4):
                    inward(4 * (i - g_slots) + k).wait_send()

        slot = g.at[i % g_slots]
        if i < n_down:
            begin, lane = i // 2 * 2 * CHUNK, i % 2 * CHUNK

            def step(k, none):
                value = dot_tn(hid[:, begin : begin + 2 * CHUNK], cot[:, strip(k * width + lane, CHUNK)]).astype(bf16)
                slot[k, 0] = value[:CHUNK]
                slot[k, 1] = value[CHUNK:]
                return none
        elif n_down + n_up <= i < n_down + n_up + n_out:
            left, begin, right = attended, (i - n_down - n_up) * CHUNK, part

            def step(k, none):
                value = dot_tn(left[:, begin : begin + CHUNK], right[:, strip(k * width, width)]).astype(bf16)
                slot[k, 0] = value[:, :CHUNK]
                slot[k, 1] = value[:, CHUNK:]
                return none
        else:
            if i < n_down + n_up:
                left, right, begin = n2, dup, (i - n_down) * CHUNK
            else:
                left, right, begin = std, d_mix, (i - n_down - n_up - n_out) * CHUNK

            def step(k, none):
                value = dot_tn(left[:, strip(k * width, width)], right[:, begin : begin + CHUNK]).astype(bf16)
                slot[k, 0] = value[:CHUNK]
                slot[k, 1] = value[CHUNK:]
                return none

        lax.fori_loop(0, row_count, step, 0)

    def launch(u):
        @pl.when(outer)
        def _():
            if u >= r_slots:
                pl.semaphore_wait(credit, 1)
            inward(u).start()

    def add(first, second, target):
        for k in range(row_count):
            target[k] = (first[k].astype(f32) + second[k].astype(f32)).astype(bf16)

    def middle(u):
        @pl.when(inner)
        def _():
            inward(u).wait_recv()
            add(made(u), r_land.at[u % r_slots], s.at[u % s_slots])
            across(u).start()
            if u + r_slots < pieces:
                pl.semaphore_signal(credit, inc=1, device_id=to_outer, device_id_type=MESH)

    def finish_inner(u):
        @pl.when(inner)
        def _():
            if u >= t_slots:
                outward(u - t_slots).wait_send()
                sent_home(u - t_slots, t.at[u % t_slots])
            across(u).wait_recv()
            add(s.at[u % s_slots], m_land.at[u % m_slots], t.at[u % t_slots])
            outward(u).start()
            send_home(u, t.at[u % t_slots])
            across(u).wait_send()

    def finish_outer(u):
        @pl.when(outer)
        def _():
            outward(u).wait_recv()
            send_home(u, b_land.at[u])

    ahead = 4

    def pass_on(u):
        middle(u)
        if u >= 2:
            finish_inner(u - 2)
        if u + ahead < pieces:
            if u % 4 == 0:
                produce((u + ahead) // 4)
            launch(u + ahead)
        if u >= 3:
            finish_outer(u - 3)

    set_a = (got_a, diag_a, hx_a, hy_a, ts_a, fx_a)
    set_b = (got_b, diag_b, hx_b, hy_b, ts_b, fx_b)
    gain2 = vec_all[3:4, :]
    heads = mixed.shape[1] // (3 * HEAD)
    here = strip(row * width, width)
    tile = 64
    first = reduce_steps(part, own_sum, *set_a, p_send, p_recv, 0, mostly_x=True)
    second = spread_steps(tot, rows, width, p_send, p_recv, 10, mostly_x=True)
    third = reduce_steps(cot, own_sum, *set_b, p_send, p_recv, 20, mostly_x=True)
    fourth = reduce_steps(tot, own_sum, *set_a, p_send, p_recv, 30, mostly_x=True)

    def down_here():
        down_own.wait()
        for copy in down_recvs:
            copy.wait_recv()
        loads[9].start()

    def upper_step(k, none):
        down, across_ = k // (units // CHUNK), k % (units // CHUNK)
        at, lanes = strip(down * rows, rows), strip(across_ * CHUNK, CHUNK)
        dup[at, lanes] = (dot_nt(cot[at, :], tot[lanes, :]) * dup[at, lanes].astype(f32)).astype(bf16)
        return none

    def uppers(part_of):
        if part_of == 0:
            for k in (2, 3, 4, 9):
                loads[k].wait()
        count = (length // rows) * (units // CHUNK) // 2
        lax.fori_loop(part_of * count, (part_of + 1) * count, upper_step, 0)

    def d_normed2(part_of):
        tiled_nt(dup, upw, part, units, 1024, 256, (part_of, part_of + 1, 2))
        if part_of == 1:
            loads[6].start()
            next(first)

    def gather_start():
        next(first, None)
        block(tot, col, side, core, rows, width)[...] = own_sum[...].astype(bf16)
        next(second)

    def norm_step(k, none):
        at = strip(k * tile, tile)
        grad, standard, inverse = tot[at, :].astype(f32), std[at, :].astype(f32), stats[at, 0:1]
        scaled = grad * gain2
        mean_one = jnp.sum(scaled, axis=1, keepdims=True) / full
        mean_two = jnp.sum(scaled * standard, axis=1, keepdims=True) / full
        top = cot[at, :].astype(f32)
        low = (top + inverse * (scaled - mean_one - standard * mean_two)).astype(bf16)
        part[at, :] = low
        sums[0:1, :] += jnp.sum(grad * standard, axis=0, keepdims=True)
        sums[1:2, :] += jnp.sum(grad, axis=0, keepdims=True)
        sums[2:3, :] += jnp.sum(low.astype(f32), axis=0, keepdims=True)
        sums[3:4, :] += jnp.sum(top, axis=0, keepdims=True)

        @pl.when(k // (rows // tile) == col)
        def _():
            own = tot[at, here].astype(f32) * vec_all[3:4, here]
            dres_own[strip(k % (rows // tile) * tile, tile), :] = cot[at, here].astype(f32) + inverse * (
                own - mean_one - std[at, here].astype(f32) * mean_two
            )

        return none

    def norm_back(part_of):
        if part_of == 0:
            for k in (5, 11, 12, 13, 14):
                loads[k].wait()
        count = length // tile // 2
        lax.fori_loop(part_of * count, (part_of + 1) * count, norm_step, 0)
        if part_of == 1:
            loads[7].start()

    def d_attended():
        tiled_nt(part, outw, d_att, full, 512, 256)

    factor = 1.0 / math.sqrt(HEAD)
    blocks = length // SPAN
    spots = (SPAN, SPAN)
    earlier = lax.broadcasted_iota(jnp.int32, spots, 1) <= lax.broadcasted_iota(jnp.int32, spots, 0)

    def attention_back(head, begin, end):
        base = head * 3 * HEAD
        at_q, at_k, at_v = pl.ds(base, HEAD), pl.ds(base + HEAD, HEAD), pl.ds(base + 2 * HEAD, HEAD)
        at_o = pl.ds(head * HEAD, HEAD)
        if begin == 0:
            dk_acc[...] = jnp.zeros_like(dk_acc)
            dv_acc[...] = jnp.zeros_like(dv_acc)
        for k in range(begin, end):
            now = pl.ds(k * SPAN, SPAN)
            seen = (k + 1) * SPAN
            query, dout = mixed[now, at_q], d_att[now, at_o]
            keys, values = mixed[:seen, at_k], mixed[:seen, at_v]
            scores = dot_nt(query, keys) * factor
            last = jnp.where(earlier | (marks[k : k + 1, :1] > 0), scores[:, seen - SPAN :], masked_score)
            scores = last if k == 0 else jnp.concatenate([scores[:, : seen - SPAN], last], axis=1)
            probs = jnp.exp(scores - stats[now, 1 + head : 2 + head])
            d_probs = dot_nt(dout, values)
            dots = jnp.sum(probs * d_probs, axis=1, keepdims=True)
            d_scores = (probs * (d_probs - dots)).astype(bf16)
            d_mix[now, at_q] = (jnp.dot(d_scores, keys, preferred_element_type=f32) * factor).astype(bf16)
            dk_acc[:seen] += dot_tn(d_scores, query)
            dv_acc[:seen] += dot_tn(probs.astype(bf16), dout)
        if end == blocks:
            d_mix[:, at_k] = (dk_acc[...] * factor).astype(bf16)
            d_mix[:, at_v] = dv_acc[...].astype(bf16)

    def d_normed1(part_of):
        if part_of == 0:
            loads[6].wait()
        tiled_nt(d_mix, upw, cot, d_mix.shape[1], 1024, 256, (part_of, part_of + 1, 2))
        if part_of == 1:
            next(third)

    def output_sums(part_of):
        if part_of == 0:
            loads[8].wait()
        tiled_nn(hid, n2, tot, 1024, 256, (part_of, part_of + 1, 2))
        if part_of == 1:
            next(fourth)

    grad1 = own_sum
    stat_sends, stat_recvs, dp_sends, dp_recvs, row_sends, row_recvs = [], [], [], [], [], []
    for step in range(1, row_count):
        target, source = (row + step) % row_count, (row + row_count - step) % row_count
        to, since = {"row": target}, {"row": source}
        stat_sends.append(put(stat_land.at[row], stat_land.at[row], p_send, p_recv, 43 + step - 1, to))
        stat_recvs.append(put(stat_land.at[source], stat_land.at[source], p_send, p_recv, 43 + step - 1, since))
        row_sends.append(put(small_out.at[row], small_out.at[row], p_send, p_recv, 50 + step - 1, to))
        row_recvs.append(put(small_out.at[source], small_out.at[source], p_send, p_recv, 50 + step - 1, since))
    for step in range(1, dp_count):
        target, source = (plane + step) % dp_count, (plane + dp_count - step) % dp_count
        dp_sends.append(put(dp_land.at[plane], dp_land.at[plane], p_send, p_recv, 47 + step - 1, {"dp": target}))
        dp_recvs.append(put(dp_land.at[source], dp_land.at[source], p_send, p_recv, 47 + step - 1, {"dp": source}))
    x_copy = put(small.at[pl.ds(0, 8)], x_land, p_send, p_recv, 46, partners()[0])

    def row_stats():
        next(third, None)
        scaled = grad1[...] * vec_all[0:1, here]
        first_sum = jnp.sum(scaled, axis=1, keepdims=True)
        second_sum = jnp.sum(scaled * std1_own[...].astype(f32), axis=1, keepdims=True)
        lane = lax.broadcasted_iota(jnp.int32, (rows, 128), 1)
        pair = jnp.where(lane == 0, first_sum, jnp.where(lane == 1, second_sum, 0.0))
        stat_land[row] = pair.T[:8]
        for copy in stat_sends:
            copy.start()

    def small_sums():
        small[...] = jnp.zeros_like(small)
        small[0:1, :] = jnp.sum(grad1[...] * std1_own[...].astype(f32), axis=0, keepdims=True)
        small[1:2, :] = jnp.sum(grad1[...], axis=0, keepdims=True)
        small[2:6, :] = sums[0:4, here]
        totals = jnp.sum(dup[...].astype(f32), axis=0, keepdims=True)
        for k in range(units // width):
            small[8 + k : 9 + k, :] = totals[:, k * width : (k + 1) * width]
        mixes = jnp.sum(d_mix[...].astype(f32), axis=0, keepdims=True)
        spot = 8 + units // width
        picked = [
            mixes[:, (head * 3 + kind) * HEAD : (head * 3 + kind + 1) * HEAD] for head in range(heads) for kind in (0, 2)
        ]
        small[spot : spot + 1, : 2 * heads * HEAD] = jnp.concatenate(picked, axis=1)
        x_copy.start()

    def tokens_out():
        for copy in stat_recvs:
            copy.wait_recv()
        both = stat_land[0]
        for k in range(1, row_count):
            both = both + stat_land[k]
        both = jnp.concatenate([both, jnp.zeros((120, rows), f32)], axis=0).T
        scaled = grad1[...] * vec_all[0:1, here]
        d_norm1 = inv1_own[...] * (
            scaled - both[:, 0:1] / full - std1_own[...].astype(f32) * (both[:, 1:2] / full)
        )
        tokens_block[...] = (dres_own[...] + d_norm1).astype(bf16)
        loads[10].start()

    def dp_start():
        x_copy.wait_recv()
        x_copy.wait_send()
        small[0:2, :] += x_land[0:2, :]
        dp_land[plane] = small[...]
        for copy in dp_sends:
            copy.start()

    def output_out():
        next(fourth, None)
        loads[10].wait()
        out_block[...] = (dres_own[...] + (own_sum[...] + down_bias[...])).astype(bf16)

    def rows_start():
        for copy in dp_recvs:
            copy.wait_recv()
        together = dp_land[0]
        for k in range(1, dp_count):
            together = together + dp_land[k]
        small_out[row] = together
        for copy in row_sends:
            copy.start()

    tasks = {
        6: [down_here],
        8: [lambda: uppers(0)],
        9: [lambda: uppers(1)],
        10: [lambda: d_normed2(0)],
        11: [lambda: d_normed2(1)],
        13: [lambda: next(first)],
        16: [lambda: next(first)],
        19: [gather_start],
        22: [lambda: next(second)],
        24: [lambda: next(second)],
        25: [lambda: next(second, None), loads[8].start],
        26: [lambda: norm_back(0)],
        27: [lambda: norm_back(1)],
        28: [d_attended],
        29: [lambda: attention_back(0, 0, blocks - 1)],
        30: [lambda: attention_back(0, blocks - 1, blocks), lambda: attention_back(1, 0, blocks // 2)],
        31: [lambda: attention_back(1, blocks // 2, blocks), loads[7].wait],
        32: [lambda: d_normed1(0)],
        33: [lambda: d_normed1(1)],
        34: [lambda: next(third), lambda: output_sums(0)],
        35: [lambda: output_sums(1)],
        36: [lambda: next(fourth)],
        37: [lambda: next(third)],
        39: [lambda: next(fourth)],
        40: [row_stats],
        41: [small_sums],
        42: [tokens_out],
        43: [dp_start],
        44: [output_out],
        45: [rows_start],
    }
    sums[...] = jnp.zeros_like(sums)
    loads[0].wait()
    loads[1].wait()
    produce(0)
    for k in range(ahead):
        launch(k)
    for u in range(pieces):
        pass_on(u)
        for task in tasks.get(u, ()):
            task()
    finish_inner(pieces - 2)
    finish_inner(pieces - 1)
    finish_outer(pieces - 3)
    finish_outer(pieces - 2)
    finish_outer(pieces - 1)
    for copy in row_recvs:
        copy.wait_recv()
    for copy in down_sends + stat_sends + dp_sends + row_sends:
        copy.wait_send()

    @pl.when(outer)
    def _():
        for u in range(pieces - 4 * g_slots, pieces):
            inward(u).wait_send()
        for u in range(pieces):
            sent_home(u, b_land.at[u])

    @pl.when(inner)
    def _():
        for u in range(pieces - t_slots, pieces):
            outward(u).wait_send()
            sent_home(u, t.at[u % t_slots])

    for u in range(pieces):
        for step in range(1, row_count):
            source = (row + row_count - step) % row_count
            put(t.at[0, source], place(u, source), a_send, a_recv, 3 * u + step - 1, {"row": source}).wait_recv()


def backward_plane(
    cid, hid, cot, slope, n2, upw, std, n1, qkvw, down_nat, resid_own, attended, outw, mixed, std1_own, stats, marks, vec_all, inv1_own, down_bias
):
    f32, bf16 = jnp.float32, jnp.bfloat16
    length, full = cot.shape
    rows, width = length // lax.axis_size("col"), full // lax.axis_size("row")
    row_count, dp_count = full // width, lax.axis_size("dp")
    counts = (slope.shape[1] // CHUNK, slope.shape[1] // CHUNK, attended.shape[1] // CHUNK, mixed.shape[1] // CHUNK)
    total = sum(counts)
    unit = (row_count, LINES, CHUNK)
    shape = jax.ShapeDtypeStruct
    away, near = pl.BlockSpec(memory_space=pl.ANY), pl.BlockSpec(memory_space=pltpu.VMEM)
    vmem, dma = pltpu.VMEM, pltpu.SemaphoreType.DMA
    sets = [
        vmem((4, rows, width), bf16),
        vmem((rows, width), bf16),
        vmem((rows // 2, width), bf16),
        vmem((rows // 2, width), bf16),
        vmem((2, rows, width), bf16),
        vmem((2, rows, width), bf16),
    ]
    return pl.pallas_call(
        functools.partial(backward_kernel, counts),
        out_shape=[
            shape((row_count * counts[0], CHUNK, width), bf16),
            shape((2, CHUNK, row_count * counts[1] * CHUNK), bf16),
            shape((row_count * counts[2], CHUNK, width), bf16),
            shape((2, CHUNK, row_count * counts[3] * CHUNK), bf16),
            shape((4 * total,) + unit, bf16),
            shape((hid.shape[1], full), bf16),
            shape((rows, width), bf16),
            shape((rows, width), bf16),
            shape((row_count, 16, width), f32),
        ],
        in_specs=[away] * 14 + [near] * 5,
        out_specs=[away] * 6 + [near] * 3,
        scratch_shapes=[
            vmem((length, full), bf16),
            vmem((length, full), bf16),
            vmem((length, full), bf16),
            vmem((length, full), bf16),
            vmem((length, full), bf16),
            vmem(upw.shape, bf16),
            vmem(hid.shape, bf16),
            vmem(slope.shape, bf16),
            vmem(attended.shape, bf16),
            vmem(outw.shape, bf16),
            vmem(mixed.shape, bf16),
            vmem(std1_own.shape, bf16),
            vmem(attended.shape, bf16),
            vmem(mixed.shape, bf16),
            vmem((length, HEAD), f32),
            vmem((length, HEAD), f32),
            vmem((2, row_count, width // CHUNK, CHUNK, CHUNK), bf16),
            vmem((3,) + unit, bf16),
            vmem((4,) + unit, bf16),
            vmem((6,) + unit, bf16),
            vmem((6,) + unit, bf16),
        ]
        + sets
        + sets
        + [
            vmem((rows, width), f32),
            vmem((rows, width), f32),
            vmem((8, full), f32),
            vmem((16, width), f32),
            vmem((8, width), f32),
            vmem((dp_count, 16, width), f32),
            vmem((row_count, 8, rows), f32),
            dma((15,)),
            pltpu.SemaphoreType.REGULAR,
            dma((4 * total + 1,)),
            dma((12 * total,)),
            dma((12 * total,)),
            dma((12 * total,)),
            dma((12 * total,)),
            dma((53,)),
            dma((53,)),
        ],
        compiler_params=pltpu.CompilerParams(
            collective_id=cid, has_side_effects=True, vmem_limit_bytes=64 * 1024 * 1024 - 65536
        ),
        cost_estimate=pl.CostEstimate(flops=40_000_000_000, bytes_accessed=100_000_000, transcendentals=4_000_000),
    )(hid, cot, slope, n2, upw, std, n1, qkvw, down_nat, resid_own, attended, outw, mixed, std1_own, stats, marks, vec_all, inv1_own, down_bias)


class Moves:
    def __init__(self, source, target, cut, parts, sends, recvs, base):
        row, plane = lax.axis_index("row"), lax.axis_index("dp")
        side, core = row // 2, row % 2
        parity = plane % 2
        other = {"dp": plane + 1 - 2 * parity}
        twin = side * 2 + 1 - core
        far = ((1 - side) * 2 + core, (1 - side) * 2 + 1 - core)
        self.sibling = put(source(twin), target(row), sends, recvs, base, {"row": twin})
        self.sibling_in = put(source(twin), target(twin), sends, recvs, base, {"row": twin})
        self.outs, self.ins, self.passes, self.gets = [], [], [], []
        at = base + 1
        for step in range(parts // 2):
            for k, device in enumerate(far):
                mine, theirs = 2 * step + parity, 2 * step + 1 - parity
                there, here = cut(target(row), mine), cut(target(device), mine)
                self.outs.append(put(cut(source(device), mine), there, sends, recvs, at, {"row": device}))
                self.ins.append(put(cut(source(device), mine), here, sends, recvs, at, {"row": device}))
                self.passes.append(put(here, here, sends, recvs, at + 1, other))
                lands = cut(target(device), theirs)
                self.gets.append(put(lands, lands, sends, recvs, at + 1, other))
                at += 2

    @staticmethod
    def count(parts):
        return 1 + 2 * parts

    def start(self):
        self.sibling.start()
        self.start_far()

    def start_far(self):
        for copy in self.outs:
            copy.start()

    def forward(self, begin=0, end=None):
        for came, passed in list(zip(self.ins, self.passes))[begin:end]:
            came.wait_recv()
            passed.start()

    def finish(self):
        self.sibling_in.wait_recv()
        for copy in self.gets:
            copy.wait_recv()

    def drain(self):
        self.sibling.wait_send()
        for copy in self.outs + self.passes:
            copy.wait_send()


FAR_PARTS = 8


def forward_kernel(
    tokens,
    cot_in,
    ln1_gain,
    ln1_shift,
    out_bias_in,
    ln2_gain,
    ln2_shift,
    qv_bias,
    up_bias_in,
    spans,
    qkv_in,
    out_nat,
    up_nat,
    cot_all,
    n1_out,
    n2_out,
    std_out,
    upw_out,
    qkvw_out,
    outw_out,
    mixed_out,
    attended_out,
    hid_out,
    slope_out,
    stats,
    marks,
    vec_all,
    resid_own,
    std1_own,
    inv1_own,
    tok,
    n1,
    part,
    tot,
    qkvw,
    upw,
    outw,
    mixed,
    attended,
    hid,
    slope,
    own_sum,
    got,
    diag,
    hx,
    hy,
    ts,
    fx,
    qkv_raw,
    qkv_nat,
    mixed_bias,
    local_sem,
    w_send,
    w_recv,
    p_send,
    p_recv,
):
    f32, bf16 = jnp.float32, jnp.bfloat16
    plane, row, col = lax.axis_index("dp"), lax.axis_index("row"), lax.axis_index("col")
    side, core = row // 2, row % 2
    rows, width = tokens.shape
    length, full = tok.shape
    row_count = full // width
    heads_width = attended.shape[1]
    units = hid.shape[1]

    barrier = pltpu.get_barrier_semaphore()
    twins = ({"row": (1 - side) * 2 + 1 - core}, {"dp": plane + 1 - 2 * (plane % 2)})
    for partner in partners() + twins:
        pl.semaphore_signal(barrier, inc=1, device_id=partner, device_id_type=MESH)
    pl.semaphore_wait(barrier, 5)

    def cut_rows(ref, part):
        count = ref.shape[0] // FAR_PARTS
        return ref.at[strip(part * count, count)]

    per = qkvw.shape[1]
    count = Moves.count(FAR_PARTS)
    qkv_moves = Moves(
        lambda r: qkv_nat.at[:, strip(r * per, per)],
        lambda r: qkvw.at[strip(r * width, width), :],
        cut_rows,
        FAR_PARTS,
        w_send,
        w_recv,
        0,
    )
    out_moves = Moves(
        lambda r: out_nat.at[strip(r * heads_width, heads_width), :],
        lambda r: outw.at[:, strip(r * width, width)],
        cut_rows,
        FAR_PARTS,
        w_send,
        w_recv,
        count,
    )
    up_moves = Moves(
        lambda r: up_nat.at[:, strip(r * units, units)],
        lambda r: upw.at[strip(r * width, width), :],
        cut_rows,
        FAR_PARTS,
        w_send,
        w_recv,
        2 * count,
    )
    locals_ = [
        (qkv_nat.at[:, strip(row * per, per)], qkvw.at[strip(row * width, width), :]),
        (out_nat.at[strip(row * heads_width, heads_width), :], outw.at[:, strip(row * width, width)]),
        (up_nat.at[:, strip(row * units, units)], upw.at[strip(row * width, width), :]),
        (cot_in, block(cot_all, col, side, core, rows, width)),
        (n1, n1_out),
        (part, n2_out),
        (n1, std_out),
        (upw, upw_out),
        (qkvw, qkvw_out),
        (outw, outw_out),
        (mixed, mixed_out),
        (attended, attended_out),
        (hid, hid_out),
        (slope, slope_out),
        (qkv_in, qkv_raw),
    ]
    local = [pltpu.make_async_copy(a, b, local_sem.at[k]) for k, (a, b) in enumerate(locals_)]
    local[14].start()
    for k in range(1, 4):
        local[k].start()

    block(tok, col, side, core, rows, width)[...] = tokens[...]
    gather = spread_steps(tok, rows, width, p_send, p_recv, 0, mostly_x=True)
    next(gather)
    here = strip(row * width, width)
    vec_all[:, here] = jnp.zeros((vec_all.shape[0], width), f32)
    for k, vector in enumerate((ln1_gain, ln1_shift, out_bias_in, ln2_gain, ln2_shift)):
        vec_all[k : k + 1, here] = vector[...]
    vec_sends, vec_recvs = [], []
    for step in range(1, row_count):
        target, source = (row + step) % row_count, (row + row_count - step) % row_count
        here, there = vec_all.at[:, strip(row * width, width)], vec_all.at[:, strip(source * width, width)]
        vec_sends.append(put(here, here, p_send, p_recv, 10 + step - 1, {"row": target}))
        vec_recvs.append(put(there, there, p_send, p_recv, 10 + step - 1, {"row": source}))
        vec_sends[-1].start()
    out_moves.sibling.start()
    up_moves.sibling.start()
    local[14].wait()
    for kind in range(3):
        flat = qkv_raw[:, kind].reshape(width, qkv_raw.shape[2] * HEAD)
        for head in range(qkv_raw.shape[2]):
            qkv_nat[:, pl.ds((head * 3 + kind) * HEAD, HEAD)] = flat[:, head * HEAD : (head + 1) * HEAD]
    local[0].start()
    qkv_moves.sibling.start()
    qkv_moves.start_far()
    next(gather)
    next(gather)
    next(gather, None)
    for copy in vec_recvs:
        copy.wait_recv()
    lines = lax.broadcasted_iota(jnp.int32, marks.shape, 0) * SPAN
    found = jnp.zeros(marks.shape, f32)
    for k in range(spans.shape[1]):
        found = jnp.where(lines == spans[0:1, k : k + 1] // SPAN * SPAN, 1.0, found)
    marks[...] = found

    tile = 64
    gain1, shift1 = vec_all[0:1, :], vec_all[1:2, :]

    def norm1_step(k, none):
        at = strip(k * tile, tile)
        values = tok[at, :].astype(f32)
        center = jnp.sum(values, axis=1, keepdims=True) / full
        inverse = lax.rsqrt(jnp.sum(values * values, axis=1, keepdims=True) / full - center * center + epsilon)
        n1[at, :] = ((values - center) * inverse * gain1 + shift1).astype(bf16)

        @pl.when(k // (rows // tile) == col)
        def _():
            here = strip(k % (rows // tile) * tile, tile)
            std1_own[here, :] = ((tok[at, strip(row * width, width)].astype(f32) - center) * inverse).astype(bf16)
            inv1_own[here, :] = inverse

        return none

    half_steps = length // tile // 2
    quarter = half_steps // 2
    for k in range(4):
        qkv_moves.forward(2 * k, 2 * k + 1)
        lax.fori_loop(k * quarter, (k + 1) * quarter, norm1_step, 0)
        qkv_moves.forward(2 * k + 1, 2 * k + 2)
    local[4].start()
    out_moves.start_far()
    up_moves.start_far()
    qkv_moves.finish()
    local[0].wait()

    mixed_bias[...] = jnp.zeros_like(mixed_bias)
    for head in range(heads_width // HEAD):
        for k in range(2):
            lanes = pl.ds((head * 3 + 2 * k) * HEAD, HEAD)
            mixed_bias[:, lanes] = qv_bias[row * (heads_width // HEAD) + head, k : k + 1, :]
    up_bias = up_bias_in.at[:, strip(row * units, units)]

    def mixed_step(k, none):
        down, across = k // (per // CHUNK), k % (per // CHUNK)
        at, lanes = strip(down * rows, rows), strip(across * CHUNK, CHUNK)
        value = jnp.dot(n1[at, :], qkvw[:, lanes], preferred_element_type=f32)
        mixed[at, lanes] = (value + mixed_bias[:, lanes]).astype(bf16)
        return none

    lax.fori_loop(0, (length // rows) * (per // CHUNK), mixed_step, 0)
    local[8].start()
    local[10].start()
    local[4].wait()

    heads = heads_width // HEAD
    factor = 1.0 / math.sqrt(HEAD)
    blocks = length // SPAN
    spots = (SPAN, SPAN)
    earlier = lax.broadcasted_iota(jnp.int32, spots, 1) <= lax.broadcasted_iota(jnp.int32, spots, 0)

    def head_step(head, none):
        base = head * 3 * HEAD
        at_q, at_k, at_v = strip(base, HEAD), strip(base + HEAD, HEAD), strip(base + 2 * HEAD, HEAD)
        for k in range(blocks):
            here = pl.ds(k * SPAN, SPAN)
            seen = (k + 1) * SPAN
            scores = dot_nt(mixed[here, at_q], mixed[:seen, at_k]) * factor
            last = jnp.where(earlier | (marks[k : k + 1, :1] > 0), scores[:, seen - SPAN :], masked_score)
            scores = last if k == 0 else jnp.concatenate([scores[:, : seen - SPAN], last], axis=1)
            highest = jnp.max(scores, axis=1, keepdims=True)
            weights = jnp.exp(scores - highest)
            weight_sum = jnp.sum(weights, axis=1, keepdims=True)
            stats[here, 1 + head : 2 + head] = highest + jnp.log(weight_sum)
            value = jnp.dot((weights / weight_sum).astype(bf16), mixed[:seen, at_v], preferred_element_type=f32)
            attended[here, strip(head * HEAD, HEAD)] = value.astype(bf16)
        return none

    for head in range(heads):
        head_step(head, 0)
        if head == 0:
            out_moves.forward()
    local[11].start()
    up_moves.forward(0, 4)
    out_moves.finish()
    local[1].wait()
    tiled_nn(attended, outw, part, rows, 512)
    local[9].start()
    add_up = reduce_steps(part, own_sum, got, diag, hx, hy, ts, fx, p_send, p_recv, 13)
    next(add_up)
    next(add_up)
    next(add_up)
    up_moves.forward(4, 8)
    next(add_up, None)
    block(tot, col, side, core, rows, width)[...] = own_sum[...].astype(bf16)
    again = spread_steps(tot, rows, width, p_send, p_recv, 23)
    next(again)
    next(again)
    local[3].wait()
    cot_gather = spread_steps(cot_all, rows, width, p_send, p_recv, 33)
    next(cot_gather)
    next(again)
    next(again, None)

    gain2, shift2, out_bias = vec_all[3:4, :], vec_all[4:5, :], vec_all[2:3, :]

    def norm2_step(k, none):
        at = strip(k * tile, tile)
        values = tok[at, :].astype(f32) + (tot[at, :].astype(f32) + out_bias)
        center = jnp.sum(values, axis=1, keepdims=True) / full
        inverse = lax.rsqrt(jnp.sum(values * values, axis=1, keepdims=True) / full - center * center + epsilon)
        standard = (values - center) * inverse
        stats[at, 0:1] = inverse
        n1[at, :] = standard.astype(bf16)
        part[at, :] = (standard * gain2 + shift2).astype(bf16)

        @pl.when(k // (rows // tile) == col)
        def _():
            own = strip(row * width, width)
            here = strip(k % (rows // tile) * tile, tile)
            resid_own[here, :] = tok[at, own].astype(f32) + (tot[at, own].astype(f32) + vec_all[2:3, own])

        return none

    lax.fori_loop(0, 2 * half_steps, norm2_step, 0)
    local[5].start()
    local[6].start()
    next(cot_gather)
    up_moves.finish()
    local[2].wait()
    local[7].start()

    def up_step(k, none):
        down, across = k // (units // CHUNK), k % (units // CHUNK)
        at, lanes = strip(down * rows, rows), strip(across * CHUNK, CHUNK)
        u = jnp.dot(part[at, :], upw[:, lanes], preferred_element_type=f32) + up_bias[:, lanes]
        bent = jnp.tanh(0.7978845608028654 * (u + 0.044715 * u * u * u))
        hid[at, lanes] = (0.5 * u * (1.0 + bent)).astype(bf16)
        inside = 0.7978845608028654 * (1.0 + 3 * 0.044715 * u * u)
        slope[at, lanes] = (0.5 * (1.0 + bent) + 0.5 * u * (1.0 - bent * bent) * inside).astype(bf16)
        return none

    lax.fori_loop(0, (length // rows) * (units // CHUNK), up_step, 0)
    local[12].start()
    local[13].start()
    next(cot_gather)
    next(cot_gather, None)
    for k in range(5, 14):
        local[k].wait()
    for moves in (qkv_moves, out_moves, up_moves):
        moves.drain()
    for copy in vec_sends:
        copy.wait_send()


def forward_plane(cid, tokens, cot, vectors, qv_bias, up_bias, spans, qkv_in, out_nat, up_nat):
    f32, bf16 = jnp.float32, jnp.bfloat16
    rows, width = tokens.shape
    row_count = lax.axis_size("row")
    length, full = rows * lax.axis_size("col"), width * row_count
    per, heads_width, units = qkv_in.shape[1] * qkv_in.shape[2] * HEAD // row_count, out_nat.shape[0] // row_count, up_nat.shape[1] // row_count
    shape = jax.ShapeDtypeStruct
    away, near = pl.BlockSpec(memory_space=pl.ANY), pl.BlockSpec(memory_space=pltpu.VMEM)
    vmem, dma = pltpu.VMEM, pltpu.SemaphoreType.DMA
    wide = shape((length, full), bf16)
    moved = 3 * Moves.count(FAR_PARTS)
    return pl.pallas_call(
        forward_kernel,
        out_shape=[
            wide,
            wide,
            wide,
            wide,
            shape((full, units), bf16),
            shape((full, per), bf16),
            shape((heads_width, full), bf16),
            shape((length, per), bf16),
            shape((length, heads_width), bf16),
            shape((length, units), bf16),
            shape((length, units), bf16),
            shape((length, 8), f32),
            shape((8, 128), f32),
            shape((8, full), f32),
            shape((rows, width), f32),
            shape((rows, width), bf16),
            shape((rows, 1), f32),
        ],
        in_specs=[near] * (5 + len(vectors)) + [away] * 3,
        out_specs=[away] * 11 + [near] * 6,
        scratch_shapes=[
            vmem((length, full), bf16),
            vmem((length, full), bf16),
            vmem((length, full), bf16),
            vmem((length, full), bf16),
            vmem((full, per), bf16),
            vmem((full, units), bf16),
            vmem((heads_width, full), bf16),
            vmem((length, per), bf16),
            vmem((length, heads_width), bf16),
            vmem((length, units), bf16),
            vmem((length, units), bf16),
            vmem((rows, width), f32),
            vmem((4, rows, width), bf16),
            vmem((rows, width), bf16),
            vmem((rows // 2, width), bf16),
            vmem((rows // 2, width), bf16),
            vmem((2, rows, width), bf16),
            vmem((2, rows, width), bf16),
            vmem(qkv_in.shape, bf16),
            vmem((width, row_count * per), bf16),
            vmem((1, per), f32),
            dma((15,)),
            dma((moved,)),
            dma((moved,)),
            dma((43,)),
            dma((43,)),
        ],
        compiler_params=pltpu.CompilerParams(
            collective_id=cid, has_side_effects=True, vmem_limit_bytes=60 * 1024 * 1024
        ),
        cost_estimate=pl.CostEstimate(flops=10_000_000_000, bytes_accessed=60_000_000, transcendentals=4_000_000),
    )(tokens, cot, *[vector[None] for vector in vectors], qv_bias, up_bias[None], spans, qkv_in, out_nat, up_nat)


def results_kernel(
    down, up, out, output, tokens, qkv, small, down_result, up_result, out_result, output_result, tokens_result, qkv_result, *vectors
):
    *sums, up_bias, qv_bias = vectors
    f32 = jnp.float32
    down_result[...] = down[...].astype(f32)
    up_result[...] = up[...].astype(f32)
    out_result[...] = out[...].astype(f32)
    output_result[...] = output[...]
    tokens_result[...] = tokens[...]
    for head in range(qkv_result.shape[2]):
        for kind in range(3):
            begin = (head * 3 + kind) * HEAD
            qkv_result[:, kind, head, :] = qkv[:, begin : begin + HEAD].astype(f32)

    @pl.when(pl.program_id(0) == 0)
    def _():
        row = lax.axis_index("row")
        for k, result in enumerate(sums):
            result[...] = small[row, k : k + 1, :]
        count, _, width = small.shape
        lines = up_bias.shape[1] // (count * width)
        heads = qv_bias.shape[0] // count
        for source in range(count):
            for k in range(lines):
                begin = (source * lines + k) * width
                up_bias[:, begin : begin + width] = small[source, 8 + k : 9 + k, :]
            for head in range(heads):
                for k in range(2):
                    begin = (head * 2 + k) * HEAD
                    line = small[source, 8 + lines : 9 + lines, begin : begin + HEAD]
                    qv_bias[source * heads + head, k : k + 1, :] = line


def results(down, up, out, output, tokens, qkv, small):
    f32 = jnp.float32
    shape = jax.ShapeDtypeStruct
    rows, heads = qkv.shape[0], qkv.shape[1] // (3 * HEAD)
    width, units = small.shape[2], up.shape[1]
    steps = 8

    def cut(array):
        return pl.BlockSpec((array.shape[0] // steps, array.shape[1]), lambda k: (k, 0))

    def whole(*dims):
        return pl.BlockSpec(dims, lambda k: (0,) * len(dims))

    line = whole(1, width)
    *made, up_bias, qv_bias = pl.pallas_call(
        results_kernel,
        grid=(steps,),
        out_shape=[shape(a.shape, f32) for a in (down, up, out)]
        + [shape(a.shape, a.dtype) for a in (output, tokens)]
        + [shape((rows, 3, heads, HEAD), f32)]
        + [shape((1, width), f32)] * 6
        + [shape((1, units), f32), shape((heads, 2, HEAD), f32)],
        in_specs=[cut(a) for a in (down, up, out, output, tokens, qkv)] + [whole(*small.shape)],
        out_specs=[cut(a) for a in (down, up, out, output, tokens)]
        + [pl.BlockSpec((rows // steps, 3, heads, HEAD), lambda k: (k, 0, 0, 0))]
        + [line] * 6
        + [whole(1, units), whole(heads, 2, HEAD)],
        compiler_params=pltpu.CompilerParams(vmem_limit_bytes=63 * 1024 * 1024),
    )(down, up, out, output, tokens, qkv, small)
    made[5] = jnp.swapaxes(made[5], 1, 2)
    return made[:6], [sums[0] for sums in made[6:]], up_bias[0], qv_bias


def plane_plan(
    tokens,
    ln1_gain,
    ln1_shift,
    qkv_weight,
    qv_bias,
    out_weight,
    out_bias,
    ln2_gain,
    ln2_shift,
    up_weight,
    up_bias,
    down_weight,
    down_bias,
    span_starts,
    cotangent,
):
    width = tokens.shape[1]
    (
        cot_all, n1, n2, standard2, upw, qkvw, outw, mixed, attended, hidden, slope,
        stats, marks, vec_all, residual_own, standard1_own, inverse1_own,
    ) = forward_plane(
        1,
        tokens,
        cotangent,
        (ln1_gain, ln1_shift, out_bias, ln2_gain, ln2_shift),
        qv_bias,
        up_bias,
        span_starts,
        jnp.swapaxes(qkv_weight, 1, 2),
        out_weight.reshape(-1, width),
        up_weight,
    )
    down_grad, up_grad, out_grad, qkv_grad, _, _, output, tokens_grad, small = backward_plane(
        2, hidden, cot_all, slope, n2, upw, standard2, n1, qkvw, down_weight, residual_own, attended, outw, mixed, standard1_own,
        stats, marks, vec_all, inverse1_own, down_bias[None],
    )
    grads, sums, up_bias_grad, qv_bias_grad = results(
        down_grad.reshape(-1, width), up_grad.reshape(width, -1), out_grad.reshape(-1, width), output, tokens_grad,
        qkv_grad.reshape(width, -1), small
    )
    return (
        grads[3],
        grads[4],
        sums[0],
        sums[1],
        grads[5],
        qv_bias_grad,
        grads[2].reshape(out_weight.shape),
        sums[4],
        sums[2],
        sums[3],
        grads[1],
        up_bias_grad,
        grads[0],
        sums[5],
    )


def solution(mesh):
    sizes = dict(mesh.shape)
    flat = sizes == {"dp": 4, "row": 4, "col": 2}
    per_device = plane_plan if flat else general_plan
    placed = (
        P(("dp", "col"), "row"),
        P("row"),
        P("row"),
        P("row", "col", None, None),
        P("col", None, None),
        P("col", None, "row"),
        P("row"),
        P("row"),
        P("row"),
        P("row", "col"),
        P("col"),
        P("col", "row"),
        P("row"),
        P("dp", None),
        P(("dp", "col"), "row"),
    )
    return jax.shard_map(
        per_device,
        mesh=mesh,
        in_specs=placed,
        out_specs=(
            P(("dp", "col"), "row"),
            P(("dp", "col"), "row"),
            P("row"),
            P("row"),
            P("row", "col", None, None),
            P("col", None, None),
            P("col", None, "row"),
            P("row"),
            P("row"),
            P("row"),
            P("row", "col"),
            P("col"),
            P("col", "row"),
            P("row"),
        ),
        check_vma=False,
    )
```

```python
import functools
import math

import jax
import jax.numpy as jnp
from jax import lax
from jax.experimental import pallas as pl
from jax.experimental.pallas import tpu as pltpu
from jax.sharding import PartitionSpec as P

MESH = pl.DeviceIdType.MESH

D = 2048
HEAD = 128
SEQS = 1
SPAN = 256
BLOCK = 512


epsilon = 1e-05
masked_score = -1e30


def gelu_tanh(values):
    return (
        0.5
        * values
        * (1.0 + jnp.tanh(0.7978845608028654 * (values + 0.044715 * values * values * values)))
    )


def gather_columns(block_data):
    return lax.all_gather(block_data, "col", axis=0, tiled=True)


def gather_rows(block_data):
    return lax.all_gather(block_data, "row", axis=0, tiled=True)


def product(left_side, right_side, flipped):
    if flipped:
        return lax.dot_general(
            left_side, right_side, (((1,), (1,)), ((), ())), preferred_element_type=jnp.float32
        )
    return jnp.dot(left_side, right_side, preferred_element_type=jnp.float32)


def outer_sum(left_side, right_side):
    return lax.dot_general(
        left_side, right_side, (((0,), (0,)), ((), ())), preferred_element_type=jnp.float32
    )


def sum_rows(left_side, right_side, flipped):
    wide_left = lax.all_to_all(left_side, "row", split_axis=0, concat_axis=1, tiled=True)
    if flipped:
        wide_right = lax.all_gather(right_side, "row", axis=1, tiled=True)
    else:
        wide_right = lax.all_gather(right_side, "row", axis=0, tiled=True)
    return product(wide_left, wide_right, flipped)


def sum_columns(left_side, right_side, flipped):
    return lax.psum_scatter(
        product(left_side, right_side, flipped), "col", scatter_dimension=0, tiled=True
    )


def row_totals(first_sum, second_sum):
    return lax.psum((first_sum, second_sum), "row")


def norm_forward(values, gain_row, bias_row):
    totals, squares = row_totals(jnp.sum(values, axis=1), jnp.sum(values * values, axis=1))
    center = totals / D
    spread = squares / D - center * center
    inverse = lax.rsqrt(spread + epsilon)
    standard = (values - center[:, None]) * inverse[:, None]
    return (standard, inverse, (standard * gain_row + bias_row).astype(jnp.bfloat16))


def norm_backward(upstream, standard, inverse, gain_row):
    scaled = upstream * gain_row
    first_sum, second_sum = row_totals(jnp.sum(scaled, axis=1), jnp.sum(scaled * standard, axis=1))
    gradient = inverse[:, None] * (
        scaled - first_sum[:, None] / D - standard * (second_sum[:, None] / D)
    )
    return (gradient, jnp.sum(upstream * standard, axis=0), jnp.sum(upstream, axis=0))


def visible(query_pos, query_image, key_pos):
    earlier = key_pos[None, :] <= query_pos[:, None]
    same_span = (key_pos[None, :] // SPAN == query_pos[:, None] // SPAN) & (
        query_image[:, None] > 0
    )
    return earlier | same_span


def attention_forward(queries, key_value, token_image, row_offset, seq_length, block_rows):
    own_rows, head_count, width = queries.shape
    factor = 1.0 / math.sqrt(width)

    def block_forward(block_index):
        local = block_index * block_rows
        start_pos = row_offset + local
        query_block = lax.dynamic_slice_in_dim(queries, local, block_rows, 0)
        query_pos = start_pos + jnp.arange(block_rows, dtype=jnp.int32)
        query_image = lax.dynamic_slice_in_dim(token_image, start_pos, block_rows, 0)
        begin = start_pos // seq_length * seq_length // block_rows
        finish = start_pos // block_rows + 1

        def key_step(key_index, state_in):
            running, weight_sum, gathered = state_in
            key_begin = key_index * block_rows
            key_block = lax.dynamic_slice_in_dim(key_value, key_begin, block_rows, 0)
            key_pos = key_begin + jnp.arange(block_rows, dtype=jnp.int32)
            allowed = visible(query_pos, query_image, key_pos)
            scores = (
                jnp.einsum(
                    "qhd,khd->hqk",
                    query_block,
                    key_block[:, :, 0],
                    preferred_element_type=jnp.float32,
                )
                * factor
            )
            scores = jnp.where(allowed[None], scores, masked_score)
            highest = jnp.maximum(running, jnp.max(scores, axis=2))
            weights = jnp.exp(scores - highest[:, :, None])
            shrink = jnp.exp(running - highest)
            weight_sum = weight_sum * shrink + jnp.sum(weights, axis=2)
            gathered = gathered * shrink.T[:, :, None] + jnp.einsum(
                "hqk,khd->qhd",
                weights.astype(jnp.bfloat16),
                key_block[:, :, 1],
                preferred_element_type=jnp.float32,
            )
            return (highest, weight_sum, gathered)

        initial = (
            jnp.full((head_count, block_rows), masked_score, jnp.float32),
            jnp.zeros((head_count, block_rows), jnp.float32),
            jnp.zeros((block_rows, head_count, width), jnp.float32),
        )
        running, weight_sum, gathered = lax.fori_loop(begin, finish, key_step, initial)
        return (gathered / weight_sum.T[:, :, None], running + jnp.log(weight_sum))

    result, logsum = lax.map(block_forward, jnp.arange(own_rows // block_rows, dtype=jnp.int32))
    return (result.reshape(own_rows, head_count, width), logsum)


def attention_backward(
    queries,
    key_value,
    attended_full,
    logsum,
    d_attended,
    token_image,
    row_offset,
    seq_length,
    block_rows,
):
    own_rows, head_count, width = queries.shape
    factor = 1.0 / math.sqrt(width)
    row_dots = jnp.sum(d_attended.astype(jnp.float32) * attended_full, axis=2)

    def block_backward(block_index, state_out):
        d_queries, d_pairs = state_out
        local = block_index * block_rows
        start_pos = row_offset + local
        query_block = lax.dynamic_slice_in_dim(queries, local, block_rows, 0)
        dout_block = lax.dynamic_slice_in_dim(d_attended, local, block_rows, 0)
        dots_block = lax.dynamic_slice_in_dim(row_dots, local, block_rows, 0).T
        logsum_block = logsum[block_index]
        query_pos = start_pos + jnp.arange(block_rows, dtype=jnp.int32)
        query_image = lax.dynamic_slice_in_dim(token_image, start_pos, block_rows, 0)
        begin = start_pos // seq_length * seq_length // block_rows
        finish = start_pos // block_rows + 1

        def key_step(key_index, state_in):
            d_query, d_keys = state_in
            key_begin = key_index * block_rows
            key_block = lax.dynamic_slice_in_dim(key_value, key_begin, block_rows, 0)
            key_pos = key_begin + jnp.arange(block_rows, dtype=jnp.int32)
            allowed = visible(query_pos, query_image, key_pos)
            scores = (
                jnp.einsum(
                    "qhd,khd->hqk",
                    query_block,
                    key_block[:, :, 0],
                    preferred_element_type=jnp.float32,
                )
                * factor
            )
            scores = jnp.where(allowed[None], scores, masked_score)
            probabilities = jnp.exp(scores - logsum_block[:, :, None])
            d_probs = jnp.einsum(
                "qhd,khd->hqk", dout_block, key_block[:, :, 1], preferred_element_type=jnp.float32
            )
            d_scores = (probabilities * (d_probs - dots_block[:, :, None])).astype(jnp.bfloat16)
            d_query = d_query + jnp.einsum(
                "hqk,khd->qhd", d_scores, key_block[:, :, 0], preferred_element_type=jnp.float32
            )
            d_key = (
                jnp.einsum(
                    "hqk,qhd->khd", d_scores, query_block, preferred_element_type=jnp.float32
                )
                * factor
            )
            d_value = jnp.einsum(
                "hqk,qhd->khd",
                probabilities.astype(jnp.bfloat16),
                dout_block,
                preferred_element_type=jnp.float32,
            )
            previous = lax.dynamic_slice_in_dim(d_keys, key_begin, block_rows, 0)
            d_keys = lax.dynamic_update_slice_in_dim(
                d_keys, previous + jnp.stack([d_key, d_value], axis=2), key_begin, 0
            )
            return (d_query, d_keys)

        d_query, d_pairs = lax.fori_loop(
            begin,
            finish,
            key_step,
            (jnp.zeros((block_rows, head_count, width), jnp.float32), d_pairs),
        )
        d_queries = lax.dynamic_update_slice_in_dim(d_queries, d_query * factor, local, 0)
        return (d_queries, d_pairs)

    initial = (
        jnp.zeros((own_rows, head_count, width), jnp.float32),
        jnp.zeros((key_value.shape[0], head_count, 2, width), jnp.float32),
    )
    return lax.fori_loop(0, own_rows // block_rows, block_backward, initial)


def general_plan(
    tokens,
    ln1_gain,
    ln1_shift,
    qkv_weight,
    qv_bias,
    out_weight,
    out_bias,
    ln2_gain,
    ln2_shift,
    up_weight,
    up_bias,
    down_weight,
    down_bias,
    span_starts,
    cotangent,
):
    col_rows, row_width = tokens.shape
    group_rows = col_rows * lax.axis_size("col")
    own_rows = group_rows // lax.axis_size("row")
    head_count = qkv_weight.shape[1]
    seq_length = group_rows // SEQS
    block_rows = BLOCK - own_rows % BLOCK
    row_offset = lax.axis_index("row") * own_rows
    slot_count = seq_length // SPAN
    image_marks = jnp.sum(
        (
            span_starts[:, :, None] // SPAN
            == jnp.arange(slot_count, dtype=jnp.int32)[None, None, :]
        ).astype(jnp.int32),
        axis=1,
    )
    token_image = jnp.broadcast_to(
        image_marks.reshape(-1)[:, None], (group_rows // SPAN, SPAN)
    ).reshape(group_rows)
    qkv_flat = qkv_weight.reshape(row_width, head_count * 3 * HEAD)
    out_flat = out_weight.reshape(head_count * HEAD, row_width)
    inputs = tokens.astype(jnp.float32)
    standard1, inverse1, normed1 = norm_forward(inputs, ln1_gain, ln1_shift)
    normed1_all = gather_columns(normed1)
    mixed_sums = sum_rows(normed1_all, qkv_flat, False).reshape(own_rows, head_count, 3, HEAD)
    queries = (mixed_sums[:, :, 0] + qv_bias[:, 0]).astype(jnp.bfloat16)
    key_value_own = jnp.stack(
        [mixed_sums[:, :, 1], mixed_sums[:, :, 2] + qv_bias[:, 1]], axis=2
    ).astype(jnp.bfloat16)
    key_value = gather_rows(key_value_own)
    attended_full, logsum = attention_forward(
        queries, key_value, token_image, row_offset, seq_length, block_rows
    )
    attended = attended_full.astype(jnp.bfloat16).reshape(own_rows, head_count * HEAD)
    attended_all = gather_rows(attended)
    residual = inputs + (sum_columns(attended_all, out_flat, False) + out_bias)
    standard2, inverse2, normed2 = norm_forward(residual, ln2_gain, ln2_shift)
    normed2_all = gather_columns(normed2)
    up_sums = sum_rows(normed2_all, up_weight, False) + up_bias
    hidden = gelu_tanh(up_sums).astype(jnp.bfloat16)
    hidden_all = gather_rows(hidden)
    output = (residual + (sum_columns(hidden_all, down_weight, False) + down_bias)).astype(
        jnp.bfloat16
    )
    d_output = cotangent.astype(jnp.float32)
    d_output_all = gather_columns(cotangent)
    down_grad = outer_sum(hidden_all, d_output_all)
    down_bias_grad = jnp.sum(d_output_all, axis=0, dtype=jnp.float32)
    d_hidden = sum_rows(d_output_all, down_weight, True)
    d_upper = jax.vjp(gelu_tanh, up_sums)[1](d_hidden)[0].astype(jnp.bfloat16)
    d_upper_all = gather_rows(d_upper)
    normed2_use = gather_columns(normed2)
    up_grad = outer_sum(normed2_use, d_upper_all)
    up_bias_grad = jnp.sum(d_upper_all, axis=0, dtype=jnp.float32)
    d_normed2 = sum_columns(d_upper_all, up_weight, True)
    d_norm2, gain2_grad, shift2_grad = norm_backward(d_normed2, standard2, inverse2, ln2_gain)
    d_residual = d_output + d_norm2
    d_branch = d_residual.astype(jnp.bfloat16)
    d_branch_all = gather_columns(d_branch)
    out_grad = outer_sum(attended_all, d_branch_all)
    out_bias_grad = jnp.sum(d_branch_all, axis=0, dtype=jnp.float32)
    d_attended = (
        sum_rows(d_branch_all, out_flat, True)
        .astype(jnp.bfloat16)
        .reshape(own_rows, head_count, HEAD)
    )
    d_queries, d_pairs = attention_backward(
        queries,
        key_value,
        attended_full,
        logsum,
        d_attended,
        token_image,
        row_offset,
        seq_length,
        block_rows,
    )
    d_pairs_own = lax.psum_scatter(d_pairs, "row", scatter_dimension=0, tiled=True)
    d_mixed = jnp.concatenate([d_queries[:, :, None], d_pairs_own], axis=2).astype(jnp.bfloat16)
    d_mixed_all = gather_rows(d_mixed)
    normed1_use = gather_columns(normed1)
    d_mixed_flat = d_mixed_all.reshape(group_rows, head_count * 3 * HEAD)
    qkv_grad = outer_sum(normed1_use, d_mixed_flat)
    mixed_totals = jnp.sum(d_mixed_all, axis=0, dtype=jnp.float32)
    qv_bias_grad = jnp.stack([mixed_totals[:, 0], mixed_totals[:, 2]], axis=1)
    d_normed1 = sum_columns(d_mixed_flat, qkv_flat, True)
    d_norm1, gain1_grad, shift1_grad = norm_backward(d_normed1, standard1, inverse1, ln1_gain)
    tokens_grad = (d_residual + d_norm1).astype(jnp.bfloat16)
    norm_sums = lax.psum((gain1_grad, shift1_grad, gain2_grad, shift2_grad), ("dp", "col"))
    weight_sums = lax.psum(
        (
            qkv_grad,
            qv_bias_grad,
            out_grad,
            out_bias_grad,
            up_grad,
            up_bias_grad,
            down_grad,
            down_bias_grad,
        ),
        "dp",
    )
    return (
        output,
        tokens_grad,
        norm_sums[0],
        norm_sums[1],
        weight_sums[0].reshape(row_width, head_count, 3, HEAD),
        weight_sums[1],
        weight_sums[2].reshape(head_count, HEAD, row_width),
        weight_sums[3],
        norm_sums[2],
        norm_sums[3],
        weight_sums[4],
        weight_sums[5],
        weight_sums[6],
        weight_sums[7],
    )


def places():
    row, col = lax.axis_index("row"), lax.axis_index("col")
    return col, row // 2, row % 2


def partners():
    col, side, core = places()
    return ({"col": 1 - col}, {"row": (1 - side) * 2 + core}, {"row": side * 2 + 1 - core})


def block(ref, col, side, core, rows, width, part=None):
    begin, count = col * rows, rows
    if part is not None:
        begin, count = begin + part * (rows // 2), rows // 2
    return ref.at[strip(begin, count), strip((side * 2 + core) * width, width)]


def put(ref_from, ref_to, sends, recvs, at, partner):
    return pltpu.make_async_remote_copy(
        src_ref=ref_from,
        dst_ref=ref_to,
        send_sem=sends.at[at],
        recv_sem=recvs.at[at],
        device_id=partner,
        device_id_type=MESH,
    )


def strip(begin, count):
    return pl.ds(pl.multiple_of(begin, count), count)


def dot_nt(left, right):
    return lax.dot_general(left, right, (((1,), (1,)), ((), ())), preferred_element_type=jnp.float32)


def dot_tn(left, right):
    return lax.dot_general(left, right, (((0,), (0,)), ((), ())), preferred_element_type=jnp.float32)


def tiled_nt(left, right, target, inner, tile_rows, tile_cols, span=(0, 1, 1)):
    rows, cols = target.shape
    across = cols // tile_cols

    def step(at, none):
        down, side = at // across, at % across
        value = dot_nt(left[strip(down * tile_rows, tile_rows), :inner], right[strip(side * tile_cols, tile_cols), :inner])
        target[strip(down * tile_rows, tile_rows), strip(side * tile_cols, tile_cols)] = value.astype(target.dtype)
        return none

    count = (rows // tile_rows) * across
    lax.fori_loop(span[0] * count // span[2], span[1] * count // span[2], step, 0)


def tiled_nn(left, right, target, tile_rows, tile_cols, span=(0, 1, 1)):
    rows, cols = target.shape
    across = cols // tile_cols

    def step(at, none):
        down, side = at // across, at % across
        value = jnp.dot(
            left[strip(down * tile_rows, tile_rows), :],
            right[:, strip(side * tile_cols, tile_cols)],
            preferred_element_type=jnp.float32,
        )
        target[strip(down * tile_rows, tile_rows), strip(side * tile_cols, tile_cols)] = value.astype(target.dtype)
        return none

    count = (rows // tile_rows) * across
    lax.fori_loop(span[0] * count // span[2], span[1] * count // span[2], step, 0)


def reduce_steps(part, result, got, diag, half_x, half_y, to_send, from_xy, sends, recvs, base, mostly_x=False):
    f32 = jnp.float32
    rows, width = result.shape
    half = rows // 2
    low, high = pl.ds(0, half), pl.ds(half, half)
    col, side, core = places()
    to_x, to_y, to_core = partners()
    spots = ((1 - col, 1 - side), (col, 1 - side), (1 - col, side), (col, side))
    copies = [
        put(block(part, a, b, 1 - core, rows, width), got.at[k], sends, recvs, base + k, to_core)
        for k, (a, b) in enumerate(spots)
    ]
    for copy in copies:
        copy.start()
    mine = [block(part, a, b, core, rows, width) for a, b in spots]
    dx = put(diag.at[low], half_x, sends, recvs, base + 4, to_x)
    dy = put(diag.at[high], half_y, sends, recvs, base + 5, to_x if mostly_x else to_y)

    def onward(k, span, at, partner):
        return put(to_send.at[k, span], from_xy.at[k, span], sends, recvs, base + at, partner)

    y_high, x_low = onward(0, high, 6, to_y), onward(1, low, 7, to_x)
    y_low, x_high = onward(0, low, 8, to_y), onward(1, high, 9, to_x)

    def pair(k, span):
        return mine[k][span].astype(f32) + got[k, span].astype(f32)

    yield
    copies[0].wait_recv()
    diag[...] = (mine[0][...].astype(f32) + got[0].astype(f32)).astype(diag.dtype)
    dx.start()
    dy.start()
    copies[1].wait_recv()
    if not mostly_x:
        to_send[0, high] = pair(1, high).astype(diag.dtype)
        y_high.start()
    copies[2].wait_recv()
    to_send[1, low] = pair(2, low).astype(diag.dtype)
    x_low.start()
    if mostly_x:
        to_send[1, high] = pair(2, high).astype(diag.dtype)
        x_high.start()
    copies[3].wait_recv()
    yield
    dx.wait_recv()
    to_send[0, low] = (pair(1, low) + half_x[...].astype(f32)).astype(diag.dtype)
    y_low.start()
    dy.wait_recv()
    if mostly_x:
        to_send[0, high] = (pair(1, high) + half_y[...].astype(f32)).astype(diag.dtype)
        y_high.start()
    else:
        to_send[1, high] = (pair(2, high) + half_y[...].astype(f32)).astype(diag.dtype)
        x_high.start()
    yield
    for copy in (y_high, x_low, y_low, x_high):
        copy.wait_recv()
    near = mine[3][...].astype(f32) + got[3].astype(f32)
    result[...] = near + from_xy[0].astype(f32) + from_xy[1].astype(f32)
    for copy in copies + [dx, dy, y_high, x_low, y_low, x_high]:
        copy.wait_send()


def spread_steps(out, rows, width, sends, recvs, base, mostly_x=False):
    col, side, core = places()
    to_x, to_y, to_core = partners()

    def copy_of(at, which, partner, part=None):
        ref = block(out, *which, rows, width, part)
        return put(ref, ref, sends, recvs, base + at, partner)

    own, ox, oy, od = (col, side, core), (1 - col, side, core), (col, 1 - side, core), (1 - col, 1 - side, core)
    plan = [
        copy_of(0, own, to_x, 0),
        copy_of(1, own, to_y, 1),
        copy_of(2, own, to_x, 1),
        copy_of(3, own, to_y, 0),
        copy_of(4, own, to_core),
        copy_of(5, oy, to_x, 0) if mostly_x else copy_of(5, ox, to_y, 0),
        copy_of(6, oy, to_x, 1),
        copy_of(7, ox, to_core),
        copy_of(8, oy, to_core),
        copy_of(9, od, to_core),
    ]
    for at in range(5):
        plan[at].start()
    yield
    plan[0].wait_recv()
    if not mostly_x:
        plan[5].start()
    plan[1].wait_recv()
    plan[6].start()
    plan[2].wait_recv()
    plan[7].start()
    plan[3].wait_recv()
    plan[8].start()
    if mostly_x:
        plan[5].start()
    yield
    plan[5].wait_recv()
    plan[6].wait_recv()
    plan[9].start()
    yield
    for at in (4, 7, 8, 9):
        plan[at].wait_recv()
    for copy in plan:
        copy.wait_send()


CHUNK = 256
LINES = CHUNK // 2


def backward_kernel(
    counts,
    hid_h,
    cot_h,
    slope_h,
    n2_h,
    upw_h,
    std_h,
    n1_h,
    qkvw_h,
    down_nat,
    resid_h,
    attended_h,
    outw_h,
    mixed_h,
    std1_h,
    stats,
    marks,
    vec_all,
    inv1_own,
    down_bias,
    down_out,
    up_out,
    out_out,
    qkv_out,
    b_land,
    downw_land,
    out_block,
    tokens_block,
    small_out,
    cot,
    n2,
    std,
    part,
    tot,
    upw,
    hid,
    dup,
    attended,
    outw,
    mixed,
    std1_own,
    d_att,
    d_mix,
    dk_acc,
    dv_acc,
    g,
    s,
    t,
    r_land,
    m_land,
    got_a,
    diag_a,
    hx_a,
    hy_a,
    ts_a,
    fx_a,
    got_b,
    diag_b,
    hx_b,
    hy_b,
    ts_b,
    fx_b,
    dres_own,
    own_sum,
    sums,
    small,
    x_land,
    dp_land,
    stat_land,
    load_sem,
    credit,
    own_sem,
    z_send,
    z_recv,
    a_send,
    a_recv,
    p_send,
    p_recv,
):
    f32, bf16 = jnp.float32, jnp.bfloat16
    n_down, n_up, n_out, n_qkv = counts
    total = sum(counts)
    plane, row, col = lax.axis_index("dp"), lax.axis_index("row"), lax.axis_index("col")
    length, full = cot.shape
    rows, width = dres_own.shape
    row_count = full // width
    inner = (plane == 1) | (plane == 2)
    outer = jnp.logical_not(inner)
    to_inner = {"dp": plane // 3 + 1}
    to_middle = {"dp": 3 - plane}
    to_outer = {"dp": (plane - 1) * 3}
    side, core = row // 2, row % 2

    loads = [
        (hid_h, hid),
        (cot_h, cot),
        (slope_h, dup),
        (upw_h, upw),
        (n2_h, n2),
        (std_h, std),
        (qkvw_h, upw.at[:, : qkvw_h.shape[1]]),
        (n1_h, std),
        (downw_land, n2),
        (downw_land, tot),
        (resid_h, dres_own),
        (attended_h, attended),
        (outw_h, outw),
        (mixed_h, mixed),
        (std1_h, std1_own),
    ]
    loads = [pltpu.make_async_copy(a, b, load_sem.at[k]) for k, (a, b) in enumerate(loads)]
    for k in (0, 1, 2, 3, 4, 5, 11, 12, 13, 14):
        loads[k].start()

    dp_count = dp_land.shape[0]
    barrier = pltpu.get_barrier_semaphore()
    others = [{"row": (1 - side) * 2 + 1 - core}] + [{"dp": (plane + k) % dp_count} for k in range(1, dp_count)]
    for partner in partners() + tuple(others):
        pl.semaphore_signal(barrier, inc=1, device_id=partner, device_id_type=MESH)
    pl.semaphore_wait(barrier, 3 + len(others))

    units = hid.shape[1]
    down_sends, down_recvs = [], []
    for step in range(1, row_count):
        target, source = (row + step) % row_count, (row + row_count - step) % row_count
        here, there = downw_land.at[:, strip(row * width, width)], downw_land.at[:, strip(source * width, width)]
        piece = down_nat.at[strip(target * units, units), :]
        down_sends.append(put(piece, here, p_send, p_recv, 40 + step - 1, {"row": target}))
        down_recvs.append(put(piece, there, p_send, p_recv, 40 + step - 1, {"row": source}))
        down_sends[-1].start()
    down_own = pltpu.make_async_copy(
        down_nat.at[strip(row * units, units), :], downw_land.at[:, strip(row * width, width)], own_sem.at[4 * total]
    )
    down_own.start()

    def place(u, source):
        i, half, quarter = u // 4, u // 2 % 2, pl.ds(u % 2 * LINES, LINES)
        if i < n_down:
            return down_out.at[source * n_down + i // 2 * 2 + half, quarter, pl.ds(i % 2 * CHUNK, CHUNK)]
        i -= n_down
        if i < n_up:
            return up_out.at[half, quarter, strip(source * n_up * CHUNK + i * CHUNK, CHUNK)]
        i -= n_up
        if i < n_out:
            return out_out.at[source * n_out + i, quarter, pl.ds(half * CHUNK, CHUNK)]
        i -= n_out
        return qkv_out.at[half, quarter, strip(source * n_qkv * CHUNK + i * CHUNK, CHUNK)]

    g_slots, s_slots, t_slots, r_slots, m_slots = g.shape[0], s.shape[0], t.shape[0], r_land.shape[0], m_land.shape[0]
    pieces = 4 * total

    def made(u):
        return g.at[u // 4 % g_slots, :, u // 2 % 2, pl.ds(u % 2 * LINES, LINES)]

    def inward(u):
        return put(made(u), r_land.at[u % r_slots], z_send, z_recv, u, to_inner)

    def across(u):
        return put(s.at[u % s_slots], m_land.at[u % m_slots], z_send, z_recv, pieces + u, to_middle)

    def outward(u):
        return put(t.at[u % t_slots], b_land.at[u], z_send, z_recv, 2 * pieces + u, to_outer)

    def home(u, step, source):
        target = (row + step) % row_count
        return put(source.at[target], place(u, row), a_send, a_recv, 3 * u + step - 1, {"row": target})

    def home_own(u, source):
        return pltpu.make_async_copy(source.at[row], place(u, row), own_sem.at[u])

    def send_home(u, source):
        for step in range(1, row_count):
            home(u, step, source).start()
        home_own(u, source).start()

    def sent_home(u, source):
        for step in range(1, row_count):
            home(u, step, source).wait_send()
        home_own(u, source).wait()

    def produce(i):
        if i >= g_slots:

            @pl.when(outer)
            def _():
                for k in range(4):
                    inward(4 * (i - g_slots) + k).wait_send()

        slot = g.at[i % g_slots]
        if i < n_down:
            begin, lane = i // 2 * 2 * CHUNK, i % 2 * CHUNK

            def step(k, none):
                value = dot_tn(hid[:, begin : begin + 2 * CHUNK], cot[:, strip(k * width + lane, CHUNK)]).astype(bf16)
                slot[k, 0] = value[:CHUNK]
                slot[k, 1] = value[CHUNK:]
                return none
        elif n_down + n_up <= i < n_down + n_up + n_out:
            left, begin, right = attended, (i - n_down - n_up) * CHUNK, part

            def step(k, none):
                value = dot_tn(left[:, begin : begin + CHUNK], right[:, strip(k * width, width)]).astype(bf16)
                slot[k, 0] = value[:, :CHUNK]
                slot[k, 1] = value[:, CHUNK:]
                return none
        else:
            if i < n_down + n_up:
                left, right, begin = n2, dup, (i - n_down) * CHUNK
            else:
                left, right, begin = std, d_mix, (i - n_down - n_up - n_out) * CHUNK

            def step(k, none):
                value = dot_tn(left[:, strip(k * width, width)], right[:, begin : begin + CHUNK]).astype(bf16)
                slot[k, 0] = value[:CHUNK]
                slot[k, 1] = value[CHUNK:]
                return none

        lax.fori_loop(0, row_count, step, 0)

    def launch(u):
        @pl.when(outer)
        def _():
            if u >= r_slots:
                pl.semaphore_wait(credit, 1)
            inward(u).start()

    def add(first, second, target):
        for k in range(row_count):
            target[k] = (first[k].astype(f32) + second[k].astype(f32)).astype(bf16)

    def middle(u):
        @pl.when(inner)
        def _():
            inward(u).wait_recv()
            add(made(u), r_land.at[u % r_slots], s.at[u % s_slots])
            across(u).start()
            if u + r_slots < pieces:
                pl.semaphore_signal(credit, inc=1, device_id=to_outer, device_id_type=MESH)

    def finish_inner(u):
        @pl.when(inner)
        def _():
            if u >= t_slots:
                outward(u - t_slots).wait_send()
                sent_home(u - t_slots, t.at[u % t_slots])
            across(u).wait_recv()
            add(s.at[u % s_slots], m_land.at[u % m_slots], t.at[u % t_slots])
            outward(u).start()
            send_home(u, t.at[u % t_slots])
            across(u).wait_send()

    def finish_outer(u):
        @pl.when(outer)
        def _():
            outward(u).wait_recv()
            send_home(u, b_land.at[u])

    ahead = 4

    def pass_on(u):
        middle(u)
        if u >= 2:
            finish_inner(u - 2)
        if u + ahead < pieces:
            if u % 4 == 0:
                produce((u + ahead) // 4)
            launch(u + ahead)
        if u >= 3:
            finish_outer(u - 3)

    set_a = (got_a, diag_a, hx_a, hy_a, ts_a, fx_a)
    set_b = (got_b, diag_b, hx_b, hy_b, ts_b, fx_b)
    gain2 = vec_all[3:4, :]
    heads = mixed.shape[1] // (3 * HEAD)
    here = strip(row * width, width)
    tile = 64
    first = reduce_steps(part, own_sum, *set_a, p_send, p_recv, 0, mostly_x=True)
    second = spread_steps(tot, rows, width, p_send, p_recv, 10, mostly_x=True)
    third = reduce_steps(cot, own_sum, *set_b, p_send, p_recv, 20, mostly_x=True)
    fourth = reduce_steps(tot, own_sum, *set_a, p_send, p_recv, 30, mostly_x=True)

    def down_here():
        down_own.wait()
        for copy in down_recvs:
            copy.wait_recv()
        loads[9].start()

    def upper_step(k, none):
        down, across_ = k // (units // CHUNK), k % (units // CHUNK)
        at, lanes = strip(down * rows, rows), strip(across_ * CHUNK, CHUNK)
        dup[at, lanes] = (dot_nt(cot[at, :], tot[lanes, :]) * dup[at, lanes].astype(f32)).astype(bf16)
        return none

    def uppers(part_of):
        if part_of == 0:
            for k in (2, 3, 4, 9):
                loads[k].wait()
        count = (length // rows) * (units // CHUNK) // 2
        lax.fori_loop(part_of * count, (part_of + 1) * count, upper_step, 0)

    def d_normed2(part_of):
        tiled_nt(dup, upw, part, units, 1024, 256, (part_of, part_of + 1, 2))
        if part_of == 1:
            loads[6].start()
            next(first)

    def gather_start():
        next(first, None)
        block(tot, col, side, core, rows, width)[...] = own_sum[...].astype(bf16)
        next(second)

    def norm_step(k, none):
        at = strip(k * tile, tile)
        grad, standard, inverse = tot[at, :].astype(f32), std[at, :].astype(f32), stats[at, 0:1]
        scaled = grad * gain2
        mean_one = jnp.sum(scaled, axis=1, keepdims=True) / full
        mean_two = jnp.sum(scaled * standard, axis=1, keepdims=True) / full
        top = cot[at, :].astype(f32)
        low = (top + inverse * (scaled - mean_one - standard * mean_two)).astype(bf16)
        part[at, :] = low
        sums[0:1, :] += jnp.sum(grad * standard, axis=0, keepdims=True)
        sums[1:2, :] += jnp.sum(grad, axis=0, keepdims=True)
        sums[2:3, :] += jnp.sum(low.astype(f32), axis=0, keepdims=True)
        sums[3:4, :] += jnp.sum(top, axis=0, keepdims=True)

        @pl.when(k // (rows // tile) == col)
        def _():
            own = tot[at, here].astype(f32) * vec_all[3:4, here]
            dres_own[strip(k % (rows // tile) * tile, tile), :] = cot[at, here].astype(f32) + inverse * (
                own - mean_one - std[at, here].astype(f32) * mean_two
            )

        return none

    def norm_back(part_of):
        if part_of == 0:
            for k in (5, 11, 12, 13, 14):
                loads[k].wait()
        count = length // tile // 2
        lax.fori_loop(part_of * count, (part_of + 1) * count, norm_step, 0)
        if part_of == 1:
            loads[7].start()

    def d_attended():
        tiled_nt(part, outw, d_att, full, 512, 256)

    factor = 1.0 / math.sqrt(HEAD)
    blocks = length // SPAN
    spots = (SPAN, SPAN)
    earlier = lax.broadcasted_iota(jnp.int32, spots, 1) <= lax.broadcasted_iota(jnp.int32, spots, 0)

    def attention_back(head, begin, end):
        base = head * 3 * HEAD
        at_q, at_k, at_v = pl.ds(base, HEAD), pl.ds(base + HEAD, HEAD), pl.ds(base + 2 * HEAD, HEAD)
        at_o = pl.ds(head * HEAD, HEAD)
        if begin == 0:
            dk_acc[...] = jnp.zeros_like(dk_acc)
            dv_acc[...] = jnp.zeros_like(dv_acc)
        for k in range(begin, end):
            now = pl.ds(k * SPAN, SPAN)
            seen = (k + 1) * SPAN
            query, dout = mixed[now, at_q], d_att[now, at_o]
            keys, values = mixed[:seen, at_k], mixed[:seen, at_v]
            scores = dot_nt(query, keys) * factor
            last = jnp.where(earlier | (marks[k : k + 1, :1] > 0), scores[:, seen - SPAN :], masked_score)
            scores = last if k == 0 else jnp.concatenate([scores[:, : seen - SPAN], last], axis=1)
            probs = jnp.exp(scores - stats[now, 1 + head : 2 + head])
            d_probs = dot_nt(dout, values)
            dots = jnp.sum(probs * d_probs, axis=1, keepdims=True)
            d_scores = (probs * (d_probs - dots)).astype(bf16)
            d_mix[now, at_q] = (jnp.dot(d_scores, keys, preferred_element_type=f32) * factor).astype(bf16)
            dk_acc[:seen] += dot_tn(d_scores, query)
            dv_acc[:seen] += dot_tn(probs.astype(bf16), dout)
        if end == blocks:
            d_mix[:, at_k] = (dk_acc[...] * factor).astype(bf16)
            d_mix[:, at_v] = dv_acc[...].astype(bf16)

    def d_normed1(part_of):
        if part_of == 0:
            loads[6].wait()
        tiled_nt(d_mix, upw, cot, d_mix.shape[1], 1024, 256, (part_of, part_of + 1, 2))
        if part_of == 1:
            next(third)

    def output_sums(part_of):
        if part_of == 0:
            loads[8].wait()
        tiled_nn(hid, n2, tot, 1024, 256, (part_of, part_of + 1, 2))
        if part_of == 1:
            next(fourth)

    grad1 = own_sum
    stat_sends, stat_recvs, dp_sends, dp_recvs, row_sends, row_recvs = [], [], [], [], [], []
    for step in range(1, row_count):
        target, source = (row + step) % row_count, (row + row_count - step) % row_count
        to, since = {"row": target}, {"row": source}
        stat_sends.append(put(stat_land.at[row], stat_land.at[row], p_send, p_recv, 43 + step - 1, to))
        stat_recvs.append(put(stat_land.at[source], stat_land.at[source], p_send, p_recv, 43 + step - 1, since))
        row_sends.append(put(small_out.at[row], small_out.at[row], p_send, p_recv, 50 + step - 1, to))
        row_recvs.append(put(small_out.at[source], small_out.at[source], p_send, p_recv, 50 + step - 1, since))
    for step in range(1, dp_count):
        target, source = (plane + step) % dp_count, (plane + dp_count - step) % dp_count
        dp_sends.append(put(dp_land.at[plane], dp_land.at[plane], p_send, p_recv, 47 + step - 1, {"dp": target}))
        dp_recvs.append(put(dp_land.at[source], dp_land.at[source], p_send, p_recv, 47 + step - 1, {"dp": source}))
    x_copy = put(small.at[pl.ds(0, 8)], x_land, p_send, p_recv, 46, partners()[0])

    def row_stats():
        next(third, None)
        scaled = grad1[...] * vec_all[0:1, here]
        first_sum = jnp.sum(scaled, axis=1, keepdims=True)
        second_sum = jnp.sum(scaled * std1_own[...].astype(f32), axis=1, keepdims=True)
        lane = lax.broadcasted_iota(jnp.int32, (rows, 128), 1)
        pair = jnp.where(lane == 0, first_sum, jnp.where(lane == 1, second_sum, 0.0))
        stat_land[row] = pair.T[:8]
        for copy in stat_sends:
            copy.start()

    def small_sums():
        small[...] = jnp.zeros_like(small)
        small[0:1, :] = jnp.sum(grad1[...] * std1_own[...].astype(f32), axis=0, keepdims=True)
        small[1:2, :] = jnp.sum(grad1[...], axis=0, keepdims=True)
        small[2:6, :] = sums[0:4, here]
        totals = jnp.sum(dup[...].astype(f32), axis=0, keepdims=True)
        for k in range(units // width):
            small[8 + k : 9 + k, :] = totals[:, k * width : (k + 1) * width]
        mixes = jnp.sum(d_mix[...].astype(f32), axis=0, keepdims=True)
        spot = 8 + units // width
        picked = [
            mixes[:, (head * 3 + kind) * HEAD : (head * 3 + kind + 1) * HEAD] for head in range(heads) for kind in (0, 2)
        ]
        small[spot : spot + 1, : 2 * heads * HEAD] = jnp.concatenate(picked, axis=1)
        x_copy.start()

    def tokens_out():
        for copy in stat_recvs:
            copy.wait_recv()
        both = stat_land[0]
        for k in range(1, row_count):
            both = both + stat_land[k]
        both = jnp.concatenate([both, jnp.zeros((120, rows), f32)], axis=0).T
        scaled = grad1[...] * vec_all[0:1, here]
        d_norm1 = inv1_own[...] * (
            scaled - both[:, 0:1] / full - std1_own[...].astype(f32) * (both[:, 1:2] / full)
        )
        tokens_block[...] = (dres_own[...] + d_norm1).astype(bf16)
        loads[10].start()

    def dp_start():
        x_copy.wait_recv()
        x_copy.wait_send()
        small[0:2, :] += x_land[0:2, :]
        dp_land[plane] = small[...]
        for copy in dp_sends:
            copy.start()

    def output_out():
        next(fourth, None)
        loads[10].wait()
        out_block[...] = (dres_own[...] + (own_sum[...] + down_bias[...])).astype(bf16)

    def rows_start():
        for copy in dp_recvs:
            copy.wait_recv()
        together = dp_land[0]
        for k in range(1, dp_count):
            together = together + dp_land[k]
        small_out[row] = together
        for copy in row_sends:
            copy.start()

    tasks = {
        6: [down_here],
        8: [lambda: uppers(0)],
        9: [lambda: uppers(1)],
        10: [lambda: d_normed2(0)],
        11: [lambda: d_normed2(1)],
        13: [lambda: next(first)],
        16: [lambda: next(first)],
        19: [gather_start],
        22: [lambda: next(second)],
        24: [lambda: next(second)],
        25: [lambda: next(second, None), loads[8].start],
        26: [lambda: norm_back(0)],
        27: [lambda: norm_back(1)],
        28: [d_attended],
        29: [lambda: attention_back(0, 0, blocks)],
        30: [lambda: attention_back(1, 0, blocks)],
        31: [lambda: output_sums(0), loads[7].wait],
        32: [lambda: d_normed1(0)],
        33: [lambda: d_normed1(1)],
        34: [lambda: next(third)],
        35: [lambda: output_sums(1)],
        36: [lambda: next(fourth)],
        37: [lambda: next(third)],
        39: [lambda: next(fourth)],
        40: [row_stats],
        41: [small_sums],
        42: [tokens_out],
        43: [dp_start],
        44: [output_out],
        45: [rows_start],
    }
    sums[...] = jnp.zeros_like(sums)
    loads[0].wait()
    loads[1].wait()
    produce(0)
    for k in range(ahead):
        launch(k)
    for u in range(pieces):
        pass_on(u)
        for task in tasks.get(u, ()):
            task()
    finish_inner(pieces - 2)
    finish_inner(pieces - 1)
    finish_outer(pieces - 3)
    finish_outer(pieces - 2)
    finish_outer(pieces - 1)
    for copy in row_recvs:
        copy.wait_recv()
    for copy in down_sends + stat_sends + dp_sends + row_sends:
        copy.wait_send()

    @pl.when(outer)
    def _():
        for u in range(pieces - 4 * g_slots, pieces):
            inward(u).wait_send()
        for u in range(pieces):
            sent_home(u, b_land.at[u])

    @pl.when(inner)
    def _():
        for u in range(pieces - t_slots, pieces):
            outward(u).wait_send()
            sent_home(u, t.at[u % t_slots])

    for u in range(pieces):
        for step in range(1, row_count):
            source = (row + row_count - step) % row_count
            put(t.at[0, source], place(u, source), a_send, a_recv, 3 * u + step - 1, {"row": source}).wait_recv()


def backward_plane(
    cid, hid, cot, slope, n2, upw, std, n1, qkvw, down_nat, resid_own, attended, outw, mixed, std1_own, stats, marks, vec_all, inv1_own, down_bias
):
    f32, bf16 = jnp.float32, jnp.bfloat16
    length, full = cot.shape
    rows, width = length // lax.axis_size("col"), full // lax.axis_size("row")
    row_count, dp_count = full // width, lax.axis_size("dp")
    counts = (slope.shape[1] // CHUNK, slope.shape[1] // CHUNK, attended.shape[1] // CHUNK, mixed.shape[1] // CHUNK)
    total = sum(counts)
    unit = (row_count, LINES, CHUNK)
    shape = jax.ShapeDtypeStruct
    away, near = pl.BlockSpec(memory_space=pl.ANY), pl.BlockSpec(memory_space=pltpu.VMEM)
    vmem, dma = pltpu.VMEM, pltpu.SemaphoreType.DMA
    sets = [
        vmem((4, rows, width), bf16),
        vmem((rows, width), bf16),
        vmem((rows // 2, width), bf16),
        vmem((rows // 2, width), bf16),
        vmem((2, rows, width), bf16),
        vmem((2, rows, width), bf16),
    ]
    return pl.pallas_call(
        functools.partial(backward_kernel, counts),
        out_shape=[
            shape((row_count * counts[0], CHUNK, width), bf16),
            shape((2, CHUNK, row_count * counts[1] * CHUNK), bf16),
            shape((row_count * counts[2], CHUNK, width), bf16),
            shape((2, CHUNK, row_count * counts[3] * CHUNK), bf16),
            shape((4 * total,) + unit, bf16),
            shape((hid.shape[1], full), bf16),
            shape((rows, width), bf16),
            shape((rows, width), bf16),
            shape((row_count, 16, width), f32),
        ],
        in_specs=[away] * 14 + [near] * 5,
        out_specs=[away] * 6 + [near] * 3,
        scratch_shapes=[
            vmem((length, full), bf16),
            vmem((length, full), bf16),
            vmem((length, full), bf16),
            vmem((length, full), bf16),
            vmem((length, full), bf16),
            vmem(upw.shape, bf16),
            vmem(hid.shape, bf16),
            vmem(slope.shape, bf16),
            vmem(attended.shape, bf16),
            vmem(outw.shape, bf16),
            vmem(mixed.shape, bf16),
            vmem(std1_own.shape, bf16),
            vmem(attended.shape, bf16),
            vmem(mixed.shape, bf16),
            vmem((length, HEAD), f32),
            vmem((length, HEAD), f32),
            vmem((2, row_count, width // CHUNK, CHUNK, CHUNK), bf16),
            vmem((3,) + unit, bf16),
            vmem((4,) + unit, bf16),
            vmem((6,) + unit, bf16),
            vmem((6,) + unit, bf16),
        ]
        + sets
        + sets
        + [
            vmem((rows, width), f32),
            vmem((rows, width), f32),
            vmem((8, full), f32),
            vmem((16, width), f32),
            vmem((8, width), f32),
            vmem((dp_count, 16, width), f32),
            vmem((row_count, 8, rows), f32),
            dma((15,)),
            pltpu.SemaphoreType.REGULAR,
            dma((4 * total + 1,)),
            dma((12 * total,)),
            dma((12 * total,)),
            dma((12 * total,)),
            dma((12 * total,)),
            dma((53,)),
            dma((53,)),
        ],
        compiler_params=pltpu.CompilerParams(
            collective_id=cid, has_side_effects=True, vmem_limit_bytes=64 * 1024 * 1024 - 65536
        ),
        cost_estimate=pl.CostEstimate(flops=40_000_000_000, bytes_accessed=100_000_000, transcendentals=4_000_000),
    )(hid, cot, slope, n2, upw, std, n1, qkvw, down_nat, resid_own, attended, outw, mixed, std1_own, stats, marks, vec_all, inv1_own, down_bias)


class Moves:
    def __init__(self, source, target, cut, parts, sends, recvs, base):
        row, plane = lax.axis_index("row"), lax.axis_index("dp")
        side, core = row // 2, row % 2
        parity = plane % 2
        other = {"dp": plane + 1 - 2 * parity}
        twin = side * 2 + 1 - core
        far = ((1 - side) * 2 + core, (1 - side) * 2 + 1 - core)
        self.sibling = put(source(twin), target(row), sends, recvs, base, {"row": twin})
        self.sibling_in = put(source(twin), target(twin), sends, recvs, base, {"row": twin})
        self.outs, self.ins, self.passes, self.gets = [], [], [], []
        at = base + 1
        for step in range(parts // 2):
            for k, device in enumerate(far):
                mine, theirs = 2 * step + parity, 2 * step + 1 - parity
                there, here = cut(target(row), mine), cut(target(device), mine)
                self.outs.append(put(cut(source(device), mine), there, sends, recvs, at, {"row": device}))
                self.ins.append(put(cut(source(device), mine), here, sends, recvs, at, {"row": device}))
                self.passes.append(put(here, here, sends, recvs, at + 1, other))
                lands = cut(target(device), theirs)
                self.gets.append(put(lands, lands, sends, recvs, at + 1, other))
                at += 2

    @staticmethod
    def count(parts):
        return 1 + 2 * parts

    def start(self):
        self.sibling.start()
        self.start_far()

    def start_far(self):
        for copy in self.outs:
            copy.start()

    def forward(self, begin=0, end=None):
        for came, passed in list(zip(self.ins, self.passes))[begin:end]:
            came.wait_recv()
            passed.start()

    def finish(self):
        self.sibling_in.wait_recv()
        for copy in self.gets:
            copy.wait_recv()

    def drain(self):
        self.sibling.wait_send()
        for copy in self.outs + self.passes:
            copy.wait_send()


FAR_PARTS = 8


def forward_kernel(
    tokens,
    cot_in,
    ln1_gain,
    ln1_shift,
    out_bias_in,
    ln2_gain,
    ln2_shift,
    qv_bias,
    up_bias_in,
    spans,
    qkv_in,
    out_nat,
    up_nat,
    cot_all,
    n1_out,
    n2_out,
    std_out,
    upw_out,
    qkvw_out,
    outw_out,
    mixed_out,
    attended_out,
    hid_out,
    slope_out,
    stats,
    marks,
    vec_all,
    resid_own,
    std1_own,
    inv1_own,
    tok,
    n1,
    part,
    tot,
    qkvw,
    upw,
    outw,
    mixed,
    attended,
    hid,
    slope,
    own_sum,
    got,
    diag,
    hx,
    hy,
    ts,
    fx,
    qkv_raw,
    qkv_nat,
    mixed_bias,
    local_sem,
    w_send,
    w_recv,
    p_send,
    p_recv,
):
    f32, bf16 = jnp.float32, jnp.bfloat16
    plane, row, col = lax.axis_index("dp"), lax.axis_index("row"), lax.axis_index("col")
    side, core = row // 2, row % 2
    rows, width = tokens.shape
    length, full = tok.shape
    row_count = full // width
    heads_width = attended.shape[1]
    units = hid.shape[1]

    barrier = pltpu.get_barrier_semaphore()
    twins = ({"row": (1 - side) * 2 + 1 - core}, {"dp": plane + 1 - 2 * (plane % 2)})
    for partner in partners() + twins:
        pl.semaphore_signal(barrier, inc=1, device_id=partner, device_id_type=MESH)
    pl.semaphore_wait(barrier, 5)

    def cut_rows(ref, part):
        count = ref.shape[0] // FAR_PARTS
        return ref.at[strip(part * count, count)]

    per = qkvw.shape[1]
    count = Moves.count(FAR_PARTS)
    qkv_moves = Moves(
        lambda r: qkv_nat.at[:, strip(r * per, per)],
        lambda r: qkvw.at[strip(r * width, width), :],
        cut_rows,
        FAR_PARTS,
        w_send,
        w_recv,
        0,
    )
    out_moves = Moves(
        lambda r: out_nat.at[strip(r * heads_width, heads_width), :],
        lambda r: outw.at[:, strip(r * width, width)],
        cut_rows,
        FAR_PARTS,
        w_send,
        w_recv,
        count,
    )
    up_moves = Moves(
        lambda r: up_nat.at[:, strip(r * units, units)],
        lambda r: upw.at[strip(r * width, width), :],
        cut_rows,
        FAR_PARTS,
        w_send,
        w_recv,
        2 * count,
    )
    locals_ = [
        (qkv_nat.at[:, strip(row * per, per)], qkvw.at[strip(row * width, width), :]),
        (out_nat.at[strip(row * heads_width, heads_width), :], outw.at[:, strip(row * width, width)]),
        (up_nat.at[:, strip(row * units, units)], upw.at[strip(row * width, width), :]),
        (cot_in, block(cot_all, col, side, core, rows, width)),
        (n1, n1_out),
        (part, n2_out),
        (n1, std_out),
        (upw, upw_out),
        (qkvw, qkvw_out),
        (outw, outw_out),
        (mixed, mixed_out),
        (attended, attended_out),
        (hid, hid_out),
        (slope, slope_out),
        (qkv_in, qkv_raw),
    ]
    local = [pltpu.make_async_copy(a, b, local_sem.at[k]) for k, (a, b) in enumerate(locals_)]
    local[14].start()
    for k in range(1, 4):
        local[k].start()

    block(tok, col, side, core, rows, width)[...] = tokens[...]
    gather = spread_steps(tok, rows, width, p_send, p_recv, 0, mostly_x=True)
    next(gather)
    here = strip(row * width, width)
    vec_all[:, here] = jnp.zeros((vec_all.shape[0], width), f32)
    for k, vector in enumerate((ln1_gain, ln1_shift, out_bias_in, ln2_gain, ln2_shift)):
        vec_all[k : k + 1, here] = vector[...]
    vec_sends, vec_recvs = [], []
    for step in range(1, row_count):
        target, source = (row + step) % row_count, (row + row_count - step) % row_count
        here, there = vec_all.at[:, strip(row * width, width)], vec_all.at[:, strip(source * width, width)]
        vec_sends.append(put(here, here, p_send, p_recv, 10 + step - 1, {"row": target}))
        vec_recvs.append(put(there, there, p_send, p_recv, 10 + step - 1, {"row": source}))
        vec_sends[-1].start()
    out_moves.sibling.start()
    up_moves.sibling.start()
    local[14].wait()
    for kind in range(3):
        flat = qkv_raw[:, kind].reshape(width, qkv_raw.shape[2] * HEAD)
        for head in range(qkv_raw.shape[2]):
            qkv_nat[:, pl.ds((head * 3 + kind) * HEAD, HEAD)] = flat[:, head * HEAD : (head + 1) * HEAD]
    local[0].start()
    qkv_moves.sibling.start()
    qkv_moves.start_far()
    next(gather)
    next(gather)
    next(gather, None)
    for copy in vec_recvs:
        copy.wait_recv()
    lines = lax.broadcasted_iota(jnp.int32, marks.shape, 0) * SPAN
    found = jnp.zeros(marks.shape, f32)
    for k in range(spans.shape[1]):
        found = jnp.where(lines == spans[0:1, k : k + 1] // SPAN * SPAN, 1.0, found)
    marks[...] = found

    tile = 64
    gain1, shift1 = vec_all[0:1, :], vec_all[1:2, :]

    def norm1_step(k, none):
        at = strip(k * tile, tile)
        values = tok[at, :].astype(f32)
        center = jnp.sum(values, axis=1, keepdims=True) / full
        inverse = lax.rsqrt(jnp.sum(values * values, axis=1, keepdims=True) / full - center * center + epsilon)
        n1[at, :] = ((values - center) * inverse * gain1 + shift1).astype(bf16)

        @pl.when(k // (rows // tile) == col)
        def _():
            here = strip(k % (rows // tile) * tile, tile)
            std1_own[here, :] = ((tok[at, strip(row * width, width)].astype(f32) - center) * inverse).astype(bf16)
            inv1_own[here, :] = inverse

        return none

    half_steps = length // tile // 2
    quarter = half_steps // 2
    for k in range(4):
        qkv_moves.forward(2 * k, 2 * k + 1)
        lax.fori_loop(k * quarter, (k + 1) * quarter, norm1_step, 0)
        qkv_moves.forward(2 * k + 1, 2 * k + 2)
    local[4].start()
    out_moves.start_far()
    up_moves.start_far()
    qkv_moves.finish()
    local[0].wait()

    mixed_bias[...] = jnp.zeros_like(mixed_bias)
    for head in range(heads_width // HEAD):
        for k in range(2):
            lanes = pl.ds((head * 3 + 2 * k) * HEAD, HEAD)
            mixed_bias[:, lanes] = qv_bias[row * (heads_width // HEAD) + head, k : k + 1, :]
    up_bias = up_bias_in.at[:, strip(row * units, units)]

    def mixed_step(k, none):
        down, across = k // (per // CHUNK), k % (per // CHUNK)
        at, lanes = strip(down * rows, rows), strip(across * CHUNK, CHUNK)
        value = jnp.dot(n1[at, :], qkvw[:, lanes], preferred_element_type=f32)
        mixed[at, lanes] = (value + mixed_bias[:, lanes]).astype(bf16)
        return none

    lax.fori_loop(0, (length // rows) * (per // CHUNK), mixed_step, 0)
    local[8].start()
    local[10].start()
    local[4].wait()

    heads = heads_width // HEAD
    factor = 1.0 / math.sqrt(HEAD)
    blocks = length // SPAN
    spots = (SPAN, SPAN)
    earlier = lax.broadcasted_iota(jnp.int32, spots, 1) <= lax.broadcasted_iota(jnp.int32, spots, 0)

    def head_step(head, none):
        base = head * 3 * HEAD
        at_q, at_k, at_v = strip(base, HEAD), strip(base + HEAD, HEAD), strip(base + 2 * HEAD, HEAD)
        for k in range(blocks):
            here = pl.ds(k * SPAN, SPAN)
            seen = (k + 1) * SPAN
            scores = dot_nt(mixed[here, at_q], mixed[:seen, at_k]) * factor
            last = jnp.where(earlier | (marks[k : k + 1, :1] > 0), scores[:, seen - SPAN :], masked_score)
            scores = last if k == 0 else jnp.concatenate([scores[:, : seen - SPAN], last], axis=1)
            highest = jnp.max(scores, axis=1, keepdims=True)
            weights = jnp.exp(scores - highest)
            weight_sum = jnp.sum(weights, axis=1, keepdims=True)
            stats[here, 1 + head : 2 + head] = highest + jnp.log(weight_sum)
            value = jnp.dot((weights / weight_sum).astype(bf16), mixed[:seen, at_v], preferred_element_type=f32)
            attended[here, strip(head * HEAD, HEAD)] = value.astype(bf16)
        return none

    for head in range(heads):
        head_step(head, 0)
        if head == 0:
            out_moves.forward()
            up_moves.forward(0, 2)
    local[11].start()
    up_moves.forward(2, 4)
    out_moves.finish()
    local[1].wait()
    tiled_nn(attended, outw, part, rows, 512)
    local[9].start()
    add_up = reduce_steps(part, own_sum, got, diag, hx, hy, ts, fx, p_send, p_recv, 13)
    next(add_up)
    next(add_up)
    next(add_up)
    up_moves.forward(4, 8)
    next(add_up, None)
    block(tot, col, side, core, rows, width)[...] = own_sum[...].astype(bf16)
    again = spread_steps(tot, rows, width, p_send, p_recv, 23)
    next(again)
    next(again)
    local[3].wait()
    cot_gather = spread_steps(cot_all, rows, width, p_send, p_recv, 33)
    next(cot_gather)
    next(again)
    next(again, None)

    gain2, shift2, out_bias = vec_all[3:4, :], vec_all[4:5, :], vec_all[2:3, :]

    def norm2_step(k, none):
        at = strip(k * tile, tile)
        values = tok[at, :].astype(f32) + (tot[at, :].astype(f32) + out_bias)
        center = jnp.sum(values, axis=1, keepdims=True) / full
        inverse = lax.rsqrt(jnp.sum(values * values, axis=1, keepdims=True) / full - center * center + epsilon)
        standard = (values - center) * inverse
        stats[at, 0:1] = inverse
        n1[at, :] = standard.astype(bf16)
        part[at, :] = (standard * gain2 + shift2).astype(bf16)

        @pl.when(k // (rows // tile) == col)
        def _():
            own = strip(row * width, width)
            here = strip(k % (rows // tile) * tile, tile)
            resid_own[here, :] = tok[at, own].astype(f32) + (tot[at, own].astype(f32) + vec_all[2:3, own])

        return none

    lax.fori_loop(0, 2 * half_steps, norm2_step, 0)
    local[5].start()
    local[6].start()
    next(cot_gather)
    up_moves.finish()
    local[2].wait()
    local[7].start()

    def up_step(k, none):
        down, across = k // (units // CHUNK), k % (units // CHUNK)
        at, lanes = strip(down * rows, rows), strip(across * CHUNK, CHUNK)
        u = jnp.dot(part[at, :], upw[:, lanes], preferred_element_type=f32) + up_bias[:, lanes]
        bent = jnp.tanh(0.7978845608028654 * (u + 0.044715 * u * u * u))
        hid[at, lanes] = (0.5 * u * (1.0 + bent)).astype(bf16)
        inside = 0.7978845608028654 * (1.0 + 3 * 0.044715 * u * u)
        slope[at, lanes] = (0.5 * (1.0 + bent) + 0.5 * u * (1.0 - bent * bent) * inside).astype(bf16)
        return none

    lax.fori_loop(0, (length // rows) * (units // CHUNK), up_step, 0)
    local[12].start()
    local[13].start()
    next(cot_gather)
    next(cot_gather, None)
    for k in range(5, 14):
        local[k].wait()
    for moves in (qkv_moves, out_moves, up_moves):
        moves.drain()
    for copy in vec_sends:
        copy.wait_send()


def forward_plane(cid, tokens, cot, vectors, qv_bias, up_bias, spans, qkv_in, out_nat, up_nat):
    f32, bf16 = jnp.float32, jnp.bfloat16
    rows, width = tokens.shape
    row_count = lax.axis_size("row")
    length, full = rows * lax.axis_size("col"), width * row_count
    per, heads_width, units = qkv_in.shape[1] * qkv_in.shape[2] * HEAD // row_count, out_nat.shape[0] // row_count, up_nat.shape[1] // row_count
    shape = jax.ShapeDtypeStruct
    away, near = pl.BlockSpec(memory_space=pl.ANY), pl.BlockSpec(memory_space=pltpu.VMEM)
    vmem, dma = pltpu.VMEM, pltpu.SemaphoreType.DMA
    wide = shape((length, full), bf16)
    moved = 3 * Moves.count(FAR_PARTS)
    return pl.pallas_call(
        forward_kernel,
        out_shape=[
            wide,
            wide,
            wide,
            wide,
            shape((full, units), bf16),
            shape((full, per), bf16),
            shape((heads_width, full), bf16),
            shape((length, per), bf16),
            shape((length, heads_width), bf16),
            shape((length, units), bf16),
            shape((length, units), bf16),
            shape((length, 8), f32),
            shape((8, 128), f32),
            shape((8, full), f32),
            shape((rows, width), f32),
            shape((rows, width), bf16),
            shape((rows, 1), f32),
        ],
        in_specs=[near] * (5 + len(vectors)) + [away] * 3,
        out_specs=[away] * 11 + [near] * 6,
        scratch_shapes=[
            vmem((length, full), bf16),
            vmem((length, full), bf16),
            vmem((length, full), bf16),
            vmem((length, full), bf16),
            vmem((full, per), bf16),
            vmem((full, units), bf16),
            vmem((heads_width, full), bf16),
            vmem((length, per), bf16),
            vmem((length, heads_width), bf16),
            vmem((length, units), bf16),
            vmem((length, units), bf16),
            vmem((rows, width), f32),
            vmem((4, rows, width), bf16),
            vmem((rows, width), bf16),
            vmem((rows // 2, width), bf16),
            vmem((rows // 2, width), bf16),
            vmem((2, rows, width), bf16),
            vmem((2, rows, width), bf16),
            vmem(qkv_in.shape, bf16),
            vmem((width, row_count * per), bf16),
            vmem((1, per), f32),
            dma((15,)),
            dma((moved,)),
            dma((moved,)),
            dma((43,)),
            dma((43,)),
        ],
        compiler_params=pltpu.CompilerParams(
            collective_id=cid, has_side_effects=True, vmem_limit_bytes=60 * 1024 * 1024
        ),
        cost_estimate=pl.CostEstimate(flops=10_000_000_000, bytes_accessed=60_000_000, transcendentals=4_000_000),
    )(tokens, cot, *[vector[None] for vector in vectors], qv_bias, up_bias[None], spans, qkv_in, out_nat, up_nat)


def results_kernel(
    down, up, out, output, tokens, qkv, small, down_result, up_result, out_result, output_result, tokens_result, qkv_result, *vectors
):
    *sums, up_bias, qv_bias = vectors
    f32 = jnp.float32
    down_result[...] = down[...].astype(f32)
    up_result[...] = up[...].astype(f32)
    out_result[...] = out[...].astype(f32)
    output_result[...] = output[...]
    tokens_result[...] = tokens[...]
    for head in range(qkv_result.shape[2]):
        for kind in range(3):
            begin = (head * 3 + kind) * HEAD
            qkv_result[:, kind, head, :] = qkv[:, begin : begin + HEAD].astype(f32)

    @pl.when(pl.program_id(0) == 0)
    def _():
        row = lax.axis_index("row")
        for k, result in enumerate(sums):
            result[...] = small[row, k : k + 1, :]
        count, _, width = small.shape
        lines = up_bias.shape[1] // (count * width)
        heads = qv_bias.shape[0] // count
        for source in range(count):
            for k in range(lines):
                begin = (source * lines + k) * width
                up_bias[:, begin : begin + width] = small[source, 8 + k : 9 + k, :]
            for head in range(heads):
                for k in range(2):
                    begin = (head * 2 + k) * HEAD
                    line = small[source, 8 + lines : 9 + lines, begin : begin + HEAD]
                    qv_bias[source * heads + head, k : k + 1, :] = line


def results(down, up, out, output, tokens, qkv, small):
    f32 = jnp.float32
    shape = jax.ShapeDtypeStruct
    rows, heads = qkv.shape[0], qkv.shape[1] // (3 * HEAD)
    width, units = small.shape[2], up.shape[1]
    steps = 8

    def cut(array):
        return pl.BlockSpec((array.shape[0] // steps, array.shape[1]), lambda k: (k, 0))

    def whole(*dims):
        return pl.BlockSpec(dims, lambda k: (0,) * len(dims))

    line = whole(1, width)
    *made, up_bias, qv_bias = pl.pallas_call(
        results_kernel,
        grid=(steps,),
        out_shape=[shape(a.shape, f32) for a in (down, up, out)]
        + [shape(a.shape, a.dtype) for a in (output, tokens)]
        + [shape((rows, 3, heads, HEAD), f32)]
        + [shape((1, width), f32)] * 6
        + [shape((1, units), f32), shape((heads, 2, HEAD), f32)],
        in_specs=[cut(a) for a in (down, up, out, output, tokens, qkv)] + [whole(*small.shape)],
        out_specs=[cut(a) for a in (down, up, out, output, tokens)]
        + [pl.BlockSpec((rows // steps, 3, heads, HEAD), lambda k: (k, 0, 0, 0))]
        + [line] * 6
        + [whole(1, units), whole(heads, 2, HEAD)],
        compiler_params=pltpu.CompilerParams(vmem_limit_bytes=63 * 1024 * 1024),
    )(down, up, out, output, tokens, qkv, small)
    made[5] = jnp.swapaxes(made[5], 1, 2)
    return made[:6], [sums[0] for sums in made[6:]], up_bias[0], qv_bias


def plane_plan(
    tokens,
    ln1_gain,
    ln1_shift,
    qkv_weight,
    qv_bias,
    out_weight,
    out_bias,
    ln2_gain,
    ln2_shift,
    up_weight,
    up_bias,
    down_weight,
    down_bias,
    span_starts,
    cotangent,
):
    width = tokens.shape[1]
    (
        cot_all, n1, n2, standard2, upw, qkvw, outw, mixed, attended, hidden, slope,
        stats, marks, vec_all, residual_own, standard1_own, inverse1_own,
    ) = forward_plane(
        1,
        tokens,
        cotangent,
        (ln1_gain, ln1_shift, out_bias, ln2_gain, ln2_shift),
        qv_bias,
        up_bias,
        span_starts,
        jnp.swapaxes(qkv_weight, 1, 2),
        out_weight.reshape(-1, width),
        up_weight,
    )
    down_grad, up_grad, out_grad, qkv_grad, _, _, output, tokens_grad, small = backward_plane(
        2, hidden, cot_all, slope, n2, upw, standard2, n1, qkvw, down_weight, residual_own, attended, outw, mixed, standard1_own,
        stats, marks, vec_all, inverse1_own, down_bias[None],
    )
    grads, sums, up_bias_grad, qv_bias_grad = results(
        down_grad.reshape(-1, width), up_grad.reshape(width, -1), out_grad.reshape(-1, width), output, tokens_grad,
        qkv_grad.reshape(width, -1), small
    )
    return (
        grads[3],
        grads[4],
        sums[0],
        sums[1],
        grads[5],
        qv_bias_grad,
        grads[2].reshape(out_weight.shape),
        sums[4],
        sums[2],
        sums[3],
        grads[1],
        up_bias_grad,
        grads[0],
        sums[5],
    )


def solution(mesh):
    sizes = dict(mesh.shape)
    flat = sizes == {"dp": 4, "row": 4, "col": 2}
    per_device = plane_plan if flat else general_plan
    placed = (
        P(("dp", "col"), "row"),
        P("row"),
        P("row"),
        P("row", "col", None, None),
        P("col", None, None),
        P("col", None, "row"),
        P("row"),
        P("row"),
        P("row"),
        P("row", "col"),
        P("col"),
        P("col", "row"),
        P("row"),
        P("dp", None),
        P(("dp", "col"), "row"),
    )
    return jax.shard_map(
        per_device,
        mesh=mesh,
        in_specs=placed,
        out_specs=(
            P(("dp", "col"), "row"),
            P(("dp", "col"), "row"),
            P("row"),
            P("row"),
            P("row", "col", None, None),
            P("col", None, None),
            P("col", None, "row"),
            P("row"),
            P("row"),
            P("row"),
            P("row", "col"),
            P("col"),
            P("col", "row"),
            P("row"),
        ),
        check_vma=False,
    )
```
